32 devices in a mesh: batch: 4 (over y, core), wide: 8 (over z, x).
Axes of the slice: x: 2, y: 2, z: 4, core: 2. Of those that a mesh axis runs over, the one named last changes fastest.
Arguments:
- inputs: bfloat16 [32, 512, 768], P(('batch', 'wide')), may hold values from -6 to 6
- lengths: int32 [32], P(('batch', 'wide')), may hold values from 1 to 512, 6553 in all
- cotangent: bfloat16 [32, 512, 768], P(('batch', 'wide')), may hold values from -6 to 6
- w_qkv: bfloat16 [768, 2304], P(('batch', 'wide')), may hold values from -0.21875 to 0.21875
- w_out: bfloat16 [768, 768], P(('batch', 'wide')), may hold values from -3.5 to 3.5
- conv_taps: bfloat16 [2304, 3], P(('batch', 'wide')), may hold values from -3.5 to 3.5
- gain_one: bfloat16 [768], P(('batch', 'wide')), may hold values from 0.099609375 to 1.8984375
- gain_two: bfloat16 [768], P(('batch', 'wide')), may hold values from 0.099609375 to 1.8984375
- w_in: bfloat16 [768, 3072], P(None, 'wide'), may hold values from -0.21875 to 0.21875
- w_fc2: bfloat16 [3072, 768], P('wide'), may hold values from -0.109375 to 0.109375
Outputs:
- output: bfloat16 [32, 512, 768], P(('batch', 'wide'))
- grad_inputs: bfloat16 [32, 512, 768], P(('batch', 'wide'))
- grad_w_qkv: float32 [768, 2304], P(('batch', 'wide'))
- grad_w_out: float32 [768, 768], P(('batch', 'wide'))
- grad_conv_taps: float32 [2304, 3], P(('batch', 'wide'))
- grad_gain_one: float32 [768], P(('batch', 'wide'))
- grad_gain_two: float32 [768], P(('batch', 'wide'))
- grad_w_in: float32 [768, 3072], P('batch', 'wide')
- grad_w_fc2: float32 [3072, 768], P('wide', 'batch')
The draws below stay inside these ranges and needn't reach their ends.
Inputs may be any that keep to these rules, and one draw needn't show every extreme that they name: lengths[s] is the number of real tokens of sequence s; the longest has exactly 512.
All inputs are finite; a program needn't handle non-finite values. No bound on the sum of `lengths` on one device may be relied on, other than what follows from the above.
Results may differ from the reference program's by a relative error of at most 0.017.
Values may be sent and summed in bfloat16 or wider, within the bound.
No kernel may reach another device: no remote copies, remote signals or barrier semaphores. Data moves between devices by JAX's collectives and lax.ppermute only.
A program may use at most 256 MiB of HBM per device.

```python
import math
import jax
import jax.numpy as jnp
import numpy as np
from jax import lax

D = 768
HEADS = 12
HD = 64
FF = 3072
S = 512
SEQS = 32


def shard_levels(rng, extent, cuts, smallest, high):
    factor_of = 1.0
    for position, blocks in cuts:
        steps = jax.random.uniform(jax.random.fold_in(jax.random.fold_in(rng, 6), position), (blocks,), jnp.float32, smallest / len(cuts), high / len(cuts))
        factor_of = factor_of * jnp.repeat(jnp.exp(steps), extent[position] // blocks).reshape((-1,) + (1,) * (len(extent) - 1 - position))
    return factor_of


def length_profile(number_of, total, bound, skew):
    weights = [(1 << 20) // math.isqrt(standing ** skew) + 1 for standing in range(2, number_of + 1)]
    surplus, holding = total - bound - (number_of - 1), [1] * (number_of - 1)
    while surplus > 0:
        movable = [i for i in range(number_of - 1) if holding[i] < bound]
        pool, budget = sum([weights[i] for i in movable]), surplus
        for i in movable:
            extra = min(bound - holding[i], max(1, budget * weights[i] // pool), surplus)
            holding[i] = holding[i] + extra
            surplus = surplus - extra
    return np.array([bound] + holding)


def uneven_parts(stream_key, amount, total, bound, slope):
    if amount == 2:
        one = jax.random.randint(stream_key, (), max(1, total - bound), min(bound, total - 1) + 1)
        return jnp.stack([one, total - one])
    sizes = jnp.asarray(length_profile(amount, total, bound, slope), jnp.int32)
    couples = (amount - 1) // 2
    source_of, taker = sizes[1:1 + 2 * couples:2], sizes[2:2 + 2 * couples:2]
    slack = jnp.minimum(source_of - 1, bound - taker)
    shifted = jax.random.randint(jax.random.fold_in(stream_key, 1), (couples,), 0, 1 << 20) % (slack + 1)
    sizes = sizes.at[1:1 + 2 * couples:2].set(source_of - shifted).at[2:2 + 2 * couples:2].set(taker + shifted)
    return sizes[jax.random.permutation(jax.random.fold_in(stream_key, 2), amount)]


def centred(rng, dims, width, most, shards=(), kind=jnp.bfloat16):
    array = jax.random.normal(rng, dims, jnp.float32) * width
    if len(shards) > 0:
        array = shard_levels(rng, dims, shards, -0.22, 0.18) * array
    return jnp.clip(array, min=-most, max=most).astype(kind)


def setup_inputs(seed: int = 0) -> dict:
    streams_of = jax.random.split(jax.random.key(seed), 11)
    inputs = centred(streams_of[0], (SEQS, S, D), 1.0, 6.0, ((0, 32),))
    lengths = uneven_parts(streams_of[1], SEQS, SEQS * S * 2 // 5, S, 2).astype(jnp.int32)
    cotangent = centred(streams_of[2], (SEQS, S, D), 1.0, 6.0, ((0, 32),))
    w_qkv = centred(streams_of[3], (D, 3 * D), D ** -0.5, 0.21875, ((0, 32),))
    w_out = centred(streams_of[4], (D, D), (D // 256) ** -0.5, 3.5, ((0, 32),))
    conv_taps = centred(streams_of[5], (3 * D, 3), 3 ** -0.5, 3.5, ((0, 32),))
    gain_one = jnp.clip(1.0 + 0.18 * jax.random.normal(streams_of[6], (D,), jnp.float32), 0.099609375, 1.8984375).astype(jnp.bfloat16)
    gain_two = jnp.clip(1.0 + 0.18 * jax.random.normal(streams_of[7], (D,), jnp.float32), 0.099609375, 1.8984375).astype(jnp.bfloat16)
    w_in = centred(streams_of[8], (D, FF), D ** -0.5, 0.21875, ((1, 8),))
    w_fc2 = centred(streams_of[9], (FF, D), FF ** -0.5, 0.109375, ((0, 8),))
    return dict(inputs=inputs, lengths=lengths, cotangent=cotangent, w_qkv=w_qkv, w_out=w_out, conv_taps=conv_taps, gain_one=gain_one, gain_two=gain_two, w_in=w_in, w_fc2=w_fc2)


@jax.custom_vjp
def low(v):
    return lax.optimization_barrier(v.astype(jnp.bfloat16)).astype(jnp.float32)

@jax.custom_vjp
def low_back(v):
    return v

def low_keep(v):
    return (low(v), None)

def low_pass(kept, grad):
    return (grad,)

def back_keep(v):
    return (v, None)

def back_low(kept, grad):
    return (low(grad),)
low.defvjp(low_keep, low_pass)
low_back.defvjp(back_keep, back_low)
epsilon = 1e-05
highest = lax.Precision.HIGHEST

def layer_norm(values_in, gain_vec):
    centered = values_in - lax.optimization_barrier(jnp.mean(values_in, axis=-1, keepdims=True))
    variance = lax.optimization_barrier(jnp.mean(centered * centered, axis=-1, keepdims=True))
    return centered * lax.rsqrt(variance + epsilon) * gain_vec

def causal_taps(signal, taps):
    seq_length = signal.shape[1]
    padded = jnp.pad(signal, ((0, 0), (2, 0), (0, 0)))
    return padded[:, 2:, :] * taps[:, 0] + padded[:, 1:seq_length + 1, :] * taps[:, 1] + padded[:, :seq_length, :] * taps[:, 2]

def attend(query, keys, values, lens):
    seq_count, seq_length = (query.shape[0], query.shape[1])
    rows_block = min(512, seq_length)
    num_blocks = seq_length // rows_block
    key_pos = jnp.arange(seq_length)
    key_live = key_pos[None, :] < lens[:, None]

    def one_block(element):
        query_block, start_row = element
        scores = jnp.einsum('nqhd,nkhd->nhqk', query_block, keys, precision=highest) * 0.125
        scores = low_back(scores)
        query_pos = start_row + jnp.arange(rows_block)
        allowed = (key_pos[None, :] <= query_pos[:, None])[None, None] & key_live[:, None, None, :]
        masked = jnp.where(allowed, scores, -1e+30)
        top_score = lax.optimization_barrier(jnp.max(masked, axis=-1, keepdims=True))
        exp_terms = jnp.exp(masked - top_score)
        probs = low(exp_terms / lax.optimization_barrier(jnp.sum(exp_terms, axis=-1, keepdims=True)))
        return jnp.einsum('nhqk,nkhd->nqhd', probs, values, precision=highest)
    stacked = query.reshape(seq_count, num_blocks, rows_block, HEADS, HD).transpose(1, 0, 2, 3, 4)
    starts = jnp.arange(num_blocks) * rows_block
    results = lax.map(jax.checkpoint(one_block), (stacked, starts))
    return results.transpose(1, 0, 2, 3, 4).reshape(seq_count, seq_length, HEADS * HD)

def forward(inputs, lens, w_qkv, w_out, conv_taps, gain_one, gain_two, w_in, w_fc2):
    seq_count, seq_length = (inputs.shape[0], inputs.shape[1])
    live = (jnp.arange(seq_length)[None, :] < lens[:, None]).astype(inputs.dtype)
    normed_one = low(layer_norm(inputs, gain_one))
    projected = low_back(jnp.einsum('nsd,de->nse', normed_one, w_qkv, precision=highest))
    mixed = low(causal_taps(projected, conv_taps))
    query = mixed[..., :D].reshape(seq_count, seq_length, HEADS, HD)
    keys = mixed[..., D:2 * D].reshape(seq_count, seq_length, HEADS, HD)
    values = mixed[..., 2 * D:].reshape(seq_count, seq_length, HEADS, HD)
    attended = low_back(low(attend(query, keys, values, lens)))
    branch_attn = low_back(jnp.einsum('nsd,de->nse', attended, w_out, precision=highest))
    residual = inputs + branch_attn
    normed_two = low(layer_norm(residual, gain_two))
    pre_act = low_back(jnp.einsum('nsd,df->nsf', normed_two, w_in, precision=highest))
    activ = low(jnp.square(jax.nn.relu(pre_act)))
    branch_ffn = jnp.einsum('nsf,fd->nsd', activ, w_fc2, precision=highest)
    return live[..., None] * (residual + branch_ffn)

def reference(inputs, lengths, cotangent, w_qkv, w_out, conv_taps, gain_one, gain_two, w_in, w_fc2):
    group = math.gcd(SEQS, max(1, 4096 // S))
    rounds = SEQS // group
    params = tuple((weight_arr.astype(jnp.float32) for weight_arr in (w_qkv, w_out, conv_taps, gain_one, gain_two, w_in, w_fc2)))

    def step(totals, element):
        inputs_block, lens_block, cot_block = element

        def run(inputs_f, *weights_f):
            return forward(inputs_f, lens_block, *weights_f)
        result, pullback = jax.vjp(run, inputs_block.astype(jnp.float32), *params)
        grads = pullback(cot_block.astype(jnp.float32))
        new_totals = jax.tree.map(jnp.add, totals, tuple(grads[1:]))
        return (new_totals, (result.astype(jnp.bfloat16), grads[0].astype(jnp.bfloat16)))
    init = tuple((jnp.zeros(weight_arr.shape, jnp.float32) for weight_arr in params))
    totals, (results, grad_in) = lax.scan(step, init, (inputs.reshape(rounds, group, S, D), lengths.reshape(rounds, group), cotangent.reshape(rounds, group, S, D)))
    return (results.reshape(SEQS, S, D), grad_in.reshape(SEQS, S, D), totals[0], totals[1], totals[2], totals[3], totals[4], totals[5], totals[6])
```

```python
import functools
import jax
import jax.numpy as jnp
from jax import lax
from jax.experimental import pallas as pl
from jax.experimental.pallas import tpu as pltpu
from jax.sharding import PartitionSpec as P

HEADS = 12
HD = 64


epsilon = 1e-05


def contract_first(left, right):
    return lax.dot_general(
        left, right, (((0,), (0,)), ((), ())), preferred_element_type=jnp.float32
    )


def contract_last(left, right):
    return lax.dot_general(
        left, right, (((1,), (1,)), ((), ())), preferred_element_type=jnp.float32
    )


def norm_parts(values_in):
    centered = values_in - jnp.mean(values_in, axis=-1, keepdims=True)
    inv_std = lax.rsqrt(jnp.mean(centered * centered, axis=-1, keepdims=True) + epsilon)
    return (centered * inv_std, inv_std)


def norm_back(grad_normed, gain_vec, normed_hat, inv_std):
    grad_hat = grad_normed * gain_vec
    mean_first = jnp.mean(grad_hat, axis=-1, keepdims=True)
    mean_second = jnp.mean(grad_hat * normed_hat, axis=-1, keepdims=True)
    grad_value = inv_std * (grad_hat - mean_first - normed_hat * mean_second)
    return (grad_value, jnp.sum(grad_normed * normed_hat, axis=0))


def shift_down(signal, steps):
    filler = jnp.zeros((steps, signal.shape[1]), signal.dtype)
    return jnp.concatenate([filler, signal[:-steps]], axis=0)


def shift_up(signal, steps):
    filler = jnp.zeros((steps, signal.shape[1]), signal.dtype)
    return jnp.concatenate([signal[steps:], filler], axis=0)


def scores_block(query_block, keys, start_row, seq_live):
    rows_block = query_block.shape[0]
    scores = (
        jnp.einsum("qhd,khd->hqk", query_block, keys, preferred_element_type=jnp.float32) * 0.125
    )
    query_pos = start_row + jnp.arange(rows_block)
    key_pos = jnp.arange(keys.shape[0])
    allowed = (key_pos[None, :] <= query_pos[:, None]) & (key_pos[None, :] < seq_live)
    return (scores, allowed[None])


def shards(inputs, lengths, cotangent, w_qkv, w_out, conv_taps, gain_one, gain_two, w_in, w_fc2):
    full_qkv, full_out, full_taps, full_gain_one, full_gain_two = (
        lax.all_gather(w_qkv, ("batch", "wide"), axis=0, tiled=True),
        lax.all_gather(w_out, ("batch", "wide"), axis=0, tiled=True),
        lax.all_gather(conv_taps, ("batch", "wide"), axis=0, tiled=True),
        lax.all_gather(gain_one, ("batch", "wide"), axis=0, tiled=True),
        lax.all_gather(gain_two, ("batch", "wide"), axis=0, tiled=True),
    )
    seq_length, width = (inputs.shape[1], inputs.shape[2])
    tokens_in = inputs[0].astype(jnp.float32)
    seq_live = lengths[0]
    live_rows = jnp.arange(seq_length) < seq_live
    taps = full_taps.astype(jnp.float32)
    gain_first = full_gain_one.astype(jnp.float32)
    gain_second = full_gain_two.astype(jnp.float32)
    hat_one, inv_one = norm_parts(tokens_in)
    normed_one = (hat_one * gain_first).astype(jnp.bfloat16)
    projected = jnp.dot(normed_one, full_qkv, preferred_element_type=jnp.float32)
    mixed = (
        projected * taps[:, 0]
        + shift_down(projected, 1) * taps[:, 1]
        + shift_down(projected, 2) * taps[:, 2]
    ).astype(jnp.bfloat16)
    query = mixed[:, :width].reshape(seq_length, HEADS, HD)
    keys = mixed[:, width : 2 * width].reshape(seq_length, HEADS, HD)
    values = mixed[:, 2 * width :].reshape(seq_length, HEADS, HD)
    rows_block = min(512, seq_length)
    block_index = 0
    start_row = block_index * rows_block
    scores, allowed = scores_block(query, keys, start_row, seq_live)
    masked = jnp.where(allowed, scores, -1e30)
    top_score = jnp.max(masked, axis=-1, keepdims=True)
    exp_terms = jnp.exp(masked - top_score)
    row_totals = jnp.sum(exp_terms, axis=-1, keepdims=True)
    probs_low = (exp_terms / row_totals).astype(jnp.bfloat16)
    out_parts = jnp.einsum("hqk,khd->qhd", probs_low, values, preferred_element_type=jnp.float32)
    lse_parts = [top_score + jnp.log(row_totals)]
    attended_low = out_parts.reshape(seq_length, width).astype(jnp.bfloat16)
    branch_attn = jnp.dot(attended_low, full_out, preferred_element_type=jnp.float32)
    residual = tokens_in + branch_attn
    hat_two, inv_two = norm_parts(residual)
    normed_two = (hat_two * gain_second).astype(jnp.bfloat16)
    grad_out = jnp.where(live_rows[:, None], cotangent[0], jnp.zeros_like(cotangent[0]))
    row_set = lax.all_gather(normed_two[None], "wide", axis=0, tiled=True).reshape(-1, width)
    pre_act = jnp.dot(row_set, w_in, preferred_element_type=jnp.float32)
    activ = jnp.square(jax.nn.relu(pre_act)).astype(jnp.bfloat16)
    piece = activ
    branch_ffn = lax.psum_scatter(
        jnp.dot(piece, w_fc2, preferred_element_type=jnp.float32).astype(jnp.bfloat16),
        "wide",
        scatter_dimension=0,
        tiled=True,
    ).astype(jnp.float32)
    grad_set = lax.all_gather(grad_out[None], "wide", axis=0, tiled=True).reshape(-1, width)
    grad_act = contract_last(grad_set, w_fc2)
    grad_fc2_part = contract_first(activ, grad_set)
    grad_pre = (grad_act * 2.0 * jax.nn.relu(pre_act)).astype(jnp.bfloat16)
    grad_in_part = contract_first(row_set, grad_pre)
    piece = grad_pre
    grad_normed_two = lax.psum_scatter(
        contract_last(piece, w_in).astype(jnp.bfloat16), "wide", scatter_dimension=0, tiled=True
    ).astype(jnp.float32)
    grad_w_in, grad_w_fc2 = (
        lax.psum_scatter(
            grad_in_part.astype(jnp.bfloat16), "batch", scatter_dimension=0, tiled=True
        ).astype(jnp.float32),
        lax.psum_scatter(
            grad_fc2_part.astype(jnp.bfloat16), "batch", scatter_dimension=1, tiled=True
        ).astype(jnp.float32),
    )
    output = jnp.where(live_rows[:, None], residual + branch_ffn, 0.0).astype(jnp.bfloat16)[None]
    grad_ln_two, grad_gain_second = norm_back(grad_normed_two, gain_second, hat_two, inv_two)
    grad_residual = grad_out.astype(jnp.float32) + grad_ln_two
    grad_branch = grad_residual.astype(jnp.bfloat16)
    grad_w_out_part = contract_first(attended_low, grad_branch)
    grad_attended = contract_last(grad_branch, full_out).astype(jnp.bfloat16)
    grad_att_heads = grad_attended.reshape(seq_length, HEADS, HD)
    delta_all = jnp.sum(grad_att_heads.astype(jnp.float32) * out_parts, axis=-1)
    block_index = 0
    start_row = block_index * rows_block
    scores, allowed = scores_block(query, keys, start_row, seq_live)
    probs_full = jnp.where(allowed, jnp.exp(scores - lse_parts[block_index]), 0.0)
    probs_low = probs_full.astype(jnp.bfloat16)
    grad_probs = jnp.einsum(
        "qhd,khd->hqk", grad_att_heads, values, preferred_element_type=jnp.float32
    )
    delta_block = jnp.transpose(delta_all)[:, :, None]
    grad_scores = (probs_full * (grad_probs - delta_block)).astype(jnp.bfloat16)
    grad_query_parts = 0.125 * jnp.einsum(
        "hqk,khd->qhd", grad_scores, keys, preferred_element_type=jnp.float32
    )
    grad_keys = 0.125 * jnp.einsum(
        "hqk,qhd->khd", grad_scores, query, preferred_element_type=jnp.float32
    )
    grad_values = jnp.einsum(
        "hqk,qhd->khd", probs_low, grad_att_heads, preferred_element_type=jnp.float32
    )
    grad_mixed = jnp.concatenate(
        [
            grad_query_parts.reshape(seq_length, width),
            grad_keys.reshape(seq_length, width),
            grad_values.reshape(seq_length, width),
        ],
        axis=1,
    )
    grad_taps_part = jnp.stack(
        [
            jnp.sum(grad_mixed * projected, axis=0),
            jnp.sum(grad_mixed * shift_down(projected, 1), axis=0),
            jnp.sum(grad_mixed * shift_down(projected, 2), axis=0),
        ],
        axis=1,
    )
    grad_projected = (
        grad_mixed * taps[:, 0]
        + shift_up(grad_mixed, 1) * taps[:, 1]
        + shift_up(grad_mixed, 2) * taps[:, 2]
    ).astype(jnp.bfloat16)
    grad_qkv_part = contract_first(normed_one, grad_projected)
    grad_normed_one = contract_last(grad_projected, full_qkv)
    grad_ln_one, grad_gain_first = norm_back(grad_normed_one, gain_first, hat_one, inv_one)
    grad_inputs = (grad_residual + grad_ln_one).astype(jnp.bfloat16)[None]
    grad_w_qkv, grad_w_out, grad_conv_taps, grad_gain_one, grad_gain_two = (
        lax.psum_scatter(grad_qkv_part, ("batch", "wide"), scatter_dimension=0, tiled=True),
        lax.psum_scatter(grad_w_out_part, ("batch", "wide"), scatter_dimension=0, tiled=True),
        lax.psum_scatter(grad_taps_part, ("batch", "wide"), scatter_dimension=0, tiled=True),
        lax.psum_scatter(grad_gain_first, ("batch", "wide"), scatter_dimension=0, tiled=True),
        lax.psum_scatter(grad_gain_second, ("batch", "wide"), scatter_dimension=0, tiled=True),
    )
    return (
        output,
        grad_inputs,
        grad_w_qkv,
        grad_w_out,
        grad_conv_taps,
        grad_gain_one,
        grad_gain_two,
        grad_w_in,
        grad_w_fc2,
    )


BF = jnp.bfloat16
F32 = jnp.float32
AXES = ("batch", "wide")
LANES = 256
WIDE_PART = 256


def fits(mesh, args):
    inputs, w_qkv, w_in = args[0], args[3], args[8]
    count = mesh.shape["batch"] * mesh.shape["wide"]
    return (
        mesh.shape["batch"] == 4
        and mesh.shape["wide"] == 8
        and inputs.shape[0] == count
        and inputs.shape[1] % LANES == 0
        and w_qkv.shape[0] % (count * 8) == 0
        and w_qkv.shape[0] % LANES == 0
        and w_qkv.shape[0] // HEADS == HD
        and w_in.shape[1] == 8 * (WIDE_PART + WIDE_PART // 2)
        and (w_in.shape[0] // 4) % 16 == 0
    )


def dot(left, right, left_dim, right_dim):
    return lax.dot_general(
        left, right, (((left_dim,), (right_dim,)), ((), ())), preferred_element_type=F32
    )


def flip_pairs(rule):
    return [(i, i ^ rule(i)) for i in range(32)]


def send(array, rule):
    return lax.ppermute(array, AXES, flip_pairs(rule))


def over_core(i):
    return 8


def over_first(i):
    return 16 if i & 8 else 1


def over_second(i):
    return 1 if i & 8 else 16


def over_z(step):
    return lambda i: 2 * step


def gather_blocks(block):
    part = block[None]
    part = jnp.concatenate([part] + [send(part, over_z(s)) for s in (1, 2, 3)])
    part = jnp.concatenate([part, send(part, over_first)])
    part = jnp.concatenate([part, send(part, over_second)])
    return jnp.concatenate([part, send(part, over_core)])


def scatter_core(keep, away):
    return keep.astype(F32) + send(away, over_core).astype(F32)


def scatter_rest(total, wire=BF):
    for rule in (over_second, over_first):
        half = total.shape[0] // 2
        come = send(total[half:].astype(wire), rule)
        total = total[:half] + come.astype(F32)
    come = [send(total[s].astype(wire), over_z(s)) for s in (1, 2, 3)]
    return total[0] + come[0].astype(F32) + come[1].astype(F32) + come[2].astype(F32)


def place_of(me, other):
    apart = me ^ other
    x_bit, z_bits = apart & 1, (apart >> 1) & 3
    core_bit, y_bit = (apart >> 3) & 1, (apart >> 4) & 1
    on_first = ((other >> 3) & 1) == 0
    high = jnp.where(on_first, y_bit, x_bit)
    low = jnp.where(on_first, x_bit, y_bit)
    return core_bit * 16 + high * 8 + low * 4 + z_bits


def call(kernel, grid, in_specs, out_specs, out_shape, scratch=(), flops=0, nbytes=0, name=None, aliases=None):
    return pl.pallas_call(
        kernel,
        grid_spec=pltpu.PrefetchScalarGridSpec(
            num_scalar_prefetch=1,
            grid=grid,
            in_specs=in_specs,
            out_specs=out_specs,
            scratch_shapes=list(scratch),
        ),
        out_shape=out_shape,
        compiler_params=pltpu.CompilerParams(
            dimension_semantics=("arbitrary",) * len(grid), vmem_limit_bytes=60 * 1024 * 1024
        ),
        cost_estimate=pl.CostEstimate(flops=flops, bytes_accessed=nbytes, transcendentals=0),
        name=name,
        input_output_aliases=aliases or {},
    )


def whole(shape):
    zeros = (0,) * len(shape)
    return pl.BlockSpec(shape, lambda *_: zeros)


def hat_of(values_in):
    centered = values_in - jnp.mean(values_in, axis=-1, keepdims=True)
    inv_std = lax.rsqrt(jnp.mean(centered * centered, axis=-1, keepdims=True) + epsilon)
    return centered * inv_std, inv_std


def turned(value):
    return jnp.transpose(value.astype(F32)).astype(BF)


def prepare_kernel(meta, cot_ref, go_ref, got_ref):
    seq = cot_ref.shape[0]
    quarter = got_ref.shape[1]
    live = lax.broadcasted_iota(jnp.int32, (seq, 1), 0) < meta[33]
    value = jnp.where(live, cot_ref[...].astype(F32), 0.0)
    go_ref[...] = value.astype(BF)
    flipped = jnp.transpose(value).astype(BF)
    for b in range(4):
        got_ref[b ^ meta[32]] = flipped[b * quarter : (b + 1) * quarter]


def project_kernel(meta, x_ref, gain_ref, taps_ref, w_ref, proj_ref, mixed_ref, wn_ref, nt_ref, normed):
    rows = w_ref.shape[1]

    @pl.when(pl.program_id(0) == 0)
    def _():
        hat, _ = hat_of(x_ref[...].astype(F32))
        low = (hat * gain_ref[...]).astype(BF)
        normed[...] = low
        flipped = turned(low)
        for i in range(32):
            nt_ref[meta[i]] = flipped[i * rows : (i + 1) * rows]

    for i in range(32):
        wn_ref[i * rows : (i + 1) * rows, :] = w_ref[meta[i]]
    value = dot(normed[...], wn_ref[...], 1, 0)
    at = lax.broadcasted_iota(jnp.int32, value.shape, 0)
    one = jnp.where(at >= 1, pltpu.roll(value, 1, 0), 0.0)
    two = jnp.where(at >= 2, pltpu.roll(value, 2, 0), 0.0)
    mixed = value * taps_ref[0:1, :] + one * taps_ref[1:2, :] + two * taps_ref[2:3, :]
    proj_ref[...] = value.astype(BF)
    mixed_ref[...] = mixed.astype(BF)


def head_row(head, scale=1.0):
    lane = lax.broadcasted_iota(jnp.int32, (1, LANES), 1)
    return jnp.where(lane // HD == head, scale, 0.0).astype(BF)


def allowed_in(meta, keys, first_query, queries):
    key = lax.broadcasted_iota(jnp.int32, (keys, queries), 0)
    query = first_query + lax.broadcasted_iota(jnp.int32, (1, queries), 1)
    return key < jnp.minimum(query + 1, meta[33])


def attend_kernel(meta, q_ref, k_ref, v_ref, out_ref, lse_ref, flipped):
    seq = q_ref.shape[0]
    tile = LANES
    values_t = turned(v_ref[...])
    keys = k_ref[...]
    for t in range(seq // tile):
        upto = (t + 1) * tile
        allowed = allowed_in(meta, upto, t * tile, tile)
        query = q_ref[t * tile : upto, :]
        for head in range(LANES // HD):
            scores = dot(keys[:upto], query * head_row(head, 0.125), 1, 1)
            scores = jnp.where(allowed, scores, -1e30)
            top = jnp.max(scores, axis=0, keepdims=True)
            terms = jnp.exp(scores - top)
            total = jnp.sum(terms, axis=0, keepdims=True)
            probs = (terms * (1.0 / total)).astype(BF)
            flipped[head * HD : (head + 1) * HD, t * tile : upto] = dot(
                values_t[head * HD : (head + 1) * HD, :upto], probs, 1, 0
            )
            lse_ref[0, head : head + 1, t * tile : upto] = top + jnp.log(total)
    out_ref[...] = jnp.transpose(flipped[...]).astype(BF)


def mend_kernel(meta, att_ref, blocks_ref, x_ref, gain_ref, res_ref, n2_ref, n2t_ref, at_ref, wn_ref, held, sem):
    first = blocks_ref.shape[1] - held.shape[1]
    copy = pltpu.make_async_copy(blocks_ref.at[:, pl.ds(first, held.shape[1]), :], held, sem)
    copy.start()
    flipped = turned(att_ref[...])
    rows = at_ref.shape[1]
    for i in range(32):
        at_ref[meta[i]] = flipped[i * rows : (i + 1) * rows]
    copy.wait()
    lanes = held.shape[2]
    for i in range(32):
        for c in range(wn_ref.shape[1] // lanes):
            wn_ref[i * rows : (i + 1) * rows, c * lanes : (c + 1) * lanes] = held[
                meta[i], c * rows : (c + 1) * rows, :
            ]
    residual = x_ref[...].astype(F32) + dot(att_ref[...], wn_ref[...], 1, 0)
    res_ref[...] = residual
    hat, _ = hat_of(residual)
    low = (hat * gain_ref[...]).astype(BF)
    n2_ref[...] = low
    flipped = turned(low)
    quarter = n2t_ref.shape[1]
    for b in range(4):
        n2t_ref[b ^ meta[32]] = flipped[b * quarter : (b + 1) * quarter]


def ffn_kernel(per_step, first, meta, n2_ref, go_ref, n2t_ref, got_ref, *refs):
    tiles, refs = refs[: 4 * per_step], refs[4 * per_step :]
    if not first:
        branch_in, grad_in = refs[:2]
        refs = refs[2:]
    branch_ref, grad_ref, keep_ref, away_ref = refs
    step = pl.program_id(0)

    @pl.when(step == 0)
    def _():
        if first:
            branch_ref[...] = jnp.zeros_like(branch_ref)
            grad_ref[...] = jnp.zeros_like(grad_ref)
        else:
            branch_ref[...] = branch_in[...]
            grad_ref[...] = grad_in[...]

    quarter = tiles[0].shape[1] // 2
    lanes = tiles[0].shape[2]

    def joined(start):
        columns = [
            jnp.concatenate(
                [tiles[4 * k + b][0, start : start + quarter, :] for b in range(4)], axis=0
            )
            for k in range(per_step)
        ]
        return columns[0] if per_step == 1 else jnp.concatenate(columns, axis=1)

    w_up, w_down = joined(0), joined(quarter)
    pre = jnp.maximum(dot(n2_ref[...], w_up, 1, 0), 0.0)
    activ = (pre * pre).astype(BF)
    grad_pre = (dot(go_ref[...], w_down, 1, 0) * 2.0 * pre).astype(BF)
    branch_ref[...] += dot(activ, w_down, 1, 1)
    grad_ref[...] += dot(grad_pre, w_up, 1, 1)
    for start, result in (
        (0, dot(n2t_ref[...], grad_pre, 1, 0)),
        (quarter, dot(got_ref[...], activ, 1, 0)),
    ):
        for apart in range(4):
            target = away_ref if apart & 1 else keep_ref
            for k in range(per_step):
                place = meta[(apart ^ meta[32]) * 8 + step * per_step + k] & 15
                target[place, start : start + quarter, :] = result[
                    apart * quarter : (apart + 1) * quarter, k * lanes : (k + 1) * lanes
                ].astype(BF)


def turn_kernel(meta, grad_ref, branch_ref, res_ref, gain_ref, go_ref, at_ref, wn_ref, out_ref, gres_ref, gatt_ref, ggain_ref, keep_ref, away_ref):
    residual = res_ref[...]
    seq = residual.shape[0]
    live = lax.broadcasted_iota(jnp.int32, (seq, 1), 0) < meta[33]
    out_ref[...] = jnp.where(live, residual + branch_ref[...], 0.0).astype(BF)
    hat, inv_std = hat_of(residual)
    grad = grad_ref[...]
    ggain_ref[...] = jnp.sum(grad * hat, axis=0, keepdims=True)
    scaled = grad * gain_ref[...]
    mean_first = jnp.mean(scaled, axis=-1, keepdims=True)
    mean_second = jnp.mean(scaled * hat, axis=-1, keepdims=True)
    grad_res = go_ref[...].astype(F32) + inv_std * (scaled - mean_first - hat * mean_second)
    gres_ref[...] = grad_res
    low = grad_res.astype(BF)
    gatt_ref[...] = dot(low, wn_ref[...], 1, 1).astype(BF)
    result = dot(at_ref[...], low, 1, 0)
    lanes = keep_ref.shape[2]
    chunks = result.shape[1] // lanes
    rows = keep_ref.shape[1] // chunks
    for i in range(32):
        target = away_ref if i >= 16 else keep_ref
        for c in range(chunks):
            target[i & 15, c * rows : (c + 1) * rows, :] = result[
                i * rows : (i + 1) * rows, c * lanes : (c + 1) * lanes
            ].astype(BF)


def attend_back_kernel(
    meta, q_ref, k_ref, v_ref, pq_ref, pk_ref, pv_ref, tq_ref, tk_ref, tv_ref, go_ref, out_ref, lse_ref,
    gq_ref, gk_ref, gv_ref, dtq_ref, dtk_ref, dtv_ref, flipped,
):
    seq = q_ref.shape[0]
    tile = LANES
    keys, values = k_ref[...], v_ref[...]
    keys_t = turned(keys)
    delta_t = jnp.transpose(go_ref[...].astype(F32) * out_ref[...].astype(F32))
    grad_keys = [jnp.zeros((tile, LANES), F32) for _ in range(seq // tile)]
    grad_values = list(grad_keys)
    for t in range(seq // tile):
        upto = (t + 1) * tile
        allowed = allowed_in(meta, upto, t * tile, tile)
        query, grad = q_ref[t * tile : upto, :], go_ref[t * tile : upto, :]
        for head in range(LANES // HD):
            lanes = slice(head * HD, (head + 1) * HD)
            query_h, grad_h = query * head_row(head, 0.125), grad * head_row(head)
            delta = jnp.sum(delta_t[lanes, t * tile : upto], axis=0, keepdims=True)
            scores = dot(keys[:upto], query_h, 1, 1)
            lse = lse_ref[0, head : head + 1, t * tile : upto]
            probs = jnp.where(allowed, jnp.exp(scores - lse), 0.0)
            grad_scores = (probs * (dot(values[:upto], grad_h, 1, 1) - delta)).astype(BF)
            flipped[lanes, t * tile : upto] = dot(keys_t[lanes, :upto], grad_scores, 1, 0) * 0.125
            add_values = dot(probs.astype(BF), grad_h, 1, 0)
            add_keys = dot(grad_scores, query_h, 1, 0)
            for s in range(t + 1):
                rows = slice(s * tile, (s + 1) * tile)
                grad_values[s] += add_values[rows]
                grad_keys[s] += add_keys[rows]
    mixed = (
        jnp.transpose(flipped[...]),
        jnp.concatenate(grad_keys, axis=0),
        jnp.concatenate(grad_values, axis=0),
    )
    at = lax.broadcasted_iota(jnp.int32, (seq, LANES), 0)
    for grad, proj_ref, taps_ref, g_ref, dt_ref in zip(
        mixed, (pq_ref, pk_ref, pv_ref), (tq_ref, tk_ref, tv_ref), (gq_ref, gk_ref, gv_ref), (dtq_ref, dtk_ref, dtv_ref)
    ):
        one = jnp.where(at < seq - 1, pltpu.roll(grad, seq - 1, 0), 0.0)
        two = jnp.where(at < seq - 2, pltpu.roll(grad, seq - 2, 0), 0.0)
        g_ref[...] = (grad * taps_ref[0:1, :] + one * taps_ref[1:2, :] + two * taps_ref[2:3, :]).astype(BF)
        proj = proj_ref[...].astype(F32)
        for tap, part in enumerate((grad, one, two)):
            dt_ref[tap : tap + 1, :] = jnp.sum(part * proj, axis=0, keepdims=True)


def weight_kernel(meta, nt_ref, gq_ref, gk_ref, gv_ref, keep_ref, away_ref):
    start = pl.program_id(0) * LANES
    width = keep_ref.shape[1] // 3
    half = keep_ref.shape[0]
    for part, g_ref in enumerate((gq_ref, gk_ref, gv_ref)):
        result = dot(nt_ref[...], g_ref[...], 1, 0).astype(BF)
        columns = pl.ds(pl.multiple_of(part * width + start, LANES), LANES)
        keep_ref[:, columns] = result[:half]
        away_ref[:, columns] = result[half:]


def last_kernel(meta, gq_ref, gk_ref, gv_ref, wq_ref, wk_ref, wv_ref, x_ref, gain_ref, gres_ref, gin_ref, ggain_ref, total):
    step = pl.program_id(0)
    part = (
        dot(gq_ref[...], wq_ref[...], 1, 1)
        + dot(gk_ref[...], wk_ref[...], 1, 1)
        + dot(gv_ref[...], wv_ref[...], 1, 1)
    )

    @pl.when(step == 0)
    def _():
        total[...] = part

    @pl.when(step > 0)
    def _():
        total[...] += part

    @pl.when(step == pl.num_programs(0) - 1)
    def _():
        hat, inv_std = hat_of(x_ref[...].astype(F32))
        grad = total[...]
        ggain_ref[...] = jnp.sum(grad * hat, axis=0, keepdims=True)
        scaled = grad * gain_ref[...]
        mean_first = jnp.mean(scaled, axis=-1, keepdims=True)
        mean_second = jnp.mean(scaled * hat, axis=-1, keepdims=True)
        back = inv_std * (scaled - mean_first - hat * mean_second)
        gin_ref[...] = (gres_ref[...] + back).astype(BF)


def own_sequence(inputs, lengths, cotangent, w_qkv, w_out, conv_taps, gain_one, gain_two, w_in, w_fc2):
    seq, width = inputs.shape[1], inputs.shape[2]
    rows = w_qkv.shape[0]
    wide = w_qkv.shape[1]
    quarter = width // 4
    part_a, part_b = WIDE_PART, WIDE_PART // 2
    batch = lax.axis_index("batch")
    me = batch * 8 + lax.axis_index("wide")
    number = jnp.arange(64, dtype=jnp.int32)
    meta = jnp.where(number < 32, place_of(me, number & 31), jnp.where(number == 32, batch, lengths[0]))
    natural = jax.nn.one_hot(meta[:32], 32, dtype=F32)
    x, cot = inputs[0], cotangent[0]
    shape = jax.ShapeDtypeStruct
    row_spec = whole((1, width))

    small = jnp.zeros((8, 128), BF)
    small = small.at[:3, : conv_taps.shape[0]].set(conv_taps.T)
    small = small.at[3, :rows].set(gain_one).at[4, :rows].set(gain_two)
    small = gather_blocks(small)
    small = jnp.einsum("dp,prl->drl", natural, small.astype(F32), precision="highest")
    taps = jnp.transpose(small[:, :3, : conv_taps.shape[0]], (1, 0, 2)).reshape(3, wide)
    taps = jnp.concatenate([taps, jnp.zeros((5, wide), F32)])
    gain_first = small[:, 3, :rows].reshape(1, width)
    gain_second = small[:, 4, :rows].reshape(1, width)
    qkv_blocks = gather_blocks(w_qkv)
    up = lax.dynamic_slice(w_in, (batch * quarter, 0), (quarter, part_a + part_b))
    down = jnp.transpose(lax.dynamic_slice(w_fc2, (0, batch * quarter), (part_a + part_b, quarter)))
    out_chunks = [w_out[:, c * part_a : (c + 1) * part_a] for c in range(width // part_a)]
    blocks_a = gather_blocks(jnp.concatenate([up[:, :part_a], down[:, :part_a]] + out_chunks))
    blocks_b = gather_blocks(jnp.concatenate([up[:, part_a:], down[:, part_a:]]))

    grad_out, grad_out_t = call(
        prepare_kernel, (1,), [whole((seq, width))], [whole((seq, width)), whole((4, quarter, seq))],
        [shape((seq, width), BF), shape((4, quarter, seq), BF)], nbytes=3 * seq * width * 2, name="prepare",
    )(meta, cot)
    lane_block = pl.BlockSpec((seq, LANES), lambda j, m: (0, j))
    projected, mixed, qkv_full, normed_t = call(
        project_kernel, (wide // LANES,),
        [whole((seq, width)), row_spec, pl.BlockSpec((8, LANES), lambda j, m: (0, j)),
         pl.BlockSpec((32, rows, LANES), lambda j, m: (0, 0, j))],
        [lane_block, lane_block, pl.BlockSpec((width, LANES), lambda j, m: (0, j)), whole((32, rows, seq))],
        [shape((seq, wide), BF), shape((seq, wide), BF), shape((width, wide), BF), shape((32, rows, seq), BF)],
        [pltpu.VMEM((seq, width), BF)], flops=2 * seq * width * wide, nbytes=12 * seq * width, name="project",
    )(meta, x, gain_first, taps, qkv_blocks)
    groups = width // LANES
    part_specs = [pl.BlockSpec((seq, LANES), lambda j, m, p=p: (0, p * groups + j)) for p in range(3)]
    lse_spec = pl.BlockSpec((1, 8, seq), lambda j, m: (j, 0, 0))
    attended, lse = call(
        attend_kernel, (groups,), part_specs, [lane_block, lse_spec],
        [shape((seq, width), BF), shape((groups, 8, seq), F32)], [pltpu.VMEM((LANES, seq), F32)],
        flops=4 * seq * seq * width, nbytes=8 * seq * width, name="attend",
    )(meta, mixed, mixed, mixed)
    out_rows = rows * (width // part_a)
    residual, normed_two, normed_two_t, attended_t, out_full = call(
        mend_kernel, (1,),
        [whole((seq, width)), pl.BlockSpec(memory_space=pl.ANY), whole((seq, width)), row_spec],
        [whole((seq, width)), whole((seq, width)), whole((4, quarter, seq)), whole((32, rows, seq)), whole((width, width))],
        [shape((seq, width), F32), shape((seq, width), BF), shape((4, quarter, seq), BF), shape((32, rows, seq), BF),
         shape((width, width), BF)],
        [pltpu.VMEM((32, out_rows, part_a), BF), pltpu.SemaphoreType.DMA],
        flops=2 * seq * width * width, nbytes=16 * seq * width, name="mend",
    )(meta, attended, blocks_a, x, gain_second)

    normed_two_t = normed_two_t.reshape(width, seq)
    grad_out_t = grad_out_t.reshape(width, seq)
    sums = ()
    grads = []
    for blocks, lanes in ((blocks_a, part_a), (blocks_b, part_b)):
        per_step = LANES // lanes
        first = not sums
        tile_specs = [
            pl.BlockSpec(
                (1, 2 * quarter, lanes),
                lambda s, m, b=b, k=k, n=per_step: (m[b * 8 + s * n + k], 0, 0),
            )
            for k in range(per_step)
            for b in range(4)
        ]
        token = whole((seq, width))
        grad_spec = whole((16, 2 * quarter, lanes))
        *sums, keep, away = call(
            functools.partial(ffn_kernel, per_step, first), (8 // per_step,),
            [token, token, whole((width, seq)), whole((width, seq))] + tile_specs + [token] * len(sums),
            [token, token, grad_spec, grad_spec],
            [shape((seq, width), F32)] * 2 + [shape((16, 2 * quarter, lanes), BF)] * 2,
            flops=12 * seq * width * lanes * 8, nbytes=8 * seq * width * 4, name="ffn",
        )(meta, normed_two, grad_out, normed_two_t, grad_out_t, *[blocks] * (4 * per_step), *sums)
        grads.append((keep, away))
    branch, grad_normed_two = sums
    grad_a = scatter_core(*grads[0])
    chunk_rows = rows * (width // part_b)
    output, grad_residual, grad_attended, grad_gain_second, keep_out, away_out = call(
        turn_kernel, (1,),
        [whole((seq, width))] * 3 + [row_spec, whole((seq, width)), whole((width, seq)), whole((width, width))],
        [whole((seq, width))] * 3 + [row_spec, whole((16, chunk_rows, part_b)), whole((16, chunk_rows, part_b))],
        [shape((seq, width), BF), shape((seq, width), F32), shape((seq, width), BF), shape((1, width), F32),
         shape((16, chunk_rows, part_b), BF), shape((16, chunk_rows, part_b), BF)],
        flops=4 * seq * width * width, nbytes=20 * seq * width, name="turn",
    )(meta, grad_normed_two, branch, residual, gain_second, grad_out, attended_t.reshape(width, seq), out_full)
    grad_a = scatter_rest(grad_a)
    grad_b = jnp.concatenate([scatter_core(*grads[1]), scatter_core(keep_out, away_out)], axis=1)
    grad_b = scatter_rest(grad_b)

    tap_specs = [pl.BlockSpec((8, LANES), lambda j, m, p=p: (0, p * groups + j)) for p in range(3)]
    tap_out = pl.BlockSpec((8, LANES), lambda j, m: (0, j))
    *grad_projected, tap_q, tap_k, tap_v = call(
        attend_back_kernel, (groups,),
        part_specs * 2 + tap_specs + [lane_block, lane_block, lse_spec],
        [lane_block] * 3 + [tap_out] * 3,
        [shape((seq, width), BF)] * 3 + [shape((8, width), F32)] * 3,
        [pltpu.VMEM((LANES, seq), F32)],
        flops=10 * seq * seq * width, nbytes=24 * seq * width, name="attend_back",
    )(meta, mixed, mixed, mixed, projected, projected, projected, taps, taps, taps, grad_attended, attended, lse)
    half_spec = whole((width // 2, wide))
    keep_qkv, away_qkv = call(
        weight_kernel, (groups,), [whole((width, seq))] + [lane_block] * 3, [half_spec, half_spec],
        [shape((width // 2, wide), BF)] * 2,
        flops=2 * seq * width * wide, nbytes=8 * seq * width, name="weight",
    )(meta, normed_t.reshape(width, seq), *grad_projected)
    by_block = (16, rows, wide)
    grad_qkv = scatter_rest(scatter_core(keep_qkv.reshape(by_block), away_qkv.reshape(by_block)))
    weight_specs = [pl.BlockSpec((width, LANES), lambda j, m, p=p: (0, p * groups + j)) for p in range(3)]
    grad_inputs, grad_gain_first = call(
        last_kernel, (groups,),
        [lane_block] * 3 + weight_specs + [whole((seq, width)), row_spec, whole((seq, width))],
        [whole((seq, width)), row_spec], [shape((seq, width), BF), shape((1, width), F32)],
        [pltpu.VMEM((seq, width), F32)],
        flops=2 * seq * width * wide, nbytes=16 * seq * width, name="last",
    )(meta, *grad_projected, qkv_full, qkv_full, qkv_full, x, gain_first, grad_residual)

    tap_grads = jnp.concatenate([tap_q[:3], tap_k[:3], tap_v[:3]], axis=1)
    tap_grads = jnp.transpose(tap_grads.reshape(3, 32, wide // 32), (1, 0, 2))
    gain_grads = jnp.stack([grad_gain_first.reshape(32, rows), grad_gain_second.reshape(32, rows)], axis=1)
    few = jnp.zeros((32, 8, 128), F32)
    few = few.at[:, :3, : wide // 32].set(tap_grads).at[:, 3:5, :rows].set(gain_grads)
    few = jnp.einsum("dp,drl->prl", natural, few, precision="highest")
    few = scatter_rest(scatter_core(few[:16], few[16:]), F32)

    ffn_a, ffn_b = grad_a, grad_b[: 2 * quarter]
    grad_out_w = grad_b[2 * quarter :]
    grad_out_w = jnp.concatenate(
        [grad_out_w[c * rows : (c + 1) * rows] for c in range(width // part_b)], axis=1
    )
    grad_in_w = jnp.concatenate([ffn_a[:quarter], ffn_b[:quarter]], axis=1)
    grad_fc2_w = jnp.transpose(jnp.concatenate([ffn_a[quarter:], ffn_b[quarter:]], axis=1))
    return (
        output[None],
        grad_inputs[None],
        grad_qkv,
        grad_out_w,
        few[:3, : wide // 32].T,
        few[3, :rows],
        few[4, :rows],
        grad_in_w,
        grad_fc2_w,
    )


def solution(mesh):
    fast = functools.partial(own_sequence)

    def program(*args):
        body = fast if fits(mesh, args) else shards
        return jax.shard_map(
            body,
            mesh=mesh,
            in_specs=(
                P(("batch", "wide"), None, None),
                P(("batch", "wide")),
                P(("batch", "wide"), None, None),
                P(("batch", "wide"), None),
                P(("batch", "wide"), None),
                P(("batch", "wide"), None),
                P(("batch", "wide")),
                P(("batch", "wide")),
                P(None, "wide"),
                P("wide", None),
            ),
            out_specs=(
                P(("batch", "wide"), None, None),
                P(("batch", "wide"), None, None),
                P(("batch", "wide"), None),
                P(("batch", "wide"), None),
                P(("batch", "wide"), None),
                P(("batch", "wide")),
                P(("batch", "wide")),
                P("batch", "wide"),
                P("wide", "batch"),
            ),
            check_vma=False,
        )(*args)

    return program
```

```python
import functools
import jax
import jax.numpy as jnp
from jax import lax
from jax.experimental import pallas as pl
from jax.experimental.pallas import tpu as pltpu
from jax.sharding import PartitionSpec as P

HEADS = 12
HD = 64


epsilon = 1e-05


def contract_first(left, right):
    return lax.dot_general(
        left, right, (((0,), (0,)), ((), ())), preferred_element_type=jnp.float32
    )


def contract_last(left, right):
    return lax.dot_general(
        left, right, (((1,), (1,)), ((), ())), preferred_element_type=jnp.float32
    )


def norm_parts(values_in):
    centered = values_in - jnp.mean(values_in, axis=-1, keepdims=True)
    inv_std = lax.rsqrt(jnp.mean(centered * centered, axis=-1, keepdims=True) + epsilon)
    return (centered * inv_std, inv_std)


def norm_back(grad_normed, gain_vec, normed_hat, inv_std):
    grad_hat = grad_normed * gain_vec
    mean_first = jnp.mean(grad_hat, axis=-1, keepdims=True)
    mean_second = jnp.mean(grad_hat * normed_hat, axis=-1, keepdims=True)
    grad_value = inv_std * (grad_hat - mean_first - normed_hat * mean_second)
    return (grad_value, jnp.sum(grad_normed * normed_hat, axis=0))


def shift_down(signal, steps):
    filler = jnp.zeros((steps, signal.shape[1]), signal.dtype)
    return jnp.concatenate([filler, signal[:-steps]], axis=0)


def shift_up(signal, steps):
    filler = jnp.zeros((steps, signal.shape[1]), signal.dtype)
    return jnp.concatenate([signal[steps:], filler], axis=0)


def scores_block(query_block, keys, start_row, seq_live):
    rows_block = query_block.shape[0]
    scores = (
        jnp.einsum("qhd,khd->hqk", query_block, keys, preferred_element_type=jnp.float32) * 0.125
    )
    query_pos = start_row + jnp.arange(rows_block)
    key_pos = jnp.arange(keys.shape[0])
    allowed = (key_pos[None, :] <= query_pos[:, None]) & (key_pos[None, :] < seq_live)
    return (scores, allowed[None])


def shards(inputs, lengths, cotangent, w_qkv, w_out, conv_taps, gain_one, gain_two, w_in, w_fc2):
    full_qkv, full_out, full_taps, full_gain_one, full_gain_two = (
        lax.all_gather(w_qkv, ("batch", "wide"), axis=0, tiled=True),
        lax.all_gather(w_out, ("batch", "wide"), axis=0, tiled=True),
        lax.all_gather(conv_taps, ("batch", "wide"), axis=0, tiled=True),
        lax.all_gather(gain_one, ("batch", "wide"), axis=0, tiled=True),
        lax.all_gather(gain_two, ("batch", "wide"), axis=0, tiled=True),
    )
    seq_length, width = (inputs.shape[1], inputs.shape[2])
    tokens_in = inputs[0].astype(jnp.float32)
    seq_live = lengths[0]
    live_rows = jnp.arange(seq_length) < seq_live
    taps = full_taps.astype(jnp.float32)
    gain_first = full_gain_one.astype(jnp.float32)
    gain_second = full_gain_two.astype(jnp.float32)
    hat_one, inv_one = norm_parts(tokens_in)
    normed_one = (hat_one * gain_first).astype(jnp.bfloat16)
    projected = jnp.dot(normed_one, full_qkv, preferred_element_type=jnp.float32)
    mixed = (
        projected * taps[:, 0]
        + shift_down(projected, 1) * taps[:, 1]
        + shift_down(projected, 2) * taps[:, 2]
    ).astype(jnp.bfloat16)
    query = mixed[:, :width].reshape(seq_length, HEADS, HD)
    keys = mixed[:, width : 2 * width].reshape(seq_length, HEADS, HD)
    values = mixed[:, 2 * width :].reshape(seq_length, HEADS, HD)
    rows_block = min(512, seq_length)
    block_index = 0
    start_row = block_index * rows_block
    scores, allowed = scores_block(query, keys, start_row, seq_live)
    masked = jnp.where(allowed, scores, -1e30)
    top_score = jnp.max(masked, axis=-1, keepdims=True)
    exp_terms = jnp.exp(masked - top_score)
    row_totals = jnp.sum(exp_terms, axis=-1, keepdims=True)
    probs_low = (exp_terms / row_totals).astype(jnp.bfloat16)
    out_parts = jnp.einsum("hqk,khd->qhd", probs_low, values, preferred_element_type=jnp.float32)
    lse_parts = [top_score + jnp.log(row_totals)]
    attended_low = out_parts.reshape(seq_length, width).astype(jnp.bfloat16)
    branch_attn = jnp.dot(attended_low, full_out, preferred_element_type=jnp.float32)
    residual = tokens_in + branch_attn
    hat_two, inv_two = norm_parts(residual)
    normed_two = (hat_two * gain_second).astype(jnp.bfloat16)
    grad_out = jnp.where(live_rows[:, None], cotangent[0], jnp.zeros_like(cotangent[0]))
    row_set = lax.all_gather(normed_two[None], "wide", axis=0, tiled=True).reshape(-1, width)
    pre_act = jnp.dot(row_set, w_in, preferred_element_type=jnp.float32)
    activ = jnp.square(jax.nn.relu(pre_act)).astype(jnp.bfloat16)
    piece = activ
    branch_ffn = lax.psum_scatter(
        jnp.dot(piece, w_fc2, preferred_element_type=jnp.float32).astype(jnp.bfloat16),
        "wide",
        scatter_dimension=0,
        tiled=True,
    ).astype(jnp.float32)
    grad_set = lax.all_gather(grad_out[None], "wide", axis=0, tiled=True).reshape(-1, width)
    grad_act = contract_last(grad_set, w_fc2)
    grad_fc2_part = contract_first(activ, grad_set)
    grad_pre = (grad_act * 2.0 * jax.nn.relu(pre_act)).astype(jnp.bfloat16)
    grad_in_part = contract_first(row_set, grad_pre)
    piece = grad_pre
    grad_normed_two = lax.psum_scatter(
        contract_last(piece, w_in).astype(jnp.bfloat16), "wide", scatter_dimension=0, tiled=True
    ).astype(jnp.float32)
    grad_w_in, grad_w_fc2 = (
        lax.psum_scatter(
            grad_in_part.astype(jnp.bfloat16), "batch", scatter_dimension=0, tiled=True
        ).astype(jnp.float32),
        lax.psum_scatter(
            grad_fc2_part.astype(jnp.bfloat16), "batch", scatter_dimension=1, tiled=True
        ).astype(jnp.float32),
    )
    output = jnp.where(live_rows[:, None], residual + branch_ffn, 0.0).astype(jnp.bfloat16)[None]
    grad_ln_two, grad_gain_second = norm_back(grad_normed_two, gain_second, hat_two, inv_two)
    grad_residual = grad_out.astype(jnp.float32) + grad_ln_two
    grad_branch = grad_residual.astype(jnp.bfloat16)
    grad_w_out_part = contract_first(attended_low, grad_branch)
    grad_attended = contract_last(grad_branch, full_out).astype(jnp.bfloat16)
    grad_att_heads = grad_attended.reshape(seq_length, HEADS, HD)
    delta_all = jnp.sum(grad_att_heads.astype(jnp.float32) * out_parts, axis=-1)
    block_index = 0
    start_row = block_index * rows_block
    scores, allowed = scores_block(query, keys, start_row, seq_live)
    probs_full = jnp.where(allowed, jnp.exp(scores - lse_parts[block_index]), 0.0)
    probs_low = probs_full.astype(jnp.bfloat16)
    grad_probs = jnp.einsum(
        "qhd,khd->hqk", grad_att_heads, values, preferred_element_type=jnp.float32
    )
    delta_block = jnp.transpose(delta_all)[:, :, None]
    grad_scores = (probs_full * (grad_probs - delta_block)).astype(jnp.bfloat16)
    grad_query_parts = 0.125 * jnp.einsum(
        "hqk,khd->qhd", grad_scores, keys, preferred_element_type=jnp.float32
    )
    grad_keys = 0.125 * jnp.einsum(
        "hqk,qhd->khd", grad_scores, query, preferred_element_type=jnp.float32
    )
    grad_values = jnp.einsum(
        "hqk,qhd->khd", probs_low, grad_att_heads, preferred_element_type=jnp.float32
    )
    grad_mixed = jnp.concatenate(
        [
            grad_query_parts.reshape(seq_length, width),
            grad_keys.reshape(seq_length, width),
            grad_values.reshape(seq_length, width),
        ],
        axis=1,
    )
    grad_taps_part = jnp.stack(
        [
            jnp.sum(grad_mixed * projected, axis=0),
            jnp.sum(grad_mixed * shift_down(projected, 1), axis=0),
            jnp.sum(grad_mixed * shift_down(projected, 2), axis=0),
        ],
        axis=1,
    )
    grad_projected = (
        grad_mixed * taps[:, 0]
        + shift_up(grad_mixed, 1) * taps[:, 1]
        + shift_up(grad_mixed, 2) * taps[:, 2]
    ).astype(jnp.bfloat16)
    grad_qkv_part = contract_first(normed_one, grad_projected)
    grad_normed_one = contract_last(grad_projected, full_qkv)
    grad_ln_one, grad_gain_first = norm_back(grad_normed_one, gain_first, hat_one, inv_one)
    grad_inputs = (grad_residual + grad_ln_one).astype(jnp.bfloat16)[None]
    grad_w_qkv, grad_w_out, grad_conv_taps, grad_gain_one, grad_gain_two = (
        lax.psum_scatter(grad_qkv_part, ("batch", "wide"), scatter_dimension=0, tiled=True),
        lax.psum_scatter(grad_w_out_part, ("batch", "wide"), scatter_dimension=0, tiled=True),
        lax.psum_scatter(grad_taps_part, ("batch", "wide"), scatter_dimension=0, tiled=True),
        lax.psum_scatter(grad_gain_first, ("batch", "wide"), scatter_dimension=0, tiled=True),
        lax.psum_scatter(grad_gain_second, ("batch", "wide"), scatter_dimension=0, tiled=True),
    )
    return (
        output,
        grad_inputs,
        grad_w_qkv,
        grad_w_out,
        grad_conv_taps,
        grad_gain_one,
        grad_gain_two,
        grad_w_in,
        grad_w_fc2,
    )


BF = jnp.bfloat16
F32 = jnp.float32
AXES = ("batch", "wide")
LANES = 256
PART = 128
PARTS = 3


def fits(mesh, args):
    inputs, w_qkv, w_in = args[0], args[3], args[8]
    count = mesh.shape["batch"] * mesh.shape["wide"]
    return (
        mesh.shape["batch"] == 4
        and mesh.shape["wide"] == 8
        and inputs.shape[0] == count
        and inputs.shape[1] % LANES == 0
        and w_qkv.shape[0] % (count * 8) == 0
        and w_qkv.shape[0] % LANES == 0
        and w_qkv.shape[0] // HEADS == HD
        and w_in.shape[1] == 8 * PART * PARTS
        and (w_in.shape[0] // 4) % 16 == 0
    )


def dot(left, right, left_dim, right_dim):
    return lax.dot_general(
        left, right, (((left_dim,), (right_dim,)), ((), ())), preferred_element_type=F32
    )


def flip_pairs(rule):
    return [(i, i ^ rule(i)) for i in range(32)]


def send(array, rule):
    return lax.ppermute(array, AXES, flip_pairs(rule))


def over_core(i):
    return 8


def over_first(i):
    return 16 if i & 8 else 1


def over_second(i):
    return 1 if i & 8 else 16


def over_z(step):
    return lambda i: 2 * step


def tie(value, *others):
    return lax.optimization_barrier((value,) + others)[0]


def z_hops(block):
    return [block[None]] + [send(block[None], over_z(s)) for s in (1, 2, 3)]


def join(parts):
    return jnp.concatenate(parts)


def add_core(keep, come):
    half = keep.shape[0] // 2
    total = keep.astype(F32) + come.astype(F32)
    return total[:half], total[half:]


def add_half(total, come):
    half = total.shape[0] // 2
    total = total + come.astype(F32)
    return total[:half], total[half:]


def add_z(total, come):
    return total[0] + (come[0].astype(F32) + (come[1].astype(F32) + come[2].astype(F32)))


def z_sends(total, wire=BF):
    return [send(total[s].astype(wire), over_z(s)) for s in (1, 2, 3)]


def place_of(me, other):
    apart = me ^ other
    x_bit, z_bits = apart & 1, (apart >> 1) & 3
    core_bit, y_bit = (apart >> 3) & 1, (apart >> 4) & 1
    on_first = ((other >> 3) & 1) == 0
    high = jnp.where(on_first, y_bit, x_bit)
    low = jnp.where(on_first, x_bit, y_bit)
    return core_bit * 16 + high * 8 + low * 4 + z_bits


def call(kernel, grid, in_specs, out_specs, out_shape, scratch=(), busy=1, name=None, aliases=None):
    return pl.pallas_call(
        kernel,
        grid_spec=pltpu.PrefetchScalarGridSpec(
            num_scalar_prefetch=1,
            grid=grid,
            in_specs=in_specs,
            out_specs=out_specs,
            scratch_shapes=list(scratch),
        ),
        out_shape=out_shape,
        compiler_params=pltpu.CompilerParams(
            dimension_semantics=("arbitrary",) * len(grid), vmem_limit_bytes=60 * 1024 * 1024
        ),
        cost_estimate=pl.CostEstimate(flops=int(busy * 1.15e9), bytes_accessed=0, transcendentals=0),
        name=name,
        input_output_aliases=aliases or {},
    )


def whole(shape):
    zeros = (0,) * len(shape)
    return pl.BlockSpec(shape, lambda *_: zeros)


def hat_of(values_in):
    centered = values_in - jnp.mean(values_in, axis=-1, keepdims=True)
    inv_std = lax.rsqrt(jnp.mean(centered * centered, axis=-1, keepdims=True) + epsilon)
    return centered * inv_std, inv_std


def turned(value):
    return jnp.transpose(value.astype(F32)).astype(BF)


def prepare_kernel(meta, cot_ref, go_ref, got_ref):
    seq = cot_ref.shape[0]
    quarter = got_ref.shape[1]
    live = lax.broadcasted_iota(jnp.int32, (seq, 1), 0) < meta[33]
    value = jnp.where(live, cot_ref[...].astype(F32), 0.0)
    go_ref[...] = value.astype(BF)
    flipped = jnp.transpose(value).astype(BF)
    for b in range(4):
        got_ref[b ^ meta[32]] = flipped[b * quarter : (b + 1) * quarter]


def block_of(meta, i, own_ref, other_ref):
    place = meta[i]
    return jnp.where(place < 16, own_ref[place & 15], other_ref[place & 15])


def project_kernel(meta, x_ref, gain_ref, taps_ref, own_ref, other_ref, proj_ref, mixed_ref, wn_ref, nt_ref, normed):
    rows = own_ref.shape[1]

    @pl.when(pl.program_id(0) == 0)
    def _():
        hat, _ = hat_of(x_ref[...].astype(F32))
        low = (hat * gain_ref[...]).astype(BF)
        normed[...] = low
        flipped = turned(low)
        for i in range(32):
            nt_ref[meta[i]] = flipped[i * rows : (i + 1) * rows]

    for i in range(32):
        wn_ref[i * rows : (i + 1) * rows, :] = block_of(meta, i, own_ref, other_ref)
    value = dot(normed[...], wn_ref[...], 1, 0)
    at = lax.broadcasted_iota(jnp.int32, value.shape, 0)
    one = jnp.where(at >= 1, pltpu.roll(value, 1, 0), 0.0)
    two = jnp.where(at >= 2, pltpu.roll(value, 2, 0), 0.0)
    mixed = value * taps_ref[0:1, :] + one * taps_ref[1:2, :] + two * taps_ref[2:3, :]
    proj_ref[...] = value.astype(BF)
    mixed_ref[...] = mixed.astype(BF)


def head_row(head, scale=1.0):
    lane = lax.broadcasted_iota(jnp.int32, (1, LANES), 1)
    return jnp.where(lane // HD == head, scale, 0.0).astype(BF)


def allowed_in(meta, keys, first_query, queries):
    key = lax.broadcasted_iota(jnp.int32, (keys, queries), 0)
    query = first_query + lax.broadcasted_iota(jnp.int32, (1, queries), 1)
    return key < jnp.minimum(query + 1, meta[33])


def attend_kernel(meta, q_ref, k_ref, v_ref, out_ref, lse_ref, flipped):
    seq = q_ref.shape[0]
    tile = LANES
    values_t = turned(v_ref[...])
    keys = k_ref[...]
    for t in range(seq // tile):
        upto = (t + 1) * tile
        allowed = allowed_in(meta, upto, t * tile, tile)
        query = q_ref[t * tile : upto, :]
        for head in range(LANES // HD):
            scores = dot(keys[:upto], query * head_row(head, 0.125), 1, 1)
            scores = jnp.where(allowed, scores, -1e30)
            top = jnp.max(scores, axis=0, keepdims=True)
            terms = jnp.exp(scores - top)
            total = jnp.sum(terms, axis=0, keepdims=True)
            probs = (terms * (1.0 / total)).astype(BF)
            flipped[head * HD : (head + 1) * HD, t * tile : upto] = dot(
                values_t[head * HD : (head + 1) * HD, :upto], probs, 1, 0
            )
            lse_ref[0, head : head + 1, t * tile : upto] = top + jnp.log(total)
    out_ref[...] = jnp.transpose(flipped[...]).astype(BF)


def mend_kernel(meta, att_ref, own_ref, other_ref, x_ref, gain_ref, res_ref, n2_ref, n2t_ref, at_ref, wn_ref):
    flipped = turned(att_ref[...])
    rows = at_ref.shape[1]
    for i in range(32):
        at_ref[meta[i]] = flipped[i * rows : (i + 1) * rows]
        wn_ref[i * rows : (i + 1) * rows, :] = block_of(meta, i, own_ref, other_ref)
    residual = x_ref[...].astype(F32) + dot(att_ref[...], wn_ref[...], 1, 0)
    res_ref[...] = residual
    hat, _ = hat_of(residual)
    low = (hat * gain_ref[...]).astype(BF)
    n2_ref[...] = low
    flipped = turned(low)
    quarter = n2t_ref.shape[1]
    for b in range(4):
        n2t_ref[b ^ meta[32]] = flipped[b * quarter : (b + 1) * quarter]


def ffn_kernel(per_step, first, meta, n2_ref, go_ref, n2t_ref, got_ref, *refs):
    count = 4 * per_step
    own, other, refs = refs[:count], refs[count : 2 * count], refs[2 * count :]
    if not first:
        branch_in, grad_in = refs[:2]
        refs = refs[2:]
    branch_ref, grad_ref, keep_ref, away_ref = refs
    step = pl.program_id(0)

    @pl.when(step == 0)
    def _():
        if first:
            branch_ref[...] = jnp.zeros_like(branch_ref)
            grad_ref[...] = jnp.zeros_like(grad_ref)
        else:
            branch_ref[...] = branch_in[...]
            grad_ref[...] = grad_in[...]

    quarter = own[0].shape[1] // 2
    lanes = own[0].shape[2]

    def tile(b, k, start):
        place = meta[b * 8 + step * per_step + k]
        rows = slice(start, start + quarter)
        return jnp.where(place < 16, own[4 * k + b][0, rows, :], other[4 * k + b][0, rows, :])

    def joined(start):
        columns = [jnp.concatenate([tile(b, k, start) for b in range(4)], axis=0) for k in range(per_step)]
        return columns[0] if per_step == 1 else jnp.concatenate(columns, axis=1)

    w_up, w_down = joined(0), joined(quarter)
    pre = jnp.maximum(dot(n2_ref[...], w_up, 1, 0), 0.0)
    activ = (pre * pre).astype(BF)
    grad_pre = (dot(go_ref[...], w_down, 1, 0) * 2.0 * pre).astype(BF)
    branch_ref[...] += dot(activ, w_down, 1, 1)
    grad_ref[...] += dot(grad_pre, w_up, 1, 1)
    for start, result in (
        (0, dot(n2t_ref[...], grad_pre, 1, 0)),
        (quarter, dot(got_ref[...], activ, 1, 0)),
    ):
        for apart in range(4):
            target = away_ref if apart & 1 else keep_ref
            for k in range(per_step):
                place = meta[(apart ^ meta[32]) * 8 + step * per_step + k] & 15
                target[place, start : start + quarter, :] = result[
                    apart * quarter : (apart + 1) * quarter, k * lanes : (k + 1) * lanes
                ].astype(BF)


def turn_kernel(meta, grad_ref, branch_ref, res_ref, gain_ref, go_ref, at_ref, wn_ref, out_ref, gres_ref, gatt_ref, ggain_ref, keep_ref, away_ref):
    residual = res_ref[...]
    seq = residual.shape[0]
    live = lax.broadcasted_iota(jnp.int32, (seq, 1), 0) < meta[33]
    out_ref[...] = jnp.where(live, residual + branch_ref[...], 0.0).astype(BF)
    hat, inv_std = hat_of(residual)
    grad = grad_ref[...]
    ggain_ref[...] = jnp.sum(grad * hat, axis=0, keepdims=True)
    scaled = grad * gain_ref[...]
    mean_first = jnp.mean(scaled, axis=-1, keepdims=True)
    mean_second = jnp.mean(scaled * hat, axis=-1, keepdims=True)
    grad_res = go_ref[...].astype(F32) + inv_std * (scaled - mean_first - hat * mean_second)
    gres_ref[...] = grad_res
    low = grad_res.astype(BF)
    gatt_ref[...] = dot(low, wn_ref[...], 1, 1).astype(BF)
    result = dot(at_ref[...], low, 1, 0)
    lanes = keep_ref.shape[2]
    chunks = result.shape[1] // lanes
    rows = keep_ref.shape[1] // chunks
    for i in range(32):
        target = away_ref if i >= 16 else keep_ref
        for c in range(chunks):
            target[i & 15, c * rows : (c + 1) * rows, :] = result[
                i * rows : (i + 1) * rows, c * lanes : (c + 1) * lanes
            ].astype(BF)


def attend_back_kernel(
    meta, q_ref, k_ref, v_ref, pq_ref, pk_ref, pv_ref, tq_ref, tk_ref, tv_ref, go_ref, out_ref, lse_ref,
    gq_ref, gk_ref, gv_ref, dtq_ref, dtk_ref, dtv_ref, flipped,
):
    seq = q_ref.shape[0]
    tile = LANES
    keys, values = k_ref[...], v_ref[...]
    keys_t = turned(keys)
    delta_t = jnp.transpose(go_ref[...].astype(F32) * out_ref[...].astype(F32))
    grad_keys = [jnp.zeros((tile, LANES), F32) for _ in range(seq // tile)]
    grad_values = list(grad_keys)
    for t in range(seq // tile):
        upto = (t + 1) * tile
        allowed = allowed_in(meta, upto, t * tile, tile)
        query, grad = q_ref[t * tile : upto, :], go_ref[t * tile : upto, :]
        for head in range(LANES // HD):
            lanes = slice(head * HD, (head + 1) * HD)
            query_h, grad_h = query * head_row(head, 0.125), grad * head_row(head)
            delta = jnp.sum(delta_t[lanes, t * tile : upto], axis=0, keepdims=True)
            scores = dot(keys[:upto], query_h, 1, 1)
            lse = lse_ref[0, head : head + 1, t * tile : upto]
            probs = jnp.where(allowed, jnp.exp(scores - lse), 0.0)
            grad_scores = (probs * (dot(values[:upto], grad_h, 1, 1) - delta)).astype(BF)
            flipped[lanes, t * tile : upto] = dot(keys_t[lanes, :upto], grad_scores, 1, 0) * 0.125
            add_values = dot(probs.astype(BF), grad_h, 1, 0)
            add_keys = dot(grad_scores, query_h, 1, 0)
            for s in range(t + 1):
                rows = slice(s * tile, (s + 1) * tile)
                grad_values[s] += add_values[rows]
                grad_keys[s] += add_keys[rows]
    mixed = (
        jnp.transpose(flipped[...]),
        jnp.concatenate(grad_keys, axis=0),
        jnp.concatenate(grad_values, axis=0),
    )
    at = lax.broadcasted_iota(jnp.int32, (seq, LANES), 0)
    for grad, proj_ref, taps_ref, g_ref, dt_ref in zip(
        mixed, (pq_ref, pk_ref, pv_ref), (tq_ref, tk_ref, tv_ref), (gq_ref, gk_ref, gv_ref), (dtq_ref, dtk_ref, dtv_ref)
    ):
        one = jnp.where(at < seq - 1, pltpu.roll(grad, seq - 1, 0), 0.0)
        two = jnp.where(at < seq - 2, pltpu.roll(grad, seq - 2, 0), 0.0)
        g_ref[...] = (grad * taps_ref[0:1, :] + one * taps_ref[1:2, :] + two * taps_ref[2:3, :]).astype(BF)
        proj = proj_ref[...].astype(F32)
        for tap, part in enumerate((grad, one, two)):
            dt_ref[tap : tap + 1, :] = jnp.sum(part * proj, axis=0, keepdims=True)


def weight_kernel(meta, nt_ref, *refs):
    keep_ref, away_ref = refs[-2:]
    half = keep_ref.shape[0]
    for j, g_ref in enumerate(refs[:-2]):
        result = dot(nt_ref[...], g_ref[...], 1, 0).astype(BF)
        columns = slice(j * LANES, (j + 1) * LANES)
        keep_ref[:, columns] = result[:half]
        away_ref[:, columns] = result[half:]


def last_kernel(meta, *refs):
    grads, (w_ref, x_ref, gain_ref, gres_ref, gin_ref, ggain_ref) = refs[:-6], refs[-6:]
    grad = dot(jnp.concatenate([g_ref[...] for g_ref in grads], axis=1), w_ref[...], 1, 1)
    hat, inv_std = hat_of(x_ref[...].astype(F32))
    ggain_ref[...] = jnp.sum(grad * hat, axis=0, keepdims=True)
    scaled = grad * gain_ref[...]
    mean_first = jnp.mean(scaled, axis=-1, keepdims=True)
    mean_second = jnp.mean(scaled * hat, axis=-1, keepdims=True)
    back = inv_std * (scaled - mean_first - hat * mean_second)
    gin_ref[...] = (gres_ref[...] + back).astype(BF)


def own_sequence(inputs, lengths, cotangent, w_qkv, w_out, conv_taps, gain_one, gain_two, w_in, w_fc2):
    seq, width = inputs.shape[1], inputs.shape[2]
    rows = w_qkv.shape[0]
    wide = w_qkv.shape[1]
    quarter = width // 4
    tap_rows = conv_taps.shape[0]
    batch = lax.axis_index("batch")
    me = batch * 8 + lax.axis_index("wide")
    number = jnp.arange(64, dtype=jnp.int32)
    meta = jnp.where(number < 32, place_of(me, number & 31), jnp.where(number == 32, batch, lengths[0]))
    natural = jax.nn.one_hot(meta[:32], 32, dtype=F32)
    x, cot = inputs[0], cotangent[0]
    shape = jax.ShapeDtypeStruct
    row_spec = whole((1, width))
    token = whole((seq, width))
    groups = width // LANES

    qkv_z = z_hops(w_qkv)
    small = jnp.zeros((rows, 128), BF)
    small = small.at[:3, :tap_rows].set(conv_taps.T)
    small = small.at[3, :rows].set(gain_one).at[4, :rows].set(gain_two)
    out_z = z_hops(jnp.concatenate([w_out, small], axis=1))
    grad_out, grad_out_t = call(
        prepare_kernel, (1,), [token], [token, whole((4, quarter, seq))],
        [shape((seq, width), BF), shape((4, quarter, seq), BF)], busy=3, name="prepare",
    )(meta, cot)
    up = lax.dynamic_slice(w_in, (batch * quarter, 0), (quarter, PART * PARTS))
    down = jnp.transpose(lax.dynamic_slice(w_fc2, (0, batch * quarter), (PART * PARTS, quarter)))
    ffn = [
        jnp.concatenate([up[:, c * PART : (c + 1) * PART], down[:, c * PART : (c + 1) * PART]])
        for c in range(PARTS)
    ]
    qkv4 = join(qkv_z)
    qkv_first = send(qkv4, over_first)
    f0_z = z_hops(tie(ffn[0], qkv_z[3]))
    out4 = join(out_z)
    out_first = send(out4, over_first)
    qkv8 = join([qkv4, tie(qkv_first, grad_out)])
    qkv_second = send(qkv8, over_second)
    out8 = join([out4, out_first])
    out_second = send(out8, over_second)
    qkv16 = join([qkv8, qkv_second])
    qkv_core = send(qkv16, over_core)
    out16 = join([out8, out_second])
    out_core = send(out16, over_core)
    f0_4 = join(f0_z)
    f0_first = send(tie(f0_4, qkv_second), over_first)
    f1_z = z_hops(tie(ffn[1], f0_z[3]))

    few = jnp.concatenate([out16[:, :, width:], out_core[:, :, width:]])
    few = jnp.einsum("dp,prl->drl", natural, few.astype(F32), precision="highest")
    taps = jnp.transpose(few[:, :3, :tap_rows], (1, 0, 2)).reshape(3, wide)
    taps = jnp.concatenate([taps, jnp.zeros((5, wide), F32)])
    gain_first = few[:, 3, :rows].reshape(1, width)
    gain_second = few[:, 4, :rows].reshape(1, width)

    lane_block = pl.BlockSpec((seq, LANES), lambda j, m: (0, j))
    half_block = pl.BlockSpec((16, rows, LANES), lambda j, m: (0, 0, j))
    projected, mixed, qkv_full, normed_t = call(
        project_kernel, (wide // LANES,),
        [token, row_spec, pl.BlockSpec((8, LANES), lambda j, m: (0, j)), half_block, half_block],
        [lane_block, lane_block, pl.BlockSpec((width, LANES), lambda j, m: (0, j)), whole((32, rows, seq))],
        [shape((seq, wide), BF), shape((seq, wide), BF), shape((width, wide), BF), shape((32, rows, seq), BF)],
        [pltpu.VMEM((seq, width), BF)], busy=11.5, name="project",
    )(meta, tie(x, f0_4), gain_first, taps, qkv16, qkv_core)

    f0_8 = join([f0_4, tie(f0_first, mixed)])
    f0_second = send(f0_8, over_second)
    f1_4 = join([f1_z[0]] + [tie(part, mixed) for part in f1_z[1:]])
    f1_first = send(f1_4, over_first)
    f2_z = z_hops(tie(ffn[2], f1_4))
    part_specs = [pl.BlockSpec((seq, LANES), lambda j, m, p=p: (0, p * groups + j)) for p in range(3)]
    lse_spec = pl.BlockSpec((1, 8, seq), lambda j, m: (j, 0, 0))
    ready = tie(mixed, f0_8, f1_4)
    attended, lse = call(
        attend_kernel, (groups,), part_specs, [lane_block, lse_spec],
        [shape((seq, width), BF), shape((groups, 8, seq), F32)], [pltpu.VMEM((LANES, seq), F32)],
        busy=11, name="attend",
    )(meta, ready, ready, ready)

    f0_16 = join([f0_8, tie(f0_second, attended)])
    f0_core = send(f0_16, over_core)
    f1_8 = join([f1_4, tie(f1_first, attended)])
    f1_second = send(f1_8, over_second)
    f2_4 = join([f2_z[0]] + [tie(part, attended) for part in f2_z[1:]])
    f2_first = send(f2_4, over_first)
    out_half = pl.BlockSpec((16, rows, width), lambda j, m: (0, 0, 0))
    residual, normed_two, normed_two_t, attended_t, out_full = call(
        mend_kernel, (1,),
        [token, out_half, out_half, token, row_spec],
        [token, token, whole((4, quarter, seq)), whole((32, rows, seq)), whole((width, width))],
        [shape((seq, width), F32), shape((seq, width), BF), shape((4, quarter, seq), BF), shape((32, rows, seq), BF),
         shape((width, width), BF)],
        busy=6.3, name="mend",
    )(meta, tie(attended, f0_16, f1_8, f2_4), out16, out_core, x, gain_second)

    normed_two_t = normed_two_t.reshape(width, seq)
    grad_out_t = grad_out_t.reshape(width, seq)
    per_step = LANES // PART
    grad_spec = whole((16, 2 * quarter, PART))

    def feed_forward(own, other, sums, wait_for):
        tile_specs = [
            pl.BlockSpec(
                (1, 2 * quarter, PART),
                lambda s, m, b=b, k=k, h=h: (
                    jnp.where((m[b * 8 + s * per_step + k] >> 4) == h, m[b * 8 + s * per_step + k] & 15, 0), 0, 0
                ),
            )
            for h in range(2)
            for k in range(per_step)
            for b in range(4)
        ]
        return call(
            functools.partial(ffn_kernel, per_step, not sums), (8 // per_step,),
            [token, token, whole((width, seq)), whole((width, seq))] + tile_specs + [token] * len(sums),
            [token, token, grad_spec, grad_spec],
            [shape((seq, width), F32)] * 2 + [shape((16, 2 * quarter, PART), BF)] * 2,
            busy=9, name="ffn",
        )(meta, tie(normed_two, *wait_for), grad_out, normed_two_t, grad_out_t,
          *[own] * (4 * per_step), *[other] * (4 * per_step), *sums)

    f0_core = tie(f0_core, normed_two)
    f2_8 = join([f2_4, tie(f2_first, normed_two)])
    f2_second = send(f2_8, over_second)
    f1_16 = join([f1_8, tie(f1_second, normed_two)])
    f1_core = send(f1_16, over_core)
    branch, grad_two, keep0, away0 = feed_forward(f0_16, f0_core, (), (f1_16, f2_8))

    f2_16 = join([f2_8, tie(f2_second, branch)])
    f2_core = send(f2_16, over_core)
    r0_core = send(away0, over_core)
    f1_core = tie(f1_core, branch)
    branch, grad_two, keep1, away1 = feed_forward(f1_16, f1_core, (branch, grad_two), (f2_16, away0))

    f2_core = tie(f2_core, branch)
    r0_keep, r0_go = add_core(keep0, tie(r0_core, branch))
    r0_go = r0_go.astype(BF)
    r0_second = send(r0_go, over_second)
    r1_core = send(away1, over_core)
    branch, grad_two, keep2, away2 = feed_forward(f2_16, f2_core, (branch, grad_two), (r0_go, away1))

    r0_keep, r0_go = add_half(r0_keep, tie(r0_second, branch))
    r0_go = r0_go.astype(BF)
    r0_first = send(r0_go, over_first)
    r1_keep, r1_go = add_core(keep1, tie(r1_core, branch))
    r1_go = r1_go.astype(BF)
    r1_second = send(r1_go, over_second)
    r2_core = send(away2, over_core)
    half_out = shape((16, rows * (width // PART), PART), BF)
    output, grad_residual, grad_attended, grad_gain_second, keep_out, away_out = call(
        turn_kernel, (1,),
        [token] * 3 + [row_spec, token, whole((width, seq)), whole((width, width))],
        [token] * 3 + [row_spec, whole(half_out.shape), whole(half_out.shape)],
        [shape((seq, width), BF), shape((seq, width), F32), shape((seq, width), BF), shape((1, width), F32),
         half_out, half_out],
        busy=7, name="turn",
    )(meta, tie(grad_two, r0_go, r1_go, away2), branch, residual, gain_second, grad_out,
      attended_t.reshape(width, seq), out_full)

    def attend_back(j, wait_for):
        specs = [pl.BlockSpec((seq, LANES), lambda i, m, p=p: (0, p * groups + j)) for p in range(3)]
        tap_specs = [pl.BlockSpec((8, LANES), lambda i, m, p=p: (0, p * groups + j)) for p in range(3)]
        block = pl.BlockSpec((seq, LANES), lambda i, m: (0, j))
        return call(
            attend_back_kernel, (1,),
            specs * 2 + tap_specs + [block, block, pl.BlockSpec((1, 8, seq), lambda i, m: (j, 0, 0))],
            [whole((seq, LANES))] * 3 + [whole((8, LANES))] * 3,
            [shape((seq, LANES), BF)] * 3 + [shape((8, LANES), F32)] * 3,
            [pltpu.VMEM((LANES, seq), F32)],
            busy=5.5, name="attend_back",
        )(meta, mixed, mixed, mixed, projected, projected, projected, taps, taps, taps,
          tie(grad_attended, *wait_for), attended, lse)

    r0_total = r0_keep + tie(r0_first, grad_attended).astype(F32)
    r0_z = z_sends(r0_total)
    r1_keep, r1_go = add_half(r1_keep, tie(r1_second, grad_attended))
    r1_go = r1_go.astype(BF)
    r1_first = send(r1_go, over_first)
    r2_keep, r2_go = add_core(keep2, tie(r2_core, grad_attended))
    out_come = send(away_out, over_core)
    back0 = attend_back(0, (r0_total, r1_go, away_out))

    r0_z = [tie(part, back0[0]) for part in r0_z]
    r1_total = r1_keep + tie(r1_first, back0[0]).astype(F32)
    r1_z = z_sends(r1_total)
    out_keep, out_go = add_core(keep_out, tie(out_come, back0[0]))
    r2_keep = jnp.concatenate([r2_keep, out_keep], axis=1)
    r2_go = jnp.concatenate([r2_go.astype(BF), out_go.astype(BF)], axis=1)
    r2_second = send(r2_go, over_second)
    back1 = attend_back(1, (back0[0], r1_total, r2_go))

    r1_z = [tie(part, back1[0]) for part in r1_z]
    r2_keep, r2_go = add_half(r2_keep, tie(r2_second, back1[0]))
    r2_go = r2_go.astype(BF)
    r2_first = send(r2_go, over_first)
    back2 = attend_back(2, (back1[0], r2_go))

    r2_total = r2_keep + tie(r2_first, back2[0]).astype(F32)
    r2_z = z_sends(r2_total)
    backs = (back0, back1, back2)
    grad_projected = [back[part] for part in range(3) for back in backs]
    half_spec = whole((width // 2, wide))
    keep_qkv, away_qkv = call(
        weight_kernel, (1,), [whole((width, seq))] + [whole((seq, LANES))] * (3 * groups), [half_spec, half_spec],
        [shape((width // 2, wide), BF)] * 2, busy=6.7, name="weight",
    )(meta, tie(normed_t.reshape(width, seq), r2_total), *grad_projected)
    by_block = (16, rows, wide)
    keep_qkv, away_qkv = keep_qkv.reshape(by_block), away_qkv.reshape(by_block)
    r2_z = [tie(part, away_qkv) for part in r2_z]
    qkv_keep, qkv_go = add_core(keep_qkv, send(away_qkv, over_core))
    qkv_go = qkv_go.astype(BF)
    q_second = send(qkv_go, over_second)
    grad_inputs, grad_gain_first = call(
        last_kernel, (1,),
        [whole((seq, LANES))] * (3 * groups) + [whole((width, wide)), token, row_spec, token],
        [token, row_spec], [shape((seq, width), BF), shape((1, width), F32)],
        busy=8.7, name="last",
    )(meta, *grad_projected, qkv_full, x, gain_first, tie(grad_residual, qkv_go))
    qkv_keep, qkv_go = add_half(qkv_keep, tie(q_second, grad_gain_first))
    qkv_first = send(qkv_go.astype(BF), over_first)

    tap_grads = jnp.concatenate([back[3 + part][:3] for part in range(3) for back in backs], axis=1)
    tap_grads = jnp.transpose(tap_grads.reshape(3, 32, tap_rows), (1, 0, 2))
    gain_grads = jnp.stack([grad_gain_first.reshape(32, rows), grad_gain_second.reshape(32, rows)], axis=1)
    few = jnp.zeros((32, 8, 128), F32)
    few = few.at[:, :3, :tap_rows].set(tap_grads).at[:, 3:5, :rows].set(gain_grads)
    few = jnp.einsum("dp,drl->prl", natural, few, precision="highest")
    few_keep, few_go = add_core(few[:16], send(few[16:], over_core))
    few_keep, few_go = add_half(few_keep, send(few_go, over_second))
    few_total = few_keep + send(few_go, over_first)
    few = add_z(few_total, z_sends(few_total, F32))
    qkv_total = qkv_keep + qkv_first.astype(F32)
    grad_qkv = add_z(qkv_total, z_sends(qkv_total))

    grad0 = add_z(r0_total, r0_z)
    grad1 = add_z(r1_total, r1_z)
    grad2 = add_z(r2_total, r2_z)
    grad_out_w = grad2[2 * quarter :]
    grad_out_w = jnp.concatenate(
        [grad_out_w[c * rows : (c + 1) * rows] for c in range(width // PART)], axis=1
    )
    grad_in_w = jnp.concatenate([grad0[:quarter], grad1[:quarter], grad2[:quarter]], axis=1)
    grad_fc2_w = jnp.concatenate([g[quarter : 2 * quarter] for g in (grad0, grad1, grad2)], axis=1)
    return (
        output[None],
        grad_inputs[None],
        grad_qkv,
        grad_out_w,
        few[:3, :tap_rows].T,
        few[3, :rows],
        few[4, :rows],
        grad_in_w,
        jnp.transpose(grad_fc2_w),
    )


def solution(mesh):
    fast = functools.partial(own_sequence)

    def program(*args):
        body = fast if fits(mesh, args) else shards
        return jax.shard_map(
            body,
            mesh=mesh,
            in_specs=(
                P(("batch", "wide"), None, None),
                P(("batch", "wide")),
                P(("batch", "wide"), None, None),
                P(("batch", "wide"), None),
                P(("batch", "wide"), None),
                P(("batch", "wide"), None),
                P(("batch", "wide")),
                P(("batch", "wide")),
                P(None, "wide"),
                P("wide", None),
            ),
            out_specs=(
                P(("batch", "wide"), None, None),
                P(("batch", "wide"), None, None),
                P(("batch", "wide"), None),
                P(("batch", "wide"), None),
                P(("batch", "wide"), None),
                P(("batch", "wide")),
                P(("batch", "wide")),
                P("batch", "wide"),
                P("wide", "batch"),
            ),
            check_vma=False,
        )(*args)

    return program
```

```python
import functools
import jax
import jax.numpy as jnp
from jax import lax
from jax.experimental import pallas as pl
from jax.experimental.pallas import tpu as pltpu
from jax.sharding import PartitionSpec as P

HEADS = 12
HD = 64


epsilon = 1e-05


def contract_first(left, right):
    return lax.dot_general(
        left, right, (((0,), (0,)), ((), ())), preferred_element_type=jnp.float32
    )


def contract_last(left, right):
    return lax.dot_general(
        left, right, (((1,), (1,)), ((), ())), preferred_element_type=jnp.float32
    )


def norm_parts(values_in):
    centered = values_in - jnp.mean(values_in, axis=-1, keepdims=True)
    inv_std = lax.rsqrt(jnp.mean(centered * centered, axis=-1, keepdims=True) + epsilon)
    return (centered * inv_std, inv_std)


def norm_back(grad_normed, gain_vec, normed_hat, inv_std):
    grad_hat = grad_normed * gain_vec
    mean_first = jnp.mean(grad_hat, axis=-1, keepdims=True)
    mean_second = jnp.mean(grad_hat * normed_hat, axis=-1, keepdims=True)
    grad_value = inv_std * (grad_hat - mean_first - normed_hat * mean_second)
    return (grad_value, jnp.sum(grad_normed * normed_hat, axis=0))


def shift_down(signal, steps):
    filler = jnp.zeros((steps, signal.shape[1]), signal.dtype)
    return jnp.concatenate([filler, signal[:-steps]], axis=0)


def shift_up(signal, steps):
    filler = jnp.zeros((steps, signal.shape[1]), signal.dtype)
    return jnp.concatenate([signal[steps:], filler], axis=0)


def scores_block(query_block, keys, start_row, seq_live):
    rows_block = query_block.shape[0]
    scores = (
        jnp.einsum("qhd,khd->hqk", query_block, keys, preferred_element_type=jnp.float32) * 0.125
    )
    query_pos = start_row + jnp.arange(rows_block)
    key_pos = jnp.arange(keys.shape[0])
    allowed = (key_pos[None, :] <= query_pos[:, None]) & (key_pos[None, :] < seq_live)
    return (scores, allowed[None])


def shards(inputs, lengths, cotangent, w_qkv, w_out, conv_taps, gain_one, gain_two, w_in, w_fc2):
    full_qkv, full_out, full_taps, full_gain_one, full_gain_two = (
        lax.all_gather(w_qkv, ("batch", "wide"), axis=0, tiled=True),
        lax.all_gather(w_out, ("batch", "wide"), axis=0, tiled=True),
        lax.all_gather(conv_taps, ("batch", "wide"), axis=0, tiled=True),
        lax.all_gather(gain_one, ("batch", "wide"), axis=0, tiled=True),
        lax.all_gather(gain_two, ("batch", "wide"), axis=0, tiled=True),
    )
    seq_length, width = (inputs.shape[1], inputs.shape[2])
    tokens_in = inputs[0].astype(jnp.float32)
    seq_live = lengths[0]
    live_rows = jnp.arange(seq_length) < seq_live
    taps = full_taps.astype(jnp.float32)
    gain_first = full_gain_one.astype(jnp.float32)
    gain_second = full_gain_two.astype(jnp.float32)
    hat_one, inv_one = norm_parts(tokens_in)
    normed_one = (hat_one * gain_first).astype(jnp.bfloat16)
    projected = jnp.dot(normed_one, full_qkv, preferred_element_type=jnp.float32)
    mixed = (
        projected * taps[:, 0]
        + shift_down(projected, 1) * taps[:, 1]
        + shift_down(projected, 2) * taps[:, 2]
    ).astype(jnp.bfloat16)
    query = mixed[:, :width].reshape(seq_length, HEADS, HD)
    keys = mixed[:, width : 2 * width].reshape(seq_length, HEADS, HD)
    values = mixed[:, 2 * width :].reshape(seq_length, HEADS, HD)
    rows_block = min(512, seq_length)
    block_index = 0
    start_row = block_index * rows_block
    scores, allowed = scores_block(query, keys, start_row, seq_live)
    masked = jnp.where(allowed, scores, -1e30)
    top_score = jnp.max(masked, axis=-1, keepdims=True)
    exp_terms = jnp.exp(masked - top_score)
    row_totals = jnp.sum(exp_terms, axis=-1, keepdims=True)
    probs_low = (exp_terms / row_totals).astype(jnp.bfloat16)
    out_parts = jnp.einsum("hqk,khd->qhd", probs_low, values, preferred_element_type=jnp.float32)
    lse_parts = [top_score + jnp.log(row_totals)]
    attended_low = out_parts.reshape(seq_length, width).astype(jnp.bfloat16)
    branch_attn = jnp.dot(attended_low, full_out, preferred_element_type=jnp.float32)
    residual = tokens_in + branch_attn
    hat_two, inv_two = norm_parts(residual)
    normed_two = (hat_two * gain_second).astype(jnp.bfloat16)
    grad_out = jnp.where(live_rows[:, None], cotangent[0], jnp.zeros_like(cotangent[0]))
    row_set = lax.all_gather(normed_two[None], "wide", axis=0, tiled=True).reshape(-1, width)
    pre_act = jnp.dot(row_set, w_in, preferred_element_type=jnp.float32)
    activ = jnp.square(jax.nn.relu(pre_act)).astype(jnp.bfloat16)
    piece = activ
    branch_ffn = lax.psum_scatter(
        jnp.dot(piece, w_fc2, preferred_element_type=jnp.float32).astype(jnp.bfloat16),
        "wide",
        scatter_dimension=0,
        tiled=True,
    ).astype(jnp.float32)
    grad_set = lax.all_gather(grad_out[None], "wide", axis=0, tiled=True).reshape(-1, width)
    grad_act = contract_last(grad_set, w_fc2)
    grad_fc2_part = contract_first(activ, grad_set)
    grad_pre = (grad_act * 2.0 * jax.nn.relu(pre_act)).astype(jnp.bfloat16)
    grad_in_part = contract_first(row_set, grad_pre)
    piece = grad_pre
    grad_normed_two = lax.psum_scatter(
        contract_last(piece, w_in).astype(jnp.bfloat16), "wide", scatter_dimension=0, tiled=True
    ).astype(jnp.float32)
    grad_w_in, grad_w_fc2 = (
        lax.psum_scatter(
            grad_in_part.astype(jnp.bfloat16), "batch", scatter_dimension=0, tiled=True
        ).astype(jnp.float32),
        lax.psum_scatter(
            grad_fc2_part.astype(jnp.bfloat16), "batch", scatter_dimension=1, tiled=True
        ).astype(jnp.float32),
    )
    output = jnp.where(live_rows[:, None], residual + branch_ffn, 0.0).astype(jnp.bfloat16)[None]
    grad_ln_two, grad_gain_second = norm_back(grad_normed_two, gain_second, hat_two, inv_two)
    grad_residual = grad_out.astype(jnp.float32) + grad_ln_two
    grad_branch = grad_residual.astype(jnp.bfloat16)
    grad_w_out_part = contract_first(attended_low, grad_branch)
    grad_attended = contract_last(grad_branch, full_out).astype(jnp.bfloat16)
    grad_att_heads = grad_attended.reshape(seq_length, HEADS, HD)
    delta_all = jnp.sum(grad_att_heads.astype(jnp.float32) * out_parts, axis=-1)
    block_index = 0
    start_row = block_index * rows_block
    scores, allowed = scores_block(query, keys, start_row, seq_live)
    probs_full = jnp.where(allowed, jnp.exp(scores - lse_parts[block_index]), 0.0)
    probs_low = probs_full.astype(jnp.bfloat16)
    grad_probs = jnp.einsum(
        "qhd,khd->hqk", grad_att_heads, values, preferred_element_type=jnp.float32
    )
    delta_block = jnp.transpose(delta_all)[:, :, None]
    grad_scores = (probs_full * (grad_probs - delta_block)).astype(jnp.bfloat16)
    grad_query_parts = 0.125 * jnp.einsum(
        "hqk,khd->qhd", grad_scores, keys, preferred_element_type=jnp.float32
    )
    grad_keys = 0.125 * jnp.einsum(
        "hqk,qhd->khd", grad_scores, query, preferred_element_type=jnp.float32
    )
    grad_values = jnp.einsum(
        "hqk,qhd->khd", probs_low, grad_att_heads, preferred_element_type=jnp.float32
    )
    grad_mixed = jnp.concatenate(
        [
            grad_query_parts.reshape(seq_length, width),
            grad_keys.reshape(seq_length, width),
            grad_values.reshape(seq_length, width),
        ],
        axis=1,
    )
    grad_taps_part = jnp.stack(
        [
            jnp.sum(grad_mixed * projected, axis=0),
            jnp.sum(grad_mixed * shift_down(projected, 1), axis=0),
            jnp.sum(grad_mixed * shift_down(projected, 2), axis=0),
        ],
        axis=1,
    )
    grad_projected = (
        grad_mixed * taps[:, 0]
        + shift_up(grad_mixed, 1) * taps[:, 1]
        + shift_up(grad_mixed, 2) * taps[:, 2]
    ).astype(jnp.bfloat16)
    grad_qkv_part = contract_first(normed_one, grad_projected)
    grad_normed_one = contract_last(grad_projected, full_qkv)
    grad_ln_one, grad_gain_first = norm_back(grad_normed_one, gain_first, hat_one, inv_one)
    grad_inputs = (grad_residual + grad_ln_one).astype(jnp.bfloat16)[None]
    grad_w_qkv, grad_w_out, grad_conv_taps, grad_gain_one, grad_gain_two = (
        lax.psum_scatter(grad_qkv_part, ("batch", "wide"), scatter_dimension=0, tiled=True),
        lax.psum_scatter(grad_w_out_part, ("batch", "wide"), scatter_dimension=0, tiled=True),
        lax.psum_scatter(grad_taps_part, ("batch", "wide"), scatter_dimension=0, tiled=True),
        lax.psum_scatter(grad_gain_first, ("batch", "wide"), scatter_dimension=0, tiled=True),
        lax.psum_scatter(grad_gain_second, ("batch", "wide"), scatter_dimension=0, tiled=True),
    )
    return (
        output,
        grad_inputs,
        grad_w_qkv,
        grad_w_out,
        grad_conv_taps,
        grad_gain_one,
        grad_gain_two,
        grad_w_in,
        grad_w_fc2,
    )


BF = jnp.bfloat16
F32 = jnp.float32
AXES = ("batch", "wide")
LANES = 256
LIMIT = {"ffn": 40}
PART = 128
PARTS = 3


def fits(mesh, args):
    inputs, w_qkv, w_in = args[0], args[3], args[8]
    count = mesh.shape["batch"] * mesh.shape["wide"]
    return (
        mesh.shape["batch"] == 4
        and mesh.shape["wide"] == 8
        and inputs.shape[0] == count
        and inputs.shape[1] % LANES == 0
        and w_qkv.shape[0] % (count * 8) == 0
        and w_qkv.shape[0] % LANES == 0
        and w_qkv.shape[0] // HEADS == HD
        and w_in.shape[1] == 8 * PART * PARTS
        and (w_in.shape[0] // 4) % 16 == 0
    )


def dot(left, right, left_dim, right_dim):
    return lax.dot_general(
        left, right, (((left_dim,), (right_dim,)), ((), ())), preferred_element_type=F32
    )


def flip_pairs(rule):
    return [(i, i ^ rule(i)) for i in range(32)]


def send(array, rule):
    return lax.ppermute(array, AXES, flip_pairs(rule))


def over_core(i):
    return 8


def over_first(i):
    return 16 if i & 8 else 1


def over_second(i):
    return 1 if i & 8 else 16


def over_z(step):
    return lambda i: 2 * step


def tie(value, *others):
    return lax.optimization_barrier((value,) + others)[0]


def z_hops(block):
    return [block[None]] + [send(block[None], over_z(s)) for s in (1, 2, 3)]


def join(parts):
    return jnp.concatenate(parts)


def add_core(keep, come):
    half = keep.shape[0] // 2
    total = keep.astype(F32) + come.astype(F32)
    return total[:half], total[half:]


def add_half(total, come):
    half = total.shape[0] // 2
    total = total + come.astype(F32)
    return total[:half], total[half:]


def add_z(total, come):
    return total[0] + (come[0].astype(F32) + (come[1].astype(F32) + come[2].astype(F32)))


def z_sends(total, wire=BF):
    return [send(total[s].astype(wire), over_z(s)) for s in (1, 2, 3)]


def place_of(me, other):
    apart = me ^ other
    x_bit, z_bits = apart & 1, (apart >> 1) & 3
    core_bit, y_bit = (apart >> 3) & 1, (apart >> 4) & 1
    on_first = ((other >> 3) & 1) == 0
    high = jnp.where(on_first, y_bit, x_bit)
    low = jnp.where(on_first, x_bit, y_bit)
    return core_bit * 16 + high * 8 + low * 4 + z_bits


def call(kernel, grid, in_specs, out_specs, out_shape, scratch=(), busy=1, name=None, aliases=None):
    return pl.pallas_call(
        kernel,
        grid_spec=pltpu.PrefetchScalarGridSpec(
            num_scalar_prefetch=1,
            grid=grid,
            in_specs=in_specs,
            out_specs=out_specs,
            scratch_shapes=list(scratch),
        ),
        out_shape=out_shape,
        compiler_params=pltpu.CompilerParams(
            dimension_semantics=("arbitrary",) * len(grid), vmem_limit_bytes=LIMIT.get(name, 24) * 1024 * 1024
        ),
        cost_estimate=pl.CostEstimate(flops=int(busy * 1.15e9), bytes_accessed=0, transcendentals=0),
        name=name,
        input_output_aliases=aliases or {},
    )


def whole(shape):
    zeros = (0,) * len(shape)
    return pl.BlockSpec(shape, lambda *_: zeros)


def hat_of(values_in):
    centered = values_in - jnp.mean(values_in, axis=-1, keepdims=True)
    inv_std = lax.rsqrt(jnp.mean(centered * centered, axis=-1, keepdims=True) + epsilon)
    return centered * inv_std, inv_std


def turned(value):
    return jnp.transpose(value.astype(F32)).astype(BF)


def prepare_kernel(meta, cot_ref, go_ref, got_ref):
    seq = cot_ref.shape[0]
    quarter = got_ref.shape[1]
    live = lax.broadcasted_iota(jnp.int32, (seq, 1), 0) < meta[33]
    value = jnp.where(live, cot_ref[...].astype(F32), 0.0)
    go_ref[...] = value.astype(BF)
    flipped = jnp.transpose(value).astype(BF)
    for b in range(4):
        got_ref[b ^ meta[32]] = flipped[b * quarter : (b + 1) * quarter]


def block_of(meta, i, own_ref, other_ref):
    place = meta[i]
    return jnp.where(place < 16, own_ref[place & 15], other_ref[place & 15])


def project_kernel(meta, x_ref, gain_ref, taps_ref, own_ref, other_ref, proj_ref, mixed_ref, wn_ref, nt_ref, normed):
    rows = own_ref.shape[1]

    @pl.when(pl.program_id(0) == 0)
    def _():
        hat, _ = hat_of(x_ref[...].astype(F32))
        low = (hat * gain_ref[...]).astype(BF)
        normed[...] = low
        flipped = turned(low)
        for i in range(32):
            nt_ref[meta[i]] = flipped[i * rows : (i + 1) * rows]

    for i in range(32):
        wn_ref[i * rows : (i + 1) * rows, :] = block_of(meta, i, own_ref, other_ref)
    value = dot(normed[...], wn_ref[...], 1, 0)
    at = lax.broadcasted_iota(jnp.int32, value.shape, 0)
    one = jnp.where(at >= 1, pltpu.roll(value, 1, 0), 0.0)
    two = jnp.where(at >= 2, pltpu.roll(value, 2, 0), 0.0)
    mixed = value * taps_ref[0:1, :] + one * taps_ref[1:2, :] + two * taps_ref[2:3, :]
    proj_ref[...] = value.astype(BF)
    mixed_ref[...] = mixed.astype(BF)


def head_row(head, scale=1.0):
    lane = lax.broadcasted_iota(jnp.int32, (1, LANES), 1)
    return jnp.where(lane // HD == head, scale, 0.0).astype(BF)


def allowed_in(meta, keys, first_query, queries):
    key = lax.broadcasted_iota(jnp.int32, (keys, queries), 0)
    query = first_query + lax.broadcasted_iota(jnp.int32, (1, queries), 1)
    return key < jnp.minimum(query + 1, meta[33])


def attend_kernel(meta, q_ref, k_ref, v_ref, out_ref, lse_ref, flipped):
    seq = q_ref.shape[0]
    tile = LANES
    values_t = turned(v_ref[...])
    keys = k_ref[...]
    for t in range(seq // tile):
        upto = (t + 1) * tile
        allowed = allowed_in(meta, upto, t * tile, tile)
        query = q_ref[t * tile : upto, :]
        for head in range(LANES // HD):
            scores = dot(keys[:upto], query * head_row(head, 0.125), 1, 1)
            scores = jnp.where(allowed, scores, -1e30)
            top = jnp.max(scores, axis=0, keepdims=True)
            terms = jnp.exp(scores - top)
            total = jnp.sum(terms, axis=0, keepdims=True)
            probs = (terms * (1.0 / total)).astype(BF)
            flipped[head * HD : (head + 1) * HD, t * tile : upto] = dot(
                values_t[head * HD : (head + 1) * HD, :upto], probs, 1, 0
            )
            lse_ref[0, head : head + 1, t * tile : upto] = top + jnp.log(total)
    out_ref[...] = jnp.transpose(flipped[...]).astype(BF)


def mend_kernel(meta, att_ref, own_ref, other_ref, x_ref, gain_ref, res_ref, n2_ref, n2t_ref, at_ref, wn_ref):
    flipped = turned(att_ref[...])
    rows = at_ref.shape[1]
    for i in range(32):
        at_ref[meta[i]] = flipped[i * rows : (i + 1) * rows]
        wn_ref[i * rows : (i + 1) * rows, :] = block_of(meta, i, own_ref, other_ref)
    residual = x_ref[...].astype(F32) + dot(att_ref[...], wn_ref[...], 1, 0)
    res_ref[...] = residual
    hat, _ = hat_of(residual)
    low = (hat * gain_ref[...]).astype(BF)
    n2_ref[...] = low
    flipped = turned(low)
    quarter = n2t_ref.shape[1]
    for b in range(4):
        n2t_ref[b ^ meta[32]] = flipped[b * quarter : (b + 1) * quarter]


def ffn_kernel(per_step, first, meta, n2_ref, go_ref, n2t_ref, got_ref, *refs):
    count = 4 * per_step
    own, other, refs = refs[:count], refs[count : 2 * count], refs[2 * count :]
    if not first:
        branch_in, grad_in = refs[:2]
        refs = refs[2:]
    branch_ref, grad_ref, keep_ref, away_ref = refs
    step = pl.program_id(0)

    @pl.when(step == 0)
    def _():
        if first:
            branch_ref[...] = jnp.zeros_like(branch_ref)
            grad_ref[...] = jnp.zeros_like(grad_ref)
        else:
            branch_ref[...] = branch_in[...]
            grad_ref[...] = grad_in[...]

    quarter = own[0].shape[1] // 2
    lanes = own[0].shape[2]

    def tile(b, k, start):
        place = meta[b * 8 + step * per_step + k]
        rows = slice(start, start + quarter)
        return jnp.where(place < 16, own[4 * k + b][0, rows, :], other[4 * k + b][0, rows, :])

    def joined(start):
        columns = [jnp.concatenate([tile(b, k, start) for b in range(4)], axis=0) for k in range(per_step)]
        return columns[0] if per_step == 1 else jnp.concatenate(columns, axis=1)

    w_up, w_down = joined(0), joined(quarter)
    pre = jnp.maximum(dot(n2_ref[...], w_up, 1, 0), 0.0)
    activ = (pre * pre).astype(BF)
    grad_pre = (dot(go_ref[...], w_down, 1, 0) * 2.0 * pre).astype(BF)
    branch_ref[...] += dot(activ, w_down, 1, 1)
    grad_ref[...] += dot(grad_pre, w_up, 1, 1)
    for start, result in (
        (0, dot(n2t_ref[...], grad_pre, 1, 0)),
        (quarter, dot(got_ref[...], activ, 1, 0)),
    ):
        for apart in range(4):
            target = away_ref if apart & 1 else keep_ref
            for k in range(per_step):
                place = meta[(apart ^ meta[32]) * 8 + step * per_step + k] & 15
                target[place, start : start + quarter, :] = result[
                    apart * quarter : (apart + 1) * quarter, k * lanes : (k + 1) * lanes
                ].astype(BF)


def turn_kernel(meta, grad_ref, branch_ref, res_ref, gain_ref, go_ref, at_ref, wn_ref, out_ref, gres_ref, gatt_ref, ggain_ref, keep_ref, away_ref):
    residual = res_ref[...]
    seq = residual.shape[0]
    live = lax.broadcasted_iota(jnp.int32, (seq, 1), 0) < meta[33]
    out_ref[...] = jnp.where(live, residual + branch_ref[...], 0.0).astype(BF)
    hat, inv_std = hat_of(residual)
    grad = grad_ref[...]
    ggain_ref[...] = jnp.sum(grad * hat, axis=0, keepdims=True)
    scaled = grad * gain_ref[...]
    mean_first = jnp.mean(scaled, axis=-1, keepdims=True)
    mean_second = jnp.mean(scaled * hat, axis=-1, keepdims=True)
    grad_res = go_ref[...].astype(F32) + inv_std * (scaled - mean_first - hat * mean_second)
    gres_ref[...] = grad_res
    low = grad_res.astype(BF)
    gatt_ref[...] = dot(low, wn_ref[...], 1, 1).astype(BF)
    result = dot(at_ref[...], low, 1, 0)
    lanes = keep_ref.shape[2]
    chunks = result.shape[1] // lanes
    rows = keep_ref.shape[1] // chunks
    for i in range(32):
        target = away_ref if i >= 16 else keep_ref
        for c in range(chunks):
            target[i & 15, c * rows : (c + 1) * rows, :] = result[
                i * rows : (i + 1) * rows, c * lanes : (c + 1) * lanes
            ].astype(BF)


def attend_back_kernel(
    meta, q_ref, k_ref, v_ref, pq_ref, pk_ref, pv_ref, tq_ref, tk_ref, tv_ref, go_ref, out_ref, lse_ref,
    gq_ref, gk_ref, gv_ref, dtq_ref, dtk_ref, dtv_ref, flipped,
):
    seq = q_ref.shape[0]
    tile = LANES
    keys, values = k_ref[...], v_ref[...]
    keys_t = turned(keys)
    delta_t = jnp.transpose(go_ref[...].astype(F32) * out_ref[...].astype(F32))
    grad_keys = [jnp.zeros((tile, LANES), F32) for _ in range(seq // tile)]
    grad_values = list(grad_keys)
    for t in range(seq // tile):
        upto = (t + 1) * tile
        allowed = allowed_in(meta, upto, t * tile, tile)
        query, grad = q_ref[t * tile : upto, :], go_ref[t * tile : upto, :]
        for head in range(LANES // HD):
            lanes = slice(head * HD, (head + 1) * HD)
            query_h, grad_h = query * head_row(head, 0.125), grad * head_row(head)
            delta = jnp.sum(delta_t[lanes, t * tile : upto], axis=0, keepdims=True)
            scores = dot(keys[:upto], query_h, 1, 1)
            lse = lse_ref[0, head : head + 1, t * tile : upto]
            probs = jnp.where(allowed, jnp.exp(scores - lse), 0.0)
            grad_scores = (probs * (dot(values[:upto], grad_h, 1, 1) - delta)).astype(BF)
            flipped[lanes, t * tile : upto] = dot(keys_t[lanes, :upto], grad_scores, 1, 0) * 0.125
            add_values = dot(probs.astype(BF), grad_h, 1, 0)
            add_keys = dot(grad_scores, query_h, 1, 0)
            for s in range(t + 1):
                rows = slice(s * tile, (s + 1) * tile)
                grad_values[s] += add_values[rows]
                grad_keys[s] += add_keys[rows]
    mixed = (
        jnp.transpose(flipped[...]),
        jnp.concatenate(grad_keys, axis=0),
        jnp.concatenate(grad_values, axis=0),
    )
    at = lax.broadcasted_iota(jnp.int32, (seq, LANES), 0)
    for grad, proj_ref, taps_ref, g_ref, dt_ref in zip(
        mixed, (pq_ref, pk_ref, pv_ref), (tq_ref, tk_ref, tv_ref), (gq_ref, gk_ref, gv_ref), (dtq_ref, dtk_ref, dtv_ref)
    ):
        one = jnp.where(at < seq - 1, pltpu.roll(grad, seq - 1, 0), 0.0)
        two = jnp.where(at < seq - 2, pltpu.roll(grad, seq - 2, 0), 0.0)
        g_ref[...] = (grad * taps_ref[0:1, :] + one * taps_ref[1:2, :] + two * taps_ref[2:3, :]).astype(BF)
        proj = proj_ref[...].astype(F32)
        for tap, part in enumerate((grad, one, two)):
            dt_ref[tap : tap + 1, :] = jnp.sum(part * proj, axis=0, keepdims=True)


def weight_kernel(meta, nt_ref, *refs):
    keep_ref, away_ref = refs[-2:]
    half = keep_ref.shape[0]
    for j, g_ref in enumerate(refs[:-2]):
        result = dot(nt_ref[...], g_ref[...], 1, 0).astype(BF)
        columns = slice(j * LANES, (j + 1) * LANES)
        keep_ref[:, columns] = result[:half]
        away_ref[:, columns] = result[half:]


def last_kernel(meta, *refs):
    grads, (w_ref, x_ref, gain_ref, gres_ref, gin_ref, ggain_ref) = refs[:-6], refs[-6:]
    grad = dot(jnp.concatenate([g_ref[...] for g_ref in grads], axis=1), w_ref[...], 1, 1)
    hat, inv_std = hat_of(x_ref[...].astype(F32))
    ggain_ref[...] = jnp.sum(grad * hat, axis=0, keepdims=True)
    scaled = grad * gain_ref[...]
    mean_first = jnp.mean(scaled, axis=-1, keepdims=True)
    mean_second = jnp.mean(scaled * hat, axis=-1, keepdims=True)
    back = inv_std * (scaled - mean_first - hat * mean_second)
    gin_ref[...] = (gres_ref[...] + back).astype(BF)


def own_sequence(inputs, lengths, cotangent, w_qkv, w_out, conv_taps, gain_one, gain_two, w_in, w_fc2):
    seq, width = inputs.shape[1], inputs.shape[2]
    rows = w_qkv.shape[0]
    wide = w_qkv.shape[1]
    quarter = width // 4
    tap_rows = conv_taps.shape[0]
    batch = lax.axis_index("batch")
    me = batch * 8 + lax.axis_index("wide")
    number = jnp.arange(64, dtype=jnp.int32)
    meta = jnp.where(number < 32, place_of(me, number & 31), jnp.where(number == 32, batch, lengths[0]))
    natural = jax.nn.one_hot(meta[:32], 32, dtype=F32)
    x, cot = inputs[0], cotangent[0]
    shape = jax.ShapeDtypeStruct
    row_spec = whole((1, width))
    token = whole((seq, width))
    groups = width // LANES

    qkv_z = z_hops(w_qkv)
    small = jnp.zeros((rows, 128), BF)
    small = small.at[:3, :tap_rows].set(conv_taps.T)
    small = small.at[3, :rows].set(gain_one).at[4, :rows].set(gain_two)
    out_z = z_hops(jnp.concatenate([w_out, small], axis=1))
    grad_out, grad_out_t = call(
        prepare_kernel, (1,), [token], [token, whole((4, quarter, seq))],
        [shape((seq, width), BF), shape((4, quarter, seq), BF)], busy=3, name="prepare",
    )(meta, cot)
    up = lax.dynamic_slice(w_in, (batch * quarter, 0), (quarter, PART * PARTS))
    down = jnp.transpose(lax.dynamic_slice(w_fc2, (0, batch * quarter), (PART * PARTS, quarter)))
    ffn = [
        jnp.concatenate([up[:, c * PART : (c + 1) * PART], down[:, c * PART : (c + 1) * PART]])
        for c in range(PARTS)
    ]
    qkv4 = join(qkv_z)
    qkv_first = send(qkv4, over_first)
    f0_z = z_hops(tie(ffn[0], qkv_z[3]))
    out4 = join(out_z)
    out_first = send(out4, over_first)
    qkv8 = join([qkv4, tie(qkv_first, grad_out)])
    qkv_second = send(qkv8, over_second)
    out8 = join([out4, out_first])
    out_second = send(out8, over_second)
    qkv16 = join([qkv8, qkv_second])
    qkv_core = send(qkv16, over_core)
    out16 = join([out8, out_second])
    out_core = send(out16, over_core)
    f0_4 = join(f0_z)
    f0_first = send(tie(f0_4, qkv_second), over_first)
    f1_z = z_hops(tie(ffn[1], f0_z[3]))

    few = jnp.concatenate([out16[:, :, width:], out_core[:, :, width:]])
    few = jnp.einsum("dp,prl->drl", natural, few.astype(F32), precision="highest")
    taps = jnp.transpose(few[:, :3, :tap_rows], (1, 0, 2)).reshape(3, wide)
    taps = jnp.concatenate([taps, jnp.zeros((5, wide), F32)])
    gain_first = few[:, 3, :rows].reshape(1, width)
    gain_second = few[:, 4, :rows].reshape(1, width)

    lane_block = pl.BlockSpec((seq, LANES), lambda j, m: (0, j))
    half_block = pl.BlockSpec((16, rows, LANES), lambda j, m: (0, 0, j))
    projected, mixed, qkv_full, normed_t = call(
        project_kernel, (wide // LANES,),
        [token, row_spec, pl.BlockSpec((8, LANES), lambda j, m: (0, j)), half_block, half_block],
        [lane_block, lane_block, pl.BlockSpec((width, LANES), lambda j, m: (0, j)), whole((32, rows, seq))],
        [shape((seq, wide), BF), shape((seq, wide), BF), shape((width, wide), BF), shape((32, rows, seq), BF)],
        [pltpu.VMEM((seq, width), BF)], busy=11.5, name="project",
    )(meta, tie(x, f0_4), gain_first, taps, qkv16, qkv_core)

    f0_8 = join([f0_4, tie(f0_first, mixed)])
    f0_second = send(f0_8, over_second)
    f1_4 = join([f1_z[0]] + [tie(part, mixed) for part in f1_z[1:]])
    f1_first = send(f1_4, over_first)
    f2_z = z_hops(tie(ffn[2], f1_4))
    part_specs = [pl.BlockSpec((seq, LANES), lambda j, m, p=p: (0, p * groups + j)) for p in range(3)]
    lse_spec = pl.BlockSpec((1, 8, seq), lambda j, m: (j, 0, 0))
    ready = tie(mixed, f0_8, f1_4)
    attended, lse = call(
        attend_kernel, (groups,), part_specs, [lane_block, lse_spec],
        [shape((seq, width), BF), shape((groups, 8, seq), F32)], [pltpu.VMEM((LANES, seq), F32)],
        busy=11, name="attend",
    )(meta, ready, ready, ready)

    f0_16 = join([f0_8, tie(f0_second, attended)])
    f0_core = send(f0_16, over_core)
    f1_8 = join([f1_4, tie(f1_first, attended)])
    f1_second = send(f1_8, over_second)
    f2_4 = join([f2_z[0]] + [tie(part, attended) for part in f2_z[1:]])
    f2_first = send(f2_4, over_first)
    out_half = pl.BlockSpec((16, rows, width), lambda j, m: (0, 0, 0))
    residual, normed_two, normed_two_t, attended_t, out_full = call(
        mend_kernel, (1,),
        [token, out_half, out_half, token, row_spec],
        [token, token, whole((4, quarter, seq)), whole((32, rows, seq)), whole((width, width))],
        [shape((seq, width), F32), shape((seq, width), BF), shape((4, quarter, seq), BF), shape((32, rows, seq), BF),
         shape((width, width), BF)],
        busy=6.3, name="mend",
    )(meta, tie(attended, f0_16, f1_8, f2_4), out16, out_core, x, gain_second)

    normed_two_t = normed_two_t.reshape(width, seq)
    grad_out_t = grad_out_t.reshape(width, seq)
    per_step = LANES // PART
    grad_spec = whole((16, 2 * quarter, PART))

    def feed_forward(own, other, sums, wait_for):
        tile_specs = [
            pl.BlockSpec(
                (1, 2 * quarter, PART),
                lambda s, m, b=b, k=k, h=h: (
                    jnp.where((m[b * 8 + s * per_step + k] >> 4) == h, m[b * 8 + s * per_step + k] & 15, 0), 0, 0
                ),
            )
            for h in range(2)
            for k in range(per_step)
            for b in range(4)
        ]
        return call(
            functools.partial(ffn_kernel, per_step, not sums), (8 // per_step,),
            [token, token, whole((width, seq)), whole((width, seq))] + tile_specs + [token] * len(sums),
            [token, token, grad_spec, grad_spec],
            [shape((seq, width), F32)] * 2 + [shape((16, 2 * quarter, PART), BF)] * 2,
            busy=9, name="ffn",
        )(meta, tie(normed_two, *wait_for), grad_out, normed_two_t, grad_out_t,
          *[own] * (4 * per_step), *[other] * (4 * per_step), *sums)

    f0_core = tie(f0_core, normed_two)
    f2_8 = join([f2_4, tie(f2_first, normed_two)])
    f2_second = send(f2_8, over_second)
    f1_16 = join([f1_8, tie(f1_second, normed_two)])
    f1_core = send(f1_16, over_core)
    branch, grad_two, keep0, away0 = feed_forward(f0_16, f0_core, (), (f1_16, f2_8))

    f2_16 = join([f2_8, tie(f2_second, branch)])
    f2_core = send(f2_16, over_core)
    r0_core = send(away0, over_core)
    f1_core = tie(f1_core, branch)
    branch, grad_two, keep1, away1 = feed_forward(f1_16, f1_core, (branch, grad_two), (f2_16, away0))

    f2_core = tie(f2_core, branch)
    r0_keep, r0_go = add_core(keep0, tie(r0_core, branch))
    r0_go = r0_go.astype(BF)
    r0_second = send(r0_go, over_second)
    r1_core = send(away1, over_core)
    branch, grad_two, keep2, away2 = feed_forward(f2_16, f2_core, (branch, grad_two), (r0_go, away1))

    r0_keep, r0_go = add_half(r0_keep, tie(r0_second, branch))
    r0_go = r0_go.astype(BF)
    r0_first = send(r0_go, over_first)
    r1_keep, r1_go = add_core(keep1, tie(r1_core, branch))
    r1_go = r1_go.astype(BF)
    r1_second = send(r1_go, over_second)
    r2_core = send(away2, over_core)
    half_out = shape((16, rows * (width // PART), PART), BF)
    output, grad_residual, grad_attended, grad_gain_second, keep_out, away_out = call(
        turn_kernel, (1,),
        [token] * 3 + [row_spec, token, whole((width, seq)), whole((width, width))],
        [token] * 3 + [row_spec, whole(half_out.shape), whole(half_out.shape)],
        [shape((seq, width), BF), shape((seq, width), F32), shape((seq, width), BF), shape((1, width), F32),
         half_out, half_out],
        busy=7, name="turn",
    )(meta, tie(grad_two, r0_go, r1_go, away2), branch, residual, gain_second, grad_out,
      attended_t.reshape(width, seq), out_full)

    def attend_back(j, wait_for):
        specs = [pl.BlockSpec((seq, LANES), lambda i, m, p=p: (0, p * groups + j)) for p in range(3)]
        tap_specs = [pl.BlockSpec((8, LANES), lambda i, m, p=p: (0, p * groups + j)) for p in range(3)]
        block = pl.BlockSpec((seq, LANES), lambda i, m: (0, j))
        return call(
            attend_back_kernel, (1,),
            specs * 2 + tap_specs + [block, block, pl.BlockSpec((1, 8, seq), lambda i, m: (j, 0, 0))],
            [whole((seq, LANES))] * 3 + [whole((8, LANES))] * 3,
            [shape((seq, LANES), BF)] * 3 + [shape((8, LANES), F32)] * 3,
            [pltpu.VMEM((LANES, seq), F32)],
            busy=5.5, name="attend_back",
        )(meta, mixed, mixed, mixed, projected, projected, projected, taps, taps, taps,
          tie(grad_attended, *wait_for), attended, lse)

    r0_total = r0_keep + tie(r0_first, grad_attended).astype(F32)
    r0_z = z_sends(r0_total)
    r1_keep, r1_go = add_half(r1_keep, tie(r1_second, grad_attended))
    r1_go = r1_go.astype(BF)
    r1_first = send(r1_go, over_first)
    r2_keep, r2_go = add_core(keep2, tie(r2_core, grad_attended))
    out_come = send(away_out, over_core)
    back0 = attend_back(0, (r0_total, r1_go, away_out))

    r0_z = [tie(part, back0[0]) for part in r0_z]
    r1_total = r1_keep + tie(r1_first, back0[0]).astype(F32)
    r1_z = z_sends(r1_total)
    out_keep, out_go = add_core(keep_out, tie(out_come, back0[0]))
    r2_keep = jnp.concatenate([r2_keep, out_keep], axis=1)
    r2_go = jnp.concatenate([r2_go.astype(BF), out_go.astype(BF)], axis=1)
    r2_second = send(r2_go, over_second)
    back1 = attend_back(1, (back0[0], r1_total, r2_go))

    r1_z = [tie(part, back1[0]) for part in r1_z]
    r2_keep, r2_go = add_half(r2_keep, tie(r2_second, back1[0]))
    r2_go = r2_go.astype(BF)
    r2_first = send(r2_go, over_first)
    back2 = attend_back(2, (back1[0], r2_go))

    r2_total = r2_keep + tie(r2_first, back2[0]).astype(F32)
    r2_z = z_sends(r2_total)
    backs = (back0, back1, back2)
    grad_projected = [back[part] for part in range(3) for back in backs]
    half_spec = whole((width // 2, wide))
    keep_qkv, away_qkv = call(
        weight_kernel, (1,), [whole((width, seq))] + [whole((seq, LANES))] * (3 * groups), [half_spec, half_spec],
        [shape((width // 2, wide), BF)] * 2, busy=6.7, name="weight",
    )(meta, tie(normed_t.reshape(width, seq), r2_total), *grad_projected)
    by_block = (16, rows, wide)
    keep_qkv, away_qkv = keep_qkv.reshape(by_block), away_qkv.reshape(by_block)
    r2_z = [tie(part, away_qkv) for part in r2_z]
    qkv_keep, qkv_go = add_core(keep_qkv, send(away_qkv, over_core))
    qkv_go = qkv_go.astype(BF)
    q_second = send(qkv_go, over_second)
    grad_inputs, grad_gain_first = call(
        last_kernel, (1,),
        [whole((seq, LANES))] * (3 * groups) + [whole((width, wide)), token, row_spec, token],
        [token, row_spec], [shape((seq, width), BF), shape((1, width), F32)],
        busy=8.7, name="last",
    )(meta, *grad_projected, qkv_full, x, gain_first, tie(grad_residual, qkv_go))
    qkv_keep, qkv_go = add_half(qkv_keep, tie(q_second, grad_gain_first))
    qkv_first = send(qkv_go.astype(BF), over_first)

    tap_grads = jnp.concatenate([back[3 + part][:3] for part in range(3) for back in backs], axis=1)
    tap_grads = jnp.transpose(tap_grads.reshape(3, 32, tap_rows), (1, 0, 2))
    gain_grads = jnp.stack([grad_gain_first.reshape(32, rows), grad_gain_second.reshape(32, rows)], axis=1)
    few = jnp.zeros((32, 8, 128), F32)
    few = few.at[:, :3, :tap_rows].set(tap_grads).at[:, 3:5, :rows].set(gain_grads)
    few = jnp.einsum("dp,drl->prl", natural, few, precision="highest")
    few_keep, few_go = add_core(few[:16], send(few[16:], over_core))
    few_keep, few_go = add_half(few_keep, send(few_go, over_second))
    few_total = few_keep + send(few_go, over_first)
    few = add_z(few_total, z_sends(few_total, F32))
    qkv_total = qkv_keep + qkv_first.astype(F32)
    grad_qkv = add_z(qkv_total, z_sends(qkv_total))

    grad0 = add_z(r0_total, r0_z)
    grad1 = add_z(r1_total, r1_z)
    grad2 = add_z(r2_total, r2_z)
    grad_out_w = grad2[2 * quarter :]
    grad_out_w = jnp.concatenate(
        [grad_out_w[c * rows : (c + 1) * rows] for c in range(width // PART)], axis=1
    )
    grad_in_w = jnp.concatenate([grad0[:quarter], grad1[:quarter], grad2[:quarter]], axis=1)
    grad_fc2_w = jnp.concatenate([g[quarter : 2 * quarter] for g in (grad0, grad1, grad2)], axis=1)
    return (
        output[None],
        grad_inputs[None],
        grad_qkv,
        grad_out_w,
        few[:3, :tap_rows].T,
        few[3, :rows],
        few[4, :rows],
        grad_in_w,
        jnp.transpose(grad_fc2_w),
    )


def solution(mesh):
    fast = functools.partial(own_sequence)

    def program(*args):
        body = fast if fits(mesh, args) else shards
        return jax.shard_map(
            body,
            mesh=mesh,
            in_specs=(
                P(("batch", "wide"), None, None),
                P(("batch", "wide")),
                P(("batch", "wide"), None, None),
                P(("batch", "wide"), None),
                P(("batch", "wide"), None),
                P(("batch", "wide"), None),
                P(("batch", "wide")),
                P(("batch", "wide")),
                P(None, "wide"),
                P("wide", None),
            ),
            out_specs=(
                P(("batch", "wide"), None, None),
                P(("batch", "wide"), None, None),
                P(("batch", "wide"), None),
                P(("batch", "wide"), None),
                P(("batch", "wide"), None),
                P(("batch", "wide")),
                P(("batch", "wide")),
                P("batch", "wide"),
                P("wide", "batch"),
            ),
            check_vma=False,
        )(*args)

    return program
```

```python
import functools
import jax
import jax.numpy as jnp
from jax import lax
from jax.experimental import pallas as pl
from jax.experimental.pallas import tpu as pltpu
from jax.sharding import PartitionSpec as P

HEADS = 12
HD = 64


epsilon = 1e-05


def contract_first(left, right):
    return lax.dot_general(
        left, right, (((0,), (0,)), ((), ())), preferred_element_type=jnp.float32
    )


def contract_last(left, right):
    return lax.dot_general(
        left, right, (((1,), (1,)), ((), ())), preferred_element_type=jnp.float32
    )


def norm_parts(values_in):
    centered = values_in - jnp.mean(values_in, axis=-1, keepdims=True)
    inv_std = lax.rsqrt(jnp.mean(centered * centered, axis=-1, keepdims=True) + epsilon)
    return (centered * inv_std, inv_std)


def norm_back(grad_normed, gain_vec, normed_hat, inv_std):
    grad_hat = grad_normed * gain_vec
    mean_first = jnp.mean(grad_hat, axis=-1, keepdims=True)
    mean_second = jnp.mean(grad_hat * normed_hat, axis=-1, keepdims=True)
    grad_value = inv_std * (grad_hat - mean_first - normed_hat * mean_second)
    return (grad_value, jnp.sum(grad_normed * normed_hat, axis=0))


def shift_down(signal, steps):
    filler = jnp.zeros((steps, signal.shape[1]), signal.dtype)
    return jnp.concatenate([filler, signal[:-steps]], axis=0)


def shift_up(signal, steps):
    filler = jnp.zeros((steps, signal.shape[1]), signal.dtype)
    return jnp.concatenate([signal[steps:], filler], axis=0)


def scores_block(query_block, keys, start_row, seq_live):
    rows_block = query_block.shape[0]
    scores = (
        jnp.einsum("qhd,khd->hqk", query_block, keys, preferred_element_type=jnp.float32) * 0.125
    )
    query_pos = start_row + jnp.arange(rows_block)
    key_pos = jnp.arange(keys.shape[0])
    allowed = (key_pos[None, :] <= query_pos[:, None]) & (key_pos[None, :] < seq_live)
    return (scores, allowed[None])


def shards(inputs, lengths, cotangent, w_qkv, w_out, conv_taps, gain_one, gain_two, w_in, w_fc2):
    full_qkv, full_out, full_taps, full_gain_one, full_gain_two = (
        lax.all_gather(w_qkv, ("batch", "wide"), axis=0, tiled=True),
        lax.all_gather(w_out, ("batch", "wide"), axis=0, tiled=True),
        lax.all_gather(conv_taps, ("batch", "wide"), axis=0, tiled=True),
        lax.all_gather(gain_one, ("batch", "wide"), axis=0, tiled=True),
        lax.all_gather(gain_two, ("batch", "wide"), axis=0, tiled=True),
    )
    seq_length, width = (inputs.shape[1], inputs.shape[2])
    tokens_in = inputs[0].astype(jnp.float32)
    seq_live = lengths[0]
    live_rows = jnp.arange(seq_length) < seq_live
    taps = full_taps.astype(jnp.float32)
    gain_first = full_gain_one.astype(jnp.float32)
    gain_second = full_gain_two.astype(jnp.float32)
    hat_one, inv_one = norm_parts(tokens_in)
    normed_one = (hat_one * gain_first).astype(jnp.bfloat16)
    projected = jnp.dot(normed_one, full_qkv, preferred_element_type=jnp.float32)
    mixed = (
        projected * taps[:, 0]
        + shift_down(projected, 1) * taps[:, 1]
        + shift_down(projected, 2) * taps[:, 2]
    ).astype(jnp.bfloat16)
    query = mixed[:, :width].reshape(seq_length, HEADS, HD)
    keys = mixed[:, width : 2 * width].reshape(seq_length, HEADS, HD)
    values = mixed[:, 2 * width :].reshape(seq_length, HEADS, HD)
    rows_block = min(512, seq_length)
    block_index = 0
    start_row = block_index * rows_block
    scores, allowed = scores_block(query, keys, start_row, seq_live)
    masked = jnp.where(allowed, scores, -1e30)
    top_score = jnp.max(masked, axis=-1, keepdims=True)
    exp_terms = jnp.exp(masked - top_score)
    row_totals = jnp.sum(exp_terms, axis=-1, keepdims=True)
    probs_low = (exp_terms / row_totals).astype(jnp.bfloat16)
    out_parts = jnp.einsum("hqk,khd->qhd", probs_low, values, preferred_element_type=jnp.float32)
    lse_parts = [top_score + jnp.log(row_totals)]
    attended_low = out_parts.reshape(seq_length, width).astype(jnp.bfloat16)
    branch_attn = jnp.dot(attended_low, full_out, preferred_element_type=jnp.float32)
    residual = tokens_in + branch_attn
    hat_two, inv_two = norm_parts(residual)
    normed_two = (hat_two * gain_second).astype(jnp.bfloat16)
    grad_out = jnp.where(live_rows[:, None], cotangent[0], jnp.zeros_like(cotangent[0]))
    row_set = lax.all_gather(normed_two[None], "wide", axis=0, tiled=True).reshape(-1, width)
    pre_act = jnp.dot(row_set, w_in, preferred_element_type=jnp.float32)
    activ = jnp.square(jax.nn.relu(pre_act)).astype(jnp.bfloat16)
    piece = activ
    branch_ffn = lax.psum_scatter(
        jnp.dot(piece, w_fc2, preferred_element_type=jnp.float32).astype(jnp.bfloat16),
        "wide",
        scatter_dimension=0,
        tiled=True,
    ).astype(jnp.float32)
    grad_set = lax.all_gather(grad_out[None], "wide", axis=0, tiled=True).reshape(-1, width)
    grad_act = contract_last(grad_set, w_fc2)
    grad_fc2_part = contract_first(activ, grad_set)
    grad_pre = (grad_act * 2.0 * jax.nn.relu(pre_act)).astype(jnp.bfloat16)
    grad_in_part = contract_first(row_set, grad_pre)
    piece = grad_pre
    grad_normed_two = lax.psum_scatter(
        contract_last(piece, w_in).astype(jnp.bfloat16), "wide", scatter_dimension=0, tiled=True
    ).astype(jnp.float32)
    grad_w_in, grad_w_fc2 = (
        lax.psum_scatter(
            grad_in_part.astype(jnp.bfloat16), "batch", scatter_dimension=0, tiled=True
        ).astype(jnp.float32),
        lax.psum_scatter(
            grad_fc2_part.astype(jnp.bfloat16), "batch", scatter_dimension=1, tiled=True
        ).astype(jnp.float32),
    )
    output = jnp.where(live_rows[:, None], residual + branch_ffn, 0.0).astype(jnp.bfloat16)[None]
    grad_ln_two, grad_gain_second = norm_back(grad_normed_two, gain_second, hat_two, inv_two)
    grad_residual = grad_out.astype(jnp.float32) + grad_ln_two
    grad_branch = grad_residual.astype(jnp.bfloat16)
    grad_w_out_part = contract_first(attended_low, grad_branch)
    grad_attended = contract_last(grad_branch, full_out).astype(jnp.bfloat16)
    grad_att_heads = grad_attended.reshape(seq_length, HEADS, HD)
    delta_all = jnp.sum(grad_att_heads.astype(jnp.float32) * out_parts, axis=-1)
    block_index = 0
    start_row = block_index * rows_block
    scores, allowed = scores_block(query, keys, start_row, seq_live)
    probs_full = jnp.where(allowed, jnp.exp(scores - lse_parts[block_index]), 0.0)
    probs_low = probs_full.astype(jnp.bfloat16)
    grad_probs = jnp.einsum(
        "qhd,khd->hqk", grad_att_heads, values, preferred_element_type=jnp.float32
    )
    delta_block = jnp.transpose(delta_all)[:, :, None]
    grad_scores = (probs_full * (grad_probs - delta_block)).astype(jnp.bfloat16)
    grad_query_parts = 0.125 * jnp.einsum(
        "hqk,khd->qhd", grad_scores, keys, preferred_element_type=jnp.float32
    )
    grad_keys = 0.125 * jnp.einsum(
        "hqk,qhd->khd", grad_scores, query, preferred_element_type=jnp.float32
    )
    grad_values = jnp.einsum(
        "hqk,qhd->khd", probs_low, grad_att_heads, preferred_element_type=jnp.float32
    )
    grad_mixed = jnp.concatenate(
        [
            grad_query_parts.reshape(seq_length, width),
            grad_keys.reshape(seq_length, width),
            grad_values.reshape(seq_length, width),
        ],
        axis=1,
    )
    grad_taps_part = jnp.stack(
        [
            jnp.sum(grad_mixed * projected, axis=0),
            jnp.sum(grad_mixed * shift_down(projected, 1), axis=0),
            jnp.sum(grad_mixed * shift_down(projected, 2), axis=0),
        ],
        axis=1,
    )
    grad_projected = (
        grad_mixed * taps[:, 0]
        + shift_up(grad_mixed, 1) * taps[:, 1]
        + shift_up(grad_mixed, 2) * taps[:, 2]
    ).astype(jnp.bfloat16)
    grad_qkv_part = contract_first(normed_one, grad_projected)
    grad_normed_one = contract_last(grad_projected, full_qkv)
    grad_ln_one, grad_gain_first = norm_back(grad_normed_one, gain_first, hat_one, inv_one)
    grad_inputs = (grad_residual + grad_ln_one).astype(jnp.bfloat16)[None]
    grad_w_qkv, grad_w_out, grad_conv_taps, grad_gain_one, grad_gain_two = (
        lax.psum_scatter(grad_qkv_part, ("batch", "wide"), scatter_dimension=0, tiled=True),
        lax.psum_scatter(grad_w_out_part, ("batch", "wide"), scatter_dimension=0, tiled=True),
        lax.psum_scatter(grad_taps_part, ("batch", "wide"), scatter_dimension=0, tiled=True),
        lax.psum_scatter(grad_gain_first, ("batch", "wide"), scatter_dimension=0, tiled=True),
        lax.psum_scatter(grad_gain_second, ("batch", "wide"), scatter_dimension=0, tiled=True),
    )
    return (
        output,
        grad_inputs,
        grad_w_qkv,
        grad_w_out,
        grad_conv_taps,
        grad_gain_one,
        grad_gain_two,
        grad_w_in,
        grad_w_fc2,
    )


BF = jnp.bfloat16
F32 = jnp.float32
AXES = ("batch", "wide")
LANES = 256
PART = 128
VMEM_MIB = {"ffn": 36}


def fits(mesh, args):
    inputs, w_qkv, w_in = args[0], args[3], args[8]
    count = mesh.shape["batch"] * mesh.shape["wide"]
    return (
        mesh.shape["batch"] == 4
        and mesh.shape["wide"] == 8
        and inputs.shape[0] == count
        and inputs.shape[1] % LANES == 0
        and w_qkv.shape[0] % (count * 8) == 0
        and w_qkv.shape[0] % LANES == 0
        and w_qkv.shape[0] // HEADS == HD
        and w_in.shape[1] == 8 * 3 * PART
        and (w_in.shape[0] // 4) % 16 == 0
    )


def dot(left, right, left_dim, right_dim):
    return lax.dot_general(
        left, right, (((left_dim,), (right_dim,)), ((), ())), preferred_element_type=F32
    )


def flip_pairs(rule):
    return [(i, i ^ rule(i)) for i in range(32)]


def send(array, rule):
    return lax.ppermute(array, AXES, flip_pairs(rule))


def over_core(i):
    return 8


def over_first(i):
    return 16 if i & 8 else 1


def over_second(i):
    return 1 if i & 8 else 16


def over_z(step):
    return lambda i: 2 * step


def tie(value, *others):
    return lax.optimization_barrier((value,) + others)[0]


def join(parts):
    return jnp.concatenate(parts)


def added(keep, come):
    return (keep.astype(F32) + come.astype(F32)).astype(BF)


def halved(keep, come):
    half = keep.shape[0] // 2
    return added(keep[:half], come[:half]), added(keep[half:], come[half:])


def place_of(me, other):
    apart = me ^ other
    x_bit, z_bits = apart & 1, (apart & 2) | ((apart >> 2) & 1)
    core_bit, y_bit = (apart >> 3) & 1, (apart >> 4) & 1
    on_first = ((other >> 3) & 1) == 0
    high = jnp.where(on_first, y_bit, x_bit)
    low = jnp.where(on_first, x_bit, y_bit)
    return core_bit * 16 + high * 8 + low * 4 + z_bits


def call(kernel, grid, in_specs, out_specs, out_shape, scratch=(), busy=1, name=None, aliases=None):
    return pl.pallas_call(
        kernel,
        grid_spec=pltpu.PrefetchScalarGridSpec(
            num_scalar_prefetch=1,
            grid=grid,
            in_specs=in_specs,
            out_specs=out_specs,
            scratch_shapes=list(scratch),
        ),
        out_shape=out_shape,
        compiler_params=pltpu.CompilerParams(
            dimension_semantics=("arbitrary",) * len(grid), vmem_limit_bytes=VMEM_MIB.get(name, 20) * 1024 * 1024
        ),
        cost_estimate=pl.CostEstimate(flops=int(busy * 1.15e9), bytes_accessed=0, transcendentals=0),
        name=name,
        input_output_aliases=aliases or {},
    )


def whole(shape):
    zeros = (0,) * len(shape)
    return pl.BlockSpec(shape, lambda *_: zeros, pipeline_mode=pl.Buffered(1))


def hat_of(values_in):
    centered = values_in - jnp.mean(values_in, axis=-1, keepdims=True)
    inv_std = lax.rsqrt(jnp.mean(centered * centered, axis=-1, keepdims=True) + epsilon)
    return centered * inv_std, inv_std


def turned(value):
    return jnp.transpose(value.astype(F32)).astype(BF)


def prepare_kernel(meta, cot_ref, go_ref, got_ref):
    live = lax.broadcasted_iota(jnp.int32, (cot_ref.shape[0], 1), 0) < meta[33]
    value = jnp.where(live, cot_ref[...].astype(F32), 0.0)
    go_ref[...] = value.astype(BF)
    got_ref[...] = jnp.transpose(value).astype(BF)


def pack_kernel(meta, up_ref, down_ref, out_ref, a_ref, b_ref):
    half = up_ref.shape[0] // 2
    second_half, second_core = (meta[32] >> 1) == 1, (meta[32] & 1) == 1
    up = jnp.where(second_half, up_ref[half:, :], up_ref[:half, :])
    down = turned(jnp.where(second_half, down_ref[:, half:], down_ref[:, :half]))
    for i, part in enumerate((up, down)):
        a_ref[0, i * half : (i + 1) * half, :] = jnp.where(second_core, part[:, PART : 2 * PART], part[:, :PART])
    left, right = swap_halves(up[:, 2 * PART :], down[:, 2 * PART :])
    b_ref[0, :half, :] = jnp.where(second_core, right, left).astype(BF)
    rows = out_ref.shape[0]
    for c in range(out_ref.shape[1] // PART):
        b_ref[0, half + c * rows : half + (c + 1) * rows, :] = out_ref[:, c * PART : (c + 1) * PART]


def block_of(meta, i, own_ref, other_ref):
    place = meta[i]
    return jnp.where(place < 16, own_ref[place & 15], other_ref[place & 15])


def project_kernel(
    meta, x_ref, own_ref, other_ref, few_own_ref, few_other_ref,
    proj_ref, mixed_ref, wn_ref, nt_ref, taps_ref, gains_ref, normed,
):
    rows = own_ref.shape[1]
    step = pl.program_id(0)

    def few_of(device, lanes):
        block = block_of(meta, device, few_own_ref, few_other_ref)[:8].astype(F32)
        return jnp.concatenate([block, jnp.zeros((8, lanes - PART), F32)], axis=1)

    @pl.when(step == 0)
    def _():
        width = gains_ref.shape[1]
        lane = lax.broadcasted_iota(jnp.int32, (8, width), 1)
        gains = jnp.zeros((8, width), F32)
        for i in range(32):
            first = i * rows
            moved = pltpu.roll(few_of(i, width), first, 1)
            gains = jnp.where((lane >= first) & (lane < first + rows), moved, gains)
        gains_ref[...] = gains
        hat, _ = hat_of(x_ref[...].astype(F32))
        low = (hat * gains[3:4, :]).astype(BF)
        normed[...] = low
        flipped = turned(low)
        for i in range(32):
            nt_ref[meta[i]] = flipped[i * rows : (i + 1) * rows]

    channels = 3 * rows
    lane = lax.broadcasted_iota(jnp.int32, (8, LANES), 1)
    taps = jnp.zeros((8, LANES), F32)
    for i in range(LANES // channels + 2):
        device = jnp.minimum((step * LANES) // channels + i, 31)
        first = device * channels - step * LANES
        moved = pltpu.roll(few_of(device, LANES), (first + 2 * LANES) & (LANES - 1), 1)
        taps = jnp.where((lane >= first) & (lane < first + channels), moved, taps)
    taps_ref[...] = taps
    for i in range(32):
        wn_ref[i * rows : (i + 1) * rows, :] = block_of(meta, i, own_ref, other_ref)
    value = dot(normed[...], wn_ref[...], 1, 0)
    at = lax.broadcasted_iota(jnp.int32, value.shape, 0)
    one = jnp.where(at >= 1, pltpu.roll(value, 1, 0), 0.0)
    two = jnp.where(at >= 2, pltpu.roll(value, 2, 0), 0.0)
    mixed = value * taps[0:1, :] + one * taps[1:2, :] + two * taps[2:3, :]
    proj_ref[...] = value.astype(BF)
    mixed_ref[...] = mixed.astype(BF)


def head_row(head, scale=1.0):
    lane = lax.broadcasted_iota(jnp.int32, (1, LANES), 1)
    return jnp.where(lane // HD == head, scale, 0.0).astype(BF)


def allowed_in(meta, keys, first_query, queries):
    key = lax.broadcasted_iota(jnp.int32, (keys, queries), 0)
    query = first_query + lax.broadcasted_iota(jnp.int32, (1, queries), 1)
    return key < jnp.minimum(query + 1, meta[33])


def attend_kernel(meta, q_ref, k_ref, v_ref, out_ref, lse_ref, flipped):
    seq = q_ref.shape[0]
    tile = LANES
    values_t = turned(v_ref[...])
    keys = k_ref[...]
    for t in range(seq // tile):
        upto = (t + 1) * tile
        allowed = allowed_in(meta, upto, t * tile, tile)
        query = q_ref[t * tile : upto, :]
        for head in range(LANES // HD):
            scores = dot(keys[:upto], query * head_row(head, 0.125), 1, 1)
            scores = jnp.where(allowed, scores, -1e30)
            top = jnp.max(scores, axis=0, keepdims=True)
            terms = jnp.exp(scores - top)
            total = jnp.sum(terms, axis=0, keepdims=True)
            probs = (terms * (1.0 / total)).astype(BF)
            flipped[head * HD : (head + 1) * HD, t * tile : upto] = dot(
                values_t[head * HD : (head + 1) * HD, :upto], probs, 1, 0
            )
            lse_ref[0, head : head + 1, t * tile : upto] = top + jnp.log(total)
    out_ref[...] = jnp.transpose(flipped[...]).astype(BF)


def mend_kernel(meta, att_ref, own_ref, other_ref, x_ref, gain_ref, res_ref, n2_ref, n2t_ref, at_ref, wn_ref):
    flipped = turned(att_ref[...])
    rows = at_ref.shape[1]
    for i in range(32):
        at_ref[meta[i]] = flipped[i * rows : (i + 1) * rows]
        block = block_of(meta, i, own_ref, other_ref)
        for c in range(wn_ref.shape[1] // PART):
            wn_ref[i * rows : (i + 1) * rows, c * PART : (c + 1) * PART] = block[c * rows : (c + 1) * rows]
    residual = x_ref[...].astype(F32) + dot(att_ref[...], wn_ref[...], 1, 0)
    res_ref[...] = residual
    hat, _ = hat_of(residual)
    low = (hat * gain_ref[4:5, :]).astype(BF)
    n2_ref[...] = low
    n2t_ref[...] = turned(low)


def swap_halves(left, right):
    left, right = left.astype(F32), right.astype(F32)
    low = lax.broadcasted_iota(jnp.int32, (1, PART), 1) < PART // 2
    return (
        jnp.where(low, left, pltpu.roll(right, PART // 2, 1)),
        jnp.where(low, pltpu.roll(left, PART // 2, 1), right),
    )


def ffn_kernel(packed, meta, *refs):
    token_refs, refs = (refs[:4], refs[4:8]), refs[8:]
    count = 8 if packed else 4
    tiles, refs = refs[:count], refs[count:]
    if packed:
        branch_ref, grad_ref, branch_acc, grad_acc, low_ref, high_ref = refs
    else:
        sums_in, (branch_ref, grad_ref, both_ref, low_ref, high_ref, branch_acc, grad_acc) = refs[:4], refs[4:]
    sums = (branch_ref, grad_ref, branch_acc, grad_acc)
    step = pl.program_id(0)

    @pl.when(step == 0)
    def _():
        for i, ref in enumerate(sums):
            ref[...] = jnp.zeros_like(ref) if packed else sums_in[i][...]

    half = tiles[0].shape[1] if packed else tiles[0].shape[1] // 2
    if packed:
        blocks = [jnp.concatenate([tiles[2 * k][0], tiles[2 * k + 1][0]], axis=0) for k in range(4)]
        pairs = [swap_halves(blocks[0], blocks[1]), swap_halves(blocks[2], blocks[3])]
        w_up, w_down = (jnp.concatenate([pairs[0][i], pairs[1][i]], axis=1).astype(BF) for i in range(2))
    else:
        w_up, w_down = (
            jnp.concatenate(
                [
                    jnp.concatenate([tiles[2 * k + b][0, i * half : (i + 1) * half, :] for b in range(2)], axis=0)
                    for k in range(2)
                ],
                axis=1,
            )
            for i in range(2)
        )
    up_sum = down_sum = 0.0
    for i, (n2_ref, go_ref, n2t_ref, got_ref) in enumerate(token_refs):
        pre = jnp.maximum(dot(n2_ref[...], w_up, 1, 0), 0.0)
        activ = (pre * pre).astype(BF)
        grad_pre = (dot(go_ref[...], w_down, 1, 0) * 2.0 * pre).astype(BF)
        sums[2 * i][...] += dot(activ, w_down, 1, 1)
        sums[2 * i + 1][...] += dot(grad_pre, w_up, 1, 1)
        up_sum += dot(n2t_ref[...], grad_pre, 1, 0)
        down_sum += dot(got_ref[...], activ, 1, 0)
    first_wide = step * (4 if packed else 2)
    results = []
    for k in range(2):
        lanes = slice(k * PART, (k + 1) * PART)
        if packed:
            results += [(part,) for part in swap_halves(up_sum[:, lanes], down_sum[:, lanes])]
        else:
            results.append((up_sum[:, lanes], down_sum[:, lanes]))
    for k, parts in enumerate(results):
        for b in range(2):
            place = meta[b * 16 + (meta[32] & 1) * 8 + first_wide + k]
            for is_high, target in enumerate((low_ref, high_ref)):

                @pl.when((place >> 3) == is_high)
                def _(place=place, target=target, parts=parts, b=b):
                    for i, part in enumerate(parts):
                        target[place & 7, i * half : (i + 1) * half, :] = part[b * half : (b + 1) * half].astype(BF)

    if not packed:

        @pl.when(step == pl.num_programs(0) - 1)
        def _():
            seq = branch_acc.shape[0]
            both_ref[:seq, :] = branch_acc[...].astype(BF)
            both_ref[seq:, :] = grad_acc[...].astype(BF)


def turn_kernel(meta, grad_ref, branch_ref, come_ref, res_ref, gain_ref, go_ref, at_ref, wn_ref, out_ref, gres_ref, gatt_ref, ggain_ref, keep_ref, away_ref):
    residual = res_ref[...]
    seq = residual.shape[0]
    live = lax.broadcasted_iota(jnp.int32, (seq, 1), 0) < meta[33]
    branch = branch_ref[...] + come_ref[:seq, :].astype(F32)
    out_ref[...] = jnp.where(live, residual + branch, 0.0).astype(BF)
    hat, inv_std = hat_of(residual)
    grad = grad_ref[...] + come_ref[seq:, :].astype(F32)
    ggain_ref[...] = jnp.sum(grad * hat, axis=0, keepdims=True)
    scaled = grad * gain_ref[4:5, :]
    mean_first = jnp.mean(scaled, axis=-1, keepdims=True)
    mean_second = jnp.mean(scaled * hat, axis=-1, keepdims=True)
    grad_res = go_ref[...].astype(F32) + inv_std * (scaled - mean_first - hat * mean_second)
    gres_ref[...] = grad_res
    low = grad_res.astype(BF)
    gatt_ref[...] = dot(low, wn_ref[...], 1, 1).astype(BF)
    result = dot(at_ref[...], low, 1, 0)
    lanes = keep_ref.shape[2]
    chunks = result.shape[1] // lanes
    rows = keep_ref.shape[1] // chunks
    for i in range(32):
        target = away_ref if i >= 16 else keep_ref
        for c in range(chunks):
            target[i & 15, c * rows : (c + 1) * rows, :] = result[
                i * rows : (i + 1) * rows, c * lanes : (c + 1) * lanes
            ].astype(BF)


def attend_back_kernel(
    meta, q_ref, k_ref, v_ref, pq_ref, pk_ref, pv_ref, tq_ref, tk_ref, tv_ref, go_ref, out_ref, lse_ref,
    gq_ref, gk_ref, gv_ref, dtq_ref, dtk_ref, dtv_ref, flipped,
):
    seq = q_ref.shape[0]
    tile = LANES
    keys, values = k_ref[...], v_ref[...]
    keys_t = turned(keys)
    delta_t = jnp.transpose(go_ref[...].astype(F32) * out_ref[...].astype(F32))
    grad_keys = [jnp.zeros((tile, LANES), F32) for _ in range(seq // tile)]
    grad_values = list(grad_keys)
    for t in range(seq // tile):
        upto = (t + 1) * tile
        allowed = allowed_in(meta, upto, t * tile, tile)
        query, grad = q_ref[t * tile : upto, :], go_ref[t * tile : upto, :]
        for head in range(LANES // HD):
            lanes = slice(head * HD, (head + 1) * HD)
            query_h, grad_h = query * head_row(head, 0.125), grad * head_row(head)
            delta = jnp.sum(delta_t[lanes, t * tile : upto], axis=0, keepdims=True)
            scores = dot(keys[:upto], query_h, 1, 1)
            lse = lse_ref[0, head : head + 1, t * tile : upto]
            probs = jnp.where(allowed, jnp.exp(scores - lse), 0.0)
            grad_scores = (probs * (dot(values[:upto], grad_h, 1, 1) - delta)).astype(BF)
            flipped[lanes, t * tile : upto] = dot(keys_t[lanes, :upto], grad_scores, 1, 0) * 0.125
            add_values = dot(probs.astype(BF), grad_h, 1, 0)
            add_keys = dot(grad_scores, query_h, 1, 0)
            for s in range(t + 1):
                rows = slice(s * tile, (s + 1) * tile)
                grad_values[s] += add_values[rows]
                grad_keys[s] += add_keys[rows]
    mixed = (
        jnp.transpose(flipped[...]),
        jnp.concatenate(grad_keys, axis=0),
        jnp.concatenate(grad_values, axis=0),
    )
    at = lax.broadcasted_iota(jnp.int32, (seq, LANES), 0)
    for grad, proj_ref, taps_ref, g_ref, dt_ref in zip(
        mixed, (pq_ref, pk_ref, pv_ref), (tq_ref, tk_ref, tv_ref), (gq_ref, gk_ref, gv_ref), (dtq_ref, dtk_ref, dtv_ref)
    ):
        one = jnp.where(at < seq - 1, pltpu.roll(grad, seq - 1, 0), 0.0)
        two = jnp.where(at < seq - 2, pltpu.roll(grad, seq - 2, 0), 0.0)
        g_ref[...] = (grad * taps_ref[0:1, :] + one * taps_ref[1:2, :] + two * taps_ref[2:3, :]).astype(BF)
        proj = proj_ref[...].astype(F32)
        for tap, part in enumerate((grad, one, two)):
            dt_ref[tap : tap + 1, :] = jnp.sum(part * proj, axis=0, keepdims=True)


def weight_kernel(with_few, meta, nt_ref, *refs):
    if with_few:
        (*tap_refs, gain_ref), refs, few = refs[:10], refs[10:-1], refs[-1]
    keep_ref, away_ref = refs[-2:]
    half, full = keep_ref.shape
    for j, g_ref in enumerate(refs[:-2]):
        result = dot(nt_ref[...], g_ref[...], 1, 0).astype(BF)
        columns = slice(j * LANES, (j + 1) * LANES)
        keep_ref[:, columns] = result[:half]
        away_ref[:, columns] = result[half:]
    if with_few:
        rows = half // 16
        row = lax.broadcasted_iota(jnp.int32, (8, PART), 0)
        lane = lax.broadcasted_iota(jnp.int32, (8, PART), 1)
        taps = jnp.concatenate([ref[...] for ref in tap_refs], axis=1)
        gains = jnp.broadcast_to(gain_ref[...], (8, gain_ref.shape[1]))

        def taken(values_in, first):
            start = first // PART * PART
            window = values_in[:, start : start + 2 * PART]
            return pltpu.roll(window, (start - first) % window.shape[1], 1)[:, :PART]

        for i in range(32):
            piece = jnp.where((row == 3) & (lane < rows), taken(gains, i * rows), 0.0)
            few[meta[i]] = jnp.where((row < 3) & (lane < 3 * rows), taken(taps, i * 3 * rows), piece)
        for i, ref in enumerate((keep_ref, away_ref)):
            ref[:, full - PART :] = jnp.zeros((half, PART), BF)
            for k in range(16):
                ref[k * rows : k * rows + 8, full - PART :] = few[i * 16 + k].astype(BF)


def last_kernel(meta, *refs):
    grads, (w_ref, x_ref, gain_ref, gres_ref, gin_ref) = refs[:-5], refs[-5:]
    grad = dot(jnp.concatenate([g_ref[...] for g_ref in grads], axis=1), w_ref[...], 1, 1)
    hat, inv_std = hat_of(x_ref[...].astype(F32))
    scaled = grad * gain_ref[3:4, :]
    mean_first = jnp.mean(scaled, axis=-1, keepdims=True)
    mean_second = jnp.mean(scaled * hat, axis=-1, keepdims=True)
    back = inv_std * (scaled - mean_first - hat * mean_second)
    gin_ref[...] = (gres_ref[...] + back).astype(BF)


def own_sequence(inputs, lengths, cotangent, w_qkv, w_out, conv_taps, gain_one, gain_two, w_in, w_fc2):
    seq, width = inputs.shape[1], inputs.shape[2]
    rows, wide = w_qkv.shape
    half = width // 2
    tap_rows = conv_taps.shape[0]
    batch = lax.axis_index("batch")
    core = batch & 1
    me = batch * 8 + lax.axis_index("wide")
    number = jnp.arange(64, dtype=jnp.int32)
    meta = jnp.where(number < 32, place_of(me, number & 31), jnp.where(number == 32, batch, lengths[0]))
    x, cot = inputs[0], cotangent[0]
    shape = jax.ShapeDtypeStruct
    row_spec = whole((1, width))
    gain_spec = whole((8, width))
    token = whole((seq, width))
    token_t = whole((width, seq))
    groups = width // LANES

    few_rows = [jnp.pad(conv_taps.T, ((0, 0), (0, PART - tap_rows)))]
    few_rows += [jnp.pad(gain[None], ((0, 0), (0, PART - rows))) for gain in (gain_one, gain_two)]
    few_rows = jnp.concatenate(few_rows + [jnp.zeros((rows - 5, PART), BF)])
    qkv_block = jnp.concatenate([w_qkv, few_rows], axis=1)[None]
    qkv_block, meta, first_core = lax.optimization_barrier((qkv_block, meta, core == 0))
    qkv_far = send(qkv_block, over_z(2))
    grad_out, grad_out_t = call(
        prepare_kernel, (1,), [token], [token, token_t],
        [shape((seq, width), BF), shape((width, seq), BF)], busy=1, name="prepare",
    )(meta, tie(cot, qkv_far))
    go_other = send(grad_out, over_core)
    got_other = send(grad_out_t, over_core)
    out_rows = rows * (width // PART)
    a_block, b_block = call(
        pack_kernel, (1,), [whole(w.shape) for w in (w_in, w_fc2, w_out)],
        [whole((1, width, PART)), whole((1, half + out_rows, PART))],
        [shape((1, width, PART), BF), shape((1, half + out_rows, PART), BF)], busy=2, name="pack",
    )(meta, w_in, w_fc2, w_out)

    b_far = send(tie(b_block, qkv_far), over_z(2))
    qkv2 = join([qkv_block, qkv_far])
    qkv_near = send(qkv2, over_z(1))
    qkv4 = join([qkv2, tie(qkv_near, b_far)])
    qkv_first = send(qkv4, over_first)
    b2 = join([b_block, b_far])
    b_near = send(tie(b2, qkv4), over_z(1))
    a_far = send(tie(a_block, qkv4), over_z(2))
    qkv8 = join([qkv4, tie(qkv_first, b_near)])
    qkv_second = send(qkv8, over_second)
    b4 = join([b2, b_near])
    a2 = join([a_block, tie(a_far, qkv8)])
    a_near = send(a2, over_z(1))
    qkv16 = join([qkv8, tie(qkv_second, a_near, grad_out)])
    qkv_core = send(qkv16, over_core)
    b_first = send(tie(b4, qkv16), over_first)
    a4 = join([a2, a_near])
    a_first = send(tie(a4, qkv16), over_first)

    lane_block = pl.BlockSpec((seq, LANES), lambda j, m: (0, j))
    half_block = pl.BlockSpec((16, rows, LANES), lambda j, m: (0, 0, j))
    few_block = pl.BlockSpec((16, rows, PART), lambda j, m: (0, 0, wide // PART))
    tap_block = pl.BlockSpec((8, LANES), lambda j, m: (0, j))
    projected, mixed, qkv_full, normed_t, taps, gains = call(
        project_kernel, (wide // LANES,),
        [token, half_block, half_block, few_block, few_block],
        [lane_block, lane_block, pl.BlockSpec((width, LANES), lambda j, m: (0, j)), whole((32, rows, seq)),
         tap_block, gain_spec],
        [shape((seq, wide), BF), shape((seq, wide), BF), shape((width, wide), BF), shape((32, rows, seq), BF),
         shape((8, wide), F32), shape((8, width), F32)],
        [pltpu.VMEM((seq, width), BF)], busy=7, name="project",
    )(meta, tie(x, a4, b4, go_other, got_other), qkv16, qkv_core, qkv16, qkv_core)

    b8 = join([b4, tie(b_first, mixed)])
    b_second = send(b8, over_second)
    part_specs = [pl.BlockSpec((seq, LANES), lambda j, m, p=p: (0, p * groups + j)) for p in range(3)]
    lse_spec = pl.BlockSpec((1, 8, seq), lambda j, m: (j, 0, 0))
    a8 = join([a4, tie(a_first, mixed)])
    ready = tie(mixed, b8, a8)
    attended, lse = call(
        attend_kernel, (groups,), part_specs, [lane_block, lse_spec],
        [shape((seq, width), BF), shape((groups, 8, seq), F32)], [pltpu.VMEM((LANES, seq), F32)],
        busy=9, name="attend",
    )(meta, ready, ready, ready)

    b16 = join([b8, tie(b_second, attended)])
    out16 = b16[:, half:, :]
    out_core = send(out16, over_core)
    a_second = send(tie(a8, b16), over_second)
    residual, normed_two, normed_two_t, attended_t, out_full = call(
        mend_kernel, (1,),
        [token, whole(out16.shape), whole(out16.shape), token, gain_spec],
        [token, token, token_t, whole((32, rows, seq)), whole((width, width))],
        [shape((seq, width), F32), shape((seq, width), BF), shape((width, seq), BF), shape((32, rows, seq), BF),
         shape((width, width), BF)],
        busy=2.5, name="mend",
    )(meta, attended, out16, out_core, x, gains)
    n2_other = send(normed_two, over_core)
    n2t_other = send(normed_two_t, over_core)

    sequences = [normed_two, grad_out, normed_two_t, grad_out_t, n2_other, go_other, n2t_other, got_other]
    sequence_specs = [token, token, token_t, token_t] * 2

    def tile(block_rows, per_step, k, b):
        return pl.BlockSpec(
            (1, block_rows, PART), lambda s, m: (m[b * 16 + (m[32] & 1) * 8 + s * per_step + k], 0, 0)
        )

    total = shape((seq, width), F32)
    grads_b = shape((8, half, PART), BF)
    branch, grad_two, branch_o, grad_o, b_low, b_high = call(
        functools.partial(ffn_kernel, True), (2,),
        sequence_specs + [tile(half, 4, k, b) for k in range(4) for b in range(2)],
        [token] * 4 + [whole(grads_b.shape)] * 2, [total] * 4 + [grads_b] * 2, busy=2, name="ffn",
    )(meta, *sequences, *[b16] * 8)
    a16 = join([a8, tie(a_second, branch)])
    b_sum = send(b_high, over_second)
    grads_a = shape((8, width, PART), BF)
    branch, grad_two, both, a_low, a_high = call(
        functools.partial(ffn_kernel, False), (4,),
        sequence_specs + [tile(width, 2, k, b) for k in range(2) for b in range(2)] + [token] * 4,
        [token] * 2 + [whole((2 * seq, width))] + [whole(grads_a.shape)] * 2,
        [total] * 2 + [shape((2 * seq, width), BF)] + [grads_a] * 2,
        [pltpu.VMEM((seq, width), F32)] * 2, busy=15, name="ffn",
    )(meta, tie(normed_two, b_high), *sequences[1:], *[a16] * 4, branch, grad_two, branch_o, grad_o)
    b_sum = tie(b_sum, branch)
    come = send(tie(both, b_sum), over_core)
    a_sum = send(a_high, over_second)
    b_keep, b_go = halved(b_low, b_sum)
    half_out = shape((16, rows * (width // PART), PART), BF)
    output, grad_residual, grad_attended, grad_gain_second, keep_out, away_out = call(
        turn_kernel, (1,),
        [token] * 2 + [whole((2 * seq, width)), token, gain_spec, token, token_t, whole((width, width))],
        [token] * 3 + [row_spec, whole(half_out.shape), whole(half_out.shape)],
        [shape((seq, width), BF), shape((seq, width), F32), shape((seq, width), BF), shape((1, width), F32),
         half_out, half_out],
        busy=4, name="turn",
    )(meta, tie(grad_two, a_high, b_go), branch, come, residual, gains, grad_out, attended_t.reshape(width, seq), out_full)

    def attend_back(j, wait_for):
        specs = [pl.BlockSpec((seq, LANES), lambda i, m, p=p: (0, p * groups + j)) for p in range(3)]
        tap_specs = [pl.BlockSpec((8, LANES), lambda i, m, p=p: (0, p * groups + j)) for p in range(3)]
        block = pl.BlockSpec((seq, LANES), lambda i, m: (0, j))
        return call(
            attend_back_kernel, (1,),
            specs * 2 + tap_specs + [block, block, pl.BlockSpec((1, 8, seq), lambda i, m: (j, 0, 0))],
            [whole((seq, LANES))] * 3 + [whole((8, LANES))] * 3,
            [shape((seq, LANES), BF)] * 3 + [shape((8, LANES), F32)] * 3,
            [pltpu.VMEM((LANES, seq), F32)],
            busy=4.5, name="attend_back",
        )(meta, mixed, mixed, mixed, projected, projected, projected, taps, taps, taps,
          tie(grad_attended, *wait_for), attended, lse)

    def weights(grads, few, wait_for):
        size = len(grads) * LANES + (PART if few else 0)
        spec = whole((half, size))
        keep, away = call(
            functools.partial(weight_kernel, bool(few)), (1,),
            [token_t] + [whole(part.shape) for part in few] + [whole((seq, LANES))] * len(grads),
            [spec, spec], [shape((half, size), BF)] * 2, [pltpu.VMEM((32, 8, PART), F32)] if few else (),
            busy=2, name="weight",
        )(meta, tie(normed_t.reshape(width, seq), *wait_for), *few, *grads)
        return keep.reshape(16, rows, size), away.reshape(16, rows, size)

    out_come = send(away_out, over_core)
    back0 = attend_back(0, (away_out,))

    a_keep, a_go = halved(a_low, tie(a_sum, back0[0]))
    a_sum = send(a_go, over_first)
    out_sum = added(keep_out, tie(out_come, back0[0]))
    out_go = out_sum[8:]
    out_come = send(out_go, over_second)
    back1 = attend_back(1, (back0[0], out_go, a_go))

    out_keep, out_go = halved(out_sum[:8], tie(out_come, back1[0]))
    b_keep = jnp.concatenate([b_keep, out_keep], axis=1)
    b_go = jnp.concatenate([b_go, out_go], axis=1)
    b_sum = send(b_go, over_first)
    a_keep, a_go = halved(a_keep, tie(a_sum, back1[0]))
    a_sum = send(a_go, over_z(1))
    x_keep, x_away = weights([back[part] for part in range(3) for back in (back0, back1)], [], (a_go, b_go))
    x_sum = send(x_away, over_core)
    back2 = attend_back(2, (back1[0], x_away))

    x_keep, x_go = halved(x_keep, tie(x_sum, back2[0]))
    x_sum = send(x_go, over_second)
    b_keep, b_go = halved(b_keep, tie(b_sum, back2[0]))
    b_sum = send(b_go, over_z(1))
    a_keep, a_go = halved(a_keep, tie(a_sum, back2[0]))
    a_sum = send(a_go, over_z(2))
    backs = (back0, back1, back2)
    grad_projected = [back[part] for part in range(3) for back in backs]
    few = [back[3 + part] for part in range(3) for back in backs] + [grad_gain_second]
    y_keep, y_away = weights(back2[:3], few, (x_go, a_go, b_go))
    y_sum = send(y_away, over_core)
    grad_inputs = call(
        last_kernel, (1,),
        [whole((seq, LANES))] * (3 * groups) + [whole((width, wide)), token, gain_spec, token],
        [token], [shape((seq, width), BF)], busy=4, name="last",
    )(meta, *grad_projected, qkv_full, x, gains, tie(grad_residual, y_away))[0]
    y_keep, y_go = halved(y_keep, tie(y_sum, grad_inputs))
    y_sum = send(y_go, over_second)
    grad_a = a_keep[0].astype(F32) + tie(a_sum, grad_inputs)[0].astype(F32)
    b_keep, b_go = halved(b_keep, tie(b_sum, grad_inputs))
    b_sum = send(b_go, over_z(2))
    x_keep, x_go = halved(x_keep, tie(x_sum, b_go))
    x_sum = send(x_go, over_first)
    grad_b = b_keep[0].astype(F32) + tie(b_sum, x_go)[0].astype(F32)
    grad_out_w = jnp.transpose(grad_b[half:].reshape(width // PART, rows, PART), (1, 0, 2)).reshape(rows, width)
    quarter = width // 4

    def share(swapped):
        pairs = [
            (g[first : first + quarter], g[first + quarter : first + 2 * quarter])
            for g, first in ((grad_a, 0), (grad_a, half), (grad_b, 0))
        ]
        return jnp.concatenate([jnp.where(first_core, p[swapped], p[1 - swapped]) for p in pairs])

    mine = share(0)
    theirs = send(share(1), over_core)
    mine, theirs = jnp.where(first_core, mine, theirs), jnp.where(first_core, theirs, mine)
    units = PART // 2
    grad_in_w, grad_fc2_w = (
        jnp.concatenate(
            [part[i * quarter : (i + 1) * quarter] for part in (mine, theirs)]
            + [part[2 * quarter :, i * units : (i + 1) * units] for part in (mine, theirs)],
            axis=1,
        )
        for i in range(2)
    )

    y_keep, y_go = halved(y_keep, tie(y_sum, mine))
    y_sum = send(y_go, over_first)
    x_keep, x_go = halved(x_keep, tie(x_sum, y_go))
    x_sum = send(x_go, over_z(1))
    y_keep, y_go = halved(y_keep, tie(y_sum, x_go))
    y_sum = send(y_go, over_z(1))
    x_keep, x_go = halved(x_keep, tie(x_sum, y_go))
    x_sum = send(x_go, over_z(2))
    y_keep, y_go = halved(y_keep, tie(y_sum, x_go))
    y_sum = send(y_go, over_z(2))
    x_total = x_keep[0].astype(F32) + x_sum[0].astype(F32)
    y_total = y_keep[0].astype(F32) + y_sum[0].astype(F32)
    few = y_total[:8, 3 * LANES :]
    grad_qkv = jnp.concatenate(
        [
            part
            for i in range(3)
            for part in (x_total[:, 2 * i * LANES : 2 * (i + 1) * LANES], y_total[:, i * LANES : (i + 1) * LANES])
        ],
        axis=1,
    )
    grad_gain_first = jnp.sum(grad_qkv * w_qkv.astype(F32), axis=1) / gain_one.astype(F32)
    return (
        output[None],
        grad_inputs[None],
        grad_qkv,
        grad_out_w,
        few[:3, :tap_rows].T,
        grad_gain_first,
        few[3, :rows],
        grad_in_w,
        jnp.transpose(grad_fc2_w),
    )


def solution(mesh):
    fast = functools.partial(own_sequence)

    def program(*args):
        body = fast if fits(mesh, args) else shards
        return jax.shard_map(
            body,
            mesh=mesh,
            in_specs=(
                P(("batch", "wide"), None, None),
                P(("batch", "wide")),
                P(("batch", "wide"), None, None),
                P(("batch", "wide"), None),
                P(("batch", "wide"), None),
                P(("batch", "wide"), None),
                P(("batch", "wide")),
                P(("batch", "wide")),
                P(None, "wide"),
                P("wide", None),
            ),
            out_specs=(
                P(("batch", "wide"), None, None),
                P(("batch", "wide"), None, None),
                P(("batch", "wide"), None),
                P(("batch", "wide"), None),
                P(("batch", "wide"), None),
                P(("batch", "wide")),
                P(("batch", "wide")),
                P("batch", "wide"),
                P("wide", "batch"),
            ),
            check_vma=False,
        )(*args)

    return program
```

```python
import functools
import jax
import jax.numpy as jnp
from jax import lax
from jax.experimental import pallas as pl
from jax.experimental.pallas import tpu as pltpu
from jax.sharding import PartitionSpec as P

HEADS = 12
HD = 64


epsilon = 1e-05


def contract_first(left, right):
    return lax.dot_general(
        left, right, (((0,), (0,)), ((), ())), preferred_element_type=jnp.float32
    )


def contract_last(left, right):
    return lax.dot_general(
        left, right, (((1,), (1,)), ((), ())), preferred_element_type=jnp.float32
    )


def norm_parts(values_in):
    centered = values_in - jnp.mean(values_in, axis=-1, keepdims=True)
    inv_std = lax.rsqrt(jnp.mean(centered * centered, axis=-1, keepdims=True) + epsilon)
    return (centered * inv_std, inv_std)


def norm_back(grad_normed, gain_vec, normed_hat, inv_std):
    grad_hat = grad_normed * gain_vec
    mean_first = jnp.mean(grad_hat, axis=-1, keepdims=True)
    mean_second = jnp.mean(grad_hat * normed_hat, axis=-1, keepdims=True)
    grad_value = inv_std * (grad_hat - mean_first - normed_hat * mean_second)
    return (grad_value, jnp.sum(grad_normed * normed_hat, axis=0))


def shift_down(signal, steps):
    filler = jnp.zeros((steps, signal.shape[1]), signal.dtype)
    return jnp.concatenate([filler, signal[:-steps]], axis=0)


def shift_up(signal, steps):
    filler = jnp.zeros((steps, signal.shape[1]), signal.dtype)
    return jnp.concatenate([signal[steps:], filler], axis=0)


def scores_block(query_block, keys, start_row, seq_live):
    rows_block = query_block.shape[0]
    scores = (
        jnp.einsum("qhd,khd->hqk", query_block, keys, preferred_element_type=jnp.float32) * 0.125
    )
    query_pos = start_row + jnp.arange(rows_block)
    key_pos = jnp.arange(keys.shape[0])
    allowed = (key_pos[None, :] <= query_pos[:, None]) & (key_pos[None, :] < seq_live)
    return (scores, allowed[None])


def shards(inputs, lengths, cotangent, w_qkv, w_out, conv_taps, gain_one, gain_two, w_in, w_fc2):
    full_qkv, full_out, full_taps, full_gain_one, full_gain_two = (
        lax.all_gather(w_qkv, ("batch", "wide"), axis=0, tiled=True),
        lax.all_gather(w_out, ("batch", "wide"), axis=0, tiled=True),
        lax.all_gather(conv_taps, ("batch", "wide"), axis=0, tiled=True),
        lax.all_gather(gain_one, ("batch", "wide"), axis=0, tiled=True),
        lax.all_gather(gain_two, ("batch", "wide"), axis=0, tiled=True),
    )
    seq_length, width = (inputs.shape[1], inputs.shape[2])
    tokens_in = inputs[0].astype(jnp.float32)
    seq_live = lengths[0]
    live_rows = jnp.arange(seq_length) < seq_live
    taps = full_taps.astype(jnp.float32)
    gain_first = full_gain_one.astype(jnp.float32)
    gain_second = full_gain_two.astype(jnp.float32)
    hat_one, inv_one = norm_parts(tokens_in)
    normed_one = (hat_one * gain_first).astype(jnp.bfloat16)
    projected = jnp.dot(normed_one, full_qkv, preferred_element_type=jnp.float32)
    mixed = (
        projected * taps[:, 0]
        + shift_down(projected, 1) * taps[:, 1]
        + shift_down(projected, 2) * taps[:, 2]
    ).astype(jnp.bfloat16)
    query = mixed[:, :width].reshape(seq_length, HEADS, HD)
    keys = mixed[:, width : 2 * width].reshape(seq_length, HEADS, HD)
    values = mixed[:, 2 * width :].reshape(seq_length, HEADS, HD)
    rows_block = min(512, seq_length)
    block_index = 0
    start_row = block_index * rows_block
    scores, allowed = scores_block(query, keys, start_row, seq_live)
    masked = jnp.where(allowed, scores, -1e30)
    top_score = jnp.max(masked, axis=-1, keepdims=True)
    exp_terms = jnp.exp(masked - top_score)
    row_totals = jnp.sum(exp_terms, axis=-1, keepdims=True)
    probs_low = (exp_terms / row_totals).astype(jnp.bfloat16)
    out_parts = jnp.einsum("hqk,khd->qhd", probs_low, values, preferred_element_type=jnp.float32)
    lse_parts = [top_score + jnp.log(row_totals)]
    attended_low = out_parts.reshape(seq_length, width).astype(jnp.bfloat16)
    branch_attn = jnp.dot(attended_low, full_out, preferred_element_type=jnp.float32)
    residual = tokens_in + branch_attn
    hat_two, inv_two = norm_parts(residual)
    normed_two = (hat_two * gain_second).astype(jnp.bfloat16)
    grad_out = jnp.where(live_rows[:, None], cotangent[0], jnp.zeros_like(cotangent[0]))
    row_set = lax.all_gather(normed_two[None], "wide", axis=0, tiled=True).reshape(-1, width)
    pre_act = jnp.dot(row_set, w_in, preferred_element_type=jnp.float32)
    activ = jnp.square(jax.nn.relu(pre_act)).astype(jnp.bfloat16)
    piece = activ
    branch_ffn = lax.psum_scatter(
        jnp.dot(piece, w_fc2, preferred_element_type=jnp.float32).astype(jnp.bfloat16),
        "wide",
        scatter_dimension=0,
        tiled=True,
    ).astype(jnp.float32)
    grad_set = lax.all_gather(grad_out[None], "wide", axis=0, tiled=True).reshape(-1, width)
    grad_act = contract_last(grad_set, w_fc2)
    grad_fc2_part = contract_first(activ, grad_set)
    grad_pre = (grad_act * 2.0 * jax.nn.relu(pre_act)).astype(jnp.bfloat16)
    grad_in_part = contract_first(row_set, grad_pre)
    piece = grad_pre
    grad_normed_two = lax.psum_scatter(
        contract_last(piece, w_in).astype(jnp.bfloat16), "wide", scatter_dimension=0, tiled=True
    ).astype(jnp.float32)
    grad_w_in, grad_w_fc2 = (
        lax.psum_scatter(
            grad_in_part.astype(jnp.bfloat16), "batch", scatter_dimension=0, tiled=True
        ).astype(jnp.float32),
        lax.psum_scatter(
            grad_fc2_part.astype(jnp.bfloat16), "batch", scatter_dimension=1, tiled=True
        ).astype(jnp.float32),
    )
    output = jnp.where(live_rows[:, None], residual + branch_ffn, 0.0).astype(jnp.bfloat16)[None]
    grad_ln_two, grad_gain_second = norm_back(grad_normed_two, gain_second, hat_two, inv_two)
    grad_residual = grad_out.astype(jnp.float32) + grad_ln_two
    grad_branch = grad_residual.astype(jnp.bfloat16)
    grad_w_out_part = contract_first(attended_low, grad_branch)
    grad_attended = contract_last(grad_branch, full_out).astype(jnp.bfloat16)
    grad_att_heads = grad_attended.reshape(seq_length, HEADS, HD)
    delta_all = jnp.sum(grad_att_heads.astype(jnp.float32) * out_parts, axis=-1)
    block_index = 0
    start_row = block_index * rows_block
    scores, allowed = scores_block(query, keys, start_row, seq_live)
    probs_full = jnp.where(allowed, jnp.exp(scores - lse_parts[block_index]), 0.0)
    probs_low = probs_full.astype(jnp.bfloat16)
    grad_probs = jnp.einsum(
        "qhd,khd->hqk", grad_att_heads, values, preferred_element_type=jnp.float32
    )
    delta_block = jnp.transpose(delta_all)[:, :, None]
    grad_scores = (probs_full * (grad_probs - delta_block)).astype(jnp.bfloat16)
    grad_query_parts = 0.125 * jnp.einsum(
        "hqk,khd->qhd", grad_scores, keys, preferred_element_type=jnp.float32
    )
    grad_keys = 0.125 * jnp.einsum(
        "hqk,qhd->khd", grad_scores, query, preferred_element_type=jnp.float32
    )
    grad_values = jnp.einsum(
        "hqk,qhd->khd", probs_low, grad_att_heads, preferred_element_type=jnp.float32
    )
    grad_mixed = jnp.concatenate(
        [
            grad_query_parts.reshape(seq_length, width),
            grad_keys.reshape(seq_length, width),
            grad_values.reshape(seq_length, width),
        ],
        axis=1,
    )
    grad_taps_part = jnp.stack(
        [
            jnp.sum(grad_mixed * projected, axis=0),
            jnp.sum(grad_mixed * shift_down(projected, 1), axis=0),
            jnp.sum(grad_mixed * shift_down(projected, 2), axis=0),
        ],
        axis=1,
    )
    grad_projected = (
        grad_mixed * taps[:, 0]
        + shift_up(grad_mixed, 1) * taps[:, 1]
        + shift_up(grad_mixed, 2) * taps[:, 2]
    ).astype(jnp.bfloat16)
    grad_qkv_part = contract_first(normed_one, grad_projected)
    grad_normed_one = contract_last(grad_projected, full_qkv)
    grad_ln_one, grad_gain_first = norm_back(grad_normed_one, gain_first, hat_one, inv_one)
    grad_inputs = (grad_residual + grad_ln_one).astype(jnp.bfloat16)[None]
    grad_w_qkv, grad_w_out, grad_conv_taps, grad_gain_one, grad_gain_two = (
        lax.psum_scatter(grad_qkv_part, ("batch", "wide"), scatter_dimension=0, tiled=True),
        lax.psum_scatter(grad_w_out_part, ("batch", "wide"), scatter_dimension=0, tiled=True),
        lax.psum_scatter(grad_taps_part, ("batch", "wide"), scatter_dimension=0, tiled=True),
        lax.psum_scatter(grad_gain_first, ("batch", "wide"), scatter_dimension=0, tiled=True),
        lax.psum_scatter(grad_gain_second, ("batch", "wide"), scatter_dimension=0, tiled=True),
    )
    return (
        output,
        grad_inputs,
        grad_w_qkv,
        grad_w_out,
        grad_conv_taps,
        grad_gain_one,
        grad_gain_two,
        grad_w_in,
        grad_w_fc2,
    )


BF = jnp.bfloat16
F32 = jnp.float32
AXES = ("batch", "wide")
LANES = 256
PART = 128
VMEM_MIB = {"ffn": 36}


def fits(mesh, args):
    inputs, w_qkv, w_in = args[0], args[3], args[8]
    count = mesh.shape["batch"] * mesh.shape["wide"]
    return (
        mesh.shape["batch"] == 4
        and mesh.shape["wide"] == 8
        and inputs.shape[0] == count
        and inputs.shape[1] % LANES == 0
        and w_qkv.shape[0] % (count * 8) == 0
        and w_qkv.shape[0] % LANES == 0
        and w_qkv.shape[0] // HEADS == HD
        and w_in.shape[1] == 8 * 3 * PART
        and (w_in.shape[0] // 4) % 16 == 0
    )


def dot(left, right, left_dim, right_dim):
    return lax.dot_general(
        left, right, (((left_dim,), (right_dim,)), ((), ())), preferred_element_type=F32
    )


def flip_pairs(rule):
    return [(i, i ^ rule(i)) for i in range(32)]


def send(array, rule):
    return lax.ppermute(array, AXES, flip_pairs(rule))


def over_core(i):
    return 8


def over_first(i):
    return 16 if i & 8 else 1


def over_second(i):
    return 1 if i & 8 else 16


def over_z(step):
    return lambda i: 2 * step


def tie(value, *others):
    return lax.optimization_barrier((value,) + others)[0]


def join(parts):
    return jnp.concatenate(parts)


def added(keep, come):
    return (keep.astype(F32) + come.astype(F32)).astype(BF)


def halved(keep, come):
    half = keep.shape[0] // 2
    return added(keep[:half], come[:half]), added(keep[half:], come[half:])


def place_of(me, other):
    apart = me ^ other
    x_bit, z_bits = apart & 1, (apart & 2) | ((apart >> 2) & 1)
    core_bit, y_bit = (apart >> 3) & 1, (apart >> 4) & 1
    on_first = ((other >> 3) & 1) == 0
    high = jnp.where(on_first, y_bit, x_bit)
    low = jnp.where(on_first, x_bit, y_bit)
    return core_bit * 16 + high * 8 + low * 4 + z_bits


def call(kernel, grid, in_specs, out_specs, out_shape, scratch=(), busy=1, name=None, aliases=None):
    return pl.pallas_call(
        kernel,
        grid_spec=pltpu.PrefetchScalarGridSpec(
            num_scalar_prefetch=1,
            grid=grid,
            in_specs=in_specs,
            out_specs=out_specs,
            scratch_shapes=list(scratch),
        ),
        out_shape=out_shape,
        compiler_params=pltpu.CompilerParams(
            dimension_semantics=("arbitrary",) * len(grid), vmem_limit_bytes=VMEM_MIB.get(name, 20) * 1024 * 1024
        ),
        cost_estimate=pl.CostEstimate(flops=int(busy * 1.15e9), bytes_accessed=0, transcendentals=0),
        name=name,
        input_output_aliases=aliases or {},
    )


def whole(shape):
    zeros = (0,) * len(shape)
    return pl.BlockSpec(shape, lambda *_: zeros, pipeline_mode=pl.Buffered(1))


def hat_of(values_in):
    centered = values_in - jnp.mean(values_in, axis=-1, keepdims=True)
    inv_std = lax.rsqrt(jnp.mean(centered * centered, axis=-1, keepdims=True) + epsilon)
    return centered * inv_std, inv_std


def turned(value):
    return jnp.transpose(value.astype(F32)).astype(BF)


def prepare_kernel(meta, cot_ref, go_ref, got_ref):
    live = lax.broadcasted_iota(jnp.int32, (cot_ref.shape[0], 1), 0) < meta[33]
    value = jnp.where(live, cot_ref[...].astype(F32), 0.0)
    go_ref[...] = value.astype(BF)
    got_ref[...] = jnp.transpose(value).astype(BF)


def pack_kernel(meta, up_ref, down_ref, out_ref, a_ref, b_ref):
    half = up_ref.shape[0] // 2
    second_half, second_core = (meta[32] >> 1) == 1, (meta[32] & 1) == 1
    up = jnp.where(second_half, up_ref[half:, :], up_ref[:half, :])
    down = turned(jnp.where(second_half, down_ref[:, half:], down_ref[:, :half]))
    for i, part in enumerate((up, down)):
        a_ref[0, i * half : (i + 1) * half, :] = jnp.where(second_core, part[:, PART : 2 * PART], part[:, :PART])
    left, right = swap_halves(up[:, 2 * PART :], down[:, 2 * PART :])
    b_ref[0, :half, :] = jnp.where(second_core, right, left).astype(BF)
    rows = out_ref.shape[0]
    for c in range(out_ref.shape[1] // PART):
        b_ref[0, half + c * rows : half + (c + 1) * rows, :] = out_ref[:, c * PART : (c + 1) * PART]


def block_of(meta, i, own_ref, other_ref):
    place = meta[i]
    return jnp.where(place < 16, own_ref[place & 15], other_ref[place & 15])


def project_kernel(
    meta, x_ref, own_ref, other_ref, few_own_ref, few_other_ref,
    proj_ref, mixed_ref, wn_ref, nt_ref, taps_ref, gains_ref, normed,
):
    rows = own_ref.shape[1]
    step = pl.program_id(0)

    def few_of(device, lanes):
        block = block_of(meta, device, few_own_ref, few_other_ref)[:8].astype(F32)
        return jnp.concatenate([block, jnp.zeros((8, lanes - PART), F32)], axis=1)

    @pl.when(step == 0)
    def _():
        width = gains_ref.shape[1]
        lane = lax.broadcasted_iota(jnp.int32, (8, width), 1)
        gains = jnp.zeros((8, width), F32)
        for i in range(32):
            first = i * rows
            moved = pltpu.roll(few_of(i, width), first, 1)
            gains = jnp.where((lane >= first) & (lane < first + rows), moved, gains)
        gains_ref[...] = gains
        hat, _ = hat_of(x_ref[...].astype(F32))
        low = (hat * gains[3:4, :]).astype(BF)
        normed[...] = low
        flipped = turned(low)
        for i in range(32):
            nt_ref[meta[i]] = flipped[i * rows : (i + 1) * rows]

    channels = 3 * rows
    lane = lax.broadcasted_iota(jnp.int32, (8, LANES), 1)
    taps = jnp.zeros((8, LANES), F32)
    for i in range(LANES // channels + 2):
        device = jnp.minimum((step * LANES) // channels + i, 31)
        first = device * channels - step * LANES
        moved = pltpu.roll(few_of(device, LANES), (first + 2 * LANES) & (LANES - 1), 1)
        taps = jnp.where((lane >= first) & (lane < first + channels), moved, taps)
    taps_ref[...] = taps
    for i in range(32):
        wn_ref[i * rows : (i + 1) * rows, :] = block_of(meta, i, own_ref, other_ref)
    value = dot(normed[...], wn_ref[...], 1, 0)
    at = lax.broadcasted_iota(jnp.int32, value.shape, 0)
    one = jnp.where(at >= 1, pltpu.roll(value, 1, 0), 0.0)
    two = jnp.where(at >= 2, pltpu.roll(value, 2, 0), 0.0)
    mixed = value * taps[0:1, :] + one * taps[1:2, :] + two * taps[2:3, :]
    proj_ref[...] = value.astype(BF)
    mixed_ref[...] = mixed.astype(BF)


def head_row(head, scale=1.0):
    lane = lax.broadcasted_iota(jnp.int32, (1, LANES), 1)
    return jnp.where(lane // HD == head, scale, 0.0).astype(BF)


def allowed_in(meta, keys, first_query, queries):
    key = lax.broadcasted_iota(jnp.int32, (keys, queries), 0)
    query = first_query + lax.broadcasted_iota(jnp.int32, (1, queries), 1)
    return key < jnp.minimum(query + 1, meta[33])


def attend_kernel(meta, q_ref, k_ref, v_ref, out_ref, lse_ref, flipped):
    seq = q_ref.shape[0]
    tile = LANES
    values_t = turned(v_ref[...])
    keys = k_ref[...]
    for t in range(seq // tile):
        upto = (t + 1) * tile
        allowed = allowed_in(meta, upto, t * tile, tile)
        query = q_ref[t * tile : upto, :]
        for head in range(LANES // HD):
            scores = dot(keys[:upto], query * head_row(head, 0.125), 1, 1)
            scores = jnp.where(allowed, scores, -1e30)
            top = jnp.max(scores, axis=0, keepdims=True)
            terms = jnp.exp(scores - top)
            total = jnp.sum(terms, axis=0, keepdims=True)
            probs = (terms * (1.0 / total)).astype(BF)
            flipped[head * HD : (head + 1) * HD, t * tile : upto] = dot(
                values_t[head * HD : (head + 1) * HD, :upto], probs, 1, 0
            )
            lse_ref[0, head : head + 1, t * tile : upto] = top + jnp.log(total)
    out_ref[...] = jnp.transpose(flipped[...]).astype(BF)


def mend_kernel(meta, att_ref, own_ref, other_ref, x_ref, gain_ref, res_ref, n2_ref, n2t_ref, at_ref, wn_ref):
    flipped = turned(att_ref[...])
    rows = at_ref.shape[1]
    for i in range(32):
        at_ref[meta[i]] = flipped[i * rows : (i + 1) * rows]
        block = block_of(meta, i, own_ref, other_ref)
        for c in range(wn_ref.shape[1] // PART):
            wn_ref[i * rows : (i + 1) * rows, c * PART : (c + 1) * PART] = block[c * rows : (c + 1) * rows]
    residual = x_ref[...].astype(F32) + dot(att_ref[...], wn_ref[...], 1, 0)
    res_ref[...] = residual
    hat, _ = hat_of(residual)
    low = (hat * gain_ref[4:5, :]).astype(BF)
    n2_ref[...] = low
    n2t_ref[...] = turned(low)


def swap_halves(left, right):
    left, right = left.astype(F32), right.astype(F32)
    low = lax.broadcasted_iota(jnp.int32, (1, PART), 1) < PART // 2
    return (
        jnp.where(low, left, pltpu.roll(right, PART // 2, 1)),
        jnp.where(low, pltpu.roll(left, PART // 2, 1), right),
    )


def ffn_kernel(packed, meta, *refs):
    token_refs, refs = (refs[:4], refs[4:8]), refs[8:]
    count = 8 if packed else 4
    tiles, refs = refs[:count], refs[count:]
    if packed:
        branch_ref, grad_ref, branch_acc, grad_acc, low_ref, high_ref = refs
    else:
        sums_in, (branch_ref, grad_ref, both_ref, low_ref, high_ref, branch_acc, grad_acc) = refs[:4], refs[4:]
    sums = (branch_ref, grad_ref, branch_acc, grad_acc)
    step = pl.program_id(0)

    @pl.when(step == 0)
    def _():
        for i, ref in enumerate(sums):
            ref[...] = jnp.zeros_like(ref) if packed else sums_in[i][...]

    half = tiles[0].shape[1] if packed else tiles[0].shape[1] // 2
    if packed:
        blocks = [jnp.concatenate([tiles[2 * k][0], tiles[2 * k + 1][0]], axis=0) for k in range(4)]
        pairs = [swap_halves(blocks[0], blocks[1]), swap_halves(blocks[2], blocks[3])]
        w_up, w_down = (jnp.concatenate([pairs[0][i], pairs[1][i]], axis=1).astype(BF) for i in range(2))
    else:
        w_up, w_down = (
            jnp.concatenate(
                [
                    jnp.concatenate([tiles[2 * k + b][0, i * half : (i + 1) * half, :] for b in range(2)], axis=0)
                    for k in range(2)
                ],
                axis=1,
            )
            for i in range(2)
        )
    up_sum = down_sum = 0.0
    for i, (n2_ref, go_ref, n2t_ref, got_ref) in enumerate(token_refs):
        pre = jnp.maximum(dot(n2_ref[...], w_up, 1, 0), 0.0)
        activ = (pre * pre).astype(BF)
        grad_pre = (dot(go_ref[...], w_down, 1, 0) * 2.0 * pre).astype(BF)
        sums[2 * i][...] += dot(activ, w_down, 1, 1)
        sums[2 * i + 1][...] += dot(grad_pre, w_up, 1, 1)
        up_sum += dot(n2t_ref[...], grad_pre, 1, 0)
        down_sum += dot(got_ref[...], activ, 1, 0)
    first_wide = step * (4 if packed else 2)
    results = []
    for k in range(2):
        lanes = slice(k * PART, (k + 1) * PART)
        if packed:
            results += [(part,) for part in swap_halves(up_sum[:, lanes], down_sum[:, lanes])]
        else:
            results.append((up_sum[:, lanes], down_sum[:, lanes]))
    for k, parts in enumerate(results):
        for b in range(2):
            place = meta[b * 16 + (meta[32] & 1) * 8 + first_wide + k]
            for is_high, target in enumerate((low_ref, high_ref)):

                @pl.when((place >> 3) == is_high)
                def _(place=place, target=target, parts=parts, b=b):
                    for i, part in enumerate(parts):
                        target[place & 7, i * half : (i + 1) * half, :] = part[b * half : (b + 1) * half].astype(BF)

    if not packed:

        @pl.when(step == pl.num_programs(0) - 1)
        def _():
            seq = branch_acc.shape[0]
            both_ref[:seq, :] = branch_acc[...].astype(BF)
            both_ref[seq:, :] = grad_acc[...].astype(BF)


def turn_kernel(meta, grad_ref, branch_ref, come_ref, res_ref, gain_ref, go_ref, at_ref, wn_ref, out_ref, gres_ref, gatt_ref, ggain_ref, keep_ref, away_ref):
    residual = res_ref[...]
    seq = residual.shape[0]
    live = lax.broadcasted_iota(jnp.int32, (seq, 1), 0) < meta[33]
    branch = branch_ref[...] + come_ref[:seq, :].astype(F32)
    out_ref[...] = jnp.where(live, residual + branch, 0.0).astype(BF)
    hat, inv_std = hat_of(residual)
    grad = grad_ref[...] + come_ref[seq:, :].astype(F32)
    ggain_ref[...] = jnp.sum(grad * hat, axis=0, keepdims=True)
    scaled = grad * gain_ref[4:5, :]
    mean_first = jnp.mean(scaled, axis=-1, keepdims=True)
    mean_second = jnp.mean(scaled * hat, axis=-1, keepdims=True)
    grad_res = go_ref[...].astype(F32) + inv_std * (scaled - mean_first - hat * mean_second)
    gres_ref[...] = grad_res
    low = grad_res.astype(BF)
    gatt_ref[...] = dot(low, wn_ref[...], 1, 1).astype(BF)
    result = dot(at_ref[...], low, 1, 0)
    lanes = keep_ref.shape[2]
    chunks = result.shape[1] // lanes
    rows = keep_ref.shape[1] // chunks
    for i in range(32):
        target = away_ref if i >= 16 else keep_ref
        for c in range(chunks):
            target[i & 15, c * rows : (c + 1) * rows, :] = result[
                i * rows : (i + 1) * rows, c * lanes : (c + 1) * lanes
            ].astype(BF)


def attend_back_kernel(
    meta, q_ref, k_ref, v_ref, pq_ref, pk_ref, pv_ref, tq_ref, tk_ref, tv_ref, go_ref, out_ref, lse_ref,
    gq_ref, gk_ref, gv_ref, dtq_ref, dtk_ref, dtv_ref, flipped,
):
    seq = q_ref.shape[0]
    tile = LANES
    keys, values = k_ref[...], v_ref[...]
    keys_t = turned(keys)
    delta_t = jnp.transpose(go_ref[...].astype(F32) * out_ref[...].astype(F32))
    grad_keys = [jnp.zeros((tile, LANES), F32) for _ in range(seq // tile)]
    grad_values = list(grad_keys)
    for t in range(seq // tile):
        upto = (t + 1) * tile
        allowed = allowed_in(meta, upto, t * tile, tile)
        query, grad = q_ref[t * tile : upto, :], go_ref[t * tile : upto, :]
        for head in range(LANES // HD):
            lanes = slice(head * HD, (head + 1) * HD)
            query_h, grad_h = query * head_row(head, 0.125), grad * head_row(head)
            delta = jnp.sum(delta_t[lanes, t * tile : upto], axis=0, keepdims=True)
            scores = dot(keys[:upto], query_h, 1, 1)
            lse = lse_ref[0, head : head + 1, t * tile : upto]
            probs = jnp.where(allowed, jnp.exp(scores - lse), 0.0)
            grad_scores = (probs * (dot(values[:upto], grad_h, 1, 1) - delta)).astype(BF)
            flipped[lanes, t * tile : upto] = dot(keys_t[lanes, :upto], grad_scores, 1, 0) * 0.125
            add_values = dot(probs.astype(BF), grad_h, 1, 0)
            add_keys = dot(grad_scores, query_h, 1, 0)
            for s in range(t + 1):
                rows = slice(s * tile, (s + 1) * tile)
                grad_values[s] += add_values[rows]
                grad_keys[s] += add_keys[rows]
    mixed = (
        jnp.transpose(flipped[...]),
        jnp.concatenate(grad_keys, axis=0),
        jnp.concatenate(grad_values, axis=0),
    )
    at = lax.broadcasted_iota(jnp.int32, (seq, LANES), 0)
    for grad, proj_ref, taps_ref, g_ref, dt_ref in zip(
        mixed, (pq_ref, pk_ref, pv_ref), (tq_ref, tk_ref, tv_ref), (gq_ref, gk_ref, gv_ref), (dtq_ref, dtk_ref, dtv_ref)
    ):
        one = jnp.where(at < seq - 1, pltpu.roll(grad, seq - 1, 0), 0.0)
        two = jnp.where(at < seq - 2, pltpu.roll(grad, seq - 2, 0), 0.0)
        g_ref[...] = (grad * taps_ref[0:1, :] + one * taps_ref[1:2, :] + two * taps_ref[2:3, :]).astype(BF)
        proj = proj_ref[...].astype(F32)
        for tap, part in enumerate((grad, one, two)):
            dt_ref[tap : tap + 1, :] = jnp.sum(part * proj, axis=0, keepdims=True)


def weight_kernel(with_few, meta, nt_ref, *refs):
    if with_few:
        (*tap_refs, gain_ref), refs, few = refs[:10], refs[10:-1], refs[-1]
    keep_ref, away_ref = refs[-2:]
    half, full = keep_ref.shape
    for j, g_ref in enumerate(refs[:-2]):
        result = dot(nt_ref[...], g_ref[...], 1, 0).astype(BF)
        columns = slice(j * LANES, (j + 1) * LANES)
        keep_ref[:, columns] = result[:half]
        away_ref[:, columns] = result[half:]
    if with_few:
        rows = half // 16
        row = lax.broadcasted_iota(jnp.int32, (8, PART), 0)
        lane = lax.broadcasted_iota(jnp.int32, (8, PART), 1)
        taps = jnp.concatenate([ref[...] for ref in tap_refs], axis=1)
        gains = jnp.broadcast_to(gain_ref[...], (8, gain_ref.shape[1]))

        def taken(values_in, first):
            start = first // PART * PART
            window = values_in[:, start : start + 2 * PART]
            return pltpu.roll(window, (start - first) % window.shape[1], 1)[:, :PART]

        for i in range(32):
            piece = jnp.where((row == 3) & (lane < rows), taken(gains, i * rows), 0.0)
            few[meta[i]] = jnp.where((row < 3) & (lane < 3 * rows), taken(taps, i * 3 * rows), piece)
        for i, ref in enumerate((keep_ref, away_ref)):
            ref[:, full - PART :] = jnp.zeros((half, PART), BF)
            for k in range(16):
                ref[k * rows : k * rows + 8, full - PART :] = few[i * 16 + k].astype(BF)


def last_kernel(meta, *refs):
    grads, (w_ref, x_ref, gain_ref, gres_ref, gin_ref) = refs[:-5], refs[-5:]
    grad = dot(jnp.concatenate([g_ref[...] for g_ref in grads], axis=1), w_ref[...], 1, 1)
    hat, inv_std = hat_of(x_ref[...].astype(F32))
    scaled = grad * gain_ref[3:4, :]
    mean_first = jnp.mean(scaled, axis=-1, keepdims=True)
    mean_second = jnp.mean(scaled * hat, axis=-1, keepdims=True)
    back = inv_std * (scaled - mean_first - hat * mean_second)
    gin_ref[...] = (gres_ref[...] + back).astype(BF)


def own_sequence(inputs, lengths, cotangent, w_qkv, w_out, conv_taps, gain_one, gain_two, w_in, w_fc2):
    seq, width = inputs.shape[1], inputs.shape[2]
    rows, wide = w_qkv.shape
    half = width // 2
    tap_rows = conv_taps.shape[0]
    batch = lax.axis_index("batch")
    core = batch & 1
    me = batch * 8 + lax.axis_index("wide")
    number = jnp.arange(64, dtype=jnp.int32)
    meta = jnp.where(number < 32, place_of(me, number & 31), jnp.where(number == 32, batch, lengths[0]))
    x, cot = inputs[0], cotangent[0]
    shape = jax.ShapeDtypeStruct
    row_spec = whole((1, width))
    gain_spec = whole((8, width))
    token = whole((seq, width))
    token_t = whole((width, seq))
    groups = width // LANES

    few_rows = [jnp.pad(conv_taps.T, ((0, 0), (0, PART - tap_rows)))]
    few_rows += [jnp.pad(gain[None], ((0, 0), (0, PART - rows))) for gain in (gain_one, gain_two)]
    few_rows = jnp.concatenate(few_rows + [jnp.zeros((rows - 5, PART), BF)])
    qkv_block = jnp.concatenate([w_qkv, few_rows], axis=1)[None]
    qkv_block, meta, first_core = lax.optimization_barrier((qkv_block, meta, core == 0))
    qkv_far = send(qkv_block, over_z(2))
    out_rows = rows * (width // PART)
    a_block, b_block = call(
        pack_kernel, (1,), [whole(w.shape) for w in (w_in, w_fc2, w_out)],
        [whole((1, width, PART)), whole((1, half + out_rows, PART))],
        [shape((1, width, PART), BF), shape((1, half + out_rows, PART), BF)], busy=2, name="pack",
    )(meta, w_in, w_fc2, w_out)

    b_far = send(tie(b_block, qkv_far), over_z(2))
    qkv2 = join([qkv_block, tie(qkv_far, b_block)])
    qkv_near = send(qkv2, over_z(1))
    qkv4 = join([qkv2, qkv_near])
    qkv_first = send(qkv4, over_first)
    b2 = join([b_block, tie(b_far, qkv4)])
    b_near = send(b2, over_z(1))
    a_far = send(tie(a_block, b2), over_z(2))
    qkv8 = join([qkv4, tie(qkv_first, b2)])
    qkv_second = send(qkv8, over_second)
    grad_out, grad_out_t = call(
        prepare_kernel, (1,), [token], [token, token_t],
        [shape((seq, width), BF), shape((width, seq), BF)], busy=1, name="prepare",
    )(meta, tie(cot, qkv8))
    go_other = send(grad_out, over_core)
    got_other = send(grad_out_t, over_core)
    b4 = join([b2, tie(b_near, qkv8)])
    a2 = join([a_block, tie(a_far, qkv8)])
    a_near = send(a2, over_z(1))
    qkv16 = join([qkv8, tie(qkv_second, a2, b4, grad_out)])
    qkv_core = send(qkv16, over_core)
    b_first = send(tie(b4, qkv16), over_first)
    a4 = join([a2, tie(a_near, qkv_core)])
    a_first = send(a4, over_first)

    lane_block = pl.BlockSpec((seq, LANES), lambda j, m: (0, j))
    half_block = pl.BlockSpec((16, rows, LANES), lambda j, m: (0, 0, j))
    few_block = pl.BlockSpec((16, rows, PART), lambda j, m: (0, 0, wide // PART))
    tap_block = pl.BlockSpec((8, LANES), lambda j, m: (0, j))
    projected, mixed, qkv_full, normed_t, taps, gains = call(
        project_kernel, (wide // LANES,),
        [token, half_block, half_block, few_block, few_block],
        [lane_block, lane_block, pl.BlockSpec((width, LANES), lambda j, m: (0, j)), whole((32, rows, seq)),
         tap_block, gain_spec],
        [shape((seq, wide), BF), shape((seq, wide), BF), shape((width, wide), BF), shape((32, rows, seq), BF),
         shape((8, wide), F32), shape((8, width), F32)],
        [pltpu.VMEM((seq, width), BF)], busy=7, name="project",
    )(meta, tie(x, a4), qkv16, qkv_core, qkv16, qkv_core)

    b8 = join([b4, tie(b_first, mixed)])
    b_second = send(b8, over_second)
    part_specs = [pl.BlockSpec((seq, LANES), lambda j, m, p=p: (0, p * groups + j)) for p in range(3)]
    lse_spec = pl.BlockSpec((1, 8, seq), lambda j, m: (j, 0, 0))
    a8 = join([a4, tie(a_first, mixed)])
    ready = tie(mixed, b8, a8, go_other, got_other)
    attended, lse = call(
        attend_kernel, (groups,), part_specs, [lane_block, lse_spec],
        [shape((seq, width), BF), shape((groups, 8, seq), F32)], [pltpu.VMEM((LANES, seq), F32)],
        busy=9, name="attend",
    )(meta, ready, ready, ready)

    b16 = join([b8, tie(b_second, attended)])
    out16 = b16[:, half:, :]
    out_core = send(out16, over_core)
    a_second = send(tie(a8, b16), over_second)
    residual, normed_two, normed_two_t, attended_t, out_full = call(
        mend_kernel, (1,),
        [token, whole(out16.shape), whole(out16.shape), token, gain_spec],
        [token, token, token_t, whole((32, rows, seq)), whole((width, width))],
        [shape((seq, width), F32), shape((seq, width), BF), shape((width, seq), BF), shape((32, rows, seq), BF),
         shape((width, width), BF)],
        busy=2.5, name="mend",
    )(meta, attended, out16, out_core, x, gains)
    n2_other = send(normed_two, over_core)
    n2t_other = send(normed_two_t, over_core)

    sequences = [normed_two, grad_out, normed_two_t, grad_out_t, n2_other, go_other, n2t_other, got_other]
    sequence_specs = [token, token, token_t, token_t] * 2

    def tile(block_rows, per_step, k, b):
        return pl.BlockSpec(
            (1, block_rows, PART), lambda s, m: (m[b * 16 + (m[32] & 1) * 8 + s * per_step + k], 0, 0)
        )

    total = shape((seq, width), F32)
    grads_b = shape((8, half, PART), BF)
    branch, grad_two, branch_o, grad_o, b_low, b_high = call(
        functools.partial(ffn_kernel, True), (2,),
        sequence_specs + [tile(half, 4, k, b) for k in range(4) for b in range(2)],
        [token] * 4 + [whole(grads_b.shape)] * 2, [total] * 4 + [grads_b] * 2, busy=2, name="ffn",
    )(meta, *sequences, *[b16] * 8)
    a16 = join([a8, tie(a_second, branch)])
    b_sum = send(b_high, over_second)
    grads_a = shape((8, width, PART), BF)
    branch, grad_two, both, a_low, a_high = call(
        functools.partial(ffn_kernel, False), (4,),
        sequence_specs + [tile(width, 2, k, b) for k in range(2) for b in range(2)] + [token] * 4,
        [token] * 2 + [whole((2 * seq, width))] + [whole(grads_a.shape)] * 2,
        [total] * 2 + [shape((2 * seq, width), BF)] + [grads_a] * 2,
        [pltpu.VMEM((seq, width), F32)] * 2, busy=15, name="ffn",
    )(meta, tie(normed_two, b_high), *sequences[1:], *[a16] * 4, branch, grad_two, branch_o, grad_o)
    b_sum = tie(b_sum, branch)
    come = send(tie(both, b_sum), over_core)
    a_sum = send(a_high, over_second)
    b_keep, b_go = halved(b_low, b_sum)
    half_out = shape((16, rows * (width // PART), PART), BF)
    output, grad_residual, grad_attended, grad_gain_second, keep_out, away_out = call(
        turn_kernel, (1,),
        [token] * 2 + [whole((2 * seq, width)), token, gain_spec, token, token_t, whole((width, width))],
        [token] * 3 + [row_spec, whole(half_out.shape), whole(half_out.shape)],
        [shape((seq, width), BF), shape((seq, width), F32), shape((seq, width), BF), shape((1, width), F32),
         half_out, half_out],
        busy=4, name="turn",
    )(meta, tie(grad_two, a_high, b_go), branch, come, residual, gains, grad_out, attended_t.reshape(width, seq), out_full)

    def attend_back(j, wait_for):
        specs = [pl.BlockSpec((seq, LANES), lambda i, m, p=p: (0, p * groups + j)) for p in range(3)]
        tap_specs = [pl.BlockSpec((8, LANES), lambda i, m, p=p: (0, p * groups + j)) for p in range(3)]
        block = pl.BlockSpec((seq, LANES), lambda i, m: (0, j))
        return call(
            attend_back_kernel, (1,),
            specs * 2 + tap_specs + [block, block, pl.BlockSpec((1, 8, seq), lambda i, m: (j, 0, 0))],
            [whole((seq, LANES))] * 3 + [whole((8, LANES))] * 3,
            [shape((seq, LANES), BF)] * 3 + [shape((8, LANES), F32)] * 3,
            [pltpu.VMEM((LANES, seq), F32)],
            busy=1, name="attend_back",
        )(meta, mixed, mixed, mixed, projected, projected, projected, taps, taps, taps,
          tie(grad_attended, *wait_for), attended, lse)

    def weights(grads, few, wait_for):
        size = len(grads) * LANES + (PART if few else 0)
        spec = whole((half, size))
        keep, away = call(
            functools.partial(weight_kernel, bool(few)), (1,),
            [token_t] + [whole(part.shape) for part in few] + [whole((seq, LANES))] * len(grads),
            [spec, spec], [shape((half, size), BF)] * 2, [pltpu.VMEM((32, 8, PART), F32)] if few else (),
            busy=1, name="weight",
        )(meta, tie(normed_t.reshape(width, seq), *wait_for), *few, *grads)
        return keep.reshape(16, rows, size), away.reshape(16, rows, size)

    out_come = send(away_out, over_core)
    back0 = attend_back(0, (away_out,))

    out_sum = added(keep_out, tie(out_come, back0[0]))
    out_go = out_sum[8:]
    out_come = send(out_go, over_second)
    back1 = attend_back(1, (back0[0], out_go))
    x_keep, x_away = weights([back[part] for part in range(3) for back in (back0, back1)], [], ())
    x_sum = send(x_away, over_core)
    a_keep, a_go = halved(a_low, tie(a_sum, x_away))
    a_sum = send(a_go, over_first)
    back2 = attend_back(2, (back1[0], x_away, a_go))
    backs = (back0, back1, back2)
    grad_projected = [back[part] for part in range(3) for back in backs]
    few = [back[3 + part] for part in range(3) for back in backs] + [grad_gain_second]
    y_keep, y_away = weights(back2[:3], few, ())
    y_sum = send(y_away, over_core)

    out_keep, out_go = halved(out_sum[:8], tie(out_come, y_away))
    b_keep = jnp.concatenate([b_keep, out_keep], axis=1)
    b_go = jnp.concatenate([b_go, out_go], axis=1)
    b_sum = send(b_go, over_first)
    grad_inputs = call(
        last_kernel, (1,),
        [whole((seq, LANES))] * (3 * groups) + [whole((width, wide)), token, gain_spec, token],
        [token], [shape((seq, width), BF)], busy=4, name="last",
    )(meta, *grad_projected, qkv_full, x, gains, tie(grad_residual, y_away, a_go, b_go))[0]
    x_keep, x_go = halved(x_keep, tie(x_sum, grad_inputs))
    x_sum = send(x_go, over_second)
    y_keep, y_go = halved(y_keep, tie(y_sum, x_go))
    y_sum = send(y_go, over_second)
    a_keep, a_go = halved(a_keep, tie(a_sum, y_go))
    a_sum = send(a_go, over_z(1))
    b_keep, b_go = halved(b_keep, tie(b_sum, a_go))
    b_sum = send(b_go, over_z(1))
    x_keep, x_go = halved(x_keep, tie(x_sum, b_go))
    x_sum = send(x_go, over_first)
    y_keep, y_go = halved(y_keep, tie(y_sum, x_go))
    y_sum = send(y_go, over_first)
    a_keep, a_go = halved(a_keep, tie(a_sum, y_go))
    a_sum = send(a_go, over_z(2))
    b_keep, b_go = halved(b_keep, tie(b_sum, a_go))
    b_sum = send(b_go, over_z(2))
    x_keep, x_go = halved(x_keep, tie(x_sum, b_go))
    x_sum = send(x_go, over_z(1))
    y_keep, y_go = halved(y_keep, tie(y_sum, x_go))
    y_sum = send(y_go, over_z(1))
    grad_a = a_keep[0].astype(F32) + tie(a_sum, y_go)[0].astype(F32)
    grad_b = b_keep[0].astype(F32) + tie(b_sum, y_go)[0].astype(F32)
    grad_out_w = jnp.transpose(grad_b[half:].reshape(width // PART, rows, PART), (1, 0, 2)).reshape(rows, width)
    quarter = width // 4

    def share(swapped):
        pairs = [
            (g[first : first + quarter], g[first + quarter : first + 2 * quarter])
            for g, first in ((grad_a, 0), (grad_a, half), (grad_b, 0))
        ]
        return jnp.concatenate([jnp.where(first_core, p[swapped], p[1 - swapped]) for p in pairs])

    mine = share(0)
    theirs = send(share(1), over_core)
    mine, theirs = jnp.where(first_core, mine, theirs), jnp.where(first_core, theirs, mine)
    units = PART // 2
    grad_in_w, grad_fc2_w = (
        jnp.concatenate(
            [part[i * quarter : (i + 1) * quarter] for part in (mine, theirs)]
            + [part[2 * quarter :, i * units : (i + 1) * units] for part in (mine, theirs)],
            axis=1,
        )
        for i in range(2)
    )

    x_keep, x_go = halved(x_keep, tie(x_sum, grad_a, grad_b))
    x_sum = send(x_go, over_z(2))
    y_keep, y_go = halved(y_keep, tie(y_sum, x_go))
    y_sum = send(y_go, over_z(2))
    x_total = x_keep[0].astype(F32) + x_sum[0].astype(F32)
    y_total = y_keep[0].astype(F32) + y_sum[0].astype(F32)
    few = y_total[:8, 3 * LANES :]
    grad_qkv = jnp.concatenate(
        [
            part
            for i in range(3)
            for part in (x_total[:, 2 * i * LANES : 2 * (i + 1) * LANES], y_total[:, i * LANES : (i + 1) * LANES])
        ],
        axis=1,
    )
    grad_gain_first = jnp.sum(grad_qkv * w_qkv.astype(F32), axis=1) / gain_one.astype(F32)
    return (
        output[None],
        grad_inputs[None],
        grad_qkv,
        grad_out_w,
        few[:3, :tap_rows].T,
        grad_gain_first,
        few[3, :rows],
        grad_in_w,
        jnp.transpose(grad_fc2_w),
    )


def solution(mesh):
    fast = functools.partial(own_sequence)

    def program(*args):
        body = fast if fits(mesh, args) else shards
        return jax.shard_map(
            body,
            mesh=mesh,
            in_specs=(
                P(("batch", "wide"), None, None),
                P(("batch", "wide")),
                P(("batch", "wide"), None, None),
                P(("batch", "wide"), None),
                P(("batch", "wide"), None),
                P(("batch", "wide"), None),
                P(("batch", "wide")),
                P(("batch", "wide")),
                P(None, "wide"),
                P("wide", None),
            ),
            out_specs=(
                P(("batch", "wide"), None, None),
                P(("batch", "wide"), None, None),
                P(("batch", "wide"), None),
                P(("batch", "wide"), None),
                P(("batch", "wide"), None),
                P(("batch", "wide")),
                P(("batch", "wide")),
                P("batch", "wide"),
                P("wide", "batch"),
            ),
            check_vma=False,
        )(*args)

    return program
```

```python
import functools
import jax
import jax.numpy as jnp
from jax import lax
from jax.experimental import pallas as pl
from jax.experimental.pallas import tpu as pltpu
from jax.sharding import PartitionSpec as P

HEADS = 12
HD = 64


epsilon = 1e-05


def contract_first(left, right):
    return lax.dot_general(
        left, right, (((0,), (0,)), ((), ())), preferred_element_type=jnp.float32
    )


def contract_last(left, right):
    return lax.dot_general(
        left, right, (((1,), (1,)), ((), ())), preferred_element_type=jnp.float32
    )


def norm_parts(values_in):
    centered = values_in - jnp.mean(values_in, axis=-1, keepdims=True)
    inv_std = lax.rsqrt(jnp.mean(centered * centered, axis=-1, keepdims=True) + epsilon)
    return (centered * inv_std, inv_std)


def norm_back(grad_normed, gain_vec, normed_hat, inv_std):
    grad_hat = grad_normed * gain_vec
    mean_first = jnp.mean(grad_hat, axis=-1, keepdims=True)
    mean_second = jnp.mean(grad_hat * normed_hat, axis=-1, keepdims=True)
    grad_value = inv_std * (grad_hat - mean_first - normed_hat * mean_second)
    return (grad_value, jnp.sum(grad_normed * normed_hat, axis=0))


def shift_down(signal, steps):
    filler = jnp.zeros((steps, signal.shape[1]), signal.dtype)
    return jnp.concatenate([filler, signal[:-steps]], axis=0)


def shift_up(signal, steps):
    filler = jnp.zeros((steps, signal.shape[1]), signal.dtype)
    return jnp.concatenate([signal[steps:], filler], axis=0)


def scores_block(query_block, keys, start_row, seq_live):
    rows_block = query_block.shape[0]
    scores = (
        jnp.einsum("qhd,khd->hqk", query_block, keys, preferred_element_type=jnp.float32) * 0.125
    )
    query_pos = start_row + jnp.arange(rows_block)
    key_pos = jnp.arange(keys.shape[0])
    allowed = (key_pos[None, :] <= query_pos[:, None]) & (key_pos[None, :] < seq_live)
    return (scores, allowed[None])


def shards(inputs, lengths, cotangent, w_qkv, w_out, conv_taps, gain_one, gain_two, w_in, w_fc2):
    full_qkv, full_out, full_taps, full_gain_one, full_gain_two = (
        lax.all_gather(w_qkv, ("batch", "wide"), axis=0, tiled=True),
        lax.all_gather(w_out, ("batch", "wide"), axis=0, tiled=True),
        lax.all_gather(conv_taps, ("batch", "wide"), axis=0, tiled=True),
        lax.all_gather(gain_one, ("batch", "wide"), axis=0, tiled=True),
        lax.all_gather(gain_two, ("batch", "wide"), axis=0, tiled=True),
    )
    seq_length, width = (inputs.shape[1], inputs.shape[2])
    tokens_in = inputs[0].astype(jnp.float32)
    seq_live = lengths[0]
    live_rows = jnp.arange(seq_length) < seq_live
    taps = full_taps.astype(jnp.float32)
    gain_first = full_gain_one.astype(jnp.float32)
    gain_second = full_gain_two.astype(jnp.float32)
    hat_one, inv_one = norm_parts(tokens_in)
    normed_one = (hat_one * gain_first).astype(jnp.bfloat16)
    projected = jnp.dot(normed_one, full_qkv, preferred_element_type=jnp.float32)
    mixed = (
        projected * taps[:, 0]
        + shift_down(projected, 1) * taps[:, 1]
        + shift_down(projected, 2) * taps[:, 2]
    ).astype(jnp.bfloat16)
    query = mixed[:, :width].reshape(seq_length, HEADS, HD)
    keys = mixed[:, width : 2 * width].reshape(seq_length, HEADS, HD)
    values = mixed[:, 2 * width :].reshape(seq_length, HEADS, HD)
    rows_block = min(512, seq_length)
    block_index = 0
    start_row = block_index * rows_block
    scores, allowed = scores_block(query, keys, start_row, seq_live)
    masked = jnp.where(allowed, scores, -1e30)
    top_score = jnp.max(masked, axis=-1, keepdims=True)
    exp_terms = jnp.exp(masked - top_score)
    row_totals = jnp.sum(exp_terms, axis=-1, keepdims=True)
    probs_low = (exp_terms / row_totals).astype(jnp.bfloat16)
    out_parts = jnp.einsum("hqk,khd->qhd", probs_low, values, preferred_element_type=jnp.float32)
    lse_parts = [top_score + jnp.log(row_totals)]
    attended_low = out_parts.reshape(seq_length, width).astype(jnp.bfloat16)
    branch_attn = jnp.dot(attended_low, full_out, preferred_element_type=jnp.float32)
    residual = tokens_in + branch_attn
    hat_two, inv_two = norm_parts(residual)
    normed_two = (hat_two * gain_second).astype(jnp.bfloat16)
    grad_out = jnp.where(live_rows[:, None], cotangent[0], jnp.zeros_like(cotangent[0]))
    row_set = lax.all_gather(normed_two[None], "wide", axis=0, tiled=True).reshape(-1, width)
    pre_act = jnp.dot(row_set, w_in, preferred_element_type=jnp.float32)
    activ = jnp.square(jax.nn.relu(pre_act)).astype(jnp.bfloat16)
    piece = activ
    branch_ffn = lax.psum_scatter(
        jnp.dot(piece, w_fc2, preferred_element_type=jnp.float32).astype(jnp.bfloat16),
        "wide",
        scatter_dimension=0,
        tiled=True,
    ).astype(jnp.float32)
    grad_set = lax.all_gather(grad_out[None], "wide", axis=0, tiled=True).reshape(-1, width)
    grad_act = contract_last(grad_set, w_fc2)
    grad_fc2_part = contract_first(activ, grad_set)
    grad_pre = (grad_act * 2.0 * jax.nn.relu(pre_act)).astype(jnp.bfloat16)
    grad_in_part = contract_first(row_set, grad_pre)
    piece = grad_pre
    grad_normed_two = lax.psum_scatter(
        contract_last(piece, w_in).astype(jnp.bfloat16), "wide", scatter_dimension=0, tiled=True
    ).astype(jnp.float32)
    grad_w_in, grad_w_fc2 = (
        lax.psum_scatter(
            grad_in_part.astype(jnp.bfloat16), "batch", scatter_dimension=0, tiled=True
        ).astype(jnp.float32),
        lax.psum_scatter(
            grad_fc2_part.astype(jnp.bfloat16), "batch", scatter_dimension=1, tiled=True
        ).astype(jnp.float32),
    )
    output = jnp.where(live_rows[:, None], residual + branch_ffn, 0.0).astype(jnp.bfloat16)[None]
    grad_ln_two, grad_gain_second = norm_back(grad_normed_two, gain_second, hat_two, inv_two)
    grad_residual = grad_out.astype(jnp.float32) + grad_ln_two
    grad_branch = grad_residual.astype(jnp.bfloat16)
    grad_w_out_part = contract_first(attended_low, grad_branch)
    grad_attended = contract_last(grad_branch, full_out).astype(jnp.bfloat16)
    grad_att_heads = grad_attended.reshape(seq_length, HEADS, HD)
    delta_all = jnp.sum(grad_att_heads.astype(jnp.float32) * out_parts, axis=-1)
    block_index = 0
    start_row = block_index * rows_block
    scores, allowed = scores_block(query, keys, start_row, seq_live)
    probs_full = jnp.where(allowed, jnp.exp(scores - lse_parts[block_index]), 0.0)
    probs_low = probs_full.astype(jnp.bfloat16)
    grad_probs = jnp.einsum(
        "qhd,khd->hqk", grad_att_heads, values, preferred_element_type=jnp.float32
    )
    delta_block = jnp.transpose(delta_all)[:, :, None]
    grad_scores = (probs_full * (grad_probs - delta_block)).astype(jnp.bfloat16)
    grad_query_parts = 0.125 * jnp.einsum(
        "hqk,khd->qhd", grad_scores, keys, preferred_element_type=jnp.float32
    )
    grad_keys = 0.125 * jnp.einsum(
        "hqk,qhd->khd", grad_scores, query, preferred_element_type=jnp.float32
    )
    grad_values = jnp.einsum(
        "hqk,qhd->khd", probs_low, grad_att_heads, preferred_element_type=jnp.float32
    )
    grad_mixed = jnp.concatenate(
        [
            grad_query_parts.reshape(seq_length, width),
            grad_keys.reshape(seq_length, width),
            grad_values.reshape(seq_length, width),
        ],
        axis=1,
    )
    grad_taps_part = jnp.stack(
        [
            jnp.sum(grad_mixed * projected, axis=0),
            jnp.sum(grad_mixed * shift_down(projected, 1), axis=0),
            jnp.sum(grad_mixed * shift_down(projected, 2), axis=0),
        ],
        axis=1,
    )
    grad_projected = (
        grad_mixed * taps[:, 0]
        + shift_up(grad_mixed, 1) * taps[:, 1]
        + shift_up(grad_mixed, 2) * taps[:, 2]
    ).astype(jnp.bfloat16)
    grad_qkv_part = contract_first(normed_one, grad_projected)
    grad_normed_one = contract_last(grad_projected, full_qkv)
    grad_ln_one, grad_gain_first = norm_back(grad_normed_one, gain_first, hat_one, inv_one)
    grad_inputs = (grad_residual + grad_ln_one).astype(jnp.bfloat16)[None]
    grad_w_qkv, grad_w_out, grad_conv_taps, grad_gain_one, grad_gain_two = (
        lax.psum_scatter(grad_qkv_part, ("batch", "wide"), scatter_dimension=0, tiled=True),
        lax.psum_scatter(grad_w_out_part, ("batch", "wide"), scatter_dimension=0, tiled=True),
        lax.psum_scatter(grad_taps_part, ("batch", "wide"), scatter_dimension=0, tiled=True),
        lax.psum_scatter(grad_gain_first, ("batch", "wide"), scatter_dimension=0, tiled=True),
        lax.psum_scatter(grad_gain_second, ("batch", "wide"), scatter_dimension=0, tiled=True),
    )
    return (
        output,
        grad_inputs,
        grad_w_qkv,
        grad_w_out,
        grad_conv_taps,
        grad_gain_one,
        grad_gain_two,
        grad_w_in,
        grad_w_fc2,
    )


BF = jnp.bfloat16
F32 = jnp.float32
AXES = ("batch", "wide")
LANES = 256
PART = 128
VMEM_MIB = {"ffn": 36}


def fits(mesh, args):
    inputs, w_qkv, w_in = args[0], args[3], args[8]
    count = mesh.shape["batch"] * mesh.shape["wide"]
    return (
        mesh.shape["batch"] == 4
        and mesh.shape["wide"] == 8
        and inputs.shape[0] == count
        and inputs.shape[1] % LANES == 0
        and w_qkv.shape[0] % (count * 8) == 0
        and w_qkv.shape[0] % LANES == 0
        and w_qkv.shape[0] // HEADS == HD
        and w_in.shape[1] == 8 * 3 * PART
        and (w_in.shape[0] // 4) % 16 == 0
    )


def dot(left, right, left_dim, right_dim):
    return lax.dot_general(
        left, right, (((left_dim,), (right_dim,)), ((), ())), preferred_element_type=F32
    )


def flip_pairs(rule):
    return [(i, i ^ rule(i)) for i in range(32)]


def send(array, rule):
    return lax.ppermute(array, AXES, flip_pairs(rule))


def over_core(i):
    return 8


def over_first(i):
    return 16 if i & 8 else 1


def over_second(i):
    return 1 if i & 8 else 16


def over_z(step):
    return lambda i: 2 * step


def tie(value, *others):
    return lax.optimization_barrier((value,) + others)[0]


def join(parts):
    return jnp.concatenate(parts)


def added(keep, come):
    return (keep.astype(F32) + come.astype(F32)).astype(BF)


def halved(keep, come):
    half = keep.shape[0] // 2
    return added(keep[:half], come[:half]), added(keep[half:], come[half:])


def place_of(me, other):
    apart = me ^ other
    x_bit, z_bits = apart & 1, (apart & 2) | ((apart >> 2) & 1)
    core_bit, y_bit = (apart >> 3) & 1, (apart >> 4) & 1
    on_first = ((other >> 3) & 1) == 0
    high = jnp.where(on_first, y_bit, x_bit)
    low = jnp.where(on_first, x_bit, y_bit)
    return core_bit * 16 + high * 8 + low * 4 + z_bits


def call(kernel, grid, in_specs, out_specs, out_shape, scratch=(), busy=1, name=None, aliases=None):
    return pl.pallas_call(
        kernel,
        grid_spec=pltpu.PrefetchScalarGridSpec(
            num_scalar_prefetch=1,
            grid=grid,
            in_specs=in_specs,
            out_specs=out_specs,
            scratch_shapes=list(scratch),
        ),
        out_shape=out_shape,
        compiler_params=pltpu.CompilerParams(
            dimension_semantics=("arbitrary",) * len(grid), vmem_limit_bytes=VMEM_MIB.get(name, 20) * 1024 * 1024
        ),
        cost_estimate=pl.CostEstimate(flops=int(busy * 1.15e9), bytes_accessed=0, transcendentals=0),
        name=name,
        input_output_aliases=aliases or {},
    )


def whole(shape):
    zeros = (0,) * len(shape)
    return pl.BlockSpec(shape, lambda *_: zeros, pipeline_mode=pl.Buffered(1))


def hat_of(values_in):
    centered = values_in - jnp.mean(values_in, axis=-1, keepdims=True)
    inv_std = lax.rsqrt(jnp.mean(centered * centered, axis=-1, keepdims=True) + epsilon)
    return centered * inv_std, inv_std


def turned(value):
    return jnp.transpose(value.astype(F32)).astype(BF)


def prepare_kernel(meta, cot_ref, go_ref, got_ref):
    live = lax.broadcasted_iota(jnp.int32, (cot_ref.shape[0], 1), 0) < meta[33]
    value = jnp.where(live, cot_ref[...].astype(F32), 0.0)
    go_ref[...] = value.astype(BF)
    got_ref[...] = jnp.transpose(value).astype(BF)


def pack_kernel(meta, up_ref, down_ref, out_ref, a_ref, b_ref):
    half = up_ref.shape[0] // 2
    second_half, second_core = (meta[32] >> 1) == 1, (meta[32] & 1) == 1
    up = jnp.where(second_half, up_ref[half:, :], up_ref[:half, :])
    down = turned(jnp.where(second_half, down_ref[:, half:], down_ref[:, :half]))
    for i, part in enumerate((up, down)):
        a_ref[0, i * half : (i + 1) * half, :] = jnp.where(second_core, part[:, PART : 2 * PART], part[:, :PART])
    left, right = swap_halves(up[:, 2 * PART :], down[:, 2 * PART :])
    b_ref[0, :half, :] = jnp.where(second_core, right, left).astype(BF)
    rows = out_ref.shape[0]
    for c in range(out_ref.shape[1] // PART):
        b_ref[0, half + c * rows : half + (c + 1) * rows, :] = out_ref[:, c * PART : (c + 1) * PART]


def block_of(meta, i, own_ref, other_ref):
    place = meta[i]
    return jnp.where(place < 16, own_ref[place & 15], other_ref[place & 15])


def project_kernel(
    meta, x_ref, own_ref, other_ref, few_own_ref, few_other_ref,
    proj_ref, mixed_ref, wn_ref, nt_ref, taps_ref, gains_ref, normed,
):
    rows = own_ref.shape[1]
    step = pl.program_id(0)

    def few_of(device, lanes):
        block = block_of(meta, device, few_own_ref, few_other_ref)[:8].astype(F32)
        return jnp.concatenate([block, jnp.zeros((8, lanes - PART), F32)], axis=1)

    @pl.when(step == 0)
    def _():
        width = gains_ref.shape[1]
        lane = lax.broadcasted_iota(jnp.int32, (8, width), 1)
        gains = jnp.zeros((8, width), F32)
        for i in range(32):
            first = i * rows
            moved = pltpu.roll(few_of(i, width), first, 1)
            gains = jnp.where((lane >= first) & (lane < first + rows), moved, gains)
        gains_ref[...] = gains
        hat, _ = hat_of(x_ref[...].astype(F32))
        low = (hat * gains[3:4, :]).astype(BF)
        normed[...] = low
        flipped = turned(low)
        for i in range(32):
            nt_ref[meta[i]] = flipped[i * rows : (i + 1) * rows]

    channels = 3 * rows
    lane = lax.broadcasted_iota(jnp.int32, (8, LANES), 1)
    taps = jnp.zeros((8, LANES), F32)
    for i in range(LANES // channels + 2):
        device = jnp.minimum((step * LANES) // channels + i, 31)
        first = device * channels - step * LANES
        moved = pltpu.roll(few_of(device, LANES), (first + 2 * LANES) & (LANES - 1), 1)
        taps = jnp.where((lane >= first) & (lane < first + channels), moved, taps)
    taps_ref[...] = taps
    for i in range(32):
        wn_ref[i * rows : (i + 1) * rows, :] = block_of(meta, i, own_ref, other_ref)
    value = dot(normed[...], wn_ref[...], 1, 0)
    at = lax.broadcasted_iota(jnp.int32, value.shape, 0)
    one = jnp.where(at >= 1, pltpu.roll(value, 1, 0), 0.0)
    two = jnp.where(at >= 2, pltpu.roll(value, 2, 0), 0.0)
    mixed = value * taps[0:1, :] + one * taps[1:2, :] + two * taps[2:3, :]
    proj_ref[...] = value.astype(BF)
    mixed_ref[...] = mixed.astype(BF)


def head_row(head, scale=1.0):
    lane = lax.broadcasted_iota(jnp.int32, (1, LANES), 1)
    return jnp.where(lane // HD == head, scale, 0.0).astype(BF)


def allowed_in(meta, keys, first_query, queries):
    key = lax.broadcasted_iota(jnp.int32, (keys, queries), 0)
    query = first_query + lax.broadcasted_iota(jnp.int32, (1, queries), 1)
    return key < jnp.minimum(query + 1, meta[33])


def attend_kernel(meta, q_ref, k_ref, v_ref, out_ref, lse_ref, flipped):
    seq = q_ref.shape[0]
    tile = LANES
    values_t = turned(v_ref[...])
    keys = k_ref[...]
    for t in range(seq // tile):
        upto = (t + 1) * tile
        allowed = allowed_in(meta, upto, t * tile, tile)
        query = q_ref[t * tile : upto, :]
        for head in range(LANES // HD):
            scores = dot(keys[:upto], query * head_row(head, 0.125), 1, 1)
            scores = jnp.where(allowed, scores, -1e30)
            top = jnp.max(scores, axis=0, keepdims=True)
            terms = jnp.exp(scores - top)
            total = jnp.sum(terms, axis=0, keepdims=True)
            probs = (terms * (1.0 / total)).astype(BF)
            flipped[head * HD : (head + 1) * HD, t * tile : upto] = dot(
                values_t[head * HD : (head + 1) * HD, :upto], probs, 1, 0
            )
            lse_ref[0, head : head + 1, t * tile : upto] = top + jnp.log(total)
    out_ref[...] = jnp.transpose(flipped[...]).astype(BF)


def mend_kernel(meta, att_ref, own_ref, other_ref, x_ref, gain_ref, res_ref, n2_ref, n2t_ref, at_ref, wn_ref):
    flipped = turned(att_ref[...])
    rows = at_ref.shape[1]
    for i in range(32):
        at_ref[meta[i]] = flipped[i * rows : (i + 1) * rows]
        block = block_of(meta, i, own_ref, other_ref)
        for c in range(wn_ref.shape[1] // PART):
            wn_ref[i * rows : (i + 1) * rows, c * PART : (c + 1) * PART] = block[c * rows : (c + 1) * rows]
    residual = x_ref[...].astype(F32) + dot(att_ref[...], wn_ref[...], 1, 0)
    res_ref[...] = residual
    hat, _ = hat_of(residual)
    low = (hat * gain_ref[4:5, :]).astype(BF)
    n2_ref[...] = low
    n2t_ref[...] = turned(low)


def swap_halves(left, right):
    left, right = left.astype(F32), right.astype(F32)
    low = lax.broadcasted_iota(jnp.int32, (1, PART), 1) < PART // 2
    return (
        jnp.where(low, left, pltpu.roll(right, PART // 2, 1)),
        jnp.where(low, pltpu.roll(left, PART // 2, 1), right),
    )


def ffn_kernel(packed, meta, *refs):
    token_refs, refs = (refs[:4], refs[4:8]), refs[8:]
    count = 8 if packed else 4
    tiles, refs = refs[:count], refs[count:]
    if packed:
        branch_ref, grad_ref, branch_acc, grad_acc, low_ref, high_ref = refs
    else:
        sums_in, (branch_ref, grad_ref, both_ref, low_ref, high_ref, branch_acc, grad_acc) = refs[:4], refs[4:]
    sums = (branch_ref, grad_ref, branch_acc, grad_acc)
    step = pl.program_id(0)

    @pl.when(step == 0)
    def _():
        for i, ref in enumerate(sums):
            ref[...] = jnp.zeros_like(ref) if packed else sums_in[i][...]

    half = tiles[0].shape[1] if packed else tiles[0].shape[1] // 2
    if packed:
        blocks = [jnp.concatenate([tiles[2 * k][0], tiles[2 * k + 1][0]], axis=0) for k in range(4)]
        pairs = [swap_halves(blocks[0], blocks[1]), swap_halves(blocks[2], blocks[3])]
        w_up, w_down = (jnp.concatenate([pairs[0][i], pairs[1][i]], axis=1).astype(BF) for i in range(2))
    else:
        w_up, w_down = (
            jnp.concatenate(
                [
                    jnp.concatenate([tiles[2 * k + b][0, i * half : (i + 1) * half, :] for b in range(2)], axis=0)
                    for k in range(2)
                ],
                axis=1,
            )
            for i in range(2)
        )
    up_sum = down_sum = 0.0
    for i, (n2_ref, go_ref, n2t_ref, got_ref) in enumerate(token_refs):
        pre = jnp.maximum(dot(n2_ref[...], w_up, 1, 0), 0.0)
        activ = (pre * pre).astype(BF)
        grad_pre = (dot(go_ref[...], w_down, 1, 0) * 2.0 * pre).astype(BF)
        sums[2 * i][...] += dot(activ, w_down, 1, 1)
        sums[2 * i + 1][...] += dot(grad_pre, w_up, 1, 1)
        up_sum += dot(n2t_ref[...], grad_pre, 1, 0)
        down_sum += dot(got_ref[...], activ, 1, 0)
    first_wide = step * (4 if packed else 2)
    results = []
    for k in range(2):
        lanes = slice(k * PART, (k + 1) * PART)
        if packed:
            results += [(part,) for part in swap_halves(up_sum[:, lanes], down_sum[:, lanes])]
        else:
            results.append((up_sum[:, lanes], down_sum[:, lanes]))
    for k, parts in enumerate(results):
        for b in range(2):
            place = meta[b * 16 + (meta[32] & 1) * 8 + first_wide + k]
            for is_high, target in enumerate((low_ref, high_ref)):

                @pl.when((place >> 3) == is_high)
                def _(place=place, target=target, parts=parts, b=b):
                    for i, part in enumerate(parts):
                        target[place & 7, i * half : (i + 1) * half, :] = part[b * half : (b + 1) * half].astype(BF)

    if not packed:

        @pl.when(step == pl.num_programs(0) - 1)
        def _():
            seq = branch_acc.shape[0]
            both_ref[:seq, :] = branch_acc[...].astype(BF)
            both_ref[seq:, :] = grad_acc[...].astype(BF)


def turn_kernel(meta, grad_ref, branch_ref, come_ref, res_ref, gain_ref, go_ref, at_ref, wn_ref, out_ref, gres_ref, gatt_ref, ggain_ref, keep_ref, away_ref):
    residual = res_ref[...]
    seq = residual.shape[0]
    live = lax.broadcasted_iota(jnp.int32, (seq, 1), 0) < meta[33]
    branch = branch_ref[...] + come_ref[:seq, :].astype(F32)
    out_ref[...] = jnp.where(live, residual + branch, 0.0).astype(BF)
    hat, inv_std = hat_of(residual)
    grad = grad_ref[...] + come_ref[seq:, :].astype(F32)
    ggain_ref[...] = jnp.sum(grad * hat, axis=0, keepdims=True)
    scaled = grad * gain_ref[4:5, :]
    mean_first = jnp.mean(scaled, axis=-1, keepdims=True)
    mean_second = jnp.mean(scaled * hat, axis=-1, keepdims=True)
    grad_res = go_ref[...].astype(F32) + inv_std * (scaled - mean_first - hat * mean_second)
    gres_ref[...] = grad_res
    low = grad_res.astype(BF)
    gatt_ref[...] = dot(low, wn_ref[...], 1, 1).astype(BF)
    result = dot(at_ref[...], low, 1, 0)
    lanes = keep_ref.shape[2]
    chunks = result.shape[1] // lanes
    rows = keep_ref.shape[1] // chunks
    for i in range(32):
        target = away_ref if i >= 16 else keep_ref
        for c in range(chunks):
            target[i & 15, c * rows : (c + 1) * rows, :] = result[
                i * rows : (i + 1) * rows, c * lanes : (c + 1) * lanes
            ].astype(BF)


def attend_back_kernel(
    meta, q_ref, k_ref, v_ref, pq_ref, pk_ref, pv_ref, tq_ref, tk_ref, tv_ref, go_ref, out_ref, lse_ref,
    gq_ref, gk_ref, gv_ref, dtq_ref, dtk_ref, dtv_ref, flipped,
):
    seq = q_ref.shape[0]
    tile = LANES
    keys, values = k_ref[...], v_ref[...]
    keys_t = turned(keys)
    delta_t = jnp.transpose(go_ref[...].astype(F32) * out_ref[...].astype(F32))
    grad_keys = [jnp.zeros((tile, LANES), F32) for _ in range(seq // tile)]
    grad_values = list(grad_keys)
    for t in range(seq // tile):
        upto = (t + 1) * tile
        allowed = allowed_in(meta, upto, t * tile, tile)
        query, grad = q_ref[t * tile : upto, :], go_ref[t * tile : upto, :]
        for head in range(LANES // HD):
            lanes = slice(head * HD, (head + 1) * HD)
            query_h, grad_h = query * head_row(head, 0.125), grad * head_row(head)
            delta = jnp.sum(delta_t[lanes, t * tile : upto], axis=0, keepdims=True)
            scores = dot(keys[:upto], query_h, 1, 1)
            lse = lse_ref[0, head : head + 1, t * tile : upto]
            probs = jnp.where(allowed, jnp.exp(scores - lse), 0.0)
            grad_scores = (probs * (dot(values[:upto], grad_h, 1, 1) - delta)).astype(BF)
            flipped[lanes, t * tile : upto] = dot(keys_t[lanes, :upto], grad_scores, 1, 0) * 0.125
            add_values = dot(probs.astype(BF), grad_h, 1, 0)
            add_keys = dot(grad_scores, query_h, 1, 0)
            for s in range(t + 1):
                rows = slice(s * tile, (s + 1) * tile)
                grad_values[s] += add_values[rows]
                grad_keys[s] += add_keys[rows]
    mixed = (
        jnp.transpose(flipped[...]),
        jnp.concatenate(grad_keys, axis=0),
        jnp.concatenate(grad_values, axis=0),
    )
    at = lax.broadcasted_iota(jnp.int32, (seq, LANES), 0)
    for grad, proj_ref, taps_ref, g_ref, dt_ref in zip(
        mixed, (pq_ref, pk_ref, pv_ref), (tq_ref, tk_ref, tv_ref), (gq_ref, gk_ref, gv_ref), (dtq_ref, dtk_ref, dtv_ref)
    ):
        one = jnp.where(at < seq - 1, pltpu.roll(grad, seq - 1, 0), 0.0)
        two = jnp.where(at < seq - 2, pltpu.roll(grad, seq - 2, 0), 0.0)
        g_ref[...] = (grad * taps_ref[0:1, :] + one * taps_ref[1:2, :] + two * taps_ref[2:3, :]).astype(BF)
        proj = proj_ref[...].astype(F32)
        for tap, part in enumerate((grad, one, two)):
            dt_ref[tap : tap + 1, :] = jnp.sum(part * proj, axis=0, keepdims=True)


def weight_kernel(with_few, meta, nt_ref, *refs):
    if with_few:
        (*tap_refs, gain_ref), refs, few = refs[:7], refs[7:-1], refs[-1]
    keep_ref, away_ref = refs[-2:]
    half, full = keep_ref.shape
    start = 0
    for g_ref in refs[:-2]:
        result = dot(nt_ref[...], g_ref[...], 1, 0).astype(BF)
        columns = slice(start, start + g_ref.shape[1])
        start += g_ref.shape[1]
        keep_ref[:, columns] = result[:half]
        away_ref[:, columns] = result[half:]
    if with_few:
        rows = half // 16
        row = lax.broadcasted_iota(jnp.int32, (8, PART), 0)
        lane = lax.broadcasted_iota(jnp.int32, (8, PART), 1)
        taps = jnp.concatenate([ref[...] for ref in tap_refs], axis=1)
        gains = jnp.broadcast_to(gain_ref[...], (8, gain_ref.shape[1]))

        def taken(values_in, first):
            start = first // PART * PART
            window = values_in[:, start : start + 2 * PART]
            return pltpu.roll(window, (start - first) % window.shape[1], 1)[:, :PART]

        for i in range(32):
            piece = jnp.where((row == 3) & (lane < rows), taken(gains, i * rows), 0.0)
            few[meta[i]] = jnp.where((row < 3) & (lane < 3 * rows), taken(taps, i * 3 * rows), piece)
        for i, ref in enumerate((keep_ref, away_ref)):
            ref[:, full - PART :] = jnp.zeros((half, PART), BF)
            for k in range(16):
                ref[k * rows : k * rows + 8, full - PART :] = few[i * 16 + k].astype(BF)


def last_kernel(meta, *refs):
    grads, (w_ref, x_ref, gain_ref, gres_ref, gin_ref) = refs[:-5], refs[-5:]
    grad = dot(jnp.concatenate([g_ref[...] for g_ref in grads], axis=1), w_ref[...], 1, 1)
    hat, inv_std = hat_of(x_ref[...].astype(F32))
    scaled = grad * gain_ref[3:4, :]
    mean_first = jnp.mean(scaled, axis=-1, keepdims=True)
    mean_second = jnp.mean(scaled * hat, axis=-1, keepdims=True)
    back = inv_std * (scaled - mean_first - hat * mean_second)
    gin_ref[...] = (gres_ref[...] + back).astype(BF)


def own_sequence(inputs, lengths, cotangent, w_qkv, w_out, conv_taps, gain_one, gain_two, w_in, w_fc2):
    seq, width = inputs.shape[1], inputs.shape[2]
    rows, wide = w_qkv.shape
    half = width // 2
    tap_rows = conv_taps.shape[0]
    batch = lax.axis_index("batch")
    core = batch & 1
    me = batch * 8 + lax.axis_index("wide")
    number = jnp.arange(64, dtype=jnp.int32)
    meta = jnp.where(number < 32, place_of(me, number & 31), jnp.where(number == 32, batch, lengths[0]))
    x, cot = inputs[0], cotangent[0]
    shape = jax.ShapeDtypeStruct
    row_spec = whole((1, width))
    gain_spec = whole((8, width))
    token = whole((seq, width))
    token_t = whole((width, seq))
    groups = width // LANES

    few_rows = [jnp.pad(conv_taps.T, ((0, 0), (0, PART - tap_rows)))]
    few_rows += [jnp.pad(gain[None], ((0, 0), (0, PART - rows))) for gain in (gain_one, gain_two)]
    few_rows = jnp.concatenate(few_rows + [jnp.zeros((rows - 5, PART), BF)])
    qkv_block = jnp.concatenate([w_qkv, few_rows], axis=1)[None]
    qkv_block, meta, first_core = lax.optimization_barrier((qkv_block, meta, core == 0))
    qkv_far = send(qkv_block, over_z(2))
    out_rows = rows * (width // PART)
    a_block, b_block = call(
        pack_kernel, (1,), [whole(w.shape) for w in (w_in, w_fc2, w_out)],
        [whole((1, width, PART)), whole((1, half + out_rows, PART))],
        [shape((1, width, PART), BF), shape((1, half + out_rows, PART), BF)], busy=2, name="pack",
    )(meta, w_in, w_fc2, w_out)

    b_far = send(tie(b_block, qkv_far), over_z(2))
    qkv2 = join([qkv_block, tie(qkv_far, b_block)])
    qkv_near = send(qkv2, over_z(1))
    qkv4 = join([qkv2, qkv_near])
    qkv_first = send(qkv4, over_first)
    b2 = join([b_block, tie(b_far, qkv4)])
    b_near = send(b2, over_z(1))
    a_far = send(tie(a_block, b2), over_z(2))
    qkv8 = join([qkv4, tie(qkv_first, b2)])
    qkv_second = send(qkv8, over_second)
    grad_out, grad_out_t = call(
        prepare_kernel, (1,), [token], [token, token_t],
        [shape((seq, width), BF), shape((width, seq), BF)], busy=1, name="prepare",
    )(meta, tie(cot, qkv_far))
    go_other = send(grad_out, over_core)
    got_other = send(grad_out_t, over_core)
    b4 = join([b2, tie(b_near, qkv8)])
    a2 = join([a_block, tie(a_far, qkv8)])
    a_near = send(a2, over_z(1))
    qkv16 = join([qkv8, tie(qkv_second, a2, b4)])
    qkv_core = send(qkv16, over_core)
    b_first = send(tie(b4, qkv16), over_first)
    a4 = join([a2, tie(a_near, qkv_core)])
    a_first = send(a4, over_first)

    lane_block = pl.BlockSpec((seq, LANES), lambda j, m: (0, j))
    half_block = pl.BlockSpec((16, rows, LANES), lambda j, m: (0, 0, j))
    few_block = pl.BlockSpec((16, rows, PART), lambda j, m: (0, 0, wide // PART))
    tap_block = pl.BlockSpec((8, LANES), lambda j, m: (0, j))
    projected, mixed, qkv_full, normed_t, taps, gains = call(
        project_kernel, (wide // LANES,),
        [token, half_block, half_block, few_block, few_block],
        [lane_block, lane_block, pl.BlockSpec((width, LANES), lambda j, m: (0, j)), whole((32, rows, seq)),
         tap_block, gain_spec],
        [shape((seq, wide), BF), shape((seq, wide), BF), shape((width, wide), BF), shape((32, rows, seq), BF),
         shape((8, wide), F32), shape((8, width), F32)],
        [pltpu.VMEM((seq, width), BF)], busy=7, name="project",
    )(meta, tie(x, a4), qkv16, qkv_core, qkv16, qkv_core)

    b8 = join([b4, tie(b_first, mixed)])
    b_second = send(b8, over_second)
    part_specs = [pl.BlockSpec((seq, LANES), lambda j, m, p=p: (0, p * groups + j)) for p in range(3)]
    lse_spec = pl.BlockSpec((1, 8, seq), lambda j, m: (j, 0, 0))
    a8 = join([a4, tie(a_first, mixed)])
    ready = tie(mixed, b8, a8, go_other, got_other)
    attended, lse = call(
        attend_kernel, (groups,), part_specs, [lane_block, lse_spec],
        [shape((seq, width), BF), shape((groups, 8, seq), F32)], [pltpu.VMEM((LANES, seq), F32)],
        busy=9, name="attend",
    )(meta, ready, ready, ready)

    b16 = join([b8, tie(b_second, attended)])
    out16 = b16[:, half:, :]
    out_core = send(out16, over_core)
    a_second = send(tie(a8, b16), over_second)
    residual, normed_two, normed_two_t, attended_t, out_full = call(
        mend_kernel, (1,),
        [token, whole(out16.shape), whole(out16.shape), token, gain_spec],
        [token, token, token_t, whole((32, rows, seq)), whole((width, width))],
        [shape((seq, width), F32), shape((seq, width), BF), shape((width, seq), BF), shape((32, rows, seq), BF),
         shape((width, width), BF)],
        busy=2.5, name="mend",
    )(meta, attended, out16, out_core, x, gains)
    n2_other = send(normed_two, over_core)
    n2t_other = send(normed_two_t, over_core)

    sequences = [normed_two, grad_out, normed_two_t, grad_out_t, n2_other, go_other, n2t_other, got_other]
    sequence_specs = [token, token, token_t, token_t] * 2

    def tile(block_rows, per_step, k, b):
        return pl.BlockSpec(
            (1, block_rows, PART), lambda s, m: (m[b * 16 + (m[32] & 1) * 8 + s * per_step + k], 0, 0)
        )

    total = shape((seq, width), F32)
    grads_b = shape((8, half, PART), BF)
    branch, grad_two, branch_o, grad_o, b_low, b_high = call(
        functools.partial(ffn_kernel, True), (2,),
        sequence_specs + [tile(half, 4, k, b) for k in range(4) for b in range(2)],
        [token] * 4 + [whole(grads_b.shape)] * 2, [total] * 4 + [grads_b] * 2, busy=2, name="ffn",
    )(meta, *sequences, *[b16] * 8)
    a16 = join([a8, tie(a_second, branch)])
    b_sum = send(b_high, over_second)
    grads_a = shape((8, width, PART), BF)
    branch, grad_two, both, a_low, a_high = call(
        functools.partial(ffn_kernel, False), (4,),
        sequence_specs + [tile(width, 2, k, b) for k in range(2) for b in range(2)] + [token] * 4,
        [token] * 2 + [whole((2 * seq, width))] + [whole(grads_a.shape)] * 2,
        [total] * 2 + [shape((2 * seq, width), BF)] + [grads_a] * 2,
        [pltpu.VMEM((seq, width), F32)] * 2, busy=15, name="ffn",
    )(meta, tie(normed_two, b_high), *sequences[1:], *[a16] * 4, branch, grad_two, branch_o, grad_o)
    b_sum = tie(b_sum, branch)
    come = send(tie(both, b_sum), over_core)
    a_sum = send(a_high, over_second)
    b_keep, b_go = halved(b_low, b_sum)
    half_out = shape((16, rows * (width // PART), PART), BF)
    output, grad_residual, grad_attended, grad_gain_second, keep_out, away_out = call(
        turn_kernel, (1,),
        [token] * 2 + [whole((2 * seq, width)), token, gain_spec, token, token_t, whole((width, width))],
        [token] * 3 + [row_spec, whole(half_out.shape), whole(half_out.shape)],
        [shape((seq, width), BF), shape((seq, width), F32), shape((seq, width), BF), shape((1, width), F32),
         half_out, half_out],
        busy=4, name="turn",
    )(meta, tie(grad_two, a_high, b_go), branch, come, residual, gains, grad_out, attended_t.reshape(width, seq), out_full)

    def attend_back(first, count, wait_for):
        def lanes(height, part, start):
            return pl.BlockSpec((height, LANES), lambda i, m: (0, part * groups + start + i))

        specs = [lanes(seq, p, first) for p in range(3)]
        tap_specs = [lanes(8, p, first) for p in range(3)]
        return call(
            attend_back_kernel, (count,),
            specs * 2 + tap_specs + [specs[0]] * 2 + [pl.BlockSpec((1, 8, seq), lambda i, m: (first + i, 0, 0))],
            [lanes(seq, 0, 0)] * 3 + [lanes(8, 0, 0)] * 3,
            [shape((seq, count * LANES), BF)] * 3 + [shape((8, count * LANES), F32)] * 3,
            [pltpu.VMEM((LANES, seq), F32)], busy=count, name="attend_back",
        )(meta, mixed, mixed, mixed, projected, projected, projected, taps, taps, taps,
          tie(grad_attended, *wait_for), attended, lse)

    def weights(grads, few, wait_for):
        size = sum(g.shape[1] for g in grads) + (PART if few else 0)
        spec = whole((half, size))
        keep, away = call(
            functools.partial(weight_kernel, bool(few)), (1,),
            [token_t] + [whole(part.shape) for part in [*few, *grads]],
            [spec, spec], [shape((half, size), BF)] * 2, [pltpu.VMEM((32, 8, PART), F32)] if few else (),
            busy=1, name="weight",
        )(meta, tie(normed_t.reshape(width, seq), *wait_for), *few, *grads)
        return keep.reshape(16, rows, size), away.reshape(16, rows, size)

    out_come = send(away_out, over_core)
    back0 = attend_back(0, groups - 1, (away_out,))

    out_sum = added(keep_out, tie(out_come, back0[0]))
    out_go = out_sum[8:]
    out_come = send(out_go, over_second)
    x_keep, x_away = weights(back0[:3], [], (out_go,))
    x_sum = send(x_away, over_core)
    a_keep, a_go = halved(a_low, tie(a_sum, x_away))
    a_sum = send(a_go, over_first)
    back2 = attend_back(groups - 1, 1, (back0[0], x_away, a_go))
    backs = (back0, back2)
    grad_projected = [back[part] for part in range(3) for back in backs]
    few = [back[3 + part] for part in range(3) for back in backs] + [grad_gain_second]
    y_keep, y_away = weights(back2[:3], few, ())
    y_sum = send(y_away, over_core)

    out_keep, out_go = halved(out_sum[:8], tie(out_come, y_away))
    b_keep = jnp.concatenate([b_keep, out_keep], axis=1)
    b_go = jnp.concatenate([b_go, out_go], axis=1)
    b_sum = send(b_go, over_first)
    grad_inputs = call(
        last_kernel, (1,),
        [whole(g.shape) for g in grad_projected] + [whole((width, wide)), token, gain_spec, token],
        [token], [shape((seq, width), BF)], busy=4, name="last",
    )(meta, *grad_projected, qkv_full, x, gains, tie(grad_residual, y_away, a_go, b_go))[0]
    x_keep, x_go = halved(x_keep, tie(x_sum, grad_inputs))
    x_sum = send(x_go, over_second)
    y_keep, y_go = halved(y_keep, tie(y_sum, x_go))
    y_sum = send(y_go, over_second)
    a_keep, a_go = halved(a_keep, tie(a_sum, y_go))
    a_sum = send(a_go, over_z(1))
    b_keep, b_go = halved(b_keep, tie(b_sum, a_go))
    b_sum = send(b_go, over_z(1))
    x_keep, x_go = halved(x_keep, tie(x_sum, b_go))
    x_sum = send(x_go, over_first)
    y_keep, y_go = halved(y_keep, tie(y_sum, x_go))
    y_sum = send(y_go, over_first)
    a_keep, a_go = halved(a_keep, tie(a_sum, y_go))
    a_sum = send(a_go, over_z(2))
    b_keep, b_go = halved(b_keep, tie(b_sum, a_go))
    b_sum = send(b_go, over_z(2))
    x_keep, x_go = halved(x_keep, tie(x_sum, b_go))
    x_sum = send(x_go, over_z(1))
    y_keep, y_go = halved(y_keep, tie(y_sum, x_go))
    y_sum = send(y_go, over_z(1))
    grad_a = a_keep[0].astype(F32) + tie(a_sum, y_go)[0].astype(F32)
    grad_b = b_keep[0].astype(F32) + tie(b_sum, y_go)[0].astype(F32)
    grad_out_w = jnp.transpose(grad_b[half:].reshape(width // PART, rows, PART), (1, 0, 2)).reshape(rows, width)
    quarter = width // 4

    def share(swapped):
        pairs = [
            (g[first : first + quarter], g[first + quarter : first + 2 * quarter])
            for g, first in ((grad_a, 0), (grad_a, half), (grad_b, 0))
        ]
        return jnp.concatenate([jnp.where(first_core, p[swapped], p[1 - swapped]) for p in pairs])

    mine = share(0)
    theirs = send(share(1), over_core)
    mine, theirs = jnp.where(first_core, mine, theirs), jnp.where(first_core, theirs, mine)
    units = PART // 2
    grad_in_w, grad_fc2_w = (
        jnp.concatenate(
            [part[i * quarter : (i + 1) * quarter] for part in (mine, theirs)]
            + [part[2 * quarter :, i * units : (i + 1) * units] for part in (mine, theirs)],
            axis=1,
        )
        for i in range(2)
    )

    x_keep, x_go = halved(x_keep, tie(x_sum, grad_a, grad_b))
    x_sum = send(x_go, over_z(2))
    y_keep, y_go = halved(y_keep, tie(y_sum, x_go))
    y_sum = send(y_go, over_z(2))
    x_total = x_keep[0].astype(F32) + x_sum[0].astype(F32)
    y_total = y_keep[0].astype(F32) + y_sum[0].astype(F32)
    few = y_total[:8, 3 * LANES :]
    grad_qkv = jnp.concatenate(
        [
            part
            for i in range(3)
            for part in (x_total[:, 2 * i * LANES : 2 * (i + 1) * LANES], y_total[:, i * LANES : (i + 1) * LANES])
        ],
        axis=1,
    )
    grad_gain_first = jnp.sum(grad_qkv * w_qkv.astype(F32), axis=1) / gain_one.astype(F32)
    return (
        output[None],
        grad_inputs[None],
        grad_qkv,
        grad_out_w,
        few[:3, :tap_rows].T,
        grad_gain_first,
        few[3, :rows],
        grad_in_w,
        jnp.transpose(grad_fc2_w),
    )


def solution(mesh):
    fast = functools.partial(own_sequence)

    def program(*args):
        body = fast if fits(mesh, args) else shards
        return jax.shard_map(
            body,
            mesh=mesh,
            in_specs=(
                P(("batch", "wide"), None, None),
                P(("batch", "wide")),
                P(("batch", "wide"), None, None),
                P(("batch", "wide"), None),
                P(("batch", "wide"), None),
                P(("batch", "wide"), None),
                P(("batch", "wide")),
                P(("batch", "wide")),
                P(None, "wide"),
                P("wide", None),
            ),
            out_specs=(
                P(("batch", "wide"), None, None),
                P(("batch", "wide"), None, None),
                P(("batch", "wide"), None),
                P(("batch", "wide"), None),
                P(("batch", "wide"), None),
                P(("batch", "wide")),
                P(("batch", "wide")),
                P("batch", "wide"),
                P("wide", "batch"),
            ),
            check_vma=False,
        )(*args)

    return program
```

```python
import functools
import jax
import jax.numpy as jnp
from jax import lax
from jax.experimental import pallas as pl
from jax.experimental.pallas import tpu as pltpu
from jax.sharding import PartitionSpec as P

HEADS = 12
HD = 64


epsilon = 1e-05


def contract_first(left, right):
    return lax.dot_general(
        left, right, (((0,), (0,)), ((), ())), preferred_element_type=jnp.float32
    )


def contract_last(left, right):
    return lax.dot_general(
        left, right, (((1,), (1,)), ((), ())), preferred_element_type=jnp.float32
    )


def norm_parts(values_in):
    centered = values_in - jnp.mean(values_in, axis=-1, keepdims=True)
    inv_std = lax.rsqrt(jnp.mean(centered * centered, axis=-1, keepdims=True) + epsilon)
    return (centered * inv_std, inv_std)


def norm_back(grad_normed, gain_vec, normed_hat, inv_std):
    grad_hat = grad_normed * gain_vec
    mean_first = jnp.mean(grad_hat, axis=-1, keepdims=True)
    mean_second = jnp.mean(grad_hat * normed_hat, axis=-1, keepdims=True)
    grad_value = inv_std * (grad_hat - mean_first - normed_hat * mean_second)
    return (grad_value, jnp.sum(grad_normed * normed_hat, axis=0))


def shift_down(signal, steps):
    filler = jnp.zeros((steps, signal.shape[1]), signal.dtype)
    return jnp.concatenate([filler, signal[:-steps]], axis=0)


def shift_up(signal, steps):
    filler = jnp.zeros((steps, signal.shape[1]), signal.dtype)
    return jnp.concatenate([signal[steps:], filler], axis=0)


def scores_block(query_block, keys, start_row, seq_live):
    rows_block = query_block.shape[0]
    scores = (
        jnp.einsum("qhd,khd->hqk", query_block, keys, preferred_element_type=jnp.float32) * 0.125
    )
    query_pos = start_row + jnp.arange(rows_block)
    key_pos = jnp.arange(keys.shape[0])
    allowed = (key_pos[None, :] <= query_pos[:, None]) & (key_pos[None, :] < seq_live)
    return (scores, allowed[None])


def shards(inputs, lengths, cotangent, w_qkv, w_out, conv_taps, gain_one, gain_two, w_in, w_fc2):
    full_qkv, full_out, full_taps, full_gain_one, full_gain_two = (
        lax.all_gather(w_qkv, ("batch", "wide"), axis=0, tiled=True),
        lax.all_gather(w_out, ("batch", "wide"), axis=0, tiled=True),
        lax.all_gather(conv_taps, ("batch", "wide"), axis=0, tiled=True),
        lax.all_gather(gain_one, ("batch", "wide"), axis=0, tiled=True),
        lax.all_gather(gain_two, ("batch", "wide"), axis=0, tiled=True),
    )
    seq_length, width = (inputs.shape[1], inputs.shape[2])
    tokens_in = inputs[0].astype(jnp.float32)
    seq_live = lengths[0]
    live_rows = jnp.arange(seq_length) < seq_live
    taps = full_taps.astype(jnp.float32)
    gain_first = full_gain_one.astype(jnp.float32)
    gain_second = full_gain_two.astype(jnp.float32)
    hat_one, inv_one = norm_parts(tokens_in)
    normed_one = (hat_one * gain_first).astype(jnp.bfloat16)
    projected = jnp.dot(normed_one, full_qkv, preferred_element_type=jnp.float32)
    mixed = (
        projected * taps[:, 0]
        + shift_down(projected, 1) * taps[:, 1]
        + shift_down(projected, 2) * taps[:, 2]
    ).astype(jnp.bfloat16)
    query = mixed[:, :width].reshape(seq_length, HEADS, HD)
    keys = mixed[:, width : 2 * width].reshape(seq_length, HEADS, HD)
    values = mixed[:, 2 * width :].reshape(seq_length, HEADS, HD)
    rows_block = min(512, seq_length)
    block_index = 0
    start_row = block_index * rows_block
    scores, allowed = scores_block(query, keys, start_row, seq_live)
    masked = jnp.where(allowed, scores, -1e30)
    top_score = jnp.max(masked, axis=-1, keepdims=True)
    exp_terms = jnp.exp(masked - top_score)
    row_totals = jnp.sum(exp_terms, axis=-1, keepdims=True)
    probs_low = (exp_terms / row_totals).astype(jnp.bfloat16)
    out_parts = jnp.einsum("hqk,khd->qhd", probs_low, values, preferred_element_type=jnp.float32)
    lse_parts = [top_score + jnp.log(row_totals)]
    attended_low = out_parts.reshape(seq_length, width).astype(jnp.bfloat16)
    branch_attn = jnp.dot(attended_low, full_out, preferred_element_type=jnp.float32)
    residual = tokens_in + branch_attn
    hat_two, inv_two = norm_parts(residual)
    normed_two = (hat_two * gain_second).astype(jnp.bfloat16)
    grad_out = jnp.where(live_rows[:, None], cotangent[0], jnp.zeros_like(cotangent[0]))
    row_set = lax.all_gather(normed_two[None], "wide", axis=0, tiled=True).reshape(-1, width)
    pre_act = jnp.dot(row_set, w_in, preferred_element_type=jnp.float32)
    activ = jnp.square(jax.nn.relu(pre_act)).astype(jnp.bfloat16)
    piece = activ
    branch_ffn = lax.psum_scatter(
        jnp.dot(piece, w_fc2, preferred_element_type=jnp.float32).astype(jnp.bfloat16),
        "wide",
        scatter_dimension=0,
        tiled=True,
    ).astype(jnp.float32)
    grad_set = lax.all_gather(grad_out[None], "wide", axis=0, tiled=True).reshape(-1, width)
    grad_act = contract_last(grad_set, w_fc2)
    grad_fc2_part = contract_first(activ, grad_set)
    grad_pre = (grad_act * 2.0 * jax.nn.relu(pre_act)).astype(jnp.bfloat16)
    grad_in_part = contract_first(row_set, grad_pre)
    piece = grad_pre
    grad_normed_two = lax.psum_scatter(
        contract_last(piece, w_in).astype(jnp.bfloat16), "wide", scatter_dimension=0, tiled=True
    ).astype(jnp.float32)
    grad_w_in, grad_w_fc2 = (
        lax.psum_scatter(
            grad_in_part.astype(jnp.bfloat16), "batch", scatter_dimension=0, tiled=True
        ).astype(jnp.float32),
        lax.psum_scatter(
            grad_fc2_part.astype(jnp.bfloat16), "batch", scatter_dimension=1, tiled=True
        ).astype(jnp.float32),
    )
    output = jnp.where(live_rows[:, None], residual + branch_ffn, 0.0).astype(jnp.bfloat16)[None]
    grad_ln_two, grad_gain_second = norm_back(grad_normed_two, gain_second, hat_two, inv_two)
    grad_residual = grad_out.astype(jnp.float32) + grad_ln_two
    grad_branch = grad_residual.astype(jnp.bfloat16)
    grad_w_out_part = contract_first(attended_low, grad_branch)
    grad_attended = contract_last(grad_branch, full_out).astype(jnp.bfloat16)
    grad_att_heads = grad_attended.reshape(seq_length, HEADS, HD)
    delta_all = jnp.sum(grad_att_heads.astype(jnp.float32) * out_parts, axis=-1)
    block_index = 0
    start_row = block_index * rows_block
    scores, allowed = scores_block(query, keys, start_row, seq_live)
    probs_full = jnp.where(allowed, jnp.exp(scores - lse_parts[block_index]), 0.0)
    probs_low = probs_full.astype(jnp.bfloat16)
    grad_probs = jnp.einsum(
        "qhd,khd->hqk", grad_att_heads, values, preferred_element_type=jnp.float32
    )
    delta_block = jnp.transpose(delta_all)[:, :, None]
    grad_scores = (probs_full * (grad_probs - delta_block)).astype(jnp.bfloat16)
    grad_query_parts = 0.125 * jnp.einsum(
        "hqk,khd->qhd", grad_scores, keys, preferred_element_type=jnp.float32
    )
    grad_keys = 0.125 * jnp.einsum(
        "hqk,qhd->khd", grad_scores, query, preferred_element_type=jnp.float32
    )
    grad_values = jnp.einsum(
        "hqk,qhd->khd", probs_low, grad_att_heads, preferred_element_type=jnp.float32
    )
    grad_mixed = jnp.concatenate(
        [
            grad_query_parts.reshape(seq_length, width),
            grad_keys.reshape(seq_length, width),
            grad_values.reshape(seq_length, width),
        ],
        axis=1,
    )
    grad_taps_part = jnp.stack(
        [
            jnp.sum(grad_mixed * projected, axis=0),
            jnp.sum(grad_mixed * shift_down(projected, 1), axis=0),
            jnp.sum(grad_mixed * shift_down(projected, 2), axis=0),
        ],
        axis=1,
    )
    grad_projected = (
        grad_mixed * taps[:, 0]
        + shift_up(grad_mixed, 1) * taps[:, 1]
        + shift_up(grad_mixed, 2) * taps[:, 2]
    ).astype(jnp.bfloat16)
    grad_qkv_part = contract_first(normed_one, grad_projected)
    grad_normed_one = contract_last(grad_projected, full_qkv)
    grad_ln_one, grad_gain_first = norm_back(grad_normed_one, gain_first, hat_one, inv_one)
    grad_inputs = (grad_residual + grad_ln_one).astype(jnp.bfloat16)[None]
    grad_w_qkv, grad_w_out, grad_conv_taps, grad_gain_one, grad_gain_two = (
        lax.psum_scatter(grad_qkv_part, ("batch", "wide"), scatter_dimension=0, tiled=True),
        lax.psum_scatter(grad_w_out_part, ("batch", "wide"), scatter_dimension=0, tiled=True),
        lax.psum_scatter(grad_taps_part, ("batch", "wide"), scatter_dimension=0, tiled=True),
        lax.psum_scatter(grad_gain_first, ("batch", "wide"), scatter_dimension=0, tiled=True),
        lax.psum_scatter(grad_gain_second, ("batch", "wide"), scatter_dimension=0, tiled=True),
    )
    return (
        output,
        grad_inputs,
        grad_w_qkv,
        grad_w_out,
        grad_conv_taps,
        grad_gain_one,
        grad_gain_two,
        grad_w_in,
        grad_w_fc2,
    )


BF = jnp.bfloat16
F32 = jnp.float32
AXES = ("batch", "wide")
LANES = 256
PART = 128
VMEM_MIB = {"ffn": 36}


def fits(mesh, args):
    inputs, w_qkv, w_in = args[0], args[3], args[8]
    count = mesh.shape["batch"] * mesh.shape["wide"]
    return (
        mesh.shape["batch"] == 4
        and mesh.shape["wide"] == 8
        and inputs.shape[0] == count
        and inputs.shape[1] % LANES == 0
        and w_qkv.shape[0] % (count * 8) == 0
        and w_qkv.shape[0] % LANES == 0
        and w_qkv.shape[0] // HEADS == HD
        and w_in.shape[1] == 8 * 3 * PART
        and (w_in.shape[0] // 4) % 16 == 0
    )


def dot(left, right, left_dim, right_dim):
    return lax.dot_general(
        left, right, (((left_dim,), (right_dim,)), ((), ())), preferred_element_type=F32
    )


def flip_pairs(rule):
    return [(i, i ^ rule(i)) for i in range(32)]


def send(array, rule):
    return lax.ppermute(array, AXES, flip_pairs(rule))


def over_core(i):
    return 8


def over_first(i):
    return 16 if i & 8 else 1


def over_second(i):
    return 1 if i & 8 else 16


def over_z(step):
    return lambda i: 2 * step


def tie(value, *others):
    return lax.optimization_barrier((value,) + others)[0]


def join(parts):
    return jnp.concatenate(parts)


def added(keep, come):
    return (keep.astype(F32) + come.astype(F32)).astype(BF)


def halved(keep, come):
    half = keep.shape[0] // 2
    return added(keep[:half], come[:half]), added(keep[half:], come[half:])


def place_of(me, other):
    apart = me ^ other
    x_bit, z_bits = apart & 1, (apart & 2) | ((apart >> 2) & 1)
    core_bit, y_bit = (apart >> 3) & 1, (apart >> 4) & 1
    on_first = ((other >> 3) & 1) == 0
    high = jnp.where(on_first, y_bit, x_bit)
    low = jnp.where(on_first, x_bit, y_bit)
    return core_bit * 16 + high * 8 + low * 4 + z_bits


def call(kernel, grid, in_specs, out_specs, out_shape, scratch=(), busy=1, name=None, aliases=None):
    return pl.pallas_call(
        kernel,
        grid_spec=pltpu.PrefetchScalarGridSpec(
            num_scalar_prefetch=1,
            grid=grid,
            in_specs=in_specs,
            out_specs=out_specs,
            scratch_shapes=list(scratch),
        ),
        out_shape=out_shape,
        compiler_params=pltpu.CompilerParams(
            dimension_semantics=("arbitrary",) * len(grid), vmem_limit_bytes=VMEM_MIB.get(name, 20) * 1024 * 1024
        ),
        cost_estimate=pl.CostEstimate(flops=int(busy * 1.15e9), bytes_accessed=0, transcendentals=0),
        name=name,
        input_output_aliases=aliases or {},
    )


def whole(shape):
    zeros = (0,) * len(shape)
    return pl.BlockSpec(shape, lambda *_: zeros, pipeline_mode=pl.Buffered(1))


def hat_of(values_in):
    centered = values_in - jnp.mean(values_in, axis=-1, keepdims=True)
    inv_std = lax.rsqrt(jnp.mean(centered * centered, axis=-1, keepdims=True) + epsilon)
    return centered * inv_std, inv_std


def turned(value):
    return jnp.transpose(value.astype(F32)).astype(BF)


def prepare_kernel(meta, cot_ref, go_ref, got_ref):
    live = lax.broadcasted_iota(jnp.int32, (cot_ref.shape[0], 1), 0) < meta[33]
    value = jnp.where(live, cot_ref[...].astype(F32), 0.0)
    go_ref[...] = value.astype(BF)
    got_ref[...] = jnp.transpose(value).astype(BF)


def pack_kernel(meta, up_ref, down_ref, out_ref, a_ref, b_ref):
    half = up_ref.shape[0] // 2
    second_half, second_core = (meta[32] >> 1) == 1, (meta[32] & 1) == 1
    up = jnp.where(second_half, up_ref[half:, :], up_ref[:half, :])
    down = turned(jnp.where(second_half, down_ref[:, half:], down_ref[:, :half]))
    for i, part in enumerate((up, down)):
        a_ref[0, i * half : (i + 1) * half, :] = jnp.where(second_core, part[:, PART : 2 * PART], part[:, :PART])
    left, right = swap_halves(up[:, 2 * PART :], down[:, 2 * PART :])
    b_ref[0, :half, :] = jnp.where(second_core, right, left).astype(BF)
    rows = out_ref.shape[0]
    for c in range(out_ref.shape[1] // PART):
        b_ref[0, half + c * rows : half + (c + 1) * rows, :] = out_ref[:, c * PART : (c + 1) * PART]


def block_of(meta, i, own_ref, other_ref):
    place = meta[i]
    return jnp.where(place < 16, own_ref[place & 15], other_ref[place & 15])


def project_kernel(
    meta, x_ref, own_ref, other_ref, few_own_ref, few_other_ref,
    proj_ref, mixed_ref, wn_ref, nt_ref, taps_ref, gains_ref, normed,
):
    rows = own_ref.shape[1]
    step = pl.program_id(0)

    def few_of(device, lanes):
        block = block_of(meta, device, few_own_ref, few_other_ref)[:8].astype(F32)
        return jnp.concatenate([block, jnp.zeros((8, lanes - PART), F32)], axis=1)

    @pl.when(step == 0)
    def _():
        width = gains_ref.shape[1]
        lane = lax.broadcasted_iota(jnp.int32, (8, width), 1)
        gains = jnp.zeros((8, width), F32)
        for i in range(32):
            first = i * rows
            moved = pltpu.roll(few_of(i, width), first, 1)
            gains = jnp.where((lane >= first) & (lane < first + rows), moved, gains)
        gains_ref[...] = gains
        hat, _ = hat_of(x_ref[...].astype(F32))
        low = (hat * gains[3:4, :]).astype(BF)
        normed[...] = low
        flipped = turned(low)
        for i in range(32):
            nt_ref[meta[i]] = flipped[i * rows : (i + 1) * rows]

    channels = 3 * rows
    lane = lax.broadcasted_iota(jnp.int32, (8, LANES), 1)
    taps = jnp.zeros((8, LANES), F32)
    for i in range(LANES // channels + 2):
        device = jnp.minimum((step * LANES) // channels + i, 31)
        first = device * channels - step * LANES
        moved = pltpu.roll(few_of(device, LANES), (first + 2 * LANES) & (LANES - 1), 1)
        taps = jnp.where((lane >= first) & (lane < first + channels), moved, taps)
    taps_ref[...] = taps
    for i in range(32):
        wn_ref[i * rows : (i + 1) * rows, :] = block_of(meta, i, own_ref, other_ref)
    value = dot(normed[...], wn_ref[...], 1, 0)
    at = lax.broadcasted_iota(jnp.int32, value.shape, 0)
    one = jnp.where(at >= 1, pltpu.roll(value, 1, 0), 0.0)
    two = jnp.where(at >= 2, pltpu.roll(value, 2, 0), 0.0)
    mixed = value * taps[0:1, :] + one * taps[1:2, :] + two * taps[2:3, :]
    proj_ref[...] = value.astype(BF)
    mixed_ref[...] = mixed.astype(BF)


def head_row(head, scale=1.0):
    lane = lax.broadcasted_iota(jnp.int32, (1, LANES), 1)
    return jnp.where(lane // HD == head, scale, 0.0).astype(BF)


def allowed_in(meta, keys, first_query, queries):
    key = lax.broadcasted_iota(jnp.int32, (keys, queries), 0)
    query = first_query + lax.broadcasted_iota(jnp.int32, (1, queries), 1)
    return key < jnp.minimum(query + 1, meta[33])


def attend_kernel(meta, q_ref, k_ref, v_ref, out_ref, lse_ref, flipped):
    seq = q_ref.shape[0]
    tile = LANES
    values_t = turned(v_ref[...])
    keys = k_ref[...]
    for t in range(seq // tile):
        upto = (t + 1) * tile
        allowed = allowed_in(meta, upto, t * tile, tile)
        query = q_ref[t * tile : upto, :]
        for head in range(LANES // HD):
            scores = dot(keys[:upto], query * head_row(head, 0.125), 1, 1)
            scores = jnp.where(allowed, scores, -1e30)
            top = jnp.max(scores, axis=0, keepdims=True)
            terms = jnp.exp(scores - top)
            total = jnp.sum(terms, axis=0, keepdims=True)
            probs = (terms * (1.0 / total)).astype(BF)
            flipped[head * HD : (head + 1) * HD, t * tile : upto] = dot(
                values_t[head * HD : (head + 1) * HD, :upto], probs, 1, 0
            )
            lse_ref[0, head : head + 1, t * tile : upto] = top + jnp.log(total)
    out_ref[...] = jnp.transpose(flipped[...]).astype(BF)


def mend_kernel(meta, att_ref, own_ref, other_ref, x_ref, gain_ref, res_ref, n2_ref, n2t_ref, at_ref, wn_ref):
    flipped = turned(att_ref[...])
    rows = at_ref.shape[1]
    for i in range(32):
        at_ref[meta[i]] = flipped[i * rows : (i + 1) * rows]
        block = block_of(meta, i, own_ref, other_ref)
        for c in range(wn_ref.shape[1] // PART):
            wn_ref[i * rows : (i + 1) * rows, c * PART : (c + 1) * PART] = block[c * rows : (c + 1) * rows]
    residual = x_ref[...].astype(F32) + dot(att_ref[...], wn_ref[...], 1, 0)
    res_ref[...] = residual
    hat, _ = hat_of(residual)
    low = (hat * gain_ref[4:5, :]).astype(BF)
    n2_ref[...] = low
    n2t_ref[...] = turned(low)


def swap_halves(left, right):
    left, right = left.astype(F32), right.astype(F32)
    low = lax.broadcasted_iota(jnp.int32, (1, PART), 1) < PART // 2
    return (
        jnp.where(low, left, pltpu.roll(right, PART // 2, 1)),
        jnp.where(low, pltpu.roll(left, PART // 2, 1), right),
    )


def ffn_kernel(packed, meta, *refs):
    token_refs, refs = (refs[:4], refs[4:8]), refs[8:]
    count = 8 if packed else 4
    tiles, refs = refs[:count], refs[count:]
    if packed:
        branch_ref, grad_ref, branch_acc, grad_acc, low_ref, high_ref = refs
    else:
        sums_in, (branch_ref, grad_ref, both_ref, low_ref, high_ref, branch_acc, grad_acc) = refs[:4], refs[4:]
    sums = (branch_ref, grad_ref, branch_acc, grad_acc)
    step = pl.program_id(0)

    @pl.when(step == 0)
    def _():
        for i, ref in enumerate(sums):
            ref[...] = jnp.zeros_like(ref) if packed else sums_in[i][...]

    half = tiles[0].shape[1] if packed else tiles[0].shape[1] // 2
    if packed:
        blocks = [jnp.concatenate([tiles[2 * k][0], tiles[2 * k + 1][0]], axis=0) for k in range(4)]
        pairs = [swap_halves(blocks[0], blocks[1]), swap_halves(blocks[2], blocks[3])]
        w_up, w_down = (jnp.concatenate([pairs[0][i], pairs[1][i]], axis=1).astype(BF) for i in range(2))
    else:
        w_up, w_down = (
            jnp.concatenate(
                [
                    jnp.concatenate([tiles[2 * k + b][0, i * half : (i + 1) * half, :] for b in range(2)], axis=0)
                    for k in range(2)
                ],
                axis=1,
            )
            for i in range(2)
        )
    up_sum = down_sum = 0.0
    for i, (n2_ref, go_ref, n2t_ref, got_ref) in enumerate(token_refs):
        pre = jnp.maximum(dot(n2_ref[...], w_up, 1, 0), 0.0)
        activ = (pre * pre).astype(BF)
        grad_pre = (dot(go_ref[...], w_down, 1, 0) * 2.0 * pre).astype(BF)
        sums[2 * i][...] += dot(activ, w_down, 1, 1)
        sums[2 * i + 1][...] += dot(grad_pre, w_up, 1, 1)
        up_sum += dot(n2t_ref[...], grad_pre, 1, 0)
        down_sum += dot(got_ref[...], activ, 1, 0)
    first_wide = step * (4 if packed else 2)
    results = []
    for k in range(2):
        lanes = slice(k * PART, (k + 1) * PART)
        if packed:
            results += [(part,) for part in swap_halves(up_sum[:, lanes], down_sum[:, lanes])]
        else:
            results.append((up_sum[:, lanes], down_sum[:, lanes]))
    for k, parts in enumerate(results):
        for b in range(2):
            place = meta[b * 16 + (meta[32] & 1) * 8 + first_wide + k]
            for is_high, target in enumerate((low_ref, high_ref)):

                @pl.when((place >> 3) == is_high)
                def _(place=place, target=target, parts=parts, b=b):
                    for i, part in enumerate(parts):
                        target[place & 7, i * half : (i + 1) * half, :] = part[b * half : (b + 1) * half].astype(BF)

    if not packed:

        @pl.when(step == pl.num_programs(0) - 1)
        def _():
            seq = branch_acc.shape[0]
            both_ref[:seq, :] = branch_acc[...].astype(BF)
            both_ref[seq:, :] = grad_acc[...].astype(BF)


def turn_kernel(meta, grad_ref, branch_ref, come_ref, res_ref, gain_ref, go_ref, at_ref, wn_ref, out_ref, gres_ref, gatt_ref, ggain_ref, keep_ref, away_ref):
    residual = res_ref[...]
    seq = residual.shape[0]
    live = lax.broadcasted_iota(jnp.int32, (seq, 1), 0) < meta[33]
    branch = branch_ref[...] + come_ref[:seq, :].astype(F32)
    out_ref[...] = jnp.where(live, residual + branch, 0.0).astype(BF)
    hat, inv_std = hat_of(residual)
    grad = grad_ref[...] + come_ref[seq:, :].astype(F32)
    ggain_ref[...] = jnp.sum(grad * hat, axis=0, keepdims=True)
    scaled = grad * gain_ref[4:5, :]
    mean_first = jnp.mean(scaled, axis=-1, keepdims=True)
    mean_second = jnp.mean(scaled * hat, axis=-1, keepdims=True)
    grad_res = go_ref[...].astype(F32) + inv_std * (scaled - mean_first - hat * mean_second)
    gres_ref[...] = grad_res
    low = grad_res.astype(BF)
    gatt_ref[...] = dot(low, wn_ref[...], 1, 1).astype(BF)
    result = dot(at_ref[...], low, 1, 0)
    lanes = keep_ref.shape[2]
    chunks = result.shape[1] // lanes
    rows = keep_ref.shape[1] // chunks
    for i in range(32):
        target = away_ref if i >= 16 else keep_ref
        for c in range(chunks):
            target[i & 15, c * rows : (c + 1) * rows, :] = result[
                i * rows : (i + 1) * rows, c * lanes : (c + 1) * lanes
            ].astype(BF)


def attend_back_kernel(
    meta, q_ref, k_ref, v_ref, pq_ref, pk_ref, pv_ref, tq_ref, tk_ref, tv_ref, go_ref, out_ref, lse_ref,
    gq_ref, gk_ref, gv_ref, dtq_ref, dtk_ref, dtv_ref, flipped,
):
    seq = q_ref.shape[0]
    tile = LANES
    keys, values = k_ref[...], v_ref[...]
    keys_t = turned(keys)
    delta_t = jnp.transpose(go_ref[...].astype(F32) * out_ref[...].astype(F32))
    grad_keys = [jnp.zeros((tile, LANES), F32) for _ in range(seq // tile)]
    grad_values = list(grad_keys)
    for t in range(seq // tile):
        upto = (t + 1) * tile
        allowed = allowed_in(meta, upto, t * tile, tile)
        query, grad = q_ref[t * tile : upto, :], go_ref[t * tile : upto, :]
        for head in range(LANES // HD):
            lanes = slice(head * HD, (head + 1) * HD)
            query_h, grad_h = query * head_row(head, 0.125), grad * head_row(head)
            delta = jnp.sum(delta_t[lanes, t * tile : upto], axis=0, keepdims=True)
            scores = dot(keys[:upto], query_h, 1, 1)
            lse = lse_ref[0, head : head + 1, t * tile : upto]
            probs = jnp.where(allowed, jnp.exp(scores - lse), 0.0)
            grad_scores = (probs * (dot(values[:upto], grad_h, 1, 1) - delta)).astype(BF)
            flipped[lanes, t * tile : upto] = dot(keys_t[lanes, :upto], grad_scores, 1, 0) * 0.125
            add_values = dot(probs.astype(BF), grad_h, 1, 0)
            add_keys = dot(grad_scores, query_h, 1, 0)
            for s in range(t + 1):
                rows = slice(s * tile, (s + 1) * tile)
                grad_values[s] += add_values[rows]
                grad_keys[s] += add_keys[rows]
    mixed = (
        jnp.transpose(flipped[...]),
        jnp.concatenate(grad_keys, axis=0),
        jnp.concatenate(grad_values, axis=0),
    )
    at = lax.broadcasted_iota(jnp.int32, (seq, LANES), 0)
    for grad, proj_ref, taps_ref, g_ref, dt_ref in zip(
        mixed, (pq_ref, pk_ref, pv_ref), (tq_ref, tk_ref, tv_ref), (gq_ref, gk_ref, gv_ref), (dtq_ref, dtk_ref, dtv_ref)
    ):
        one = jnp.where(at < seq - 1, pltpu.roll(grad, seq - 1, 0), 0.0)
        two = jnp.where(at < seq - 2, pltpu.roll(grad, seq - 2, 0), 0.0)
        g_ref[...] = (grad * taps_ref[0:1, :] + one * taps_ref[1:2, :] + two * taps_ref[2:3, :]).astype(BF)
        proj = proj_ref[...].astype(F32)
        for tap, part in enumerate((grad, one, two)):
            dt_ref[tap : tap + 1, :] = jnp.sum(part * proj, axis=0, keepdims=True)


def weight_kernel(with_few, meta, nt_ref, *refs):
    if with_few:
        (*tap_refs, gain_ref), refs, few = refs[:7], refs[7:-1], refs[-1]
    keep_ref, away_ref = refs[-2:]
    half, full = keep_ref.shape
    start = 0
    for g_ref in refs[:-2]:
        result = dot(nt_ref[...], g_ref[...], 1, 0).astype(BF)
        columns = slice(start, start + g_ref.shape[1])
        start += g_ref.shape[1]
        keep_ref[:, columns] = result[:half]
        away_ref[:, columns] = result[half:]
    if with_few:
        rows = half // 16
        row = lax.broadcasted_iota(jnp.int32, (8, PART), 0)
        lane = lax.broadcasted_iota(jnp.int32, (8, PART), 1)
        taps = jnp.concatenate([ref[...] for ref in tap_refs], axis=1)
        gains = jnp.broadcast_to(gain_ref[...], (8, gain_ref.shape[1]))

        def taken(values_in, first):
            start = first // PART * PART
            window = values_in[:, start : start + 2 * PART]
            return pltpu.roll(window, (start - first) % window.shape[1], 1)[:, :PART]

        for i in range(32):
            piece = jnp.where((row == 3) & (lane < rows), taken(gains, i * rows), 0.0)
            few[meta[i]] = jnp.where((row < 3) & (lane < 3 * rows), taken(taps, i * 3 * rows), piece)
        for i, ref in enumerate((keep_ref, away_ref)):
            ref[:, full - PART :] = jnp.zeros((half, PART), BF)
            for k in range(16):
                ref[k * rows : k * rows + 8, full - PART :] = few[i * 16 + k].astype(BF)


def last_kernel(meta, *refs):
    grads, (w_ref, x_ref, gain_ref, gres_ref, gin_ref) = refs[:-5], refs[-5:]
    grad = dot(jnp.concatenate([g_ref[...] for g_ref in grads], axis=1), w_ref[...], 1, 1)
    hat, inv_std = hat_of(x_ref[...].astype(F32))
    scaled = grad * gain_ref[3:4, :]
    mean_first = jnp.mean(scaled, axis=-1, keepdims=True)
    mean_second = jnp.mean(scaled * hat, axis=-1, keepdims=True)
    back = inv_std * (scaled - mean_first - hat * mean_second)
    gin_ref[...] = (gres_ref[...] + back).astype(BF)


def own_sequence(inputs, lengths, cotangent, w_qkv, w_out, conv_taps, gain_one, gain_two, w_in, w_fc2):
    seq, width = inputs.shape[1], inputs.shape[2]
    rows, wide = w_qkv.shape
    half = width // 2
    tap_rows = conv_taps.shape[0]
    batch = lax.axis_index("batch")
    core = batch & 1
    me = batch * 8 + lax.axis_index("wide")
    number = jnp.arange(64, dtype=jnp.int32)
    meta = jnp.where(number < 32, place_of(me, number & 31), jnp.where(number == 32, batch, lengths[0]))
    x, cot = inputs[0], cotangent[0]
    shape = jax.ShapeDtypeStruct
    row_spec = whole((1, width))
    gain_spec = whole((8, width))
    token = whole((seq, width))
    token_t = whole((width, seq))
    groups = width // LANES

    few_rows = [jnp.pad(conv_taps.T, ((0, 0), (0, PART - tap_rows)))]
    few_rows += [jnp.pad(gain[None], ((0, 0), (0, PART - rows))) for gain in (gain_one, gain_two)]
    few_rows = jnp.concatenate(few_rows + [jnp.zeros((rows - 5, PART), BF)])
    qkv_block = jnp.concatenate([w_qkv, few_rows], axis=1)[None]
    qkv_block, meta, first_core = lax.optimization_barrier((qkv_block, meta, core == 0))
    qkv_far = send(qkv_block, over_z(2))
    out_rows = rows * (width // PART)
    a_block, b_block = call(
        pack_kernel, (1,), [whole(w.shape) for w in (w_in, w_fc2, w_out)],
        [whole((1, width, PART)), whole((1, half + out_rows, PART))],
        [shape((1, width, PART), BF), shape((1, half + out_rows, PART), BF)], busy=2, name="pack",
    )(meta, w_in, w_fc2, w_out)

    b_far = send(tie(b_block, qkv_far), over_z(2))
    qkv2 = join([qkv_block, tie(qkv_far, b_block)])
    qkv_near = send(qkv2, over_z(1))
    qkv4 = join([qkv2, qkv_near])
    qkv_first = send(qkv4, over_first)
    b2 = join([b_block, tie(b_far, qkv4)])
    b_near = send(b2, over_z(1))
    a_far = send(tie(a_block, b2), over_z(2))
    qkv8 = join([qkv4, tie(qkv_first, b2)])
    qkv_second = send(qkv8, over_second)
    grad_out, grad_out_t = call(
        prepare_kernel, (1,), [token], [token, token_t],
        [shape((seq, width), BF), shape((width, seq), BF)], busy=1, name="prepare",
    )(meta, tie(cot, qkv_far))
    go_other = send(grad_out, over_core)
    got_other = send(grad_out_t, over_core)
    b4 = join([b2, tie(b_near, qkv8)])
    a2 = join([a_block, tie(a_far, qkv8)])
    a_near = send(a2, over_z(1))
    qkv16 = join([qkv8, tie(qkv_second, a2, b4)])
    qkv_core = send(qkv16, over_core)
    b_first = send(tie(b4, qkv16), over_first)
    a4 = join([a2, tie(a_near, qkv_core)])
    a_first = send(a4, over_first)

    lane_block = pl.BlockSpec((seq, LANES), lambda j, m: (0, j))
    half_block = pl.BlockSpec((16, rows, LANES), lambda j, m: (0, 0, j))
    few_block = pl.BlockSpec((16, rows, PART), lambda j, m: (0, 0, wide // PART))
    tap_block = pl.BlockSpec((8, LANES), lambda j, m: (0, j))
    projected, mixed, qkv_full, normed_t, taps, gains = call(
        project_kernel, (wide // LANES,),
        [token, half_block, half_block, few_block, few_block],
        [lane_block, lane_block, pl.BlockSpec((width, LANES), lambda j, m: (0, j)), whole((32, rows, seq)),
         tap_block, gain_spec],
        [shape((seq, wide), BF), shape((seq, wide), BF), shape((width, wide), BF), shape((32, rows, seq), BF),
         shape((8, wide), F32), shape((8, width), F32)],
        [pltpu.VMEM((seq, width), BF)], busy=7, name="project",
    )(meta, tie(x, a4), qkv16, qkv_core, qkv16, qkv_core)

    b8 = join([b4, tie(b_first, mixed)])
    b_second = send(b8, over_second)
    part_specs = [pl.BlockSpec((seq, LANES), lambda j, m, p=p: (0, p * groups + j)) for p in range(3)]
    lse_spec = pl.BlockSpec((1, 8, seq), lambda j, m: (j, 0, 0))
    a8 = join([a4, tie(a_first, mixed)])
    ready = tie(mixed, b8, a8, go_other, got_other)
    attended, lse = call(
        attend_kernel, (groups,), part_specs, [lane_block, lse_spec],
        [shape((seq, width), BF), shape((groups, 8, seq), F32)], [pltpu.VMEM((LANES, seq), F32)],
        busy=9, name="attend",
    )(meta, ready, ready, ready)

    b16 = join([b8, tie(b_second, attended)])
    out16 = b16[:, half:, :]
    out_core = send(out16, over_core)
    a_second = send(tie(a8, b16), over_second)
    residual, normed_two, normed_two_t, attended_t, out_full = call(
        mend_kernel, (1,),
        [token, whole(out16.shape), whole(out16.shape), token, gain_spec],
        [token, token, token_t, whole((32, rows, seq)), whole((width, width))],
        [shape((seq, width), F32), shape((seq, width), BF), shape((width, seq), BF), shape((32, rows, seq), BF),
         shape((width, width), BF)],
        busy=2.5, name="mend",
    )(meta, attended, out16, out_core, x, gains)
    n2_other = send(normed_two, over_core)
    n2t_other = send(normed_two_t, over_core)

    sequences = [normed_two, grad_out, normed_two_t, grad_out_t, n2_other, go_other, n2t_other, got_other]
    sequence_specs = [token, token, token_t, token_t] * 2

    def tile(block_rows, per_step, k, b):
        return pl.BlockSpec(
            (1, block_rows, PART), lambda s, m: (m[b * 16 + (m[32] & 1) * 8 + s * per_step + k], 0, 0)
        )

    total = shape((seq, width), F32)
    grads_b = shape((8, half, PART), BF)
    branch, grad_two, branch_o, grad_o, b_low, b_high = call(
        functools.partial(ffn_kernel, True), (2,),
        sequence_specs + [tile(half, 4, k, b) for k in range(4) for b in range(2)],
        [token] * 4 + [whole(grads_b.shape)] * 2, [total] * 4 + [grads_b] * 2, busy=2, name="ffn",
    )(meta, *sequences, *[b16] * 8)
    a16 = join([a8, tie(a_second, branch)])
    b_sum = send(b_high, over_second)
    grads_a = shape((8, width, PART), BF)
    branch, grad_two, both, a_low, a_high = call(
        functools.partial(ffn_kernel, False), (4,),
        sequence_specs + [tile(width, 2, k, b) for k in range(2) for b in range(2)] + [token] * 4,
        [token] * 2 + [whole((2 * seq, width))] + [whole(grads_a.shape)] * 2,
        [total] * 2 + [shape((2 * seq, width), BF)] + [grads_a] * 2,
        [pltpu.VMEM((seq, width), F32)] * 2, busy=15, name="ffn",
    )(meta, tie(normed_two, b_high), *sequences[1:], *[a16] * 4, branch, grad_two, branch_o, grad_o)
    b_sum = tie(b_sum, branch)
    come = send(tie(both, b_sum), over_core)
    a_sum = send(a_high, over_second)
    b_keep, b_go = halved(b_low, b_sum)
    half_out = shape((16, rows * (width // PART), PART), BF)
    output, grad_residual, grad_attended, grad_gain_second, keep_out, away_out = call(
        turn_kernel, (1,),
        [token] * 2 + [whole((2 * seq, width)), token, gain_spec, token, token_t, whole((width, width))],
        [token] * 3 + [row_spec, whole(half_out.shape), whole(half_out.shape)],
        [shape((seq, width), BF), shape((seq, width), F32), shape((seq, width), BF), shape((1, width), F32),
         half_out, half_out],
        busy=4, name="turn",
    )(meta, tie(grad_two, a_high, b_go), branch, come, residual, gains, grad_out, attended_t.reshape(width, seq), out_full)

    def attend_back(first, count, wait_for):
        def lanes(height, part, start):
            return pl.BlockSpec((height, LANES), lambda i, m: (0, part * groups + start + i))

        specs = [lanes(seq, p, first) for p in range(3)]
        tap_specs = [lanes(8, p, first) for p in range(3)]
        return call(
            attend_back_kernel, (count,),
            specs * 2 + tap_specs + [specs[0]] * 2 + [pl.BlockSpec((1, 8, seq), lambda i, m: (first + i, 0, 0))],
            [lanes(seq, 0, 0)] * 3 + [lanes(8, 0, 0)] * 3,
            [shape((seq, count * LANES), BF)] * 3 + [shape((8, count * LANES), F32)] * 3,
            [pltpu.VMEM((LANES, seq), F32)], busy=count, name="attend_back",
        )(meta, mixed, mixed, mixed, projected, projected, projected, taps, taps, taps,
          tie(grad_attended, *wait_for), attended, lse)

    def weights(grads, few, wait_for):
        size = sum(g.shape[1] for g in grads) + (PART if few else 0)
        spec = whole((half, size))
        keep, away = call(
            functools.partial(weight_kernel, bool(few)), (1,),
            [token_t] + [whole(part.shape) for part in [*few, *grads]],
            [spec, spec], [shape((half, size), BF)] * 2, [pltpu.VMEM((32, 8, PART), F32)] if few else (),
            busy=1, name="weight",
        )(meta, tie(normed_t.reshape(width, seq), *wait_for), *few, *grads)
        return keep.reshape(16, rows, size), away.reshape(16, rows, size)

    out_come = send(away_out, over_core)
    back0 = attend_back(0, groups - 1, (away_out,))

    out_sum = added(keep_out, tie(out_come, back0[0]))
    out_go = out_sum[8:]
    out_come = send(out_go, over_second)
    x_keep, x_away = weights(back0[:3], [], (out_go,))
    x_sum = send(x_away, over_core)
    a_keep, a_go = halved(a_low, tie(a_sum, x_away))
    a_sum = send(a_go, over_first)
    back2 = attend_back(groups - 1, 1, (back0[0], x_away, a_go))
    backs = (back0, back2)
    grad_projected = [back[part] for part in range(3) for back in backs]
    few = [back[3 + part] for part in range(3) for back in backs] + [grad_gain_second]
    y_keep, y_away = weights(back2[:3], few, ())
    y_sum = send(y_away, over_core)

    out_keep, out_go = halved(out_sum[:8], tie(out_come, y_away))
    b_keep = jnp.concatenate([b_keep, out_keep], axis=1)
    b_go = jnp.concatenate([b_go, out_go], axis=1)
    b_sum = send(b_go, over_first)
    x_keep, x_go = halved(x_keep, tie(x_sum, y_away))
    x_sum = send(x_go, over_second)
    a_keep, a_go = halved(a_keep, tie(a_sum, x_go))
    a_sum = send(a_go, over_z(1))
    grad_inputs = call(
        last_kernel, (1,),
        [whole(g.shape) for g in grad_projected] + [whole((width, wide)), token, gain_spec, token],
        [token], [shape((seq, width), BF)], busy=4, name="last",
    )(meta, *grad_projected, qkv_full, x, gains, tie(grad_residual, y_away, a_go, b_go, x_go))[0]
    y_keep, y_go = halved(y_keep, tie(y_sum, grad_inputs))
    y_sum = send(y_go, over_second)
    b_keep, b_go = halved(b_keep, tie(b_sum, y_go))
    b_sum = send(b_go, over_z(1))
    a_keep, a_go = halved(a_keep, tie(a_sum, b_go))
    a_sum = send(a_go, over_z(2))
    x_keep, x_go = halved(x_keep, tie(x_sum, a_go))
    x_sum = send(x_go, over_first)
    y_keep, y_go = halved(y_keep, tie(y_sum, x_go))
    y_sum = send(y_go, over_first)
    b_keep, b_go = halved(b_keep, tie(b_sum, y_go))
    b_sum = send(b_go, over_z(2))
    x_keep, x_go = halved(x_keep, tie(x_sum, b_go))
    x_sum = send(x_go, over_z(1))
    y_keep, y_go = halved(y_keep, tie(y_sum, x_go))
    y_sum = send(y_go, over_z(1))
    x_keep, x_go = halved(x_keep, tie(x_sum, y_go))
    x_sum = send(x_go, over_z(2))
    y_keep, y_go = halved(y_keep, tie(y_sum, x_go))
    y_sum = send(y_go, over_z(2))
    grad_a = a_keep[0].astype(F32) + tie(a_sum, y_go)[0].astype(F32)
    grad_b = b_keep[0].astype(F32) + tie(b_sum, y_go)[0].astype(F32)
    grad_out_w = jnp.transpose(grad_b[half:].reshape(width // PART, rows, PART), (1, 0, 2)).reshape(rows, width)
    quarter = width // 4

    def share(swapped):
        pairs = [
            (g[first : first + quarter], g[first + quarter : first + 2 * quarter])
            for g, first in ((grad_a, 0), (grad_a, half), (grad_b, 0))
        ]
        return jnp.concatenate([jnp.where(first_core, p[swapped], p[1 - swapped]) for p in pairs])

    mine = share(0)
    theirs = send(share(1), over_core)
    mine, theirs = jnp.where(first_core, mine, theirs), jnp.where(first_core, theirs, mine)
    units = PART // 2
    grad_in_w, grad_fc2_w = (
        jnp.concatenate(
            [part[i * quarter : (i + 1) * quarter] for part in (mine, theirs)]
            + [part[2 * quarter :, i * units : (i + 1) * units] for part in (mine, theirs)],
            axis=1,
        )
        for i in range(2)
    )

    x_total = x_keep[0].astype(F32) + x_sum[0].astype(F32)
    y_total = y_keep[0].astype(F32) + y_sum[0].astype(F32)
    few = y_total[:8, 3 * LANES :]
    grad_qkv = jnp.concatenate(
        [
            part
            for i in range(3)
            for part in (x_total[:, 2 * i * LANES : 2 * (i + 1) * LANES], y_total[:, i * LANES : (i + 1) * LANES])
        ],
        axis=1,
    )
    grad_gain_first = jnp.sum(grad_qkv * w_qkv.astype(F32), axis=1) / gain_one.astype(F32)
    return (
        output[None],
        grad_inputs[None],
        grad_qkv,
        grad_out_w,
        few[:3, :tap_rows].T,
        grad_gain_first,
        few[3, :rows],
        grad_in_w,
        jnp.transpose(grad_fc2_w),
    )


def solution(mesh):
    fast = functools.partial(own_sequence)

    def program(*args):
        body = fast if fits(mesh, args) else shards
        return jax.shard_map(
            body,
            mesh=mesh,
            in_specs=(
                P(("batch", "wide"), None, None),
                P(("batch", "wide")),
                P(("batch", "wide"), None, None),
                P(("batch", "wide"), None),
                P(("batch", "wide"), None),
                P(("batch", "wide"), None),
                P(("batch", "wide")),
                P(("batch", "wide")),
                P(None, "wide"),
                P("wide", None),
            ),
            out_specs=(
                P(("batch", "wide"), None, None),
                P(("batch", "wide"), None, None),
                P(("batch", "wide"), None),
                P(("batch", "wide"), None),
                P(("batch", "wide"), None),
                P(("batch", "wide")),
                P(("batch", "wide")),
                P("batch", "wide"),
                P("wide", "batch"),
            ),
            check_vma=False,
        )(*args)

    return program
```

```python
import functools
import jax
import jax.numpy as jnp
from jax import lax
from jax.experimental import pallas as pl
from jax.experimental.pallas import tpu as pltpu
from jax.sharding import PartitionSpec as P

HEADS = 12
HD = 64


epsilon = 1e-05


def contract_first(left, right):
    return lax.dot_general(
        left, right, (((0,), (0,)), ((), ())), preferred_element_type=jnp.float32
    )


def contract_last(left, right):
    return lax.dot_general(
        left, right, (((1,), (1,)), ((), ())), preferred_element_type=jnp.float32
    )


def norm_parts(values_in):
    centered = values_in - jnp.mean(values_in, axis=-1, keepdims=True)
    inv_std = lax.rsqrt(jnp.mean(centered * centered, axis=-1, keepdims=True) + epsilon)
    return (centered * inv_std, inv_std)


def norm_back(grad_normed, gain_vec, normed_hat, inv_std):
    grad_hat = grad_normed * gain_vec
    mean_first = jnp.mean(grad_hat, axis=-1, keepdims=True)
    mean_second = jnp.mean(grad_hat * normed_hat, axis=-1, keepdims=True)
    grad_value = inv_std * (grad_hat - mean_first - normed_hat * mean_second)
    return (grad_value, jnp.sum(grad_normed * normed_hat, axis=0))


def shift_down(signal, steps):
    filler = jnp.zeros((steps, signal.shape[1]), signal.dtype)
    return jnp.concatenate([filler, signal[:-steps]], axis=0)


def shift_up(signal, steps):
    filler = jnp.zeros((steps, signal.shape[1]), signal.dtype)
    return jnp.concatenate([signal[steps:], filler], axis=0)


def scores_block(query_block, keys, start_row, seq_live):
    rows_block = query_block.shape[0]
    scores = (
        jnp.einsum("qhd,khd->hqk", query_block, keys, preferred_element_type=jnp.float32) * 0.125
    )
    query_pos = start_row + jnp.arange(rows_block)
    key_pos = jnp.arange(keys.shape[0])
    allowed = (key_pos[None, :] <= query_pos[:, None]) & (key_pos[None, :] < seq_live)
    return (scores, allowed[None])


def shards(inputs, lengths, cotangent, w_qkv, w_out, conv_taps, gain_one, gain_two, w_in, w_fc2):
    full_qkv, full_out, full_taps, full_gain_one, full_gain_two = (
        lax.all_gather(w_qkv, ("batch", "wide"), axis=0, tiled=True),
        lax.all_gather(w_out, ("batch", "wide"), axis=0, tiled=True),
        lax.all_gather(conv_taps, ("batch", "wide"), axis=0, tiled=True),
        lax.all_gather(gain_one, ("batch", "wide"), axis=0, tiled=True),
        lax.all_gather(gain_two, ("batch", "wide"), axis=0, tiled=True),
    )
    seq_length, width = (inputs.shape[1], inputs.shape[2])
    tokens_in = inputs[0].astype(jnp.float32)
    seq_live = lengths[0]
    live_rows = jnp.arange(seq_length) < seq_live
    taps = full_taps.astype(jnp.float32)
    gain_first = full_gain_one.astype(jnp.float32)
    gain_second = full_gain_two.astype(jnp.float32)
    hat_one, inv_one = norm_parts(tokens_in)
    normed_one = (hat_one * gain_first).astype(jnp.bfloat16)
    projected = jnp.dot(normed_one, full_qkv, preferred_element_type=jnp.float32)
    mixed = (
        projected * taps[:, 0]
        + shift_down(projected, 1) * taps[:, 1]
        + shift_down(projected, 2) * taps[:, 2]
    ).astype(jnp.bfloat16)
    query = mixed[:, :width].reshape(seq_length, HEADS, HD)
    keys = mixed[:, width : 2 * width].reshape(seq_length, HEADS, HD)
    values = mixed[:, 2 * width :].reshape(seq_length, HEADS, HD)
    rows_block = min(512, seq_length)
    block_index = 0
    start_row = block_index * rows_block
    scores, allowed = scores_block(query, keys, start_row, seq_live)
    masked = jnp.where(allowed, scores, -1e30)
    top_score = jnp.max(masked, axis=-1, keepdims=True)
    exp_terms = jnp.exp(masked - top_score)
    row_totals = jnp.sum(exp_terms, axis=-1, keepdims=True)
    probs_low = (exp_terms / row_totals).astype(jnp.bfloat16)
    out_parts = jnp.einsum("hqk,khd->qhd", probs_low, values, preferred_element_type=jnp.float32)
    lse_parts = [top_score + jnp.log(row_totals)]
    attended_low = out_parts.reshape(seq_length, width).astype(jnp.bfloat16)
    branch_attn = jnp.dot(attended_low, full_out, preferred_element_type=jnp.float32)
    residual = tokens_in + branch_attn
    hat_two, inv_two = norm_parts(residual)
    normed_two = (hat_two * gain_second).astype(jnp.bfloat16)
    grad_out = jnp.where(live_rows[:, None], cotangent[0], jnp.zeros_like(cotangent[0]))
    row_set = lax.all_gather(normed_two[None], "wide", axis=0, tiled=True).reshape(-1, width)
    pre_act = jnp.dot(row_set, w_in, preferred_element_type=jnp.float32)
    activ = jnp.square(jax.nn.relu(pre_act)).astype(jnp.bfloat16)
    piece = activ
    branch_ffn = lax.psum_scatter(
        jnp.dot(piece, w_fc2, preferred_element_type=jnp.float32).astype(jnp.bfloat16),
        "wide",
        scatter_dimension=0,
        tiled=True,
    ).astype(jnp.float32)
    grad_set = lax.all_gather(grad_out[None], "wide", axis=0, tiled=True).reshape(-1, width)
    grad_act = contract_last(grad_set, w_fc2)
    grad_fc2_part = contract_first(activ, grad_set)
    grad_pre = (grad_act * 2.0 * jax.nn.relu(pre_act)).astype(jnp.bfloat16)
    grad_in_part = contract_first(row_set, grad_pre)
    piece = grad_pre
    grad_normed_two = lax.psum_scatter(
        contract_last(piece, w_in).astype(jnp.bfloat16), "wide", scatter_dimension=0, tiled=True
    ).astype(jnp.float32)
    grad_w_in, grad_w_fc2 = (
        lax.psum_scatter(
            grad_in_part.astype(jnp.bfloat16), "batch", scatter_dimension=0, tiled=True
        ).astype(jnp.float32),
        lax.psum_scatter(
            grad_fc2_part.astype(jnp.bfloat16), "batch", scatter_dimension=1, tiled=True
        ).astype(jnp.float32),
    )
    output = jnp.where(live_rows[:, None], residual + branch_ffn, 0.0).astype(jnp.bfloat16)[None]
    grad_ln_two, grad_gain_second = norm_back(grad_normed_two, gain_second, hat_two, inv_two)
    grad_residual = grad_out.astype(jnp.float32) + grad_ln_two
    grad_branch = grad_residual.astype(jnp.bfloat16)
    grad_w_out_part = contract_first(attended_low, grad_branch)
    grad_attended = contract_last(grad_branch, full_out).astype(jnp.bfloat16)
    grad_att_heads = grad_attended.reshape(seq_length, HEADS, HD)
    delta_all = jnp.sum(grad_att_heads.astype(jnp.float32) * out_parts, axis=-1)
    block_index = 0
    start_row = block_index * rows_block
    scores, allowed = scores_block(query, keys, start_row, seq_live)
    probs_full = jnp.where(allowed, jnp.exp(scores - lse_parts[block_index]), 0.0)
    probs_low = probs_full.astype(jnp.bfloat16)
    grad_probs = jnp.einsum(
        "qhd,khd->hqk", grad_att_heads, values, preferred_element_type=jnp.float32
    )
    delta_block = jnp.transpose(delta_all)[:, :, None]
    grad_scores = (probs_full * (grad_probs - delta_block)).astype(jnp.bfloat16)
    grad_query_parts = 0.125 * jnp.einsum(
        "hqk,khd->qhd", grad_scores, keys, preferred_element_type=jnp.float32
    )
    grad_keys = 0.125 * jnp.einsum(
        "hqk,qhd->khd", grad_scores, query, preferred_element_type=jnp.float32
    )
    grad_values = jnp.einsum(
        "hqk,qhd->khd", probs_low, grad_att_heads, preferred_element_type=jnp.float32
    )
    grad_mixed = jnp.concatenate(
        [
            grad_query_parts.reshape(seq_length, width),
            grad_keys.reshape(seq_length, width),
            grad_values.reshape(seq_length, width),
        ],
        axis=1,
    )
    grad_taps_part = jnp.stack(
        [
            jnp.sum(grad_mixed * projected, axis=0),
            jnp.sum(grad_mixed * shift_down(projected, 1), axis=0),
            jnp.sum(grad_mixed * shift_down(projected, 2), axis=0),
        ],
        axis=1,
    )
    grad_projected = (
        grad_mixed * taps[:, 0]
        + shift_up(grad_mixed, 1) * taps[:, 1]
        + shift_up(grad_mixed, 2) * taps[:, 2]
    ).astype(jnp.bfloat16)
    grad_qkv_part = contract_first(normed_one, grad_projected)
    grad_normed_one = contract_last(grad_projected, full_qkv)
    grad_ln_one, grad_gain_first = norm_back(grad_normed_one, gain_first, hat_one, inv_one)
    grad_inputs = (grad_residual + grad_ln_one).astype(jnp.bfloat16)[None]
    grad_w_qkv, grad_w_out, grad_conv_taps, grad_gain_one, grad_gain_two = (
        lax.psum_scatter(grad_qkv_part, ("batch", "wide"), scatter_dimension=0, tiled=True),
        lax.psum_scatter(grad_w_out_part, ("batch", "wide"), scatter_dimension=0, tiled=True),
        lax.psum_scatter(grad_taps_part, ("batch", "wide"), scatter_dimension=0, tiled=True),
        lax.psum_scatter(grad_gain_first, ("batch", "wide"), scatter_dimension=0, tiled=True),
        lax.psum_scatter(grad_gain_second, ("batch", "wide"), scatter_dimension=0, tiled=True),
    )
    return (
        output,
        grad_inputs,
        grad_w_qkv,
        grad_w_out,
        grad_conv_taps,
        grad_gain_one,
        grad_gain_two,
        grad_w_in,
        grad_w_fc2,
    )


BF = jnp.bfloat16
F32 = jnp.float32
AXES = ("batch", "wide")
LANES = 256
PART = 128
VMEM_MIB = {"ffn": 22}


def fits(mesh, args):
    inputs, w_qkv, w_in = args[0], args[3], args[8]
    count = mesh.shape["batch"] * mesh.shape["wide"]
    return (
        mesh.shape["batch"] == 4
        and mesh.shape["wide"] == 8
        and inputs.shape[0] == count
        and inputs.shape[1] % LANES == 0
        and w_qkv.shape[0] % (count * 8) == 0
        and w_qkv.shape[0] % LANES == 0
        and w_qkv.shape[0] // HEADS == HD
        and w_in.shape[1] == 8 * 3 * PART
        and (w_in.shape[0] // 4) % 16 == 0
    )


def dot(left, right, left_dim, right_dim):
    return lax.dot_general(
        left, right, (((left_dim,), (right_dim,)), ((), ())), preferred_element_type=F32
    )


def flip_pairs(rule):
    return [(i, i ^ rule(i)) for i in range(32)]


def send(array, rule):
    return lax.ppermute(array, AXES, flip_pairs(rule))


def over_core(i):
    return 8


def over_first(i):
    return 16 if i & 8 else 1


def over_second(i):
    return 1 if i & 8 else 16


def over_z(step):
    return lambda i: 2 * step


def tie(value, *others):
    return lax.optimization_barrier((value,) + others)[0]


def join(parts):
    return jnp.concatenate(parts)


def added(keep, come):
    return (keep.astype(F32) + come.astype(F32)).astype(BF)


def halved(keep, come):
    half = keep.shape[0] // 2
    return added(keep[:half], come[:half]), added(keep[half:], come[half:])


def place_of(me, other):
    apart = me ^ other
    x_bit, z_bits = apart & 1, (apart & 2) | ((apart >> 2) & 1)
    core_bit, y_bit = (apart >> 3) & 1, (apart >> 4) & 1
    on_first = ((other >> 3) & 1) == 0
    high = jnp.where(on_first, y_bit, x_bit)
    low = jnp.where(on_first, x_bit, y_bit)
    return core_bit * 16 + high * 8 + low * 4 + z_bits


def call(kernel, grid, in_specs, out_specs, out_shape, scratch=(), busy=1, name=None, aliases=None):
    return pl.pallas_call(
        kernel,
        grid_spec=pltpu.PrefetchScalarGridSpec(
            num_scalar_prefetch=1,
            grid=grid,
            in_specs=in_specs,
            out_specs=out_specs,
            scratch_shapes=list(scratch),
        ),
        out_shape=out_shape,
        compiler_params=pltpu.CompilerParams(
            dimension_semantics=("arbitrary",) * len(grid), vmem_limit_bytes=VMEM_MIB.get(name, 20) * 1024 * 1024
        ),
        cost_estimate=pl.CostEstimate(flops=int(busy * 1.15e9), bytes_accessed=0, transcendentals=0),
        name=name,
        input_output_aliases=aliases or {},
    )


def whole(shape):
    zeros = (0,) * len(shape)
    return pl.BlockSpec(shape, lambda *_: zeros, pipeline_mode=pl.Buffered(1))


def hat_of(values_in):
    centered = values_in - jnp.mean(values_in, axis=-1, keepdims=True)
    inv_std = lax.rsqrt(jnp.mean(centered * centered, axis=-1, keepdims=True) + epsilon)
    return centered * inv_std, inv_std


def turned(value):
    return jnp.transpose(value.astype(F32)).astype(BF)


def prepare_kernel(meta, cot_ref, go_ref, got_ref):
    live = lax.broadcasted_iota(jnp.int32, (cot_ref.shape[0], 1), 0) < meta[33]
    value = jnp.where(live, cot_ref[...].astype(F32), 0.0)
    go_ref[...] = value.astype(BF)
    got_ref[...] = jnp.transpose(value).astype(BF)


def pack_kernel(meta, up_ref, down_ref, out_ref, a_ref, b_ref):
    half = up_ref.shape[0] // 2
    second_half, second_core = (meta[32] >> 1) == 1, (meta[32] & 1) == 1
    up = jnp.where(second_half, up_ref[half:, :], up_ref[:half, :])
    down = turned(jnp.where(second_half, down_ref[:, half:], down_ref[:, :half]))
    for i, part in enumerate((up, down)):
        a_ref[0, i * half : (i + 1) * half, :] = jnp.where(second_core, part[:, PART : 2 * PART], part[:, :PART])
    left, right = swap_halves(up[:, 2 * PART :], down[:, 2 * PART :])
    b_ref[0, :half, :] = jnp.where(second_core, right, left).astype(BF)
    rows = out_ref.shape[0]
    for c in range(out_ref.shape[1] // PART):
        b_ref[0, half + c * rows : half + (c + 1) * rows, :] = out_ref[:, c * PART : (c + 1) * PART]


def block_of(meta, i, own_ref, other_ref):
    place = meta[i]
    return jnp.where(place < 16, own_ref[place & 15], other_ref[place & 15])


def project_kernel(
    meta, x_ref, own_ref, other_ref, few_own_ref, few_other_ref,
    proj_ref, mixed_ref, wn_ref, nt_ref, taps_ref, gains_ref, normed,
):
    rows = own_ref.shape[1]
    step = pl.program_id(0)

    def few_of(device, lanes):
        block = block_of(meta, device, few_own_ref, few_other_ref)[:8].astype(F32)
        return jnp.concatenate([block, jnp.zeros((8, lanes - PART), F32)], axis=1)

    @pl.when(step == 0)
    def _():
        width = gains_ref.shape[1]
        lane = lax.broadcasted_iota(jnp.int32, (8, width), 1)
        gains = jnp.zeros((8, width), F32)
        for i in range(32):
            first = i * rows
            moved = pltpu.roll(few_of(i, width), first, 1)
            gains = jnp.where((lane >= first) & (lane < first + rows), moved, gains)
        gains_ref[...] = gains
        hat, _ = hat_of(x_ref[...].astype(F32))
        low = (hat * gains[3:4, :]).astype(BF)
        normed[...] = low
        flipped = turned(low)
        for i in range(32):
            nt_ref[meta[i]] = flipped[i * rows : (i + 1) * rows]

    channels = 3 * rows
    lane = lax.broadcasted_iota(jnp.int32, (8, LANES), 1)
    taps = jnp.zeros((8, LANES), F32)
    for i in range(LANES // channels + 2):
        device = jnp.minimum((step * LANES) // channels + i, 31)
        first = device * channels - step * LANES
        moved = pltpu.roll(few_of(device, LANES), (first + 2 * LANES) & (LANES - 1), 1)
        taps = jnp.where((lane >= first) & (lane < first + channels), moved, taps)
    taps_ref[...] = taps
    for i in range(32):
        wn_ref[i * rows : (i + 1) * rows, :] = block_of(meta, i, own_ref, other_ref)
    value = dot(normed[...], wn_ref[...], 1, 0)
    at = lax.broadcasted_iota(jnp.int32, value.shape, 0)
    one = jnp.where(at >= 1, pltpu.roll(value, 1, 0), 0.0)
    two = jnp.where(at >= 2, pltpu.roll(value, 2, 0), 0.0)
    mixed = value * taps[0:1, :] + one * taps[1:2, :] + two * taps[2:3, :]
    proj_ref[...] = value.astype(BF)
    mixed_ref[...] = mixed.astype(BF)


def head_row(head, scale=1.0):
    lane = lax.broadcasted_iota(jnp.int32, (1, LANES), 1)
    return jnp.where(lane // HD == head, scale, 0.0).astype(BF)


def allowed_in(meta, keys, first_query, queries):
    key = lax.broadcasted_iota(jnp.int32, (keys, queries), 0)
    query = first_query + lax.broadcasted_iota(jnp.int32, (1, queries), 1)
    return key < jnp.minimum(query + 1, meta[33])


def attend_kernel(meta, q_ref, k_ref, v_ref, out_ref, lse_ref, flipped):
    seq = q_ref.shape[0]
    tile = LANES
    values_t = turned(v_ref[...])
    keys = k_ref[...]
    for t in range(seq // tile):
        upto = (t + 1) * tile
        allowed = allowed_in(meta, upto, t * tile, tile)
        query = q_ref[t * tile : upto, :]
        for head in range(LANES // HD):
            scores = dot(keys[:upto], query * head_row(head, 0.125), 1, 1)
            scores = jnp.where(allowed, scores, -1e30)
            top = jnp.max(scores, axis=0, keepdims=True)
            terms = jnp.exp(scores - top)
            total = jnp.sum(terms, axis=0, keepdims=True)
            probs = (terms * (1.0 / total)).astype(BF)
            flipped[head * HD : (head + 1) * HD, t * tile : upto] = dot(
                values_t[head * HD : (head + 1) * HD, :upto], probs, 1, 0
            )
            lse_ref[0, head : head + 1, t * tile : upto] = top + jnp.log(total)
    out_ref[...] = jnp.transpose(flipped[...]).astype(BF)


def mend_kernel(meta, att_ref, own_ref, other_ref, x_ref, gain_ref, res_ref, n2_ref, n2t_ref, at_ref, wn_ref):
    flipped = turned(att_ref[...])
    rows = at_ref.shape[1]
    for i in range(32):
        at_ref[meta[i]] = flipped[i * rows : (i + 1) * rows]
        block = block_of(meta, i, own_ref, other_ref)
        for c in range(wn_ref.shape[1] // PART):
            wn_ref[i * rows : (i + 1) * rows, c * PART : (c + 1) * PART] = block[c * rows : (c + 1) * rows]
    residual = x_ref[...].astype(F32) + dot(att_ref[...], wn_ref[...], 1, 0)
    res_ref[...] = residual
    hat, _ = hat_of(residual)
    low = (hat * gain_ref[4:5, :]).astype(BF)
    n2_ref[...] = low
    n2t_ref[...] = turned(low)


def swap_halves(left, right):
    left, right = left.astype(F32), right.astype(F32)
    low = lax.broadcasted_iota(jnp.int32, (1, PART), 1) < PART // 2
    return (
        jnp.where(low, left, pltpu.roll(right, PART // 2, 1)),
        jnp.where(low, pltpu.roll(left, PART // 2, 1), right),
    )


def ffn_kernel(packed, meta, *refs):
    token_refs, refs = (refs[:4], refs[4:8]), refs[8:]
    count = 8 if packed else 4
    tiles, refs = refs[:count], refs[count:]
    if packed:
        branch_ref, grad_ref, branch_acc, grad_acc, low_ref, high_ref = refs
    else:
        sums_in, (branch_ref, grad_ref, both_ref, low_ref, high_ref, branch_acc, grad_acc) = refs[:4], refs[4:]
    sums = (branch_ref, grad_ref, branch_acc, grad_acc)
    step = pl.program_id(0)

    @pl.when(step == 0)
    def _():
        for i, ref in enumerate(sums):
            ref[...] = jnp.zeros_like(ref) if packed else sums_in[i][...]

    half = tiles[0].shape[1] if packed else tiles[0].shape[1] // 2
    if packed:
        blocks = [jnp.concatenate([tiles[2 * k][0], tiles[2 * k + 1][0]], axis=0) for k in range(4)]
        pairs = [swap_halves(blocks[0], blocks[1]), swap_halves(blocks[2], blocks[3])]
        w_up, w_down = (jnp.concatenate([pairs[0][i], pairs[1][i]], axis=1).astype(BF) for i in range(2))
    else:
        w_up, w_down = (
            jnp.concatenate(
                [
                    jnp.concatenate([tiles[2 * k + b][0, i * half : (i + 1) * half, :] for b in range(2)], axis=0)
                    for k in range(2)
                ],
                axis=1,
            )
            for i in range(2)
        )
    up_sum = down_sum = 0.0
    for i, (n2_ref, go_ref, n2t_ref, got_ref) in enumerate(token_refs):
        pre = jnp.maximum(dot(n2_ref[...], w_up, 1, 0), 0.0)
        activ = (pre * pre).astype(BF)
        grad_pre = (dot(go_ref[...], w_down, 1, 0) * 2.0 * pre).astype(BF)
        sums[2 * i][...] += dot(activ, w_down, 1, 1)
        sums[2 * i + 1][...] += dot(grad_pre, w_up, 1, 1)
        up_sum += dot(n2t_ref[...], grad_pre, 1, 0)
        down_sum += dot(got_ref[...], activ, 1, 0)
    first_wide = step * (4 if packed else 2)
    results = []
    for k in range(2):
        lanes = slice(k * PART, (k + 1) * PART)
        if packed:
            results += [(part,) for part in swap_halves(up_sum[:, lanes], down_sum[:, lanes])]
        else:
            results.append((up_sum[:, lanes], down_sum[:, lanes]))
    for k, parts in enumerate(results):
        for b in range(2):
            place = meta[b * 16 + (meta[32] & 1) * 8 + first_wide + k]
            for is_high, target in enumerate((low_ref, high_ref)):

                @pl.when((place >> 3) == is_high)
                def _(place=place, target=target, parts=parts, b=b):
                    for i, part in enumerate(parts):
                        target[place & 7, i * half : (i + 1) * half, :] = part[b * half : (b + 1) * half].astype(BF)

    if not packed:

        @pl.when(step == pl.num_programs(0) - 1)
        def _():
            seq = branch_acc.shape[0]
            both_ref[:seq, :] = branch_acc[...].astype(BF)
            both_ref[seq:, :] = grad_acc[...].astype(BF)


def turn_kernel(meta, grad_ref, branch_ref, come_ref, res_ref, gain_ref, go_ref, at_ref, wn_ref, out_ref, gres_ref, gatt_ref, ggain_ref, keep_ref, away_ref):
    residual = res_ref[...]
    seq = residual.shape[0]
    live = lax.broadcasted_iota(jnp.int32, (seq, 1), 0) < meta[33]
    branch = branch_ref[...] + come_ref[:seq, :].astype(F32)
    out_ref[...] = jnp.where(live, residual + branch, 0.0).astype(BF)
    hat, inv_std = hat_of(residual)
    grad = grad_ref[...] + come_ref[seq:, :].astype(F32)
    ggain_ref[...] = jnp.sum(grad * hat, axis=0, keepdims=True)
    scaled = grad * gain_ref[4:5, :]
    mean_first = jnp.mean(scaled, axis=-1, keepdims=True)
    mean_second = jnp.mean(scaled * hat, axis=-1, keepdims=True)
    grad_res = go_ref[...].astype(F32) + inv_std * (scaled - mean_first - hat * mean_second)
    gres_ref[...] = grad_res
    low = grad_res.astype(BF)
    gatt_ref[...] = dot(low, wn_ref[...], 1, 1).astype(BF)
    result = dot(at_ref[...], low, 1, 0)
    lanes = keep_ref.shape[2]
    chunks = result.shape[1] // lanes
    rows = keep_ref.shape[1] // chunks
    for i in range(32):
        target = away_ref if i >= 16 else keep_ref
        for c in range(chunks):
            target[i & 15, c * rows : (c + 1) * rows, :] = result[
                i * rows : (i + 1) * rows, c * lanes : (c + 1) * lanes
            ].astype(BF)


def attend_back_kernel(
    meta, q_ref, k_ref, v_ref, pq_ref, pk_ref, pv_ref, tq_ref, tk_ref, tv_ref, go_ref, out_ref, lse_ref,
    gq_ref, gk_ref, gv_ref, dtq_ref, dtk_ref, dtv_ref, flipped,
):
    seq = q_ref.shape[0]
    tile = LANES
    keys, values = k_ref[...], v_ref[...]
    keys_t = turned(keys)
    delta_t = jnp.transpose(go_ref[...].astype(F32) * out_ref[...].astype(F32))
    grad_keys = [jnp.zeros((tile, LANES), F32) for _ in range(seq // tile)]
    grad_values = list(grad_keys)
    for t in range(seq // tile):
        upto = (t + 1) * tile
        allowed = allowed_in(meta, upto, t * tile, tile)
        query, grad = q_ref[t * tile : upto, :], go_ref[t * tile : upto, :]
        for head in range(LANES // HD):
            lanes = slice(head * HD, (head + 1) * HD)
            query_h, grad_h = query * head_row(head, 0.125), grad * head_row(head)
            delta = jnp.sum(delta_t[lanes, t * tile : upto], axis=0, keepdims=True)
            scores = dot(keys[:upto], query_h, 1, 1)
            lse = lse_ref[0, head : head + 1, t * tile : upto]
            probs = jnp.where(allowed, jnp.exp(scores - lse), 0.0)
            grad_scores = (probs * (dot(values[:upto], grad_h, 1, 1) - delta)).astype(BF)
            flipped[lanes, t * tile : upto] = dot(keys_t[lanes, :upto], grad_scores, 1, 0) * 0.125
            add_values = dot(probs.astype(BF), grad_h, 1, 0)
            add_keys = dot(grad_scores, query_h, 1, 0)
            for s in range(t + 1):
                rows = slice(s * tile, (s + 1) * tile)
                grad_values[s] += add_values[rows]
                grad_keys[s] += add_keys[rows]
    mixed = (
        jnp.transpose(flipped[...]),
        jnp.concatenate(grad_keys, axis=0),
        jnp.concatenate(grad_values, axis=0),
    )
    at = lax.broadcasted_iota(jnp.int32, (seq, LANES), 0)
    for grad, proj_ref, taps_ref, g_ref, dt_ref in zip(
        mixed, (pq_ref, pk_ref, pv_ref), (tq_ref, tk_ref, tv_ref), (gq_ref, gk_ref, gv_ref), (dtq_ref, dtk_ref, dtv_ref)
    ):
        one = jnp.where(at < seq - 1, pltpu.roll(grad, seq - 1, 0), 0.0)
        two = jnp.where(at < seq - 2, pltpu.roll(grad, seq - 2, 0), 0.0)
        g_ref[...] = (grad * taps_ref[0:1, :] + one * taps_ref[1:2, :] + two * taps_ref[2:3, :]).astype(BF)
        proj = proj_ref[...].astype(F32)
        for tap, part in enumerate((grad, one, two)):
            dt_ref[tap : tap + 1, :] = jnp.sum(part * proj, axis=0, keepdims=True)


def weight_kernel(with_few, meta, nt_ref, *refs):
    if with_few:
        (*tap_refs, gain_ref), refs, few = refs[:7], refs[7:-1], refs[-1]
    keep_ref, away_ref = refs[-2:]
    half, full = keep_ref.shape
    start = 0
    for g_ref in refs[:-2]:
        result = dot(nt_ref[...], g_ref[...], 1, 0).astype(BF)
        columns = slice(start, start + g_ref.shape[1])
        start += g_ref.shape[1]
        keep_ref[:, columns] = result[:half]
        away_ref[:, columns] = result[half:]
    if with_few:
        rows = half // 16
        row = lax.broadcasted_iota(jnp.int32, (8, PART), 0)
        lane = lax.broadcasted_iota(jnp.int32, (8, PART), 1)
        taps = jnp.concatenate([ref[...] for ref in tap_refs], axis=1)
        gains = jnp.broadcast_to(gain_ref[...], (8, gain_ref.shape[1]))

        def taken(values_in, first):
            start = first // PART * PART
            window = values_in[:, start : start + 2 * PART]
            return pltpu.roll(window, (start - first) % window.shape[1], 1)[:, :PART]

        for i in range(32):
            piece = jnp.where((row == 3) & (lane < rows), taken(gains, i * rows), 0.0)
            few[meta[i]] = jnp.where((row < 3) & (lane < 3 * rows), taken(taps, i * 3 * rows), piece)
        for i, ref in enumerate((keep_ref, away_ref)):
            ref[:, full - PART :] = jnp.zeros((half, PART), BF)
            for k in range(16):
                ref[k * rows : k * rows + 8, full - PART :] = few[i * 16 + k].astype(BF)


def last_kernel(meta, *refs):
    grads, (w_ref, x_ref, gain_ref, gres_ref, gin_ref) = refs[:-5], refs[-5:]
    grad = dot(jnp.concatenate([g_ref[...] for g_ref in grads], axis=1), w_ref[...], 1, 1)
    hat, inv_std = hat_of(x_ref[...].astype(F32))
    scaled = grad * gain_ref[3:4, :]
    mean_first = jnp.mean(scaled, axis=-1, keepdims=True)
    mean_second = jnp.mean(scaled * hat, axis=-1, keepdims=True)
    back = inv_std * (scaled - mean_first - hat * mean_second)
    gin_ref[...] = (gres_ref[...] + back).astype(BF)


def own_sequence(inputs, lengths, cotangent, w_qkv, w_out, conv_taps, gain_one, gain_two, w_in, w_fc2):
    seq, width = inputs.shape[1], inputs.shape[2]
    rows, wide = w_qkv.shape
    half = width // 2
    tap_rows = conv_taps.shape[0]
    batch = lax.axis_index("batch")
    core = batch & 1
    me = batch * 8 + lax.axis_index("wide")
    number = jnp.arange(64, dtype=jnp.int32)
    meta = jnp.where(number < 32, place_of(me, number & 31), jnp.where(number == 32, batch, lengths[0]))
    x, cot = inputs[0], cotangent[0]
    shape = jax.ShapeDtypeStruct
    row_spec = whole((1, width))
    gain_spec = whole((8, width))
    token = whole((seq, width))
    token_t = whole((width, seq))
    groups = width // LANES

    few_rows = [jnp.pad(conv_taps.T, ((0, 0), (0, PART - tap_rows)))]
    few_rows += [jnp.pad(gain[None], ((0, 0), (0, PART - rows))) for gain in (gain_one, gain_two)]
    few_rows = jnp.concatenate(few_rows + [jnp.zeros((rows - 5, PART), BF)])
    qkv_block = jnp.concatenate([w_qkv, few_rows], axis=1)[None]
    qkv_block, meta, first_core = lax.optimization_barrier((qkv_block, meta, core == 0))
    qkv_far = send(qkv_block, over_z(2))
    out_rows = rows * (width // PART)
    a_block, b_block = call(
        pack_kernel, (1,), [whole(w.shape) for w in (w_in, w_fc2, w_out)],
        [whole((1, width, PART)), whole((1, half + out_rows, PART))],
        [shape((1, width, PART), BF), shape((1, half + out_rows, PART), BF)], busy=2, name="pack",
    )(meta, w_in, w_fc2, w_out)

    b_far = send(tie(b_block, qkv_far), over_z(2))
    qkv2 = join([qkv_block, tie(qkv_far, b_block)])
    qkv_near = send(qkv2, over_z(1))
    qkv4 = join([qkv2, qkv_near])
    qkv_first = send(qkv4, over_first)
    b2 = join([b_block, tie(b_far, qkv4)])
    b_near = send(b2, over_z(1))
    a_far = send(tie(a_block, b2), over_z(2))
    qkv8 = join([qkv4, tie(qkv_first, b2)])
    qkv_second = send(qkv8, over_second)
    grad_out, grad_out_t = call(
        prepare_kernel, (1,), [token], [token, token_t],
        [shape((seq, width), BF), shape((width, seq), BF)], busy=1, name="prepare",
    )(meta, tie(cot, qkv_far))
    go_other = send(grad_out, over_core)
    got_other = send(grad_out_t, over_core)
    b4 = join([b2, tie(b_near, qkv8)])
    a2 = join([a_block, tie(a_far, qkv8)])
    a_near = send(a2, over_z(1))
    qkv16 = join([qkv8, tie(qkv_second, a2, b4)])
    qkv_core = send(qkv16, over_core)
    b_first = send(tie(b4, qkv16), over_first)
    a4 = join([a2, tie(a_near, qkv_core)])
    a_first = send(a4, over_first)

    lane_block = pl.BlockSpec((seq, LANES), lambda j, m: (0, j))
    half_block = pl.BlockSpec((16, rows, LANES), lambda j, m: (0, 0, j))
    few_block = pl.BlockSpec((16, rows, PART), lambda j, m: (0, 0, wide // PART))
    tap_block = pl.BlockSpec((8, LANES), lambda j, m: (0, j))
    projected, mixed, qkv_full, normed_t, taps, gains = call(
        project_kernel, (wide // LANES,),
        [token, half_block, half_block, few_block, few_block],
        [lane_block, lane_block, pl.BlockSpec((width, LANES), lambda j, m: (0, j)), whole((32, rows, seq)),
         tap_block, gain_spec],
        [shape((seq, wide), BF), shape((seq, wide), BF), shape((width, wide), BF), shape((32, rows, seq), BF),
         shape((8, wide), F32), shape((8, width), F32)],
        [pltpu.VMEM((seq, width), BF)], busy=7, name="project",
    )(meta, tie(x, a4), qkv16, qkv_core, qkv16, qkv_core)

    b8 = join([b4, tie(b_first, mixed)])
    b_second = send(b8, over_second)
    part_specs = [pl.BlockSpec((seq, LANES), lambda j, m, p=p: (0, p * groups + j)) for p in range(3)]
    lse_spec = pl.BlockSpec((1, 8, seq), lambda j, m: (j, 0, 0))
    a8 = join([a4, tie(a_first, mixed)])
    ready = tie(mixed, b8, a8, go_other, got_other)
    attended, lse = call(
        attend_kernel, (groups,), part_specs, [lane_block, lse_spec],
        [shape((seq, width), BF), shape((groups, 8, seq), F32)], [pltpu.VMEM((LANES, seq), F32)],
        busy=9, name="attend",
    )(meta, ready, ready, ready)

    b16 = join([b8, tie(b_second, attended)])
    out16 = b16[:, half:, :]
    out_core = send(out16, over_core)
    a_second = send(tie(a8, b16), over_second)
    residual, normed_two, normed_two_t, attended_t, out_full = call(
        mend_kernel, (1,),
        [token, whole(out16.shape), whole(out16.shape), token, gain_spec],
        [token, token, token_t, whole((32, rows, seq)), whole((width, width))],
        [shape((seq, width), F32), shape((seq, width), BF), shape((width, seq), BF), shape((32, rows, seq), BF),
         shape((width, width), BF)],
        busy=2.5, name="mend",
    )(meta, attended, out16, out_core, x, gains)
    n2_other = send(normed_two, over_core)
    n2t_other = send(normed_two_t, over_core)

    sequences = [normed_two, grad_out, normed_two_t, grad_out_t, n2_other, go_other, n2t_other, got_other]
    sequence_specs = [token, token, token_t, token_t] * 2

    def tile(block_rows, per_step, k, b):
        return pl.BlockSpec(
            (1, block_rows, PART), lambda s, m: (m[b * 16 + (m[32] & 1) * 8 + s * per_step + k], 0, 0)
        )

    total = shape((seq, width), F32)
    grads_b = shape((8, half, PART), BF)
    branch, grad_two, branch_o, grad_o, b_low, b_high = call(
        functools.partial(ffn_kernel, True), (2,),
        sequence_specs + [tile(half, 4, k, b) for k in range(4) for b in range(2)],
        [token] * 4 + [whole(grads_b.shape)] * 2, [total] * 4 + [grads_b] * 2, busy=2, name="ffn",
    )(meta, *sequences, *[b16] * 8)
    a16 = join([a8, tie(a_second, branch)])
    b_sum = send(b_high, over_second)
    grads_a = shape((8, width, PART), BF)
    branch, grad_two, both, a_low, a_high = call(
        functools.partial(ffn_kernel, False), (4,),
        sequence_specs + [tile(width, 2, k, b) for k in range(2) for b in range(2)] + [token] * 4,
        [token] * 2 + [whole((2 * seq, width))] + [whole(grads_a.shape)] * 2,
        [total] * 2 + [shape((2 * seq, width), BF)] + [grads_a] * 2,
        [pltpu.VMEM((seq, width), F32)] * 2, busy=15, name="ffn",
    )(meta, tie(normed_two, b_high), *sequences[1:], *[a16] * 4, branch, grad_two, branch_o, grad_o)
    b_sum = tie(b_sum, branch)
    come = send(tie(both, b_sum), over_core)
    a_sum = send(a_high, over_second)
    b_keep, b_go = halved(b_low, b_sum)
    half_out = shape((16, rows * (width // PART), PART), BF)
    output, grad_residual, grad_attended, grad_gain_second, keep_out, away_out = call(
        turn_kernel, (1,),
        [token] * 2 + [whole((2 * seq, width)), token, gain_spec, token, token_t, whole((width, width))],
        [token] * 3 + [row_spec, whole(half_out.shape), whole(half_out.shape)],
        [shape((seq, width), BF), shape((seq, width), F32), shape((seq, width), BF), shape((1, width), F32),
         half_out, half_out],
        busy=4, name="turn",
    )(meta, tie(grad_two, a_high, b_go), branch, come, residual, gains, grad_out, attended_t.reshape(width, seq), out_full)

    def attend_back(first, count, wait_for):
        def lanes(height, part, start):
            return pl.BlockSpec((height, LANES), lambda i, m: (0, part * groups + start + i))

        specs = [lanes(seq, p, first) for p in range(3)]
        tap_specs = [lanes(8, p, first) for p in range(3)]
        return call(
            attend_back_kernel, (count,),
            specs * 2 + tap_specs + [specs[0]] * 2 + [pl.BlockSpec((1, 8, seq), lambda i, m: (first + i, 0, 0))],
            [lanes(seq, 0, 0)] * 3 + [lanes(8, 0, 0)] * 3,
            [shape((seq, count * LANES), BF)] * 3 + [shape((8, count * LANES), F32)] * 3,
            [pltpu.VMEM((LANES, seq), F32)], busy=count, name="attend_back",
        )(meta, mixed, mixed, mixed, projected, projected, projected, taps, taps, taps,
          tie(grad_attended, *wait_for), attended, lse)

    def weights(grads, few, wait_for):
        size = sum(g.shape[1] for g in grads) + (PART if few else 0)
        spec = whole((half, size))
        keep, away = call(
            functools.partial(weight_kernel, bool(few)), (1,),
            [token_t] + [whole(part.shape) for part in [*few, *grads]],
            [spec, spec], [shape((half, size), BF)] * 2, [pltpu.VMEM((32, 8, PART), F32)] if few else (),
            busy=1, name="weight",
        )(meta, tie(normed_t.reshape(width, seq), *wait_for), *few, *grads)
        return keep.reshape(16, rows, size), away.reshape(16, rows, size)

    out_come = send(away_out, over_core)
    back0 = attend_back(0, groups - 1, (away_out,))

    out_sum = added(keep_out, tie(out_come, back0[0]))
    out_go = out_sum[8:]
    out_come = send(out_go, over_second)
    x_keep, x_away = weights(back0[:3], [], (out_go,))
    x_sum = send(x_away, over_core)
    a_keep, a_go = halved(a_low, tie(a_sum, x_away))
    a_sum = send(a_go, over_first)
    back2 = attend_back(groups - 1, 1, (back0[0], x_away, a_go))
    backs = (back0, back2)
    grad_projected = [back[part] for part in range(3) for back in backs]
    few = [back[3 + part] for part in range(3) for back in backs] + [grad_gain_second]
    y_keep, y_away = weights(back2[:3], few, ())
    y_sum = send(y_away, over_core)

    out_keep, out_go = halved(out_sum[:8], tie(out_come, y_away))
    b_keep = jnp.concatenate([b_keep, out_keep], axis=1)
    b_go = jnp.concatenate([b_go, out_go], axis=1)
    b_sum = send(b_go, over_first)
    x_keep, x_go = halved(x_keep, tie(x_sum, y_away))
    x_sum = send(x_go, over_second)
    a_keep, a_go = halved(a_keep, tie(a_sum, x_go))
    a_sum = send(a_go, over_z(1))
    grad_inputs = call(
        last_kernel, (1,),
        [whole(g.shape) for g in grad_projected] + [whole((width, wide)), token, gain_spec, token],
        [token], [shape((seq, width), BF)], busy=4, name="last",
    )(meta, *grad_projected, qkv_full, x, gains, tie(grad_residual, y_away, a_go, b_go, x_go))[0]
    y_keep, y_go = halved(y_keep, tie(y_sum, grad_inputs))
    y_sum = send(y_go, over_second)
    b_keep, b_go = halved(b_keep, tie(b_sum, y_go))
    b_sum = send(b_go, over_z(1))
    a_keep, a_go = halved(a_keep, tie(a_sum, b_go))
    a_sum = send(a_go, over_z(2))
    x_keep, x_go = halved(x_keep, tie(x_sum, a_go))
    x_sum = send(x_go, over_first)
    y_keep, y_go = halved(y_keep, tie(y_sum, x_go))
    y_sum = send(y_go, over_first)
    b_keep, b_go = halved(b_keep, tie(b_sum, y_go))
    b_sum = send(b_go, over_z(2))
    x_keep, x_go = halved(x_keep, tie(x_sum, b_go))
    x_sum = send(x_go, over_z(1))
    y_keep, y_go = halved(y_keep, tie(y_sum, x_go))
    y_sum = send(y_go, over_z(1))
    x_keep, x_go = halved(x_keep, tie(x_sum, y_go))
    x_sum = send(x_go, over_z(2))
    y_keep, y_go = halved(y_keep, tie(y_sum, x_go))
    y_sum = send(y_go, over_z(2))
    grad_a = a_keep[0].astype(F32) + tie(a_sum, y_go)[0].astype(F32)
    grad_b = b_keep[0].astype(F32) + tie(b_sum, y_go)[0].astype(F32)
    grad_out_w = jnp.transpose(grad_b[half:].reshape(width // PART, rows, PART), (1, 0, 2)).reshape(rows, width)
    quarter = width // 4

    def share(swapped):
        pairs = [
            (g[first : first + quarter], g[first + quarter : first + 2 * quarter])
            for g, first in ((grad_a, 0), (grad_a, half), (grad_b, 0))
        ]
        return jnp.concatenate([jnp.where(first_core, p[swapped], p[1 - swapped]) for p in pairs])

    mine = share(0)
    theirs = send(share(1), over_core)
    mine, theirs = jnp.where(first_core, mine, theirs), jnp.where(first_core, theirs, mine)
    units = PART // 2
    grad_in_w, grad_fc2_w = (
        jnp.concatenate(
            [part[i * quarter : (i + 1) * quarter] for part in (mine, theirs)]
            + [part[2 * quarter :, i * units : (i + 1) * units] for part in (mine, theirs)],
            axis=1,
        )
        for i in range(2)
    )

    x_total = x_keep[0].astype(F32) + x_sum[0].astype(F32)
    y_total = y_keep[0].astype(F32) + y_sum[0].astype(F32)
    few = y_total[:8, 3 * LANES :]
    grad_qkv = jnp.concatenate(
        [
            part
            for i in range(3)
            for part in (x_total[:, 2 * i * LANES : 2 * (i + 1) * LANES], y_total[:, i * LANES : (i + 1) * LANES])
        ],
        axis=1,
    )
    grad_gain_first = jnp.sum(grad_qkv * w_qkv.astype(F32), axis=1) / gain_one.astype(F32)
    return (
        output[None],
        grad_inputs[None],
        grad_qkv,
        grad_out_w,
        few[:3, :tap_rows].T,
        grad_gain_first,
        few[3, :rows],
        grad_in_w,
        jnp.transpose(grad_fc2_w),
    )


def solution(mesh):
    fast = functools.partial(own_sequence)

    def program(*args):
        body = fast if fits(mesh, args) else shards
        return jax.shard_map(
            body,
            mesh=mesh,
            in_specs=(
                P(("batch", "wide"), None, None),
                P(("batch", "wide")),
                P(("batch", "wide"), None, None),
                P(("batch", "wide"), None),
                P(("batch", "wide"), None),
                P(("batch", "wide"), None),
                P(("batch", "wide")),
                P(("batch", "wide")),
                P(None, "wide"),
                P("wide", None),
            ),
            out_specs=(
                P(("batch", "wide"), None, None),
                P(("batch", "wide"), None, None),
                P(("batch", "wide"), None),
                P(("batch", "wide"), None),
                P(("batch", "wide"), None),
                P(("batch", "wide")),
                P(("batch", "wide")),
                P("batch", "wide"),
                P("wide", "batch"),
            ),
            check_vma=False,
        )(*args)

    return program
```

```python
import functools
import jax
import jax.numpy as jnp
from jax import lax
from jax.experimental import pallas as pl
from jax.experimental.pallas import tpu as pltpu
from jax.sharding import PartitionSpec as P

HEADS = 12
HD = 64


epsilon = 1e-05


def contract_first(left, right):
    return lax.dot_general(
        left, right, (((0,), (0,)), ((), ())), preferred_element_type=jnp.float32
    )


def contract_last(left, right):
    return lax.dot_general(
        left, right, (((1,), (1,)), ((), ())), preferred_element_type=jnp.float32
    )


def norm_parts(values_in):
    centered = values_in - jnp.mean(values_in, axis=-1, keepdims=True)
    inv_std = lax.rsqrt(jnp.mean(centered * centered, axis=-1, keepdims=True) + epsilon)
    return (centered * inv_std, inv_std)


def norm_back(grad_normed, gain_vec, normed_hat, inv_std):
    grad_hat = grad_normed * gain_vec
    mean_first = jnp.mean(grad_hat, axis=-1, keepdims=True)
    mean_second = jnp.mean(grad_hat * normed_hat, axis=-1, keepdims=True)
    grad_value = inv_std * (grad_hat - mean_first - normed_hat * mean_second)
    return (grad_value, jnp.sum(grad_normed * normed_hat, axis=0))


def shift_down(signal, steps):
    filler = jnp.zeros((steps, signal.shape[1]), signal.dtype)
    return jnp.concatenate([filler, signal[:-steps]], axis=0)


def shift_up(signal, steps):
    filler = jnp.zeros((steps, signal.shape[1]), signal.dtype)
    return jnp.concatenate([signal[steps:], filler], axis=0)


def scores_block(query_block, keys, start_row, seq_live):
    rows_block = query_block.shape[0]
    scores = (
        jnp.einsum("qhd,khd->hqk", query_block, keys, preferred_element_type=jnp.float32) * 0.125
    )
    query_pos = start_row + jnp.arange(rows_block)
    key_pos = jnp.arange(keys.shape[0])
    allowed = (key_pos[None, :] <= query_pos[:, None]) & (key_pos[None, :] < seq_live)
    return (scores, allowed[None])


def shards(inputs, lengths, cotangent, w_qkv, w_out, conv_taps, gain_one, gain_two, w_in, w_fc2):
    full_qkv, full_out, full_taps, full_gain_one, full_gain_two = (
        lax.all_gather(w_qkv, ("batch", "wide"), axis=0, tiled=True),
        lax.all_gather(w_out, ("batch", "wide"), axis=0, tiled=True),
        lax.all_gather(conv_taps, ("batch", "wide"), axis=0, tiled=True),
        lax.all_gather(gain_one, ("batch", "wide"), axis=0, tiled=True),
        lax.all_gather(gain_two, ("batch", "wide"), axis=0, tiled=True),
    )
    seq_length, width = (inputs.shape[1], inputs.shape[2])
    tokens_in = inputs[0].astype(jnp.float32)
    seq_live = lengths[0]
    live_rows = jnp.arange(seq_length) < seq_live
    taps = full_taps.astype(jnp.float32)
    gain_first = full_gain_one.astype(jnp.float32)
    gain_second = full_gain_two.astype(jnp.float32)
    hat_one, inv_one = norm_parts(tokens_in)
    normed_one = (hat_one * gain_first).astype(jnp.bfloat16)
    projected = jnp.dot(normed_one, full_qkv, preferred_element_type=jnp.float32)
    mixed = (
        projected * taps[:, 0]
        + shift_down(projected, 1) * taps[:, 1]
        + shift_down(projected, 2) * taps[:, 2]
    ).astype(jnp.bfloat16)
    query = mixed[:, :width].reshape(seq_length, HEADS, HD)
    keys = mixed[:, width : 2 * width].reshape(seq_length, HEADS, HD)
    values = mixed[:, 2 * width :].reshape(seq_length, HEADS, HD)
    rows_block = min(512, seq_length)
    block_index = 0
    start_row = block_index * rows_block
    scores, allowed = scores_block(query, keys, start_row, seq_live)
    masked = jnp.where(allowed, scores, -1e30)
    top_score = jnp.max(masked, axis=-1, keepdims=True)
    exp_terms = jnp.exp(masked - top_score)
    row_totals = jnp.sum(exp_terms, axis=-1, keepdims=True)
    probs_low = (exp_terms / row_totals).astype(jnp.bfloat16)
    out_parts = jnp.einsum("hqk,khd->qhd", probs_low, values, preferred_element_type=jnp.float32)
    lse_parts = [top_score + jnp.log(row_totals)]
    attended_low = out_parts.reshape(seq_length, width).astype(jnp.bfloat16)
    branch_attn = jnp.dot(attended_low, full_out, preferred_element_type=jnp.float32)
    residual = tokens_in + branch_attn
    hat_two, inv_two = norm_parts(residual)
    normed_two = (hat_two * gain_second).astype(jnp.bfloat16)
    grad_out = jnp.where(live_rows[:, None], cotangent[0], jnp.zeros_like(cotangent[0]))
    row_set = lax.all_gather(normed_two[None], "wide", axis=0, tiled=True).reshape(-1, width)
    pre_act = jnp.dot(row_set, w_in, preferred_element_type=jnp.float32)
    activ = jnp.square(jax.nn.relu(pre_act)).astype(jnp.bfloat16)
    piece = activ
    branch_ffn = lax.psum_scatter(
        jnp.dot(piece, w_fc2, preferred_element_type=jnp.float32).astype(jnp.bfloat16),
        "wide",
        scatter_dimension=0,
        tiled=True,
    ).astype(jnp.float32)
    grad_set = lax.all_gather(grad_out[None], "wide", axis=0, tiled=True).reshape(-1, width)
    grad_act = contract_last(grad_set, w_fc2)
    grad_fc2_part = contract_first(activ, grad_set)
    grad_pre = (grad_act * 2.0 * jax.nn.relu(pre_act)).astype(jnp.bfloat16)
    grad_in_part = contract_first(row_set, grad_pre)
    piece = grad_pre
    grad_normed_two = lax.psum_scatter(
        contract_last(piece, w_in).astype(jnp.bfloat16), "wide", scatter_dimension=0, tiled=True
    ).astype(jnp.float32)
    grad_w_in, grad_w_fc2 = (
        lax.psum_scatter(
            grad_in_part.astype(jnp.bfloat16), "batch", scatter_dimension=0, tiled=True
        ).astype(jnp.float32),
        lax.psum_scatter(
            grad_fc2_part.astype(jnp.bfloat16), "batch", scatter_dimension=1, tiled=True
        ).astype(jnp.float32),
    )
    output = jnp.where(live_rows[:, None], residual + branch_ffn, 0.0).astype(jnp.bfloat16)[None]
    grad_ln_two, grad_gain_second = norm_back(grad_normed_two, gain_second, hat_two, inv_two)
    grad_residual = grad_out.astype(jnp.float32) + grad_ln_two
    grad_branch = grad_residual.astype(jnp.bfloat16)
    grad_w_out_part = contract_first(attended_low, grad_branch)
    grad_attended = contract_last(grad_branch, full_out).astype(jnp.bfloat16)
    grad_att_heads = grad_attended.reshape(seq_length, HEADS, HD)
    delta_all = jnp.sum(grad_att_heads.astype(jnp.float32) * out_parts, axis=-1)
    block_index = 0
    start_row = block_index * rows_block
    scores, allowed = scores_block(query, keys, start_row, seq_live)
    probs_full = jnp.where(allowed, jnp.exp(scores - lse_parts[block_index]), 0.0)
    probs_low = probs_full.astype(jnp.bfloat16)
    grad_probs = jnp.einsum(
        "qhd,khd->hqk", grad_att_heads, values, preferred_element_type=jnp.float32
    )
    delta_block = jnp.transpose(delta_all)[:, :, None]
    grad_scores = (probs_full * (grad_probs - delta_block)).astype(jnp.bfloat16)
    grad_query_parts = 0.125 * jnp.einsum(
        "hqk,khd->qhd", grad_scores, keys, preferred_element_type=jnp.float32
    )
    grad_keys = 0.125 * jnp.einsum(
        "hqk,qhd->khd", grad_scores, query, preferred_element_type=jnp.float32
    )
    grad_values = jnp.einsum(
        "hqk,qhd->khd", probs_low, grad_att_heads, preferred_element_type=jnp.float32
    )
    grad_mixed = jnp.concatenate(
        [
            grad_query_parts.reshape(seq_length, width),
            grad_keys.reshape(seq_length, width),
            grad_values.reshape(seq_length, width),
        ],
        axis=1,
    )
    grad_taps_part = jnp.stack(
        [
            jnp.sum(grad_mixed * projected, axis=0),
            jnp.sum(grad_mixed * shift_down(projected, 1), axis=0),
            jnp.sum(grad_mixed * shift_down(projected, 2), axis=0),
        ],
        axis=1,
    )
    grad_projected = (
        grad_mixed * taps[:, 0]
        + shift_up(grad_mixed, 1) * taps[:, 1]
        + shift_up(grad_mixed, 2) * taps[:, 2]
    ).astype(jnp.bfloat16)
    grad_qkv_part = contract_first(normed_one, grad_projected)
    grad_normed_one = contract_last(grad_projected, full_qkv)
    grad_ln_one, grad_gain_first = norm_back(grad_normed_one, gain_first, hat_one, inv_one)
    grad_inputs = (grad_residual + grad_ln_one).astype(jnp.bfloat16)[None]
    grad_w_qkv, grad_w_out, grad_conv_taps, grad_gain_one, grad_gain_two = (
        lax.psum_scatter(grad_qkv_part, ("batch", "wide"), scatter_dimension=0, tiled=True),
        lax.psum_scatter(grad_w_out_part, ("batch", "wide"), scatter_dimension=0, tiled=True),
        lax.psum_scatter(grad_taps_part, ("batch", "wide"), scatter_dimension=0, tiled=True),
        lax.psum_scatter(grad_gain_first, ("batch", "wide"), scatter_dimension=0, tiled=True),
        lax.psum_scatter(grad_gain_second, ("batch", "wide"), scatter_dimension=0, tiled=True),
    )
    return (
        output,
        grad_inputs,
        grad_w_qkv,
        grad_w_out,
        grad_conv_taps,
        grad_gain_one,
        grad_gain_two,
        grad_w_in,
        grad_w_fc2,
    )


BF = jnp.bfloat16
F32 = jnp.float32
AXES = ("batch", "wide")
LANES = 256
PART = 128
VMEM_MIB = {"ffn": 22}


def fits(mesh, args):
    inputs, w_qkv, w_in = args[0], args[3], args[8]
    count = mesh.shape["batch"] * mesh.shape["wide"]
    return (
        mesh.shape["batch"] == 4
        and mesh.shape["wide"] == 8
        and inputs.shape[0] == count
        and inputs.shape[1] % LANES == 0
        and w_qkv.shape[0] % (count * 8) == 0
        and w_qkv.shape[0] % LANES == 0
        and w_qkv.shape[0] // HEADS == HD
        and w_in.shape[1] == 8 * 3 * PART
        and (w_in.shape[0] // 4) % 16 == 0
    )


def dot(left, right, left_dim, right_dim):
    return lax.dot_general(
        left, right, (((left_dim,), (right_dim,)), ((), ())), preferred_element_type=F32
    )


def flip_pairs(rule):
    return [(i, i ^ rule(i)) for i in range(32)]


def send(array, rule):
    return lax.ppermute(array, AXES, flip_pairs(rule))


def over_core(i):
    return 8


def over_first(i):
    return 16 if i & 8 else 1


def over_second(i):
    return 1 if i & 8 else 16


def over_z(step):
    return lambda i: 2 * step


def tie(value, *others):
    return lax.optimization_barrier((value,) + others)[0]


def join(parts):
    return jnp.concatenate(parts)


def added(keep, come):
    return (keep.astype(F32) + come.astype(F32)).astype(BF)


def halved(keep, come):
    half = keep.shape[0] // 2
    return added(keep[:half], come[:half]), added(keep[half:], come[half:])


def place_of(me, other):
    apart = me ^ other
    x_bit, z_bits = apart & 1, (apart & 2) | ((apart >> 2) & 1)
    core_bit, y_bit = (apart >> 3) & 1, (apart >> 4) & 1
    on_first = ((other >> 3) & 1) == 0
    high = jnp.where(on_first, y_bit, x_bit)
    low = jnp.where(on_first, x_bit, y_bit)
    return core_bit * 16 + high * 8 + low * 4 + z_bits


def call(kernel, grid, in_specs, out_specs, out_shape, scratch=(), busy=1, name=None, aliases=None):
    return pl.pallas_call(
        kernel,
        grid_spec=pltpu.PrefetchScalarGridSpec(
            num_scalar_prefetch=1,
            grid=grid,
            in_specs=in_specs,
            out_specs=out_specs,
            scratch_shapes=list(scratch),
        ),
        out_shape=out_shape,
        compiler_params=pltpu.CompilerParams(
            dimension_semantics=("arbitrary",) * len(grid), vmem_limit_bytes=VMEM_MIB.get(name, 20) * 1024 * 1024
        ),
        cost_estimate=pl.CostEstimate(flops=int(busy * 1.15e9), bytes_accessed=0, transcendentals=0),
        name=name,
        input_output_aliases=aliases or {},
    )


def whole(shape):
    zeros = (0,) * len(shape)
    return pl.BlockSpec(shape, lambda *_: zeros, pipeline_mode=pl.Buffered(1))


def hat_of(values_in):
    centered = values_in - jnp.mean(values_in, axis=-1, keepdims=True)
    inv_std = lax.rsqrt(jnp.mean(centered * centered, axis=-1, keepdims=True) + epsilon)
    return centered * inv_std, inv_std


def turned(value):
    return jnp.transpose(value.astype(F32)).astype(BF)


def prepare_kernel(meta, cot_ref, go_ref, got_ref):
    live = lax.broadcasted_iota(jnp.int32, (cot_ref.shape[0], 1), 0) < meta[33]
    value = jnp.where(live, cot_ref[...].astype(F32), 0.0)
    go_ref[...] = value.astype(BF)
    got_ref[...] = jnp.transpose(value).astype(BF)


def pack_kernel(meta, up_ref, down_ref, out_ref, a_ref, b_ref):
    half = up_ref.shape[0] // 2
    second_half, second_core = (meta[32] >> 1) == 1, (meta[32] & 1) == 1
    up = jnp.where(second_half, up_ref[half:, :], up_ref[:half, :])
    down = turned(jnp.where(second_half, down_ref[:, half:], down_ref[:, :half]))
    for i, part in enumerate((up, down)):
        a_ref[0, i * half : (i + 1) * half, :] = jnp.where(second_core, part[:, PART : 2 * PART], part[:, :PART])
    left, right = swap_halves(up[:, 2 * PART :], down[:, 2 * PART :])
    b_ref[0, :half, :] = jnp.where(second_core, right, left).astype(BF)
    rows = out_ref.shape[0]
    for c in range(out_ref.shape[1] // PART):
        b_ref[0, half + c * rows : half + (c + 1) * rows, :] = out_ref[:, c * PART : (c + 1) * PART]


def block_of(meta, i, own_ref, other_ref):
    place = meta[i]
    return jnp.where(place < 16, own_ref[place & 15], other_ref[place & 15])


def project_kernel(
    meta, x_ref, own_ref, other_ref, few_own_ref, few_other_ref,
    proj_ref, mixed_ref, wn_ref, nt_ref, taps_ref, gains_ref, normed,
):
    rows = own_ref.shape[1]
    step = pl.program_id(0)

    def few_of(device, lanes):
        block = block_of(meta, device, few_own_ref, few_other_ref)[:8].astype(F32)
        return jnp.concatenate([block, jnp.zeros((8, lanes - PART), F32)], axis=1)

    @pl.when(step == 0)
    def _():
        width = gains_ref.shape[1]
        lane = lax.broadcasted_iota(jnp.int32, (8, width), 1)
        gains = jnp.zeros((8, width), F32)
        for i in range(32):
            first = i * rows
            moved = pltpu.roll(few_of(i, width), first, 1)
            gains = jnp.where((lane >= first) & (lane < first + rows), moved, gains)
        gains_ref[...] = gains
        hat, _ = hat_of(x_ref[...].astype(F32))
        low = (hat * gains[3:4, :]).astype(BF)
        normed[...] = low
        flipped = turned(low)
        for i in range(32):
            nt_ref[meta[i]] = flipped[i * rows : (i + 1) * rows]

    channels = 3 * rows
    lane = lax.broadcasted_iota(jnp.int32, (8, LANES), 1)
    taps = jnp.zeros((8, LANES), F32)
    for i in range(LANES // channels + 2):
        device = jnp.minimum((step * LANES) // channels + i, 31)
        first = device * channels - step * LANES
        moved = pltpu.roll(few_of(device, LANES), (first + 2 * LANES) & (LANES - 1), 1)
        taps = jnp.where((lane >= first) & (lane < first + channels), moved, taps)
    taps_ref[...] = taps
    for i in range(32):
        wn_ref[i * rows : (i + 1) * rows, :] = block_of(meta, i, own_ref, other_ref)
    value = dot(normed[...], wn_ref[...], 1, 0)
    at = lax.broadcasted_iota(jnp.int32, value.shape, 0)
    one = jnp.where(at >= 1, pltpu.roll(value, 1, 0), 0.0)
    two = jnp.where(at >= 2, pltpu.roll(value, 2, 0), 0.0)
    mixed = value * taps[0:1, :] + one * taps[1:2, :] + two * taps[2:3, :]
    proj_ref[...] = value.astype(BF)
    mixed_ref[...] = mixed.astype(BF)


def head_row(head, scale=1.0):
    lane = lax.broadcasted_iota(jnp.int32, (1, LANES), 1)
    return jnp.where(lane // HD == head, scale, 0.0).astype(BF)


def allowed_in(meta, keys, first_query, queries):
    key = lax.broadcasted_iota(jnp.int32, (keys, queries), 0)
    query = first_query + lax.broadcasted_iota(jnp.int32, (1, queries), 1)
    return key < jnp.minimum(query + 1, meta[33])


def attend_kernel(meta, q_ref, k_ref, v_ref, out_ref, lse_ref, flipped):
    seq = q_ref.shape[0]
    tile = LANES
    values_t = turned(v_ref[...])
    keys = k_ref[...]
    for t in range(seq // tile):
        upto = (t + 1) * tile
        allowed = allowed_in(meta, upto, t * tile, tile)
        query = q_ref[t * tile : upto, :]
        for head in range(LANES // HD):
            scores = dot(keys[:upto], query * head_row(head, 0.125), 1, 1)
            scores = jnp.where(allowed, scores, -1e30)
            top = jnp.max(scores, axis=0, keepdims=True)
            terms = jnp.exp(scores - top)
            total = jnp.sum(terms, axis=0, keepdims=True)
            probs = (terms * (1.0 / total)).astype(BF)
            flipped[head * HD : (head + 1) * HD, t * tile : upto] = dot(
                values_t[head * HD : (head + 1) * HD, :upto], probs, 1, 0
            )
            lse_ref[0, head : head + 1, t * tile : upto] = top + jnp.log(total)
    out_ref[...] = jnp.transpose(flipped[...]).astype(BF)


def mend_kernel(meta, att_ref, own_ref, other_ref, x_ref, gain_ref, res_ref, n2_ref, n2t_ref, at_ref, wn_ref):
    flipped = turned(att_ref[...])
    rows = at_ref.shape[1]
    for i in range(32):
        at_ref[meta[i]] = flipped[i * rows : (i + 1) * rows]
        block = block_of(meta, i, own_ref, other_ref)
        for c in range(wn_ref.shape[1] // PART):
            wn_ref[i * rows : (i + 1) * rows, c * PART : (c + 1) * PART] = block[c * rows : (c + 1) * rows]
    residual = x_ref[...].astype(F32) + dot(att_ref[...], wn_ref[...], 1, 0)
    res_ref[...] = residual
    hat, _ = hat_of(residual)
    low = (hat * gain_ref[4:5, :]).astype(BF)
    n2_ref[...] = low
    n2t_ref[...] = turned(low)


def swap_halves(left, right):
    left, right = left.astype(F32), right.astype(F32)
    low = lax.broadcasted_iota(jnp.int32, (1, PART), 1) < PART // 2
    return (
        jnp.where(low, left, pltpu.roll(right, PART // 2, 1)),
        jnp.where(low, pltpu.roll(left, PART // 2, 1), right),
    )


def ffn_kernel(packed, meta, *refs):
    token_refs, refs = (refs[:4], refs[4:8]), refs[8:]
    count = 8 if packed else 4
    tiles, refs = refs[:count], refs[count:]
    if packed:
        branch_ref, grad_ref, branch_acc, grad_acc, low_ref, high_ref = refs
    else:
        sums_in, (branch_ref, grad_ref, both_ref, low_ref, high_ref, branch_acc, grad_acc) = refs[:4], refs[4:]
    sums = (branch_ref, grad_ref, branch_acc, grad_acc)
    step = pl.program_id(0)

    @pl.when(step == 0)
    def _():
        for i, ref in enumerate(sums):
            ref[...] = jnp.zeros_like(ref) if packed else sums_in[i][...]

    half = tiles[0].shape[1] if packed else tiles[0].shape[1] // 2
    if packed:
        blocks = [jnp.concatenate([tiles[2 * k][0], tiles[2 * k + 1][0]], axis=0) for k in range(4)]
        pairs = [swap_halves(blocks[0], blocks[1]), swap_halves(blocks[2], blocks[3])]
        w_up, w_down = (jnp.concatenate([pairs[0][i], pairs[1][i]], axis=1).astype(BF) for i in range(2))
    else:
        w_up, w_down = (
            jnp.concatenate(
                [
                    jnp.concatenate([tiles[2 * k + b][0, i * half : (i + 1) * half, :] for b in range(2)], axis=0)
                    for k in range(2)
                ],
                axis=1,
            )
            for i in range(2)
        )
    up_sum = down_sum = 0.0
    for i, (n2_ref, go_ref, n2t_ref, got_ref) in enumerate(token_refs):
        pre = jnp.maximum(dot(n2_ref[...], w_up, 1, 0), 0.0)
        activ = (pre * pre).astype(BF)
        grad_pre = (dot(go_ref[...], w_down, 1, 0) * 2.0 * pre).astype(BF)
        sums[2 * i][...] += dot(activ, w_down, 1, 1)
        sums[2 * i + 1][...] += dot(grad_pre, w_up, 1, 1)
        up_sum += dot(n2t_ref[...], grad_pre, 1, 0)
        down_sum += dot(got_ref[...], activ, 1, 0)
    first_wide = step * (4 if packed else 2)
    results = []
    for k in range(2):
        lanes = slice(k * PART, (k + 1) * PART)
        if packed:
            results += [(part,) for part in swap_halves(up_sum[:, lanes], down_sum[:, lanes])]
        else:
            results.append((up_sum[:, lanes], down_sum[:, lanes]))
    for k, parts in enumerate(results):
        for b in range(2):
            place = meta[b * 16 + (meta[32] & 1) * 8 + first_wide + k]
            for is_high, target in enumerate((low_ref, high_ref)):

                @pl.when((place >> 3) == is_high)
                def _(place=place, target=target, parts=parts, b=b):
                    for i, part in enumerate(parts):
                        target[place & 7, i * half : (i + 1) * half, :] = part[b * half : (b + 1) * half].astype(BF)

    if not packed:

        @pl.when(step == pl.num_programs(0) - 1)
        def _():
            seq = branch_acc.shape[0]
            both_ref[:seq, :] = branch_acc[...].astype(BF)
            both_ref[seq:, :] = grad_acc[...].astype(BF)


def turn_kernel(meta, grad_ref, branch_ref, come_ref, res_ref, gain_ref, go_ref, at_ref, wn_ref, out_ref, gres_ref, gatt_ref, ggain_ref, keep_ref, away_ref):
    residual = res_ref[...]
    seq = residual.shape[0]
    live = lax.broadcasted_iota(jnp.int32, (seq, 1), 0) < meta[33]
    branch = branch_ref[...] + come_ref[:seq, :].astype(F32)
    out_ref[...] = jnp.where(live, residual + branch, 0.0).astype(BF)
    hat, inv_std = hat_of(residual)
    grad = grad_ref[...] + come_ref[seq:, :].astype(F32)
    ggain_ref[...] = jnp.sum(grad * hat, axis=0, keepdims=True)
    scaled = grad * gain_ref[4:5, :]
    mean_first = jnp.mean(scaled, axis=-1, keepdims=True)
    mean_second = jnp.mean(scaled * hat, axis=-1, keepdims=True)
    grad_res = go_ref[...].astype(F32) + inv_std * (scaled - mean_first - hat * mean_second)
    gres_ref[...] = grad_res
    low = grad_res.astype(BF)
    gatt_ref[...] = dot(low, wn_ref[...], 1, 1).astype(BF)
    result = dot(at_ref[...], low, 1, 0)
    lanes = keep_ref.shape[2]
    chunks = result.shape[1] // lanes
    rows = keep_ref.shape[1] // chunks
    for i in range(32):
        target = away_ref if i >= 16 else keep_ref
        for c in range(chunks):
            target[i & 15, c * rows : (c + 1) * rows, :] = result[
                i * rows : (i + 1) * rows, c * lanes : (c + 1) * lanes
            ].astype(BF)


def attend_back_kernel(
    meta, q_ref, k_ref, v_ref, pq_ref, pk_ref, pv_ref, tq_ref, tk_ref, tv_ref, go_ref, out_ref, lse_ref,
    gq_ref, gk_ref, gv_ref, dtq_ref, dtk_ref, dtv_ref, flipped,
):
    seq = q_ref.shape[0]
    tile = LANES
    keys, values = k_ref[...], v_ref[...]
    keys_t = turned(keys)
    delta_t = jnp.transpose(go_ref[...].astype(F32) * out_ref[...].astype(F32))
    grad_keys = [jnp.zeros((tile, LANES), F32) for _ in range(seq // tile)]
    grad_values = list(grad_keys)
    for t in range(seq // tile):
        upto = (t + 1) * tile
        allowed = allowed_in(meta, upto, t * tile, tile)
        query, grad = q_ref[t * tile : upto, :], go_ref[t * tile : upto, :]
        for head in range(LANES // HD):
            lanes = slice(head * HD, (head + 1) * HD)
            query_h, grad_h = query * head_row(head, 0.125), grad * head_row(head)
            delta = jnp.sum(delta_t[lanes, t * tile : upto], axis=0, keepdims=True)
            scores = dot(keys[:upto], query_h, 1, 1)
            lse = lse_ref[0, head : head + 1, t * tile : upto]
            probs = jnp.where(allowed, jnp.exp(scores - lse), 0.0)
            grad_scores = (probs * (dot(values[:upto], grad_h, 1, 1) - delta)).astype(BF)
            flipped[lanes, t * tile : upto] = dot(keys_t[lanes, :upto], grad_scores, 1, 0) * 0.125
            add_values = dot(probs.astype(BF), grad_h, 1, 0)
            add_keys = dot(grad_scores, query_h, 1, 0)
            for s in range(t + 1):
                rows = slice(s * tile, (s + 1) * tile)
                grad_values[s] += add_values[rows]
                grad_keys[s] += add_keys[rows]
    mixed = (
        jnp.transpose(flipped[...]),
        jnp.concatenate(grad_keys, axis=0),
        jnp.concatenate(grad_values, axis=0),
    )
    at = lax.broadcasted_iota(jnp.int32, (seq, LANES), 0)
    for grad, proj_ref, taps_ref, g_ref, dt_ref in zip(
        mixed, (pq_ref, pk_ref, pv_ref), (tq_ref, tk_ref, tv_ref), (gq_ref, gk_ref, gv_ref), (dtq_ref, dtk_ref, dtv_ref)
    ):
        one = jnp.where(at < seq - 1, pltpu.roll(grad, seq - 1, 0), 0.0)
        two = jnp.where(at < seq - 2, pltpu.roll(grad, seq - 2, 0), 0.0)
        g_ref[...] = (grad * taps_ref[0:1, :] + one * taps_ref[1:2, :] + two * taps_ref[2:3, :]).astype(BF)
        proj = proj_ref[...].astype(F32)
        for tap, part in enumerate((grad, one, two)):
            dt_ref[tap : tap + 1, :] = jnp.sum(part * proj, axis=0, keepdims=True)


def weight_kernel(with_few, meta, nt_ref, *refs):
    if with_few:
        (*tap_refs, gain_ref), refs, few = refs[:7], refs[7:-1], refs[-1]
    keep_ref, away_ref = refs[-2:]
    half, full = keep_ref.shape
    start = 0
    for g_ref in refs[:-2]:
        result = dot(nt_ref[...], g_ref[...], 1, 0).astype(BF)
        columns = slice(start, start + g_ref.shape[1])
        start += g_ref.shape[1]
        keep_ref[:, columns] = result[:half]
        away_ref[:, columns] = result[half:]
    if with_few:
        rows = half // 16
        row = lax.broadcasted_iota(jnp.int32, (8, PART), 0)
        lane = lax.broadcasted_iota(jnp.int32, (8, PART), 1)
        taps = jnp.concatenate([ref[...] for ref in tap_refs], axis=1)
        gains = jnp.broadcast_to(gain_ref[...], (8, gain_ref.shape[1]))

        def taken(values_in, first):
            start = first // PART * PART
            window = values_in[:, start : start + 2 * PART]
            return pltpu.roll(window, (start - first) % window.shape[1], 1)[:, :PART]

        for i in range(32):
            piece = jnp.where((row == 3) & (lane < rows), taken(gains, i * rows), 0.0)
            few[meta[i]] = jnp.where((row < 3) & (lane < 3 * rows), taken(taps, i * 3 * rows), piece)
        for i, ref in enumerate((keep_ref, away_ref)):
            ref[:, full - PART :] = jnp.zeros((half, PART), BF)
            for k in range(16):
                ref[k * rows : k * rows + 8, full - PART :] = few[i * 16 + k].astype(BF)


def last_kernel(meta, *refs):
    grads, (w_ref, x_ref, gain_ref, gres_ref, gin_ref) = refs[:-5], refs[-5:]
    grad = dot(jnp.concatenate([g_ref[...] for g_ref in grads], axis=1), w_ref[...], 1, 1)
    hat, inv_std = hat_of(x_ref[...].astype(F32))
    scaled = grad * gain_ref[3:4, :]
    mean_first = jnp.mean(scaled, axis=-1, keepdims=True)
    mean_second = jnp.mean(scaled * hat, axis=-1, keepdims=True)
    back = inv_std * (scaled - mean_first - hat * mean_second)
    gin_ref[...] = (gres_ref[...] + back).astype(BF)


def own_sequence(inputs, lengths, cotangent, w_qkv, w_out, conv_taps, gain_one, gain_two, w_in, w_fc2):
    seq, width = inputs.shape[1], inputs.shape[2]
    rows, wide = w_qkv.shape
    half = width // 2
    tap_rows = conv_taps.shape[0]
    batch = lax.axis_index("batch")
    core = batch & 1
    me = batch * 8 + lax.axis_index("wide")
    number = jnp.arange(64, dtype=jnp.int32)
    meta = jnp.where(number < 32, place_of(me, number & 31), jnp.where(number == 32, batch, lengths[0]))
    x, cot = inputs[0], cotangent[0]
    shape = jax.ShapeDtypeStruct
    row_spec = whole((1, width))
    gain_spec = whole((8, width))
    token = whole((seq, width))
    token_t = whole((width, seq))
    groups = width // LANES

    few_rows = [jnp.pad(conv_taps.T, ((0, 0), (0, PART - tap_rows)))]
    few_rows += [jnp.pad(gain[None], ((0, 0), (0, PART - rows))) for gain in (gain_one, gain_two)]
    few_rows = jnp.concatenate(few_rows + [jnp.zeros((rows - 5, PART), BF)])
    qkv_block = jnp.concatenate([w_qkv, few_rows], axis=1)[None]
    qkv_block, meta, first_core = lax.optimization_barrier((qkv_block, meta, core == 0))
    qkv_far = send(qkv_block, over_z(2))
    out_rows = rows * (width // PART)
    a_block, b_block = call(
        pack_kernel, (1,), [whole(w.shape) for w in (w_in, w_fc2, w_out)],
        [whole((1, width, PART)), whole((1, half + out_rows, PART))],
        [shape((1, width, PART), BF), shape((1, half + out_rows, PART), BF)], busy=2, name="pack",
    )(meta, w_in, w_fc2, w_out)

    b_far = send(tie(b_block, qkv_far), over_z(2))
    qkv2 = join([qkv_block, tie(qkv_far, b_block)])
    qkv_near = send(qkv2, over_z(1))
    qkv4 = join([qkv2, qkv_near])
    qkv_first = send(qkv4, over_first)
    b2 = join([b_block, tie(b_far, qkv4)])
    b_near = send(b2, over_z(1))
    a_far = send(tie(a_block, b2), over_z(2))
    qkv8 = join([qkv4, tie(qkv_first, b2)])
    qkv_second = send(qkv8, over_second)
    grad_out, grad_out_t = call(
        prepare_kernel, (1,), [token], [token, token_t],
        [shape((seq, width), BF), shape((width, seq), BF)], busy=1, name="prepare",
    )(meta, tie(cot, qkv_far))
    go_other = send(grad_out, over_core)
    got_other = send(grad_out_t, over_core)
    b4 = join([b2, tie(b_near, qkv8)])
    a2 = join([a_block, tie(a_far, qkv8)])
    a_near = send(a2, over_z(1))
    qkv16 = join([qkv8, tie(qkv_second, a2, b4)])
    qkv_core = send(qkv16, over_core)
    b_first = send(tie(b4, qkv16), over_first)

    lane_block = pl.BlockSpec((seq, LANES), lambda j, m: (0, j))
    half_block = pl.BlockSpec((16, rows, LANES), lambda j, m: (0, 0, j))
    few_block = pl.BlockSpec((16, rows, PART), lambda j, m: (0, 0, wide // PART))
    tap_block = pl.BlockSpec((8, LANES), lambda j, m: (0, j))
    projected, mixed, qkv_full, normed_t, taps, gains = call(
        project_kernel, (wide // LANES,),
        [token, half_block, half_block, few_block, few_block],
        [lane_block, lane_block, pl.BlockSpec((width, LANES), lambda j, m: (0, j)), whole((32, rows, seq)),
         tap_block, gain_spec],
        [shape((seq, wide), BF), shape((seq, wide), BF), shape((width, wide), BF), shape((32, rows, seq), BF),
         shape((8, wide), F32), shape((8, width), F32)],
        [pltpu.VMEM((seq, width), BF)], busy=7, name="project",
    )(meta, tie(x, a2, b4), qkv16, qkv_core, qkv16, qkv_core)

    a4 = join([a2, tie(a_near, mixed)])
    a_first = send(a4, over_first)
    b8 = join([b4, tie(b_first, mixed)])
    b_second = send(b8, over_second)
    part_specs = [pl.BlockSpec((seq, LANES), lambda j, m, p=p: (0, p * groups + j)) for p in range(3)]
    lse_spec = pl.BlockSpec((1, 8, seq), lambda j, m: (j, 0, 0))
    ready = tie(mixed, b8, a4, go_other, got_other)
    attended, lse = call(
        attend_kernel, (groups,), part_specs, [lane_block, lse_spec],
        [shape((seq, width), BF), shape((groups, 8, seq), F32)], [pltpu.VMEM((LANES, seq), F32)],
        busy=9, name="attend",
    )(meta, ready, ready, ready)

    b16 = join([b8, tie(b_second, attended)])
    out16 = b16[:, half:, :]
    out_core = send(out16, over_core)
    a8 = join([a4, tie(a_first, attended)])
    a_second = send(tie(a8, b16), over_second)
    residual, normed_two, normed_two_t, attended_t, out_full = call(
        mend_kernel, (1,),
        [token, whole(out16.shape), whole(out16.shape), token, gain_spec],
        [token, token, token_t, whole((32, rows, seq)), whole((width, width))],
        [shape((seq, width), F32), shape((seq, width), BF), shape((width, seq), BF), shape((32, rows, seq), BF),
         shape((width, width), BF)],
        busy=2.5, name="mend",
    )(meta, attended, out16, out_core, x, gains)
    n2_other = send(normed_two, over_core)
    n2t_other = send(normed_two_t, over_core)

    sequences = [normed_two, grad_out, normed_two_t, grad_out_t, n2_other, go_other, n2t_other, got_other]
    sequence_specs = [token, token, token_t, token_t] * 2

    def tile(block_rows, per_step, k, b):
        return pl.BlockSpec(
            (1, block_rows, PART), lambda s, m: (m[b * 16 + (m[32] & 1) * 8 + s * per_step + k], 0, 0)
        )

    total = shape((seq, width), F32)
    grads_b = shape((8, half, PART), BF)
    branch, grad_two, branch_o, grad_o, b_low, b_high = call(
        functools.partial(ffn_kernel, True), (2,),
        sequence_specs + [tile(half, 4, k, b) for k in range(4) for b in range(2)],
        [token] * 4 + [whole(grads_b.shape)] * 2, [total] * 4 + [grads_b] * 2, busy=2, name="ffn",
    )(meta, *sequences, *[b16] * 8)
    a16 = join([a8, tie(a_second, branch)])
    b_sum = send(b_high, over_second)
    grads_a = shape((8, width, PART), BF)
    branch, grad_two, both, a_low, a_high = call(
        functools.partial(ffn_kernel, False), (4,),
        sequence_specs + [tile(width, 2, k, b) for k in range(2) for b in range(2)] + [token] * 4,
        [token] * 2 + [whole((2 * seq, width))] + [whole(grads_a.shape)] * 2,
        [total] * 2 + [shape((2 * seq, width), BF)] + [grads_a] * 2,
        [pltpu.VMEM((seq, width), F32)] * 2, busy=15, name="ffn",
    )(meta, tie(normed_two, b_high), *sequences[1:], *[a16] * 4, branch, grad_two, branch_o, grad_o)
    b_sum = tie(b_sum, branch)
    come = send(tie(both, b_sum), over_core)
    a_sum = send(a_high, over_second)
    b_keep, b_go = halved(b_low, b_sum)
    half_out = shape((16, rows * (width // PART), PART), BF)
    output, grad_residual, grad_attended, grad_gain_second, keep_out, away_out = call(
        turn_kernel, (1,),
        [token] * 2 + [whole((2 * seq, width)), token, gain_spec, token, token_t, whole((width, width))],
        [token] * 3 + [row_spec, whole(half_out.shape), whole(half_out.shape)],
        [shape((seq, width), BF), shape((seq, width), F32), shape((seq, width), BF), shape((1, width), F32),
         half_out, half_out],
        busy=4, name="turn",
    )(meta, tie(grad_two, a_high, b_go), branch, come, residual, gains, grad_out, attended_t.reshape(width, seq), out_full)

    def attend_back(first, count, wait_for):
        def lanes(height, part, start):
            return pl.BlockSpec((height, LANES), lambda i, m: (0, part * groups + start + i))

        specs = [lanes(seq, p, first) for p in range(3)]
        tap_specs = [lanes(8, p, first) for p in range(3)]
        return call(
            attend_back_kernel, (count,),
            specs * 2 + tap_specs + [specs[0]] * 2 + [pl.BlockSpec((1, 8, seq), lambda i, m: (first + i, 0, 0))],
            [lanes(seq, 0, 0)] * 3 + [lanes(8, 0, 0)] * 3,
            [shape((seq, count * LANES), BF)] * 3 + [shape((8, count * LANES), F32)] * 3,
            [pltpu.VMEM((LANES, seq), F32)], busy=count, name="attend_back",
        )(meta, mixed, mixed, mixed, projected, projected, projected, taps, taps, taps,
          tie(grad_attended, *wait_for), attended, lse)

    def weights(grads, few, wait_for):
        size = sum(g.shape[1] for g in grads) + (PART if few else 0)
        spec = whole((half, size))
        keep, away = call(
            functools.partial(weight_kernel, bool(few)), (1,),
            [token_t] + [whole(part.shape) for part in [*few, *grads]],
            [spec, spec], [shape((half, size), BF)] * 2, [pltpu.VMEM((32, 8, PART), F32)] if few else (),
            busy=1, name="weight",
        )(meta, tie(normed_t.reshape(width, seq), *wait_for), *few, *grads)
        return keep.reshape(16, rows, size), away.reshape(16, rows, size)

    out_come = send(away_out, over_core)
    back0 = attend_back(0, groups - 1, (away_out,))

    out_sum = added(keep_out, tie(out_come, back0[0]))
    out_go = out_sum[8:]
    out_come = send(out_go, over_second)
    x_keep, x_away = weights(back0[:3], [], (out_go,))
    x_sum = send(x_away, over_core)
    a_keep, a_go = halved(a_low, tie(a_sum, x_away))
    a_sum = send(a_go, over_first)
    back2 = attend_back(groups - 1, 1, (back0[0], x_away, a_go))
    backs = (back0, back2)
    grad_projected = [back[part] for part in range(3) for back in backs]
    few = [back[3 + part] for part in range(3) for back in backs] + [grad_gain_second]
    y_keep, y_away = weights(back2[:3], few, ())
    y_sum = send(y_away, over_core)

    out_keep, out_go = halved(out_sum[:8], tie(out_come, y_away))
    b_keep = jnp.concatenate([b_keep, out_keep], axis=1)
    b_go = jnp.concatenate([b_go, out_go], axis=1)
    b_sum = send(b_go, over_first)
    x_keep, x_go = halved(x_keep, tie(x_sum, y_away))
    x_sum = send(x_go, over_second)
    a_keep, a_go = halved(a_keep, tie(a_sum, x_go))
    a_sum = send(a_go, over_z(1))
    grad_inputs = call(
        last_kernel, (1,),
        [whole(g.shape) for g in grad_projected] + [whole((width, wide)), token, gain_spec, token],
        [token], [shape((seq, width), BF)], busy=4, name="last",
    )(meta, *grad_projected, qkv_full, x, gains, tie(grad_residual, y_away, a_go, b_go, x_go))[0]
    y_keep, y_go = halved(y_keep, tie(y_sum, grad_inputs))
    y_sum = send(y_go, over_second)
    b_keep, b_go = halved(b_keep, tie(b_sum, y_go))
    b_sum = send(b_go, over_z(1))
    a_keep, a_go = halved(a_keep, tie(a_sum, b_go))
    a_sum = send(a_go, over_z(2))
    x_keep, x_go = halved(x_keep, tie(x_sum, a_go))
    x_sum = send(x_go, over_first)
    y_keep, y_go = halved(y_keep, tie(y_sum, x_go))
    y_sum = send(y_go, over_first)
    b_keep, b_go = halved(b_keep, tie(b_sum, y_go))
    b_sum = send(b_go, over_z(2))
    x_keep, x_go = halved(x_keep, tie(x_sum, b_go))
    x_sum = send(x_go, over_z(1))
    y_keep, y_go = halved(y_keep, tie(y_sum, x_go))
    y_sum = send(y_go, over_z(1))
    x_keep, x_go = halved(x_keep, tie(x_sum, y_go))
    x_sum = send(x_go, over_z(2))
    y_keep, y_go = halved(y_keep, tie(y_sum, x_go))
    y_sum = send(y_go, over_z(2))
    grad_a = a_keep[0].astype(F32) + tie(a_sum, y_go)[0].astype(F32)
    grad_b = b_keep[0].astype(F32) + tie(b_sum, y_go)[0].astype(F32)
    grad_out_w = jnp.transpose(grad_b[half:].reshape(width // PART, rows, PART), (1, 0, 2)).reshape(rows, width)
    quarter = width // 4

    def share(swapped):
        pairs = [
            (g[first : first + quarter], g[first + quarter : first + 2 * quarter])
            for g, first in ((grad_a, 0), (grad_a, half), (grad_b, 0))
        ]
        return jnp.concatenate([jnp.where(first_core, p[swapped], p[1 - swapped]) for p in pairs])

    mine = share(0)
    theirs = send(share(1), over_core)
    mine, theirs = jnp.where(first_core, mine, theirs), jnp.where(first_core, theirs, mine)
    units = PART // 2
    grad_in_w, grad_fc2_w = (
        jnp.concatenate(
            [part[i * quarter : (i + 1) * quarter] for part in (mine, theirs)]
            + [part[2 * quarter :, i * units : (i + 1) * units] for part in (mine, theirs)],
            axis=1,
        )
        for i in range(2)
    )

    x_total = x_keep[0].astype(F32) + x_sum[0].astype(F32)
    y_total = y_keep[0].astype(F32) + y_sum[0].astype(F32)
    few = y_total[:8, 3 * LANES :]
    grad_qkv = jnp.concatenate(
        [
            part
            for i in range(3)
            for part in (x_total[:, 2 * i * LANES : 2 * (i + 1) * LANES], y_total[:, i * LANES : (i + 1) * LANES])
        ],
        axis=1,
    )
    grad_gain_first = jnp.sum(grad_qkv * w_qkv.astype(F32), axis=1) / gain_one.astype(F32)
    return (
        output[None],
        grad_inputs[None],
        grad_qkv,
        grad_out_w,
        few[:3, :tap_rows].T,
        grad_gain_first,
        few[3, :rows],
        grad_in_w,
        jnp.transpose(grad_fc2_w),
    )


def solution(mesh):
    fast = functools.partial(own_sequence)

    def program(*args):
        body = fast if fits(mesh, args) else shards
        return jax.shard_map(
            body,
            mesh=mesh,
            in_specs=(
                P(("batch", "wide"), None, None),
                P(("batch", "wide")),
                P(("batch", "wide"), None, None),
                P(("batch", "wide"), None),
                P(("batch", "wide"), None),
                P(("batch", "wide"), None),
                P(("batch", "wide")),
                P(("batch", "wide")),
                P(None, "wide"),
                P("wide", None),
            ),
            out_specs=(
                P(("batch", "wide"), None, None),
                P(("batch", "wide"), None, None),
                P(("batch", "wide"), None),
                P(("batch", "wide"), None),
                P(("batch", "wide"), None),
                P(("batch", "wide")),
                P(("batch", "wide")),
                P("batch", "wide"),
                P("wide", "batch"),
            ),
            check_vma=False,
        )(*args)

    return program
```
